32 devices in a mesh: expert: 4 (over y, core), shard: 8 (over z, x).
Axes of the slice: x: 2, y: 2, z: 4, core: 2. Of those that a mesh axis runs over, the one named last changes fastest.
Arguments:
- tokens: bfloat16 [12288, 768], P(('expert', 'shard')), may hold values from -6 to 6
- seq_lengths: int32 [32], P(('expert', 'shard')), may hold values from 96 to 384, as said below
- routes: int32 [12288, 2], P(('expert', 'shard')), may hold values from 0 to 7, all different within a row
- pair_order: int32 [32, 768], P(('expert', 'shard')), may hold values from 0 to 767, each once within a row
- prev_logits: float32 [12288, 8], P(('expert', 'shard')), may hold values from -6 to 6
- out_grad: bfloat16 [12288, 768], P(('expert', 'shard')), may hold values from -6 to 6
- qkv_weight: bfloat16 [768, 2304], P('shard'), may hold values from -0.21875 to 0.21875
- out_weight: bfloat16 [768, 768], P('shard'), may hold values from -0.875 to 0.875
- gate_weight: bfloat16 [768, 8], P('shard'), may hold values from -0.15625 to 0.15625
- const_weight: bfloat16 [768, 4], P('shard'), may hold values from -0.21875 to 0.21875
- const_vector: bfloat16 [768, 2], P('shard'), may hold values from -6 to 6
- norm1_gain: bfloat16 [768], P('shard'), may hold values from 0.5 to 1.5
- norm2_gain: bfloat16 [768], P('shard'), may hold values from 0.5 to 1.5
- gate_mix: bfloat16 [8, 8], replicated, may hold values from -1 to 1
- expert_up: bfloat16 [4, 768, 4096], P('expert', 'shard'), may hold values from -0.21875 to 0.21875
- expert_down: bfloat16 [4, 2048, 768], P('expert', 'shard'), may hold values from -0.25 to 0.25
Outputs:
- block_out: bfloat16 [12288, 768], P(('expert', 'shard'))
- tokens_grad: float32 [12288, 768], P(('expert', 'shard'))
- prev_grad: float32 [12288, 8], P(('expert', 'shard'))
- qkv_grad: float32 [768, 2304], P('shard')
- out_weight_grad: float32 [768, 768], P('shard')
- gate_grad: float32 [768, 8], P('shard')
- const_weight_grad: float32 [768, 4], P('shard')
- const_vector_grad: float32 [768, 2], P('shard')
- norm1_grad: float32 [768], P('shard')
- norm2_grad: float32 [768], P('shard')
- mix_grad: float32 [8, 8], replicated
- expert_up_grad: float32 [4, 768, 4096], P('expert', 'shard')
- expert_down_grad: float32 [4, 2048, 768], P('expert', 'shard')
The draws below stay inside these ranges and needn't reach their ends.
Inputs may be any that keep to these rules, and one draw needn't show every extreme that they name: `routes`: each token names two different experts; every expert is named by some token. `pair_order`: each row holds every pair index once. `seq_lengths`: some sequence fills all 384 slots and some uses a quarter of them.
All inputs are finite; a program needn't handle non-finite values.
Results may differ from the reference program's by a relative error of at most 0.013.
Values may be sent and summed in bfloat16 or wider, within the bound.
A program may use at most 128 MiB of HBM per device.

```python
import jax
import jax.numpy as jnp
from jax import lax

D = 768
FF = 2048
HEADS = 12
HEAD_DIM = 64
TOK_DEV = 384
FFN_EXPERTS = 4
ALL_EXPERTS = 8
TOKENS = 12288
N_EXPERT = 4
N_SHARD = 8
DEVICES = 32


def draw_seq_lengths(key, part):
    first_key = jax.random.fold_in(key, 11)
    second_key = jax.random.fold_in(key, 12)
    third_key = jax.random.fold_in(key, 13)
    lengths = jax.random.randint(first_key, (DEVICES,), TOK_DEV // 4, TOK_DEV + 1)
    longest = jax.random.randint(second_key, (), 0, DEVICES)
    shortest = (longest + 1 + jax.random.randint(third_key, (), 0, DEVICES - 1)) % DEVICES
    lengths = lengths.at[shortest].set(TOK_DEV // 4).at[longest].set(TOK_DEV)
    return lengths.astype(jnp.int32)


def with_spikes(entries, stream_key, source, target, parts, factor):
    owner, partner = [(jnp.arange(entries.shape[position]) // (entries.shape[position] // parts)).reshape([-1 if axis == position else 1 for axis in range(entries.ndim)]) for position in (source, target)]
    chosen = jax.random.permutation(stream_key, parts)[partner]
    strong = (owner == chosen) | (owner == (partner + parts // 2) % parts)
    return jnp.where(strong, factor * entries, entries)


def steps_of(key, extent, split, least, high):
    def one(dim, parts):
        steps = jax.random.uniform(jax.random.fold_in(jax.random.fold_in(key, 6), dim), (parts,), jnp.float32, least / len(split), high / len(split))
        return jnp.repeat(jnp.exp(steps), extent[dim] // parts).reshape((-1,) + (1,) * (len(extent) - dim - 1))

    factor_of = one(*split[0])
    for cut in split[1:]:
        factor_of = factor_of * one(*cut)
    return factor_of


def distinct(stream_key, rows, count, top, lift):
    order = jax.random.permutation(jax.random.fold_in(stream_key, 1), count)
    pull = order
    for power in range(3):
        pull = pull * pull // count
    pull = pull * lift // count
    tickets = jax.random.randint(jax.random.fold_in(stream_key, 2), (rows, count), 0, 4096) + pull
    holders = jax.random.permutation(jax.random.fold_in(stream_key, 3), rows)[jnp.arange(count) % rows]
    tickets = jnp.where(jnp.arange(rows)[:, None] == holders[None, :], 1 << 14, tickets)
    merit = tickets * count + jnp.arange(count)
    return lax.top_k(merit.astype(jnp.int32), top)[1].astype(jnp.int32)


def normal_values(rng, extent, deviation, reach, shards=(), held_as=jnp.bfloat16):
    values = jax.random.normal(rng, extent, jnp.float32) * deviation
    if len(shards) > 0:
        values = steps_of(rng, extent, shards, -0.22, 0.18) * values
    return jnp.clip(values, min=-reach, max=reach).astype(held_as)


def noise_with(key, shape, width, bound, shards, heavy, held_as=jnp.bfloat16):
    entries = width * jax.random.normal(key, shape, jnp.float32)
    if shards:
        entries = entries * steps_of(key, shape, shards, -0.22, 0.18)
    return jnp.clip(with_spikes(entries, jax.random.fold_in(key, 3), *heavy), -bound, bound).astype(held_as)


def setup_inputs(seed: int = 0) -> dict:
    seeds = jax.random.split(jax.random.key(seed), 17)
    tokens = noise_with(seeds[0], (TOKENS, D), 1.0, 6.0, ((0, 32),), (0, 1, 32, 2.75))
    seq_lengths = draw_seq_lengths(jax.random.fold_in(seeds[16], 71), 0)
    routes = distinct(seeds[2], TOKENS, ALL_EXPERTS, 2, 2048)
    pair_order = jax.vmap(lambda own: jax.random.permutation(own, 2 * TOK_DEV))(jax.random.split(seeds[3], (N_EXPERT * N_SHARD))).reshape((N_EXPERT * N_SHARD, 2 * TOK_DEV)).astype(jnp.int32)
    prev_logits = normal_values(seeds[4], (TOKENS, ALL_EXPERTS), 1.0, 6.0, ((0, 32),), jnp.float32)
    out_grad = normal_values(seeds[5], (TOKENS, D), 1.0, 6.0, ((0, 32),))
    qkv_weight = normal_values(seeds[6], (D, 3 * D), D ** -0.5, 0.21875, ((0, 8),))
    out_weight = normal_values(seeds[7], (D, D), (D // 16) ** -0.5, 0.875, ((0, 8),))
    gate_weight = normal_values(seeds[8], (D, ALL_EXPERTS), (2 * D) ** -0.5, 0.15625, ((0, 8),))
    const_weight = normal_values(seeds[9], (D, 4), D ** -0.5, 0.21875, ((0, 8),))
    const_vector = normal_values(seeds[10], (D, 2), 1.0, 6.0, ((0, 8),))
    norm1_gain = jnp.clip(1.0 + 0.1 * jax.random.normal(seeds[11], (D,), jnp.float32), 0.5, 1.5).astype(jnp.bfloat16)
    norm2_gain = jnp.clip(1.0 + 0.1 * jax.random.normal(seeds[12], (D,), jnp.float32), 0.5, 1.5).astype(jnp.bfloat16)
    gate_mix = normal_values(seeds[13], (ALL_EXPERTS, ALL_EXPERTS), (4 * ALL_EXPERTS) ** -0.5, 1.0)
    expert_up = normal_values(seeds[14], (FFN_EXPERTS, D, 2 * FF), D ** -0.5, 0.21875, ((0, 4), (1, 8)))
    expert_down = normal_values(seeds[15], (FFN_EXPERTS, FF, D), (FF // 4) ** -0.5, 0.25, ((0, 4), (1, 8)))
    return dict(tokens=tokens, seq_lengths=seq_lengths, routes=routes, pair_order=pair_order, prev_logits=prev_logits, out_grad=out_grad, qkv_weight=qkv_weight, out_weight=out_weight, gate_weight=gate_weight, const_weight=const_weight, const_vector=const_vector, norm1_gain=norm1_gain, norm2_gain=norm2_gain, gate_mix=gate_mix, expert_up=expert_up, expert_down=expert_down)


norm_eps = 1e-06
rotary_base = 10000.0
highest = lax.Precision.HIGHEST

@jax.custom_vjp
def low(v):
    return lax.optimization_barrier(v.astype(jnp.bfloat16)).astype(jnp.float32)

@jax.custom_vjp
def low_back(v):
    return v

def low_keep(v):
    return (low(v), None)

def low_pass(kept, grad):
    return (grad,)

def back_keep(v):
    return (v, None)

def back_low(kept, grad):
    return (low(grad),)
low.defvjp(low_keep, low_pass)
low_back.defvjp(back_keep, back_low)

def tables(tok_rows, head_dim):
    half_dim = head_dim // 2
    frequency = rotary_base ** (-(jnp.arange(half_dim, dtype=jnp.float32) * 2.0 / head_dim))
    angles = jnp.arange(tok_rows, dtype=jnp.float32)[:, None] * frequency[None, :]
    return (jnp.cos(angles)[:, None, :], jnp.sin(angles)[:, None, :])

def rotate(field, cosine, sine_table):
    half_dim = field.shape[-1] // 2
    first_half = field[..., :half_dim]
    second_half = field[..., half_dim:]
    return jnp.concatenate([first_half * cosine - second_half * sine_table, second_half * cosine + first_half * sine_table], axis=-1)

def place_pairs(route_rows, order, length, experts_ffn, capacity):
    tok_rows = route_rows.shape[0]
    token_ids = jnp.arange(tok_rows, dtype=jnp.int32)
    pair_valid = jnp.repeat(token_ids < length, 2)
    expert_flat = route_rows.reshape(-1)
    placed_expert = expert_flat[order]
    placed_live = pair_valid[order] & (placed_expert < experts_ffn)
    one_hot = (placed_expert[:, None] == jnp.arange(experts_ffn, dtype=jnp.int32)[None, :]) & placed_live[:, None]
    counts = jnp.cumsum(one_hot.astype(jnp.int32), axis=0)
    slot_index = lax.optimization_barrier(jnp.sum(jnp.where(one_hot, counts - 1, 0), axis=1)).astype(jnp.int32)
    kept_pairs = placed_live & (slot_index < capacity)
    dest_placed = jnp.where(kept_pairs, placed_expert * capacity + slot_index, experts_ffn * capacity).astype(jnp.int32)
    pair_dest = jnp.zeros((2 * tok_rows,), jnp.int32).at[order].set(dest_placed)
    slot_pair = jnp.full((experts_ffn * capacity,), 2 * tok_rows, jnp.int32).at[dest_placed].set(order.astype(jnp.int32), mode='drop')
    return (pair_dest, slot_pair)

def block_layer(inputs, prev_rows, route_rows, order, length, dense, experts):
    weight_qkv, weight_out, weight_gate, weight_const, vector_const, gain_one, gain_two, gate_mixer = dense
    weight_up, weight_down = experts
    tok_rows = inputs.shape[0]
    experts_ffn = weight_up.shape[0]
    capacity = 2 * tok_rows // (experts_ffn + 4)
    token_ids = jnp.arange(tok_rows, dtype=jnp.int32)
    valid_mask = (token_ids < length).astype(jnp.float32)[:, None]
    scale_one = lax.rsqrt(lax.optimization_barrier(jnp.mean(inputs * inputs, axis=1, keepdims=True)) + norm_eps)
    normed = low(inputs * scale_one * gain_one)
    qkv_all = low_back(jnp.dot(normed, weight_qkv, precision=highest))
    cosine, sine_table = tables(tok_rows, HEAD_DIM)
    query = low(rotate(qkv_all[:, :D].reshape(tok_rows, HEADS, HEAD_DIM), cosine, sine_table))
    keys_rot = low(rotate(qkv_all[:, D:2 * D].reshape(tok_rows, HEADS, HEAD_DIM), cosine, sine_table))
    values = low(qkv_all[:, 2 * D:].reshape(tok_rows, HEADS, HEAD_DIM))
    scores = low_back(jnp.einsum('qhd,khd->hqk', query, keys_rot, precision=highest) * HEAD_DIM ** (-0.5))
    allowed = (token_ids[None, :] <= token_ids[:, None]) & (token_ids[None, :] < length)
    scores = jnp.where(allowed[None], scores, -1e+30)
    top_score = lax.optimization_barrier(jnp.max(scores, axis=2, keepdims=True))
    expo = jnp.exp(scores - top_score)
    probs = expo / lax.optimization_barrier(jnp.sum(expo, axis=2, keepdims=True))
    mixed = jnp.einsum('hqk,khd->qhd', low(probs), values, precision=highest).reshape(tok_rows, D)
    mixed = low_back(low(mixed))
    hidden = inputs + low_back(jnp.dot(mixed, weight_out, precision=highest))
    scale_two = lax.rsqrt(lax.optimization_barrier(jnp.mean(hidden * hidden, axis=1, keepdims=True)) + norm_eps)
    normed_two = hidden * scale_two * gain_two
    normed_low = low(normed_two)
    logits = low_back(jnp.dot(normed_low, weight_gate, precision=highest)) + jnp.dot(prev_rows, gate_mixer, precision=highest)
    chosen = jnp.take_along_axis(logits, route_rows, axis=1)
    gate_exp = jnp.exp(chosen - lax.optimization_barrier(jnp.max(chosen, axis=1, keepdims=True)))
    gates = gate_exp / lax.optimization_barrier(jnp.sum(gate_exp, axis=1, keepdims=True))
    pair_dest, slot_pair = place_pairs(route_rows, order, length, experts_ffn, capacity)
    padded = jnp.concatenate([normed_low, jnp.zeros((1, D), jnp.float32)], axis=0)
    buffer = low_back(padded[slot_pair // 2]).reshape(experts_ffn, capacity, D)
    gate_up = low_back(jnp.einsum('ecd,edf->ecf', buffer, weight_up, precision=highest))
    activated = low(jax.nn.silu(gate_up[..., :FF]) * gate_up[..., FF:])
    expert_out = low_back(low(jnp.einsum('ecf,efd->ecd', activated, weight_down, precision=highest)))
    expert_pad = jnp.concatenate([expert_out.reshape(-1, D), jnp.zeros((1, D), jnp.float32)], axis=0)
    pair_ffn = expert_pad[pair_dest].reshape(tok_rows, 2, D)
    const_logits = jnp.dot(normed_low, weight_const, precision=highest).reshape(tok_rows, 2, 2)
    const_exp = jnp.exp(const_logits - lax.optimization_barrier(jnp.max(const_logits, axis=2, keepdims=True)))
    coefs = const_exp / lax.optimization_barrier(jnp.sum(const_exp, axis=2, keepdims=True))
    const_out = coefs[..., 0:1] * normed_two[:, None, :] + coefs[..., 1:2] * vector_const.T[None, :, :]
    const_select = (route_rows[:, :, None] == experts_ffn + 2 + jnp.arange(2, dtype=jnp.int32)[None, None, :]).astype(jnp.float32)
    copy_select = (route_rows == experts_ffn + 1).astype(jnp.float32)[:, :, None]
    pair_out = pair_ffn + copy_select * normed_two[:, None, :] + jnp.einsum('tkc,tcd->tkd', const_select, const_out, precision=highest)
    mixture = lax.optimization_barrier(jnp.sum(gates[:, :, None] * pair_out, axis=1))
    return valid_mask * (hidden + mixture)

def reference(tokens, seq_lengths, routes, pair_order, prev_logits, out_grad, qkv_weight, out_weight, gate_weight, const_weight, const_vector, norm1_gain, norm2_gain, gate_mix, expert_up, expert_down):
    count = seq_lengths.shape[0]
    tok_rows = tokens.shape[0] // count
    dense = tuple((array.astype(jnp.float32) for array in (qkv_weight, out_weight, gate_weight, const_weight, const_vector, norm1_gain, norm2_gain, gate_mix)))
    experts = (expert_up.astype(jnp.float32), expert_down.astype(jnp.float32))
    inputs = tokens.astype(jnp.float32).reshape(count, tok_rows, D)
    prev_all = prev_logits.reshape(count, tok_rows, -1)
    route_seq = routes.reshape(count, tok_rows, 2)
    step_fn = jax.checkpoint(block_layer)

    def forward(input_all, prev_seq, dense_args, expert_args):

        def scan_step(carry, slices):
            return (carry, step_fn(slices[0], slices[1], slices[2], slices[3], slices[4], dense_args, expert_args))
        _, outputs = lax.scan(scan_step, None, (input_all, prev_seq, route_seq, pair_order, seq_lengths))
        return outputs
    result, pullback = jax.vjp(forward, inputs, prev_all, dense, experts)
    tok_grad, prev_grad, dense_grad, expert_grad = pullback(out_grad.astype(jnp.float32).reshape(count, tok_rows, D))
    return (result.reshape(-1, D).astype(jnp.bfloat16), tok_grad.reshape(-1, D), prev_grad.reshape(prev_logits.shape), dense_grad[0], dense_grad[1], dense_grad[2], dense_grad[3], dense_grad[4], dense_grad[5], dense_grad[6], dense_grad[7], expert_grad[0], expert_grad[1])
```

```python
import functools

import jax
import jax.numpy as jnp
from jax import lax
from jax.experimental import pallas as pl
from jax.experimental.pallas import tpu as pltpu
from jax.sharding import PartitionSpec as P

D = 768
FF = 2048
HEADS = 12
HEAD_DIM = 64


norm_eps = 1e-06
rotary_base = 10000.0
highest = lax.Precision.HIGHEST


def tables(tok_rows, head_dim):
    half_dim = head_dim // 2
    frequency = rotary_base ** (-(jnp.arange(half_dim, dtype=jnp.float32) * 2.0 / head_dim))
    angles = jnp.arange(tok_rows, dtype=jnp.float32)[:, None] * frequency[None, :]
    return (jnp.cos(angles)[:, None, :], jnp.sin(angles)[:, None, :])


def rotate(field, cosine, sine_table):
    half_dim = field.shape[-1] // 2
    first_half = field[..., :half_dim]
    second_half = field[..., half_dim:]
    return jnp.concatenate(
        [
            first_half * cosine - second_half * sine_table,
            second_half * cosine + first_half * sine_table,
        ],
        axis=-1,
    )


def place_pairs(route_rows, order, length, experts_ffn, capacity):
    tok_rows = route_rows.shape[0]
    token_ids = jnp.arange(tok_rows, dtype=jnp.int32)
    pair_valid = jnp.repeat(token_ids < length, 2)
    expert_flat = route_rows.reshape(-1)
    placed_expert = expert_flat[order]
    placed_live = pair_valid[order] & (placed_expert < experts_ffn)
    one_hot = (
        placed_expert[:, None] == jnp.arange(experts_ffn, dtype=jnp.int32)[None, :]
    ) & placed_live[:, None]
    counts = jnp.cumsum(one_hot.astype(jnp.int32), axis=0)
    slot_index = jnp.sum(jnp.where(one_hot, counts - 1, 0), axis=1)
    kept_pairs = placed_live & (slot_index < capacity)
    dest_placed = jnp.where(
        kept_pairs, placed_expert * capacity + slot_index, experts_ffn * capacity
    )
    pair_dest = jnp.zeros((2 * tok_rows,), jnp.int32).at[order].set(dest_placed)
    slot_pair = (
        jnp.full((experts_ffn * capacity,), 2 * tok_rows, jnp.int32)
        .at[dest_placed]
        .set(order, mode="drop")
    )
    return (pair_dest, slot_pair)


def attend_head(head, allowed, score_scale):
    query, keys_rot, values = head
    scores = jnp.dot(query, keys_rot.T, preferred_element_type=jnp.float32) * score_scale
    scores = jnp.where(allowed, scores, -1e30)
    top_score = jnp.max(scores, axis=1, keepdims=True)
    expo = jnp.exp(scores - top_score)
    total = jnp.sum(expo, axis=1, keepdims=True)
    probs = expo / total
    mixed = jnp.dot(probs.astype(jnp.bfloat16), values, preferred_element_type=jnp.float32).astype(
        jnp.bfloat16
    )
    return (mixed, top_score + jnp.log(total))


def attend_back(head, allowed, score_scale):
    query, keys_rot, values, grad_mixed, log_total = head
    scores = jnp.dot(query, keys_rot.T, preferred_element_type=jnp.float32) * score_scale
    scores = jnp.where(allowed, scores, -1e30)
    probs = jnp.where(allowed, jnp.exp(scores - log_total), 0.0)
    grad_probs = jnp.dot(grad_mixed, values.T, preferred_element_type=jnp.float32)
    delta = jnp.sum(grad_probs * probs, axis=1, keepdims=True)
    grad_scores = (probs * (grad_probs - delta)).astype(jnp.bfloat16)
    grad_query = jnp.dot(grad_scores, keys_rot, preferred_element_type=jnp.float32) * score_scale
    grad_key = jnp.dot(grad_scores.T, query, preferred_element_type=jnp.float32) * score_scale
    grad_value = jnp.dot(
        probs.astype(jnp.bfloat16).T, grad_mixed, preferred_element_type=jnp.float32
    )
    return (grad_query, grad_key, grad_value)


def body(
    tokens,
    seq_lengths,
    routes,
    pair_order,
    prev_logits,
    out_grad,
    qkv_weight,
    out_weight,
    gate_weight,
    const_weight,
    const_vector,
    norm1_gain,
    norm2_gain,
    gate_mix,
    expert_up,
    expert_down,
):
    tok_rows = tokens.shape[0]
    experts_ffn = lax.axis_size("expert")
    capacity = 2 * tok_rows // (experts_ffn + 4)
    length = seq_lengths[0]
    order = pair_order[0]
    score_scale = HEAD_DIM ** (-0.5)
    dense_shards = (
        qkv_weight,
        out_weight,
        gate_weight,
        const_weight,
        const_vector,
        norm1_gain,
        norm2_gain,
    )
    weight_qkv, weight_out, weight_gate, weight_const, vector_const, gain_one, gain_two = (
        lax.all_gather(dense_shards[0], "shard", axis=0, tiled=True),
        lax.all_gather(dense_shards[1], "shard", axis=0, tiled=True),
        lax.all_gather(dense_shards[2], "shard", axis=0, tiled=True),
        lax.all_gather(dense_shards[3], "shard", axis=0, tiled=True),
        lax.all_gather(dense_shards[4], "shard", axis=0, tiled=True),
        lax.all_gather(dense_shards[5], "shard", axis=0, tiled=True),
        lax.all_gather(dense_shards[6], "shard", axis=0, tiled=True),
    )
    weight_up, weight_down = (
        lax.all_gather(expert_up, "shard", axis=1, tiled=True),
        lax.all_gather(expert_down, "shard", axis=1, tiled=True),
    )
    weight_up = weight_up[0]
    weight_down = weight_down[0]
    inputs = tokens.astype(jnp.float32)
    token_ids = jnp.arange(tok_rows, dtype=jnp.int32)
    valid_mask = (token_ids < length).astype(jnp.float32)[:, None]
    gain_first = gain_one.astype(jnp.float32)
    gain_second = gain_two.astype(jnp.float32)
    scale_one = lax.rsqrt(jnp.mean(inputs * inputs, axis=1, keepdims=True) + norm_eps)
    normed = (inputs * scale_one * gain_first).astype(jnp.bfloat16)
    qkv_all = jnp.dot(normed, weight_qkv, preferred_element_type=jnp.float32)
    cosine, sine_table = tables(tok_rows, HEAD_DIM)

    def heads_first(block):
        return jnp.transpose(block, (1, 0, 2)).astype(jnp.bfloat16)

    query = heads_first(
        rotate(qkv_all[:, :D].reshape(tok_rows, HEADS, HEAD_DIM), cosine, sine_table)
    )
    keys_rot = heads_first(
        rotate(qkv_all[:, D : 2 * D].reshape(tok_rows, HEADS, HEAD_DIM), cosine, sine_table)
    )
    values = heads_first(qkv_all[:, 2 * D :].reshape(tok_rows, HEADS, HEAD_DIM))
    allowed = (token_ids[None, :] <= token_ids[:, None]) & (token_ids[None, :] < length)
    mixed_heads, log_totals = lax.map(
        lambda head: attend_head(head, allowed, score_scale), (query, keys_rot, values)
    )
    mixed = jnp.transpose(mixed_heads, (1, 0, 2)).reshape(tok_rows, D)
    hidden = inputs + jnp.dot(mixed, weight_out, preferred_element_type=jnp.float32)
    scale_two = lax.rsqrt(jnp.mean(hidden * hidden, axis=1, keepdims=True) + norm_eps)
    normed_two = hidden * scale_two * gain_second
    normed_low = normed_two.astype(jnp.bfloat16)
    mixer = gate_mix.astype(jnp.float32)
    logits = jnp.dot(normed_low, weight_gate, preferred_element_type=jnp.float32) + jnp.dot(
        prev_logits, mixer, precision=highest
    )
    chosen = jnp.take_along_axis(logits, routes, axis=1)
    gate_exp = jnp.exp(chosen - jnp.max(chosen, axis=1, keepdims=True))
    gates = gate_exp / jnp.sum(gate_exp, axis=1, keepdims=True)
    pair_dest, slot_pair = place_pairs(routes, order, length, experts_ffn, capacity)
    padded = jnp.concatenate([normed_low, jnp.zeros((1, D), jnp.bfloat16)], axis=0)
    send_rows = padded[slot_pair // 2].reshape(experts_ffn, capacity, D)
    received = lax.all_to_all(send_rows, "expert", split_axis=0, concat_axis=0, tiled=True)
    lead_shape = received.shape[:2]
    flat_rows = received.reshape(-1, D)
    gate_up = jnp.dot(flat_rows, weight_up, preferred_element_type=jnp.float32)
    activated = (jax.nn.silu(gate_up[:, :FF]) * gate_up[:, FF:]).astype(jnp.bfloat16)
    expert_out = jnp.dot(activated, weight_down, preferred_element_type=jnp.float32).astype(
        jnp.bfloat16
    )
    received, gate_up, activated, expert_out = (
        received,
        gate_up.reshape(lead_shape + (2 * FF,)),
        activated.reshape(lead_shape + (FF,)),
        expert_out.reshape(received.shape),
    )
    returned = lax.all_to_all(expert_out, "expert", split_axis=0, concat_axis=0, tiled=True)
    returned_pad = jnp.concatenate(
        [returned.reshape(-1, D), jnp.zeros((1, D), jnp.bfloat16)], axis=0
    )
    pair_ffn = returned_pad[pair_dest].astype(jnp.float32).reshape(tok_rows, 2, D)
    vector_float = vector_const.astype(jnp.float32)
    const_logits = jnp.dot(normed_low, weight_const, preferred_element_type=jnp.float32).reshape(
        tok_rows, 2, 2
    )
    const_exp = jnp.exp(const_logits - jnp.max(const_logits, axis=2, keepdims=True))
    coefs = const_exp / jnp.sum(const_exp, axis=2, keepdims=True)
    const_out = (
        coefs[..., 0:1] * normed_two[:, None, :] + coefs[..., 1:2] * vector_float.T[None, :, :]
    )
    const_select = (
        routes[:, :, None] == experts_ffn + 2 + jnp.arange(2, dtype=jnp.int32)[None, None, :]
    ).astype(jnp.float32)
    copy_select = (routes == experts_ffn + 1).astype(jnp.float32)[:, :, None]
    pair_out = (
        pair_ffn
        + copy_select * normed_two[:, None, :]
        + jnp.einsum("tkc,tcd->tkd", const_select, const_out, precision=highest)
    )
    mixture = jnp.sum(gates[:, :, None] * pair_out, axis=1)
    block_out = (valid_mask * (hidden + mixture)).astype(jnp.bfloat16)
    back_dense = (
        lax.all_gather(dense_shards[0], "shard", axis=0, tiled=True),
        lax.all_gather(dense_shards[1], "shard", axis=0, tiled=True),
        lax.all_gather(dense_shards[2], "shard", axis=0, tiled=True),
        lax.all_gather(dense_shards[3], "shard", axis=0, tiled=True),
        lax.all_gather(dense_shards[4], "shard", axis=0, tiled=True),
        lax.all_gather(dense_shards[5], "shard", axis=0, tiled=True),
        lax.all_gather(dense_shards[6], "shard", axis=0, tiled=True),
    )
    back_up, back_down = (
        lax.all_gather(expert_up, "shard", axis=1, tiled=True),
        lax.all_gather(expert_down, "shard", axis=1, tiled=True),
    )
    back_up = back_up[0]
    back_down = back_down[0]
    back_qkv, back_out, back_gate, back_const = (
        back_dense[0],
        back_dense[1],
        back_dense[2],
        back_dense[3],
    )
    grad_rows = out_grad.astype(jnp.float32) * valid_mask
    grad_gates = jnp.sum(grad_rows[:, None, :] * pair_out, axis=2)
    grad_pairs = gates[:, :, None] * grad_rows[:, None, :]
    grad_chosen = gates * (grad_gates - jnp.sum(gates * grad_gates, axis=1, keepdims=True))
    route_hot = (
        routes[:, :, None] == jnp.arange(experts_ffn + 4, dtype=jnp.int32)[None, None, :]
    ).astype(jnp.float32)
    grad_logits = jnp.sum(route_hot * grad_chosen[:, :, None], axis=1)
    prev_grad = jnp.dot(grad_logits, mixer.T, precision=highest)
    mix_term = jnp.dot(prev_logits.T, grad_logits, precision=highest)
    logit_low = grad_logits.astype(jnp.bfloat16)
    gate_term = jnp.dot(normed_low.T, logit_low, preferred_element_type=jnp.float32)
    grad_normed = jnp.dot(logit_low, back_gate.T, preferred_element_type=jnp.float32)
    grad_flat = jnp.concatenate(
        [grad_pairs.reshape(2 * tok_rows, D).astype(jnp.bfloat16), jnp.zeros((1, D), jnp.bfloat16)],
        axis=0,
    )
    grad_send = grad_flat[slot_pair].reshape(experts_ffn, capacity, D)
    grad_recv = lax.all_to_all(grad_send, "expert", split_axis=0, concat_axis=0, tiled=True)
    grad_slots = grad_recv.reshape(-1, D)
    down_term = jnp.dot(activated.reshape(-1, FF).T, grad_slots, preferred_element_type=jnp.float32)
    grad_act = jnp.dot(grad_slots, back_down.T, preferred_element_type=jnp.float32)
    gate_part = gate_up[..., :FF].reshape(-1, FF)
    up_part = gate_up[..., FF:].reshape(-1, FF)
    sigmoid_gate = jax.nn.sigmoid(gate_part)
    grad_gate_up = jnp.concatenate(
        [
            grad_act * up_part * sigmoid_gate * (1.0 + gate_part * (1.0 - sigmoid_gate)),
            grad_act * gate_part * sigmoid_gate,
        ],
        axis=1,
    ).astype(jnp.bfloat16)
    up_term = jnp.dot(received.reshape(-1, D).T, grad_gate_up, preferred_element_type=jnp.float32)
    grad_input = (
        jnp.dot(grad_gate_up, back_up.T, preferred_element_type=jnp.float32)
        .astype(jnp.bfloat16)
        .reshape(received.shape)
    )
    grad_back = lax.all_to_all(grad_input, "expert", split_axis=0, concat_axis=0, tiled=True)
    back_pad = jnp.concatenate([grad_back.reshape(-1, D), jnp.zeros((1, D), jnp.bfloat16)], axis=0)
    grad_normed = grad_normed + jnp.sum(
        back_pad[pair_dest].astype(jnp.float32).reshape(tok_rows, 2, D), axis=1
    )
    grad_normed = grad_normed + jnp.sum(copy_select * grad_pairs, axis=1)
    grad_const_out = jnp.einsum("tkc,tkd->tcd", const_select, grad_pairs, precision=highest)
    grad_first = jnp.sum(grad_const_out * normed_two[:, None, :], axis=2)
    grad_second = jnp.sum(grad_const_out * vector_float.T[None, :, :], axis=2)
    grad_coefs = jnp.stack([grad_first, grad_second], axis=2)
    grad_const_logits = (
        coefs * (grad_coefs - jnp.sum(coefs * grad_coefs, axis=2, keepdims=True))
    ).reshape(tok_rows, 4)
    grad_normed = grad_normed + jnp.sum(coefs[..., 0:1] * grad_const_out, axis=1)
    grad_normed = grad_normed + jnp.dot(
        grad_const_logits, back_const.astype(jnp.float32).T, precision=highest
    )
    vector_term = jnp.einsum("tc,tcd->dc", coefs[..., 1], grad_const_out, precision=highest)
    const_term = jnp.dot(normed_low.astype(jnp.float32).T, grad_const_logits, precision=highest)
    second_gain_term = jnp.sum(grad_normed * hidden * scale_two, axis=0)
    scaled_two = gain_second * grad_normed
    grad_hidden = (
        grad_rows
        + scale_two * scaled_two
        - hidden * scale_two**3 * jnp.mean(scaled_two * hidden, axis=1, keepdims=True)
    )
    grad_attn_low = grad_hidden.astype(jnp.bfloat16)
    out_term = jnp.dot(mixed.T, grad_attn_low, preferred_element_type=jnp.float32)
    grad_mixed = jnp.dot(grad_attn_low, back_out.T, preferred_element_type=jnp.float32).astype(
        jnp.bfloat16
    )
    grad_mixed_heads = jnp.transpose(grad_mixed.reshape(tok_rows, HEADS, HEAD_DIM), (1, 0, 2))
    grad_query, grad_key, grad_value = lax.map(
        lambda head: attend_back(head, allowed, score_scale),
        (query, keys_rot, values, grad_mixed_heads, log_totals),
    )
    grad_query = rotate(jnp.transpose(grad_query, (1, 0, 2)), cosine, -sine_table).reshape(
        tok_rows, D
    )
    grad_key = rotate(jnp.transpose(grad_key, (1, 0, 2)), cosine, -sine_table).reshape(tok_rows, D)
    grad_value = jnp.transpose(grad_value, (1, 0, 2)).reshape(tok_rows, D)
    grad_qkv = jnp.concatenate([grad_query, grad_key, grad_value], axis=1).astype(jnp.bfloat16)
    qkv_term = jnp.dot(normed.T, grad_qkv, preferred_element_type=jnp.float32)
    grad_first_norm = jnp.dot(grad_qkv, back_qkv.T, preferred_element_type=jnp.float32)
    first_gain_term = jnp.sum(grad_first_norm * inputs * scale_one, axis=0)
    scaled_one = gain_first * grad_first_norm
    tokens_grad = (
        grad_hidden
        + scale_one * scaled_one
        - inputs * scale_one**3 * jnp.mean(scaled_one * inputs, axis=1, keepdims=True)
    )
    dense_all = (
        qkv_term,
        out_term,
        gate_term,
        const_term,
        vector_term,
        first_gain_term,
        second_gain_term,
    )
    dense_terms = (
        lax.psum_scatter(dense_all[0], "shard", scatter_dimension=0, tiled=True),
        lax.psum_scatter(dense_all[1], "shard", scatter_dimension=0, tiled=True),
        lax.psum_scatter(dense_all[2], "shard", scatter_dimension=0, tiled=True),
        lax.psum_scatter(dense_all[3], "shard", scatter_dimension=0, tiled=True),
        lax.psum_scatter(dense_all[4], "shard", scatter_dimension=0, tiled=True),
        lax.psum_scatter(dense_all[5], "shard", scatter_dimension=0, tiled=True),
        lax.psum_scatter(dense_all[6], "shard", scatter_dimension=0, tiled=True),
    )
    (
        qkv_grad,
        out_weight_grad,
        gate_grad,
        const_weight_grad,
        const_vector_grad,
        norm1_grad,
        norm2_grad,
    ) = lax.psum(
        (
            dense_terms[0],
            dense_terms[1],
            dense_terms[2],
            dense_terms[3],
            dense_terms[4],
            dense_terms[5],
            dense_terms[6],
        ),
        "expert",
    )
    mix_grad = lax.psum(mix_term, ("expert", "shard"))
    expert_up_grad, expert_down_grad = (
        lax.psum_scatter(up_term[None], "shard", scatter_dimension=1, tiled=True),
        lax.psum_scatter(down_term[None], "shard", scatter_dimension=1, tiled=True),
    )
    return (
        block_out,
        tokens_grad,
        prev_grad,
        qkv_grad,
        out_weight_grad,
        gate_grad,
        const_weight_grad,
        const_vector_grad,
        norm1_grad,
        norm2_grad,
        mix_grad,
        expert_up_grad,
        expert_down_grad,
    )


MESH = pl.DeviceIdType.MESH
BF = jnp.bfloat16
F32 = jnp.float32
LANES = 128
NEG = -1e30
VMEM_BYTES = 64 * 1024 * 1024
RING = 3


def dot(a, b):
    return lax.dot_general(a, b, (((1,), (0,)), ((), ())), preferred_element_type=F32)


def dot_nt(a, b):
    return lax.dot_general(a, b, (((1,), (1,)), ((), ())), preferred_element_type=F32)


def dot_tn(a, b, precision=None):
    return lax.dot_general(
        a, b, (((0,), (0,)), ((), ())), precision=precision, preferred_element_type=F32
    )


def iota(shape, dim):
    return lax.broadcasted_iota(jnp.int32, shape, dim)


def remote(src, dst, send_sem, recv_sem, target):
    return pltpu.make_async_remote_copy(
        src_ref=src,
        dst_ref=dst,
        send_sem=send_sem,
        recv_sem=recv_sem,
        device_id=target,
        device_id_type=MESH,
    )


def swap_halves(block):
    half = HEAD_DIM // 2
    width = block.shape[1]
    lower = (iota(block.shape, 1) % HEAD_DIM) < half
    return jnp.where(
        lower, pltpu.roll(block, width - half, 1), pltpu.roll(block, half, 1)
    )


def step_kernel(dims, scratch_names, *refs):
    (tok_rows, experts, lines, share, hidden_block, capacity, gate_cols) = dims
    names = IN_NAMES + OUT_NAMES + scratch_names
    r = dict(zip(names, refs))
    pairs = D // LANES
    layer = 2 * experts
    slots = experts * capacity
    half_share = share // 2
    chunk_cols = 3 * LANES
    out_chunks = D // chunk_cols
    chunks = out_chunks + pairs
    half_ffn = lines * 2 * hidden_block
    const_col = gate_cols
    vec_col = gate_cols + 8
    row_blocks = tok_rows // LANES

    e = lax.axis_index("expert")
    s = lax.axis_index("shard")
    z = s // 2
    x = s % 2
    core = e % 2
    across = 2 * z + 1 - x
    twin = e + 1 - 2 * core
    mine = 2 * e + x

    def rows(index, size):
        return pl.ds(pl.multiple_of(index * size, size), size)

    barrier = pltpu.get_barrier_semaphore()
    met = 0
    for step in range(1, 2 * lines):
        pl.semaphore_signal(
            barrier, 1, device_id=(e, (s + step) % (2 * lines)), device_id_type=MESH
        )
        met += 1
    for step in range(1, experts):
        for side in range(2):
            pl.semaphore_signal(
                barrier, 1, device_id=((e + step) % experts, 2 * z + side), device_id_type=MESH
            )
            met += 1
    pl.semaphore_wait(barrier, met)

    weights, small = r["weights"], r["small"]
    weights[rows(s, share), 0 : 3 * D] = r["qkv_in"][...]
    weights[rows(s, share), 3 * D : 4 * D] = r["out_in"][...]
    small[rows(s, share), :] = r["small_in"][...]
    spans = ((0, 3 * D // 2), (3 * D, D // 2))

    def slab(kind, zz, xx, cc):
        start, width = spans[kind]
        columns = pl.ds(pl.multiple_of(start + width * cc, LANES), width)
        return weights.at[rows(2 * zz + xx, share), columns]

    def dense_z(kind, step):
        ref = slab(kind, z, x, core)
        return remote(
            ref,
            ref,
            r["dz_send"].at[kind, step],
            r["d_recv"].at[kind, z, x, core],
            (e, ((z + step) % lines) * 2 + x),
        )

    def dense_x(kind, zz):
        ref = slab(kind, zz, x, core)
        return remote(
            ref, ref, r["dx_send"].at[kind, zz], r["d_recv"].at[kind, zz, x, core], (e, across)
        )

    def dense_core(kind, zz, xx):
        ref = slab(kind, zz, xx, core)
        return remote(
            ref,
            ref,
            r["dc_send"].at[kind, zz, xx],
            r["d_recv"].at[kind, zz, xx, core],
            (twin, s),
        )

    def dense_arrived(kind, zz, xx, cc):
        ref = slab(kind, zz, xx, cc)
        remote(
            ref, ref, r["dx_send"].at[kind, 0], r["d_recv"].at[kind, zz, xx, cc], (e, across)
        ).wait_recv()

    def dense_start(kind):
        for step in range(1, lines):
            dense_z(kind, step).start()
        dense_x(kind, z).start()

    def dense_forward(kind):
        for step in range(1, lines):
            zz = (z + lines - step) % lines
            dense_arrived(kind, zz, x, core)
            dense_x(kind, zz).start()
            dense_core(kind, zz, x).start()
        for step in range(lines):
            zz = (z + lines - step) % lines
            dense_arrived(kind, zz, 1 - x, core)
            dense_core(kind, zz, 1 - x).start()

    def dense_finish(kind):
        for step in range(lines):
            zz = (z + lines - step) % lines
            if step > 0:
                dense_arrived(kind, zz, x, 1 - core)
            dense_arrived(kind, zz, 1 - x, 1 - core)

    def dense_sent(kind):
        for step in range(1, lines):
            dense_z(kind, step).wait_send()
        for step in range(lines):
            zz = (z + lines - step) % lines
            dense_x(kind, zz).wait_send()
            if step > 0:
                dense_core(kind, zz, x).wait_send()
            dense_core(kind, zz, 1 - x).wait_send()

    def small_copy(step, origin):
        ref = small.at[rows(origin, share), :]
        return remote(
            ref,
            ref,
            r["sm_send"].at[step],
            r["sm_recv"].at[origin],
            (e, (s + step) % (2 * lines)),
        )

    dense_start(0)
    for step in range(1, 2 * lines):
        small_copy(step, s).start()
    dense_start(1)

    up, down, stage = r["up"], r["down"], r["stage"]
    up_in = r["up_in"]

    def up_columns(part, jj, xx):
        return pl.ds(
            pl.multiple_of(part * FF + hidden_block * (2 * jj + xx), hidden_block), hidden_block
        )

    own_rows = rows(s, share)
    for jj in range(lines):
        for part in range(2):
            spot = pl.ds(part * hidden_block, hidden_block)
            stage[jj, :, spot] = up_in[:, up_columns(part, jj, 1 - x)]
            up[jj, own_rows, spot] = up_in[:, up_columns(part, jj, x)]
    down[z] = r["down_in"][...]

    def up_across(origin_x):
        return remote(
            stage,
            up.at[:, rows(2 * z + origin_x, share), :],
            r["ux_send"],
            r["ux_recv"],
            (e, across),
        )

    def up_piece(zz):
        return up.at[:, rows(zz, 2 * share), :]

    def chain(kind, way, step, zz):
        ref = up_piece(zz) if kind == 0 else down.at[zz]
        target = s + 2 if way == 0 else s - 2
        return remote(
            ref,
            ref,
            r["ch_send"].at[kind, way, step],
            r["ch_recv"].at[kind, way, step],
            (e, target),
        )

    def chain_send(kind, step):
        @pl.when((z - step >= 0) & (z + 1 < lines))
        def _():
            chain(kind, 0, step, z - step).start()

        @pl.when((z + step < lines) & (z > 0))
        def _():
            chain(kind, 1, step, z + step).start()

    def chain_sent(kind, step):
        @pl.when((z - step >= 0) & (z + 1 < lines))
        def _():
            chain(kind, 0, step, z - step).wait_send()

        @pl.when((z + step < lines) & (z > 0))
        def _():
            chain(kind, 1, step, z + step).wait_send()

    def chain_arrived(kind, step):
        @pl.when(z - 1 - step >= 0)
        def _():
            chain(kind, 0, step, z - 1 - step).wait_recv()

        @pl.when(z + 1 + step < lines)
        def _():
            chain(kind, 1, step, z + 1 + step).wait_recv()

    def chain_next(kind, step):
        chain_arrived(kind, step)
        if step + 1 < lines - 1:
            chain_send(kind, step + 1)

    up_across(x).start()

    length = r["length"][0]
    pair_ids = iota((2 * tok_rows, 2 * tok_rows), 0)
    pair_names = jnp.where(pair_ids < tok_rows, 2 * pair_ids, 2 * (pair_ids - tok_rows) + 1)
    is_at = jnp.where(pair_names == r["order_row"][...], 1.0, 0.0).astype(BF)
    pair_lane = iota((16, 2 * tok_rows), 1)
    pair_token = jnp.where(pair_lane < tok_rows, pair_lane, pair_lane - tok_rows)
    expert_row = iota((16, 2 * tok_rows), 0)
    live = (expert_row == r["route_row"][...]) & (expert_row < experts) & (pair_token < length)
    placed = dot(jnp.where(live, 1.0, 0.0).astype(BF), is_at)
    before = jnp.where(
        iota((2 * tok_rows, 2 * tok_rows), 0) <= iota((2 * tok_rows, 2 * tok_rows), 1), 1.0, 0.0
    ).astype(BF)
    counts = dot(placed.astype(BF), before)
    kept = jnp.where((placed > 0.5) & (counts <= capacity + 0.5), counts, 0.0)
    taken = dot_nt(kept.astype(BF), is_at)
    slot_of = jnp.sum(
        jnp.where(taken > 0.5, taken + (expert_row * capacity).astype(F32), 0.0),
        axis=0,
        keepdims=True,
    )
    slot_col = jnp.transpose(jnp.broadcast_to(slot_of, (8, 2 * tok_rows)))
    put, take = r["put"], r["take"]
    for k in range(2):
        span = slice(k * tok_rows, (k + 1) * tok_rows)
        names_down = (iota((slots, tok_rows), 0) + 1).astype(F32)
        put[k] = jnp.where(slot_of[:, span] == names_down, 1.0, 0.0).astype(BF)
        names_right = (iota((tok_rows, slots), 1) + 1).astype(F32)
        take[k] = jnp.where(slot_col[span, 0:1] == names_right, 1.0, 0.0).astype(BF)

    for step in range(1, 2 * lines):
        origin = (s + 2 * lines - step) % (2 * lines)
        small_copy(step, origin).wait_recv()
    pick = jnp.where(iota((8, LANES), 1) == iota((8, LANES), 0) + vec_col, 1.0, 0.0).astype(BF)
    named = dot_nt(pick, small[...])
    r["rows"][...] = named
    tokens = r["tokens"]
    gain_one, gain_two = named[2:3, :], named[3:4, :]
    vec_zero, vec_one = named[0:1, :], named[1:2, :]
    cols = r["cols"]
    normed = r["normed"]
    for block in range(row_blocks):
        at = slice(block * LANES, (block + 1) * LANES)
        inputs = tokens[at, :].astype(F32)
        scale = lax.rsqrt(jnp.mean(inputs * inputs, axis=1, keepdims=True) + norm_eps)
        cols[at, 0:1] = scale
        normed[at, :] = (inputs * scale * gain_one).astype(BF)

    dense_forward(0)
    chain_send(1, 0)
    up_across(1 - x).wait_recv()
    chain_send(0, 0)
    dense_finish(0)

    heads = r["heads"]
    cosine, sine = r["cosine"], r["sine"]

    def rotated(b, _):
        block = dot(normed[...], weights[:, rows(b, LANES)])
        heads[b] = (block * cosine[...] + swap_halves(block) * sine[...]).astype(BF)
        return 0

    def plain(b, _):
        heads[b] = dot(normed[...], weights[:, rows(b, LANES)]).astype(BF)
        return 0

    lax.fori_loop(0, 2 * pairs, rotated, 0)
    lax.fori_loop(2 * pairs, 3 * pairs, plain, 0)
    dense_forward(1)
    chain_next(1, 0)

    score_scale = HEAD_DIM ** (-0.5)
    first_head = iota((tok_rows, LANES), 1) < HEAD_DIM
    mixed, log_sums = r["mixed"], r["log_sums"]

    def allowed_pairs():
        key, query = iota((tok_rows, tok_rows), 0), iota((tok_rows, tok_rows), 1)
        return (key <= query) & (key < length)

    def one_head(block, head):
        keep = first_head if head == 0 else jnp.logical_not(first_head)
        return jnp.where(keep, block, jnp.zeros_like(block))

    def attend(p, _):
        query, key, value = heads[p], heads[pairs + p], heads[2 * pairs + p]
        results = []
        for head in range(2):
            scores = dot_nt(key, one_head(query, head)) * score_scale
            scores = jnp.where(allowed_pairs(), scores, NEG)
            top = jnp.max(scores, axis=0, keepdims=True)
            expo = jnp.exp(scores - top)
            total = jnp.sum(expo, axis=0, keepdims=True)
            probs = expo * (1.0 / total)
            log_sums[p, head : head + 1, :] = top + jnp.log(total)
            results.append(dot_tn(probs.astype(BF), value))
        mixed[:, rows(p, LANES)] = jnp.where(first_head, results[0], results[1]).astype(BF)
        return 0

    lax.fori_loop(0, pairs // 2, attend, 0)
    chain_next(0, 0)
    lax.fori_loop(pairs // 2, pairs, attend, 0)
    dense_finish(1)
    chain_next(1, 1)

    hidden, normed_low = r["hidden"], r["normed_low"]
    out_grad = r["out_grad"]
    grad_low = r["grad_low"]
    for block in range(row_blocks):
        at = slice(block * LANES, (block + 1) * LANES)
        hid = tokens[at, :].astype(F32) + dot(mixed[at, :], weights[:, 3 * D : 4 * D])
        hidden[at, :] = hid
        scale = lax.rsqrt(jnp.mean(hid * hid, axis=1, keepdims=True) + norm_eps)
        cols[at, 1:2] = scale
        low = (hid * scale * gain_two).astype(BF)
        normed_low[at, :] = low
        logits = dot(low, small[...])
        lane = iota((LANES, LANES), 1)
        extra = jnp.zeros((LANES, gate_cols), F32)
        for i in range(gate_cols):
            extra = extra + r["prev"][at, i : i + 1] * r["mix"][i : i + 1, :]
        routes = r["routes"][at, :]
        chosen = []
        for k in range(2):
            hot = lane == routes[:, k : k + 1]
            part = jnp.sum(jnp.where(hot, logits, 0.0), axis=1, keepdims=True)
            chosen.append(
                part
                + jnp.sum(
                    jnp.where(
                        iota((LANES, gate_cols), 1) == routes[:, k : k + 1], extra, 0.0
                    ),
                    axis=1,
                    keepdims=True,
                )
            )
        top = jnp.maximum(chosen[0], chosen[1])
        powers = [jnp.exp(c - top) for c in chosen]
        total = powers[0] + powers[1]
        gates = [w / total for w in powers]
        on_normed = sum(
            gates[k] * (routes[:, k : k + 1] == experts + 1).astype(F32) for k in range(2)
        )
        for j in range(2):
            first = logits[:, const_col + 2 * j : const_col + 2 * j + 1]
            second = logits[:, const_col + 2 * j + 1 : const_col + 2 * j + 2]
            peak = jnp.maximum(first, second)
            first, second = jnp.exp(first - peak), jnp.exp(second - peak)
            both = first + second
            first, second = first / both, second / both
            weight = sum(
                gates[k] * (routes[:, k : k + 1] == experts + 2 + j).astype(F32)
                for k in range(2)
            )
            on_normed = on_normed + first * weight
            cols[at, 6 + 4 * j : 7 + 4 * j] = first
            cols[at, 7 + 4 * j : 8 + 4 * j] = second
            cols[at, 8 + 4 * j : 9 + 4 * j] = weight
        cols[at, 2:3] = gates[0]
        cols[at, 3:4] = gates[1]
        cols[at, 4:5] = on_normed
        valid = (iota((LANES, 1), 0) + block * LANES < length).astype(F32)
        grad = out_grad[at, :].astype(F32) * valid
        grad_low[0, at, :] = (gates[0] * grad).astype(BF)
        grad_low[1, at, :] = (gates[1] * grad).astype(BF)
        grad_low[2, at, :] = grad.astype(BF)

    sent, buffer, slot_grad = r["sent"], r["buffer"], r["slot_grad"]

    def dispatch(which, step, side, origin):
        target = (e + step) % experts
        box = buffer if which == 0 else slot_grad
        return remote(
            sent.at[which, target],
            box.at[rows(origin, capacity), :],
            r["go_send"].at[which, step, side],
            r["go_recv"].at[which, origin],
            (target, 2 * z + side),
        )

    def dispatch_each(which, step, go):
        for flip in range(2):
            side = x if flip == 0 else 1 - x
            if step > 0 or flip == 1:
                go(dispatch(which, step, side, mine))

    for step in range(experts):
        owner = (e + step) % experts
        chosen_rows = rows(owner, capacity)
        put_zero, put_one = put[0, chosen_rows, :], put[1, chosen_rows, :]
        sent[0, owner] = dot(put_zero + put_one, normed_low[...]).astype(BF)
        dispatch_each(0, step, lambda copy: copy.start())
        sent[1, owner] = (
            dot(put_zero, grad_low[0]) + dot(put_one, grad_low[1])
        ).astype(BF)
        dispatch_each(1, step, lambda copy: copy.start())
    buffer[rows(mine, capacity), :] = sent[0, e]
    slot_grad[rows(mine, capacity), :] = sent[1, e]
    chain_next(0, 1)
    chain_next(1, 2)

    def others(go):
        for step in range(experts):
            other = (e + step) % experts
            for flip in range(2):
                side = x if flip == 0 else 1 - x
                if step > 0 or flip == 1:
                    go(step, other, side, 2 * other + side)

    for which in range(2):
        others(lambda step, other, side, origin: dispatch(which, step, side, origin).wait_recv())
    chain_next(0, 2)

    up_sum, down_sum = r["up_sum"], r["down_sum"]
    up_box, down_box = r["up_box"], r["down_box"]
    up_out, down_out = r["up_out"], r["down_out"]
    final_send, final_box = stage, r["final_box"]
    ffn, slot_back = r["ffn"], r["slot_back"]
    last = lines - 1

    def up_rows(jj, zz):
        return up_sum.at[jj, rows(zz, 2 * share), :]

    def up_hop(way, k, jj, dest):
        return remote(
            up_rows(jj, dest),
            up_box.at[way, k, jj],
            r["ru_send"].at[way, k, jj],
            r["ru_recv"].at[way, k, jj],
            (e, s + 2 if way == 0 else s - 2),
        )

    def down_slot(way, jj, zz):
        return jj if way == 0 else jnp.where(jj == zz, lines, jj)

    def down_hop(way, jj, zz):
        return remote(
            down_sum.at[jj],
            down_box.at[down_slot(way, jj, zz)],
            r["rd_send"].at[way, jj],
            r["rd_recv"].at[way, jj],
            (e, s + 2 if way == 0 else s - 2),
        )

    def final_hop(jj):
        return remote(
            final_send.at[jj],
            final_box.at[jj],
            r["fx_send"].at[jj],
            r["fx_recv"].at[jj],
            (e, across),
        )

    def sum_event(k, jj):
        for way in range(2):
            place = z if way == 0 else last - z
            dest = last - k + place if way == 0 else k - place
            inside = (place <= k) & (place < last)

            @pl.when((k >= 1) & (k < last) & (place >= 1) & inside)
            def _():
                up_hop(way, k - 1, jj, dest).wait_recv()
                old = up_sum[jj, rows(dest, 2 * share), :].astype(F32)
                up_sum[jj, rows(dest, 2 * share), :] = (
                    old + up_box[way, k - 1, jj].astype(F32)
                ).astype(BF)

                @pl.when(dest == jj)
                def _():
                    down_hop(way, jj, z).wait_recv()
                    down_sum[jj] = (
                        down_sum[jj].astype(F32)
                        + down_box[down_slot(way, jj, z)].astype(F32)
                    ).astype(BF)

            @pl.when((k < last) & inside)
            def _():
                up_hop(way, k, jj, dest).start()

                @pl.when(dest == jj)
                def _():
                    down_hop(way, jj, z + 1 - 2 * way).start()

        @pl.when(k == last)
        def _():
            total = slot_back.at[0 : 2 * share, 0 : 2 * hidden_block]
            total[...] = up_sum[jj, rows(z, 2 * share), :].astype(F32)

            @pl.when(z > 0)
            def _():
                up_hop(0, last - 1, jj, z).wait_recv()
                total[...] += up_box[0, last - 1, jj].astype(F32)

            @pl.when(z < last)
            def _():
                up_hop(1, last - 1, jj, z).wait_recv()
                total[...] += up_box[1, last - 1, jj].astype(F32)

            final_send[jj] = total[rows(1 - x, share), :].astype(BF)
            final_hop(jj).start()
            own = total[rows(x, share), :]
            for part in range(2):
                up_out[:, up_columns(part, jj, x)] = own[
                    :, part * hidden_block : (part + 1) * hidden_block
                ]

            @pl.when(jj == z)
            def _():
                down_out[...] = down_sum[z].astype(F32)

                @pl.when(z > 0)
                def _():
                    down_hop(0, jj, z).wait_recv()
                    down_out[...] += down_box[down_slot(0, jj, z)].astype(F32)

                @pl.when(z < last)
                def _():
                    down_hop(1, jj, z).wait_recv()
                    down_out[...] += down_box[down_slot(1, jj, z)].astype(F32)

    def sum_sent():
        for jj in range(lines):
            for way in range(2):
                place = z if way == 0 else last - z
                for k in range(last):
                    dest = last - k + place if way == 0 else k - place

                    @pl.when((place <= k) & (place < last))
                    def _():
                        up_hop(way, k, jj, dest).wait_send()

                        @pl.when(dest == jj)
                        def _():
                            down_hop(way, jj, z + 1 - 2 * way).wait_send()

    up_across(x).wait_send()
    act, grad_gu = r["act"], r["grad_gu"]
    block_rows = 2 * LANES
    row_steps = layer * capacity // block_rows

    def expert_chunk(jj, _):
        def forward(b, _):
            at = rows(b, block_rows)
            given = dot(buffer[at, :], up[jj])
            gate, lift = given[:, 0:hidden_block], given[:, hidden_block:]
            squash = 1.0 / (1.0 + jnp.exp(-gate))
            silu = gate * squash
            low = (silu * lift).astype(BF)
            act[at, :] = low
            grad_act = dot_nt(slot_grad[at, :], down[jj])
            grads = jnp.concatenate(
                [grad_act * lift * squash * (1.0 + gate * (1.0 - squash)), grad_act * silu],
                axis=1,
            ).astype(BF)
            grad_gu[at, :] = grads
            forth = dot(low, down[jj])
            back = dot_nt(grads, up[jj])

            @pl.when(jj == 0)
            def _():
                ffn[at, :] = forth
                slot_back[at, :] = back

            @pl.when(jj > 0)
            def _():
                ffn[at, :] += forth
                slot_back[at, :] += back

            return 0

        lax.fori_loop(0, row_steps, forward, 0)
        up_sum[jj] = dot_tn(buffer[...], grad_gu[...]).astype(BF)
        down_sum[jj] = dot_tn(act[...], slot_grad[...]).astype(BF)
        sum_event(0, jj)
        return 0

    lax.fori_loop(0, lines, expert_chunk, 0)

    back_box = r["back_box"]
    for b in range(row_steps):
        at = slice(b * block_rows, (b + 1) * block_rows)
        buffer[at, :] = ffn[at, :].astype(BF)
        slot_grad[at, :] = slot_back[at, :].astype(BF)

    def come(which, step, side, origin_e, origin_x):
        target = (e + step) % experts
        box = buffer if which == 0 else slot_grad
        return remote(
            box.at[rows(2 * target + side, capacity), :],
            back_box.at[which, origin_x, rows(origin_e, capacity), :],
            r["come_send"].at[which, step, side],
            r["come_recv"].at[which, origin_e, origin_x],
            (target, 2 * z + side),
        )

    for which in range(2):
        others(lambda step, other, side, origin: come(which, step, side, e, x).start())
        box = buffer if which == 0 else slot_grad
        back_box[which, x, rows(e, capacity), :] = box[rows(mine, capacity), :]
    for which in range(2):
        others(
            lambda step, other, side, origin: come(which, step, side, other, side).wait_recv()
        )
    for which in range(2):
        back_box[which, 0] = (
            back_box[which, 0].astype(F32) + back_box[which, 1].astype(F32)
        ).astype(BF)

    named = r["rows"][...]
    gain_one, gain_two = named[2:3, :], named[3:4, :]
    vec_zero, vec_one = named[0:1, :], named[1:2, :]
    grad_hidden, grad_attn = ffn.at[0:tok_rows, :], r["grad_attn"]
    thin, wide = r["thin"], r["wide"]
    grad_logits = r["grad_logits"]
    gain_sum = jnp.zeros((1, D), F32)
    for block in range(row_blocks):
        at = slice(block * LANES, (block + 1) * LANES)
        hid = hidden[at, :]
        scale = cols[at, 1:2]
        norm = hid * scale * gain_two
        grad = grad_low[2, at, :].astype(F32)
        take_zero, take_one = take[0, at, :], take[1, at, :]
        outs = [dot(take_zero, back_box[0, 0]), dot(take_one, back_box[0, 0])]
        gates = [cols[at, 2:3], cols[at, 3:4]]
        on_normed = cols[at, 4:5]
        const = [
            (cols[at, 6 + 4 * j : 7 + 4 * j], cols[at, 7 + 4 * j : 8 + 4 * j], cols[at, 8 + 4 * j : 9 + 4 * j])
            for j in range(2)
        ]
        on_vec = [a * w for _, a, w in const]
        valid = (iota((LANES, 1), 0) + block * LANES < length).astype(F32)
        mixture = (
            gates[0] * outs[0]
            + gates[1] * outs[1]
            + on_normed * norm
            + on_vec[0] * vec_zero
            + on_vec[1] * vec_one
        )
        r["block_out"][at, :] = (valid * (hid + mixture)).astype(BF)
        routes = r["routes"][at, :]
        with_norm = jnp.sum(grad * norm, axis=1, keepdims=True)
        with_vec = [
            jnp.sum(grad * v, axis=1, keepdims=True) for v in (vec_zero, vec_one)
        ]
        gate_grads = []
        for k in range(2):
            value = jnp.sum(grad * outs[k], axis=1, keepdims=True)
            value = value + (routes[:, k : k + 1] == experts + 1).astype(F32) * with_norm
            for j in range(2):
                hit = (routes[:, k : k + 1] == experts + 2 + j).astype(F32)
                value = value + hit * (const[j][0] * with_norm + const[j][1] * with_vec[j])
            gate_grads.append(value)
        mean = gates[0] * gate_grads[0] + gates[1] * gate_grads[1]
        lane = iota((LANES, LANES), 1)
        spread = jnp.zeros((LANES, LANES), F32)
        for k in range(2):
            spread = spread + jnp.where(
                lane == routes[:, k : k + 1], gates[k] * (gate_grads[k] - mean), 0.0
            )
        grad_logits[at, :] = spread[:, 0:gate_cols]
        prev_grad = jnp.zeros((LANES, gate_cols), F32)
        for i in range(gate_cols):
            prev_grad = prev_grad + spread[:, i : i + 1] * r["mix_t"][i : i + 1, :]
        r["prev_out"][at, :] = prev_grad
        wide_block = jnp.zeros((LANES, LANES), F32)
        for j in range(2):
            first, second, weight = const[j]
            d_first, d_second = weight * with_norm, weight * with_vec[j]
            centre = first * d_first + second * d_second
            parts = (first * (d_first - centre), second * (d_second - centre))
            for i in range(2):
                high = parts[i].astype(BF).astype(F32)
                at_high = const_col + 2 * j + i
                spread = jnp.where(lane == at_high, high, spread)
                spread = jnp.where(lane == at_high + 4, parts[i] - high, spread)
            high = on_vec[j].astype(BF).astype(F32)
            wide_block = jnp.where(lane == j, high, wide_block)
            wide_block = jnp.where(lane == 2 + j, on_vec[j] - high, wide_block)
        thin[at, :] = spread.astype(BF)
        wide[at, :] = wide_block.astype(BF)
        grad_norm = (
            dot_nt(thin[at, :], small[...])
            + dot(take_zero + take_one, back_box[1, 0])
            + on_normed * grad
        )
        gain_sum = gain_sum + jnp.sum(grad_norm * hid * scale, axis=0, keepdims=True)
        scaled = gain_two * grad_norm
        grad = (
            grad
            + scale * scaled
            - hid * (scale * scale * scale) * jnp.mean(scaled * hid, axis=1, keepdims=True)
        )
        grad_hidden[at, :] = grad
        grad_attn[at, :] = grad.astype(BF)

    sums = r["sums"]
    sums[z] = jnp.zeros(sums.shape[1:], F32)
    by_small = dot_tn(thin[...], normed_low[...])
    by_vec = dot_tn(wide[...], grad_low[2])
    sums[z, 0:gate_cols, :] = by_small[0:gate_cols, :]
    sums[z, gate_cols : gate_cols + 4, :] = (
        by_small[const_col : const_col + 4, :] + by_small[const_col + 4 : const_col + 8, :]
    )
    sums[z, gate_cols + 4 : gate_cols + 6, :] = by_vec[0:2, :] + by_vec[2:4, :]
    sums[z, gate_cols + 6 : gate_cols + 7, :] = gain_sum
    mix_rows = SMALL_ROWS - 16
    sums[z, mix_rows : mix_rows + gate_cols, 0:gate_cols] = dot_tn(
        r["prev"][...], grad_logits[...], lax.Precision.HIGHEST
    )

    dense, ring = r["dense"], RING
    core_box, x_box, z_box, all_box = r["core_box"], r["x_box"], r["z_box"], r["all_box"]

    def as_chunk(block):
        return block.astype(BF).reshape(lines, 2, 2, half_share, chunk_cols)

    def core_hop(ch):
        return remote(
            dense.at[ch % ring, :, :, 1 - core],
            core_box.at[ch],
            r["gc_send"].at[ch],
            r["gc_recv"].at[ch],
            (twin, s),
        )

    def x_hop(ch):
        return remote(
            core_box.at[ch, :, 1 - x],
            x_box.at[ch],
            r["gx_send"].at[ch],
            r["gx_recv"].at[ch],
            (e, across),
        )

    def z_hop(ch, step, origin):
        zz = (z + step) % lines
        return remote(
            core_box.at[ch, zz, x],
            z_box.at[ch, origin],
            r["gz_send"].at[ch, step],
            r["gz_recv"].at[ch, origin],
            (e, 2 * zz + x),
        )

    def all_hop(ch, step, origin):
        return remote(
            all_box.at[ch, e],
            all_box.at[ch, origin],
            r["ga_send"].at[ch, step],
            r["ga_recv"].at[ch, origin],
            ((e + step) % experts, s),
        )

    def dense_event(it):
        @pl.when(it < chunks)
        def _():
            core_hop(it).start()

        @pl.when((it >= 1) & (it - 1 < chunks))
        def _():
            ch = it - 1
            core_hop(ch).wait_recv()
            core_box[ch] = (
                core_box[ch].astype(F32) + dense[ch % ring, :, :, core].astype(F32)
            ).astype(BF)
            x_hop(ch).start()

        @pl.when((it >= 2) & (it - 2 < chunks))
        def _():
            ch = it - 2
            core_hop(ch).wait_send()
            x_hop(ch).wait_recv()
            core_box[ch, :, x] = (
                core_box[ch, :, x].astype(F32) + x_box[ch].astype(F32)
            ).astype(BF)
            for step in range(1, lines):
                z_hop(ch, step, z).start()

        @pl.when((it >= 3) & (it - 3 < chunks))
        def _():
            ch = it - 3
            total = core_box[ch, z, x].astype(F32)
            for step in range(1, lines):
                origin = (z + lines - step) % lines
                z_hop(ch, step, origin).wait_recv()
                total = total + z_box[ch, origin].astype(F32)
            all_box[ch, e] = total.astype(BF)
            for step in range(1, experts):
                all_hop(ch, step, e).start()

        @pl.when((it >= 4) & (it - 4 < chunks))
        def _():
            ch = it - 4
            for step in range(1, experts):
                origin = (e + experts - step) % experts
                all_hop(ch, step, origin).wait_recv()
            for half in range(2):
                total = all_box[ch, half].astype(F32)
                for other in range(1, experts // 2):
                    total = total + all_box[ch, 2 * other + half].astype(F32)
                at = slice(half * half_share, (half + 1) * half_share)

                @pl.when(ch < out_chunks)
                def _():
                    r["out_w_out"][at, rows(ch, chunk_cols)] = total

                @pl.when(ch >= out_chunks)
                def _():
                    for part in range(3):
                        spot = pl.ds(
                            pl.multiple_of(part * D + (ch - out_chunks) * LANES, LANES), LANES
                        )
                        r["qkv_out"][at, spot] = total[:, part * LANES : (part + 1) * LANES]

    def dense_events_sent():
        def one(ch, _):
            x_hop(ch).wait_send()
            for step in range(1, lines):
                z_hop(ch, step, z).wait_send()
            for step in range(1, experts):
                all_hop(ch, step, e).wait_send()
            return 0

        lax.fori_loop(0, chunks, one, 0)

    grad_normed = ffn.at[tok_rows : 2 * tok_rows, :]
    grad_normed[...] = jnp.zeros_like(grad_normed)
    out_grads = dot_tn(mixed[...], grad_attn[...])
    for ch in range(out_chunks):
        dense[ch] = as_chunk(out_grads[:, ch * chunk_cols : (ch + 1) * chunk_cols])

    def attend_back(p):
        query, key, value = heads[p], heads[pairs + p], heads[2 * pairs + p]
        upper = dot_nt(grad_attn[...], weights[rows(p, LANES), 3 * D : 4 * D]).astype(BF)
        grads = []
        for head in range(2):
            scores = dot_nt(key, one_head(query, head)) * score_scale
            probs = jnp.where(
                allowed_pairs(), jnp.exp(scores - log_sums[p, head : head + 1, :]), 0.0
            )
            grad_probs = dot_nt(value, one_head(upper, head))
            delta = jnp.sum(grad_probs * probs, axis=0, keepdims=True)
            grad_scores = (probs * (grad_probs - delta)).astype(BF)
            grads.append(
                (
                    dot_tn(grad_scores, key),
                    dot(grad_scores, query),
                    dot(probs.astype(BF), upper),
                )
            )
        joined = [jnp.where(first_head, a, b) for a, b in zip(*grads)]
        parts = []
        for part in range(3):
            block = joined[part]
            if part < 2:
                block = block * score_scale
                block = block * cosine[...] - swap_halves(block) * sine[...]
            parts.append(block.astype(BF))
        total = grad_normed[...]
        for part in range(3):
            spot = pl.ds(pl.multiple_of(part * D + p * LANES, LANES), LANES)
            total = total + dot_nt(parts[part], weights[:, spot])
        grad_normed[...] = total
        dense[(out_chunks + p) % ring] = as_chunk(
            dot_tn(normed[...], jnp.concatenate(parts, axis=1))
        )

    last_sum = lines * lines

    def back_step(it, _):
        @pl.when((it >= out_chunks) & (it < chunks))
        def _():
            attend_back(it - out_chunks)

        dense_event(it)

        @pl.when(it + lines < last_sum)
        def _():
            sum_event((it + lines) // lines, (it + lines) % lines)

        return 0

    def tail_step(it, _):
        dense_event(it)

        @pl.when(it + lines < last_sum)
        def _():
            sum_event((it + lines) // lines, (it + lines) % lines)

        return 0

    lax.fori_loop(0, chunks, back_step, 0)

    gain_sum = jnp.zeros((1, D), F32)
    for block in range(row_blocks):
        at = slice(block * LANES, (block + 1) * LANES)
        inputs = tokens[at, :].astype(F32)
        scale = cols[at, 0:1]
        grad_norm = grad_normed[at, :]
        gain_sum = gain_sum + jnp.sum(grad_norm * inputs * scale, axis=0, keepdims=True)
        scaled = gain_one * grad_norm
        r["tokens_out"][at, :] = (
            grad_hidden[at, :]
            + scale * scaled
            - inputs * (scale * scale * scale) * jnp.mean(scaled * inputs, axis=1, keepdims=True)
        )
    sums[z, gate_cols + 7 : gate_cols + 8, :] = gain_sum

    layer_sums = r["layer_sums"]

    def sums_z(step, origin):
        return remote(
            sums.at[z],
            sums.at[origin],
            r["az_send"].at[step],
            r["az_recv"].at[origin],
            (e, ((z + step) % lines) * 2 + x),
        )

    def sums_layer(step, side, origin):
        return remote(
            layer_sums.at[mine],
            layer_sums.at[origin],
            r["al_send"].at[step, side],
            r["al_recv"].at[origin],
            ((e + step) % experts, 2 * z + side),
        )

    for step in range(1, lines):
        sums_z(step, z).start()
    lax.fori_loop(chunks, chunks + 2, tail_step, 0)
    for step in range(1, lines):
        sums_z(step, (z + lines - step) % lines).wait_recv()
    total = sums[0]
    for zz in range(1, lines):
        total = total + sums[zz]
    layer_sums[mine] = total
    others(lambda step, other, side, origin: sums_layer(step, side, mine).start())
    lax.fori_loop(chunks + 2, max(chunks + 4, last_sum - lines), tail_step, 0)
    others(lambda step, other, side, origin: sums_layer(step, side, origin).wait_recv())
    total = layer_sums[0]
    for other in range(1, layer):
        total = total + layer_sums[other]
    r["small_out"][...] = total

    for jj in range(lines):
        final_hop(jj).wait_recv()
        for part in range(2):
            up_out[:, up_columns(part, jj, 1 - x)] = final_box[
                jj, :, part * hidden_block : (part + 1) * hidden_block
            ].astype(F32)

    for kind in range(2):
        dense_sent(kind)
        for step in range(lines - 1):
            chain_sent(kind, step)
    for step in range(1, 2 * lines):
        small_copy(step, s).wait_send()
    for which in range(2):
        for step in range(experts):
            dispatch_each(which, step, lambda copy: copy.wait_send())
        others(lambda step, other, side, origin: come(which, step, side, e, x).wait_send())
    sum_sent()
    for jj in range(lines):
        final_hop(jj).wait_send()
    dense_events_sent()
    for step in range(1, lines):
        sums_z(step, z).wait_send()
    others(lambda step, other, side, origin: sums_layer(step, side, mine).wait_send())

SMALL_ROWS = 32
IN_NAMES = (
    "length", "tokens", "out_grad", "routes", "route_row", "order_row", "prev", "mix", "mix_t",
    "cosine", "sine", "qkv_in", "out_in", "small_in", "up_in", "down_in",
)
OUT_NAMES = (
    "block_out", "tokens_out", "prev_out", "qkv_out", "out_w_out", "small_out", "up_out", "down_out",
)


def scratch_list(dims):
    tok_rows, experts, lines, share, hidden_block, capacity, gate_cols = dims
    pairs = D // LANES
    chunk_cols = 3 * LANES
    chunks = D // chunk_cols + pairs
    slots = experts * capacity
    gathered = 2 * experts * capacity
    half = share // 2
    last = lines - 1
    wide = 2 * hidden_block
    vmem = {
        "weights": ((D, 4 * D), BF),
        "small": ((D, LANES), BF),
        "up": ((lines, D, wide), BF),
        "down": ((lines, hidden_block, D), BF),
        "stage": ((lines, share, wide), BF),
        "put": ((2, slots, tok_rows), BF),
        "take": ((2, tok_rows, slots), BF),
        "rows": ((8, D), F32),
        "cols": ((tok_rows, 16), F32),
        "normed": ((tok_rows, D), BF),
        "heads": ((3 * pairs, tok_rows, LANES), BF),
        "mixed": ((tok_rows, D), BF),
        "log_sums": ((pairs, 8, tok_rows), F32),
        "hidden": ((tok_rows, D), F32),
        "normed_low": ((tok_rows, D), BF),
        "grad_low": ((3, tok_rows, D), BF),
        "sent": ((2, experts, capacity, D), BF),
        "buffer": ((gathered, D), BF),
        "slot_grad": ((gathered, D), BF),
        "up_sum": ((lines, D, wide), BF),
        "down_sum": ((lines, hidden_block, D), BF),
        "up_box": ((2, last, lines, 2 * share, wide), BF),
        "down_box": ((lines + 1, hidden_block, D), BF),
        "final_box": ((lines, share, wide), BF),
        "ffn": ((gathered, D), F32),
        "slot_back": ((gathered, D), F32),
        "act": ((gathered, hidden_block), BF),
        "grad_gu": ((gathered, wide), BF),
        "back_box": ((2, 2, slots, D), BF),
        "grad_attn": ((tok_rows, D), BF),
        "thin": ((tok_rows, LANES), BF),
        "wide": ((tok_rows, LANES), BF),
        "grad_logits": ((tok_rows, gate_cols), F32),
        "sums": ((lines, SMALL_ROWS, D), F32),
        "layer_sums": ((2 * experts, SMALL_ROWS, D), F32),
        "dense": ((RING, lines, 2, 2, half, chunk_cols), BF),
        "core_box": ((chunks, lines, 2, half, chunk_cols), BF),
        "x_box": ((chunks, lines, half, chunk_cols), BF),
        "z_box": ((chunks, lines, half, chunk_cols), BF),
        "all_box": ((chunks, experts, half, chunk_cols), BF),
    }
    sems = {
        "dz_send": (2, lines),
        "dx_send": (2, lines),
        "dc_send": (2, lines, 2),
        "d_recv": (2, lines, 2, 2),
        "sm_send": (2 * lines,),
        "sm_recv": (2 * lines,),
        "ux_send": (),
        "ux_recv": (),
        "ch_send": (2, 2, last),
        "ch_recv": (2, 2, last),
        "go_send": (2, experts, 2),
        "go_recv": (2, 2 * experts),
        "come_send": (2, experts, 2),
        "come_recv": (2, experts, 2),
        "ru_send": (2, last, lines),
        "ru_recv": (2, last, lines),
        "rd_send": (2, lines),
        "rd_recv": (2, lines),
        "fx_send": (lines,),
        "fx_recv": (lines,),
        "gc_send": (chunks,),
        "gc_recv": (chunks,),
        "gx_send": (chunks,),
        "gx_recv": (chunks,),
        "gz_send": (chunks, lines),
        "gz_recv": (chunks, lines),
        "ga_send": (chunks, experts),
        "ga_recv": (chunks, experts),
        "az_send": (lines,),
        "az_recv": (lines,),
        "al_send": (experts, 2),
        "al_recv": (2 * experts,),
    }
    names = tuple(vmem) + tuple(sems)
    shapes = [pltpu.VMEM(*spec) for spec in vmem.values()]
    shapes += [pltpu.SemaphoreType.DMA(shape) for shape in sems.values()]
    return names, shapes


def kernel_body(
    tokens,
    seq_lengths,
    routes,
    pair_order,
    prev_logits,
    out_grad,
    qkv_weight,
    out_weight,
    gate_weight,
    const_weight,
    const_vector,
    norm1_gain,
    norm2_gain,
    gate_mix,
    expert_up,
    expert_down,
):
    tok_rows = tokens.shape[0]
    experts = lax.axis_size("expert")
    shards = lax.axis_size("shard")
    share = qkv_weight.shape[0]
    gate_cols = gate_weight.shape[1]
    hidden_block = expert_down.shape[1]
    capacity = 2 * tok_rows // (experts + 4)
    dims = (tok_rows, experts, shards // 2, share, hidden_block, capacity, gate_cols)
    small_in = jnp.concatenate(
        [
            gate_weight,
            const_weight,
            const_weight,
            const_vector,
            norm1_gain[:, None],
            norm2_gain[:, None],
            jnp.zeros((share, LANES - gate_cols - 12), BF),
        ],
        axis=1,
    )
    cosine, sine_table = tables(tok_rows, HEAD_DIM)
    cosine = jnp.tile(cosine[:, 0, :], (1, 2 * LANES // HEAD_DIM))
    sine_table = sine_table[:, 0, :]
    sine_table = jnp.tile(
        jnp.concatenate([-sine_table, sine_table], axis=1), (1, LANES // HEAD_DIM)
    )
    mixer = gate_mix.astype(F32)
    args = (
        seq_lengths,
        tokens,
        out_grad,
        routes,
        routes.T.reshape(1, 2 * tok_rows),
        pair_order,
        prev_logits,
        mixer,
        mixer.T,
        cosine,
        sine_table,
        qkv_weight,
        out_weight,
        small_in,
        expert_up[0],
        expert_down[0],
    )
    names, shapes = scratch_list(dims)
    vmem = pl.BlockSpec(memory_space=pltpu.VMEM)
    outs = pl.pallas_call(
        functools.partial(step_kernel, dims, names),
        out_shape=(
            jax.ShapeDtypeStruct((tok_rows, D), BF),
            jax.ShapeDtypeStruct((tok_rows, D), F32),
            jax.ShapeDtypeStruct((tok_rows, gate_cols), F32),
            jax.ShapeDtypeStruct((share, 3 * D), F32),
            jax.ShapeDtypeStruct((share, D), F32),
            jax.ShapeDtypeStruct((SMALL_ROWS, D), F32),
            jax.ShapeDtypeStruct((share, 2 * FF), F32),
            jax.ShapeDtypeStruct((hidden_block, D), F32),
        ),
        in_specs=[pl.BlockSpec(memory_space=pltpu.SMEM)] + [vmem] * (len(args) - 1),
        out_specs=(vmem,) * len(OUT_NAMES),
        scratch_shapes=shapes,
        compiler_params=pltpu.CompilerParams(
            collective_id=0, has_side_effects=True, vmem_limit_bytes=VMEM_BYTES
        ),
        name="step",
    )(*args)
    block_out, tokens_grad, prev_grad, qkv_grad, out_w_grad, small_sum, up_grad, down_grad = outs
    start = lax.axis_index("shard") * share
    own = lax.dynamic_slice(small_sum, (0, start), (gate_cols + 8, share))
    base = gate_cols
    return (
        block_out,
        tokens_grad,
        prev_grad,
        qkv_grad,
        out_w_grad,
        own[0:base].T,
        own[base : base + 4].T,
        own[base + 4 : base + 6].T,
        own[base + 7],
        own[base + 6],
        small_sum[SMALL_ROWS - 16 : SMALL_ROWS - 16 + gate_cols, 0:gate_cols],
        up_grad[None],
        down_grad[None],
    )


def fits_kernel(mesh):
    experts, shards = mesh.shape["expert"], mesh.shape["shard"]
    share, hidden_block = D // shards, FF // shards
    return (
        experts % 2 == 0
        and shards % 2 == 0
        and share % 32 == 0
        and hidden_block % LANES == 0
        and experts + 4 <= 8
    )


def solution(mesh):
    placed = (
        P(("expert", "shard"), None),
        P(("expert", "shard")),
        P(("expert", "shard"), None),
        P(("expert", "shard"), None),
        P(("expert", "shard"), None),
        P(("expert", "shard"), None),
        P("shard", None),
        P("shard", None),
        P("shard", None),
        P("shard", None),
        P("shard", None),
        P("shard"),
        P("shard"),
        P(),
        P("expert", "shard", None),
        P("expert", "shard", None),
    )
    return jax.shard_map(
        kernel_body if fits_kernel(mesh) else body,
        mesh=mesh,
        in_specs=placed,
        out_specs=(
            P(("expert", "shard"), None),
            P(("expert", "shard"), None),
            P(("expert", "shard"), None),
            P("shard", None),
            P("shard", None),
            P("shard", None),
            P("shard", None),
            P("shard", None),
            P("shard"),
            P("shard"),
            P(),
            P("expert", "shard", None),
            P("expert", "shard", None),
        ),
        check_vma=False,
    )
```

```python
import functools

import jax
import jax.numpy as jnp
import numpy as np
from jax import lax
from jax.experimental import pallas as pl
from jax.experimental.pallas import tpu as pltpu
from jax.sharding import PartitionSpec as P

D = 768
FF = 2048
HEADS = 12
HEAD_DIM = 64


norm_eps = 1e-06
rotary_base = 10000.0
highest = lax.Precision.HIGHEST


def tables(tok_rows, head_dim):
    half_dim = head_dim // 2
    frequency = rotary_base ** (-(jnp.arange(half_dim, dtype=jnp.float32) * 2.0 / head_dim))
    angles = jnp.arange(tok_rows, dtype=jnp.float32)[:, None] * frequency[None, :]
    return (jnp.cos(angles)[:, None, :], jnp.sin(angles)[:, None, :])


def rotate(field, cosine, sine_table):
    half_dim = field.shape[-1] // 2
    first_half = field[..., :half_dim]
    second_half = field[..., half_dim:]
    return jnp.concatenate(
        [
            first_half * cosine - second_half * sine_table,
            second_half * cosine + first_half * sine_table,
        ],
        axis=-1,
    )


def place_pairs(route_rows, order, length, experts_ffn, capacity):
    tok_rows = route_rows.shape[0]
    token_ids = jnp.arange(tok_rows, dtype=jnp.int32)
    pair_valid = jnp.repeat(token_ids < length, 2)
    expert_flat = route_rows.reshape(-1)
    placed_expert = expert_flat[order]
    placed_live = pair_valid[order] & (placed_expert < experts_ffn)
    one_hot = (
        placed_expert[:, None] == jnp.arange(experts_ffn, dtype=jnp.int32)[None, :]
    ) & placed_live[:, None]
    counts = jnp.cumsum(one_hot.astype(jnp.int32), axis=0)
    slot_index = jnp.sum(jnp.where(one_hot, counts - 1, 0), axis=1)
    kept_pairs = placed_live & (slot_index < capacity)
    dest_placed = jnp.where(
        kept_pairs, placed_expert * capacity + slot_index, experts_ffn * capacity
    )
    pair_dest = jnp.zeros((2 * tok_rows,), jnp.int32).at[order].set(dest_placed)
    slot_pair = (
        jnp.full((experts_ffn * capacity,), 2 * tok_rows, jnp.int32)
        .at[dest_placed]
        .set(order, mode="drop")
    )
    return (pair_dest, slot_pair)


def attend_head(head, allowed, score_scale):
    query, keys_rot, values = head
    scores = jnp.dot(query, keys_rot.T, preferred_element_type=jnp.float32) * score_scale
    scores = jnp.where(allowed, scores, -1e30)
    top_score = jnp.max(scores, axis=1, keepdims=True)
    expo = jnp.exp(scores - top_score)
    total = jnp.sum(expo, axis=1, keepdims=True)
    probs = expo / total
    mixed = jnp.dot(probs.astype(jnp.bfloat16), values, preferred_element_type=jnp.float32).astype(
        jnp.bfloat16
    )
    return (mixed, top_score + jnp.log(total))


def attend_back(head, allowed, score_scale):
    query, keys_rot, values, grad_mixed, log_total = head
    scores = jnp.dot(query, keys_rot.T, preferred_element_type=jnp.float32) * score_scale
    scores = jnp.where(allowed, scores, -1e30)
    probs = jnp.where(allowed, jnp.exp(scores - log_total), 0.0)
    grad_probs = jnp.dot(grad_mixed, values.T, preferred_element_type=jnp.float32)
    delta = jnp.sum(grad_probs * probs, axis=1, keepdims=True)
    grad_scores = (probs * (grad_probs - delta)).astype(jnp.bfloat16)
    grad_query = jnp.dot(grad_scores, keys_rot, preferred_element_type=jnp.float32) * score_scale
    grad_key = jnp.dot(grad_scores.T, query, preferred_element_type=jnp.float32) * score_scale
    grad_value = jnp.dot(
        probs.astype(jnp.bfloat16).T, grad_mixed, preferred_element_type=jnp.float32
    )
    return (grad_query, grad_key, grad_value)


def body(
    tokens,
    seq_lengths,
    routes,
    pair_order,
    prev_logits,
    out_grad,
    qkv_weight,
    out_weight,
    gate_weight,
    const_weight,
    const_vector,
    norm1_gain,
    norm2_gain,
    gate_mix,
    expert_up,
    expert_down,
):
    tok_rows = tokens.shape[0]
    experts_ffn = lax.axis_size("expert")
    capacity = 2 * tok_rows // (experts_ffn + 4)
    length = seq_lengths[0]
    order = pair_order[0]
    score_scale = HEAD_DIM ** (-0.5)
    dense_shards = (
        qkv_weight,
        out_weight,
        gate_weight,
        const_weight,
        const_vector,
        norm1_gain,
        norm2_gain,
    )
    weight_qkv, weight_out, weight_gate, weight_const, vector_const, gain_one, gain_two = (
        lax.all_gather(dense_shards[0], "shard", axis=0, tiled=True),
        lax.all_gather(dense_shards[1], "shard", axis=0, tiled=True),
        lax.all_gather(dense_shards[2], "shard", axis=0, tiled=True),
        lax.all_gather(dense_shards[3], "shard", axis=0, tiled=True),
        lax.all_gather(dense_shards[4], "shard", axis=0, tiled=True),
        lax.all_gather(dense_shards[5], "shard", axis=0, tiled=True),
        lax.all_gather(dense_shards[6], "shard", axis=0, tiled=True),
    )
    weight_up, weight_down = (
        lax.all_gather(expert_up, "shard", axis=1, tiled=True),
        lax.all_gather(expert_down, "shard", axis=1, tiled=True),
    )
    weight_up = weight_up[0]
    weight_down = weight_down[0]
    inputs = tokens.astype(jnp.float32)
    token_ids = jnp.arange(tok_rows, dtype=jnp.int32)
    valid_mask = (token_ids < length).astype(jnp.float32)[:, None]
    gain_first = gain_one.astype(jnp.float32)
    gain_second = gain_two.astype(jnp.float32)
    scale_one = lax.rsqrt(jnp.mean(inputs * inputs, axis=1, keepdims=True) + norm_eps)
    normed = (inputs * scale_one * gain_first).astype(jnp.bfloat16)
    qkv_all = jnp.dot(normed, weight_qkv, preferred_element_type=jnp.float32)
    cosine, sine_table = tables(tok_rows, HEAD_DIM)

    def heads_first(block):
        return jnp.transpose(block, (1, 0, 2)).astype(jnp.bfloat16)

    query = heads_first(
        rotate(qkv_all[:, :D].reshape(tok_rows, HEADS, HEAD_DIM), cosine, sine_table)
    )
    keys_rot = heads_first(
        rotate(qkv_all[:, D : 2 * D].reshape(tok_rows, HEADS, HEAD_DIM), cosine, sine_table)
    )
    values = heads_first(qkv_all[:, 2 * D :].reshape(tok_rows, HEADS, HEAD_DIM))
    allowed = (token_ids[None, :] <= token_ids[:, None]) & (token_ids[None, :] < length)
    mixed_heads, log_totals = lax.map(
        lambda head: attend_head(head, allowed, score_scale), (query, keys_rot, values)
    )
    mixed = jnp.transpose(mixed_heads, (1, 0, 2)).reshape(tok_rows, D)
    hidden = inputs + jnp.dot(mixed, weight_out, preferred_element_type=jnp.float32)
    scale_two = lax.rsqrt(jnp.mean(hidden * hidden, axis=1, keepdims=True) + norm_eps)
    normed_two = hidden * scale_two * gain_second
    normed_low = normed_two.astype(jnp.bfloat16)
    mixer = gate_mix.astype(jnp.float32)
    logits = jnp.dot(normed_low, weight_gate, preferred_element_type=jnp.float32) + jnp.dot(
        prev_logits, mixer, precision=highest
    )
    chosen = jnp.take_along_axis(logits, routes, axis=1)
    gate_exp = jnp.exp(chosen - jnp.max(chosen, axis=1, keepdims=True))
    gates = gate_exp / jnp.sum(gate_exp, axis=1, keepdims=True)
    pair_dest, slot_pair = place_pairs(routes, order, length, experts_ffn, capacity)
    padded = jnp.concatenate([normed_low, jnp.zeros((1, D), jnp.bfloat16)], axis=0)
    send_rows = padded[slot_pair // 2].reshape(experts_ffn, capacity, D)
    received = lax.all_to_all(send_rows, "expert", split_axis=0, concat_axis=0, tiled=True)
    lead_shape = received.shape[:2]
    flat_rows = received.reshape(-1, D)
    gate_up = jnp.dot(flat_rows, weight_up, preferred_element_type=jnp.float32)
    activated = (jax.nn.silu(gate_up[:, :FF]) * gate_up[:, FF:]).astype(jnp.bfloat16)
    expert_out = jnp.dot(activated, weight_down, preferred_element_type=jnp.float32).astype(
        jnp.bfloat16
    )
    received, gate_up, activated, expert_out = (
        received,
        gate_up.reshape(lead_shape + (2 * FF,)),
        activated.reshape(lead_shape + (FF,)),
        expert_out.reshape(received.shape),
    )
    returned = lax.all_to_all(expert_out, "expert", split_axis=0, concat_axis=0, tiled=True)
    returned_pad = jnp.concatenate(
        [returned.reshape(-1, D), jnp.zeros((1, D), jnp.bfloat16)], axis=0
    )
    pair_ffn = returned_pad[pair_dest].astype(jnp.float32).reshape(tok_rows, 2, D)
    vector_float = vector_const.astype(jnp.float32)
    const_logits = jnp.dot(normed_low, weight_const, preferred_element_type=jnp.float32).reshape(
        tok_rows, 2, 2
    )
    const_exp = jnp.exp(const_logits - jnp.max(const_logits, axis=2, keepdims=True))
    coefs = const_exp / jnp.sum(const_exp, axis=2, keepdims=True)
    const_out = (
        coefs[..., 0:1] * normed_two[:, None, :] + coefs[..., 1:2] * vector_float.T[None, :, :]
    )
    const_select = (
        routes[:, :, None] == experts_ffn + 2 + jnp.arange(2, dtype=jnp.int32)[None, None, :]
    ).astype(jnp.float32)
    copy_select = (routes == experts_ffn + 1).astype(jnp.float32)[:, :, None]
    pair_out = (
        pair_ffn
        + copy_select * normed_two[:, None, :]
        + jnp.einsum("tkc,tcd->tkd", const_select, const_out, precision=highest)
    )
    mixture = jnp.sum(gates[:, :, None] * pair_out, axis=1)
    block_out = (valid_mask * (hidden + mixture)).astype(jnp.bfloat16)
    back_dense = (
        lax.all_gather(dense_shards[0], "shard", axis=0, tiled=True),
        lax.all_gather(dense_shards[1], "shard", axis=0, tiled=True),
        lax.all_gather(dense_shards[2], "shard", axis=0, tiled=True),
        lax.all_gather(dense_shards[3], "shard", axis=0, tiled=True),
        lax.all_gather(dense_shards[4], "shard", axis=0, tiled=True),
        lax.all_gather(dense_shards[5], "shard", axis=0, tiled=True),
        lax.all_gather(dense_shards[6], "shard", axis=0, tiled=True),
    )
    back_up, back_down = (
        lax.all_gather(expert_up, "shard", axis=1, tiled=True),
        lax.all_gather(expert_down, "shard", axis=1, tiled=True),
    )
    back_up = back_up[0]
    back_down = back_down[0]
    back_qkv, back_out, back_gate, back_const = (
        back_dense[0],
        back_dense[1],
        back_dense[2],
        back_dense[3],
    )
    grad_rows = out_grad.astype(jnp.float32) * valid_mask
    grad_gates = jnp.sum(grad_rows[:, None, :] * pair_out, axis=2)
    grad_pairs = gates[:, :, None] * grad_rows[:, None, :]
    grad_chosen = gates * (grad_gates - jnp.sum(gates * grad_gates, axis=1, keepdims=True))
    route_hot = (
        routes[:, :, None] == jnp.arange(experts_ffn + 4, dtype=jnp.int32)[None, None, :]
    ).astype(jnp.float32)
    grad_logits = jnp.sum(route_hot * grad_chosen[:, :, None], axis=1)
    prev_grad = jnp.dot(grad_logits, mixer.T, precision=highest)
    mix_term = jnp.dot(prev_logits.T, grad_logits, precision=highest)
    logit_low = grad_logits.astype(jnp.bfloat16)
    gate_term = jnp.dot(normed_low.T, logit_low, preferred_element_type=jnp.float32)
    grad_normed = jnp.dot(logit_low, back_gate.T, preferred_element_type=jnp.float32)
    grad_flat = jnp.concatenate(
        [grad_pairs.reshape(2 * tok_rows, D).astype(jnp.bfloat16), jnp.zeros((1, D), jnp.bfloat16)],
        axis=0,
    )
    grad_send = grad_flat[slot_pair].reshape(experts_ffn, capacity, D)
    grad_recv = lax.all_to_all(grad_send, "expert", split_axis=0, concat_axis=0, tiled=True)
    grad_slots = grad_recv.reshape(-1, D)
    down_term = jnp.dot(activated.reshape(-1, FF).T, grad_slots, preferred_element_type=jnp.float32)
    grad_act = jnp.dot(grad_slots, back_down.T, preferred_element_type=jnp.float32)
    gate_part = gate_up[..., :FF].reshape(-1, FF)
    up_part = gate_up[..., FF:].reshape(-1, FF)
    sigmoid_gate = jax.nn.sigmoid(gate_part)
    grad_gate_up = jnp.concatenate(
        [
            grad_act * up_part * sigmoid_gate * (1.0 + gate_part * (1.0 - sigmoid_gate)),
            grad_act * gate_part * sigmoid_gate,
        ],
        axis=1,
    ).astype(jnp.bfloat16)
    up_term = jnp.dot(received.reshape(-1, D).T, grad_gate_up, preferred_element_type=jnp.float32)
    grad_input = (
        jnp.dot(grad_gate_up, back_up.T, preferred_element_type=jnp.float32)
        .astype(jnp.bfloat16)
        .reshape(received.shape)
    )
    grad_back = lax.all_to_all(grad_input, "expert", split_axis=0, concat_axis=0, tiled=True)
    back_pad = jnp.concatenate([grad_back.reshape(-1, D), jnp.zeros((1, D), jnp.bfloat16)], axis=0)
    grad_normed = grad_normed + jnp.sum(
        back_pad[pair_dest].astype(jnp.float32).reshape(tok_rows, 2, D), axis=1
    )
    grad_normed = grad_normed + jnp.sum(copy_select * grad_pairs, axis=1)
    grad_const_out = jnp.einsum("tkc,tkd->tcd", const_select, grad_pairs, precision=highest)
    grad_first = jnp.sum(grad_const_out * normed_two[:, None, :], axis=2)
    grad_second = jnp.sum(grad_const_out * vector_float.T[None, :, :], axis=2)
    grad_coefs = jnp.stack([grad_first, grad_second], axis=2)
    grad_const_logits = (
        coefs * (grad_coefs - jnp.sum(coefs * grad_coefs, axis=2, keepdims=True))
    ).reshape(tok_rows, 4)
    grad_normed = grad_normed + jnp.sum(coefs[..., 0:1] * grad_const_out, axis=1)
    grad_normed = grad_normed + jnp.dot(
        grad_const_logits, back_const.astype(jnp.float32).T, precision=highest
    )
    vector_term = jnp.einsum("tc,tcd->dc", coefs[..., 1], grad_const_out, precision=highest)
    const_term = jnp.dot(normed_low.astype(jnp.float32).T, grad_const_logits, precision=highest)
    second_gain_term = jnp.sum(grad_normed * hidden * scale_two, axis=0)
    scaled_two = gain_second * grad_normed
    grad_hidden = (
        grad_rows
        + scale_two * scaled_two
        - hidden * scale_two**3 * jnp.mean(scaled_two * hidden, axis=1, keepdims=True)
    )
    grad_attn_low = grad_hidden.astype(jnp.bfloat16)
    out_term = jnp.dot(mixed.T, grad_attn_low, preferred_element_type=jnp.float32)
    grad_mixed = jnp.dot(grad_attn_low, back_out.T, preferred_element_type=jnp.float32).astype(
        jnp.bfloat16
    )
    grad_mixed_heads = jnp.transpose(grad_mixed.reshape(tok_rows, HEADS, HEAD_DIM), (1, 0, 2))
    grad_query, grad_key, grad_value = lax.map(
        lambda head: attend_back(head, allowed, score_scale),
        (query, keys_rot, values, grad_mixed_heads, log_totals),
    )
    grad_query = rotate(jnp.transpose(grad_query, (1, 0, 2)), cosine, -sine_table).reshape(
        tok_rows, D
    )
    grad_key = rotate(jnp.transpose(grad_key, (1, 0, 2)), cosine, -sine_table).reshape(tok_rows, D)
    grad_value = jnp.transpose(grad_value, (1, 0, 2)).reshape(tok_rows, D)
    grad_qkv = jnp.concatenate([grad_query, grad_key, grad_value], axis=1).astype(jnp.bfloat16)
    qkv_term = jnp.dot(normed.T, grad_qkv, preferred_element_type=jnp.float32)
    grad_first_norm = jnp.dot(grad_qkv, back_qkv.T, preferred_element_type=jnp.float32)
    first_gain_term = jnp.sum(grad_first_norm * inputs * scale_one, axis=0)
    scaled_one = gain_first * grad_first_norm
    tokens_grad = (
        grad_hidden
        + scale_one * scaled_one
        - inputs * scale_one**3 * jnp.mean(scaled_one * inputs, axis=1, keepdims=True)
    )
    dense_all = (
        qkv_term,
        out_term,
        gate_term,
        const_term,
        vector_term,
        first_gain_term,
        second_gain_term,
    )
    dense_terms = (
        lax.psum_scatter(dense_all[0], "shard", scatter_dimension=0, tiled=True),
        lax.psum_scatter(dense_all[1], "shard", scatter_dimension=0, tiled=True),
        lax.psum_scatter(dense_all[2], "shard", scatter_dimension=0, tiled=True),
        lax.psum_scatter(dense_all[3], "shard", scatter_dimension=0, tiled=True),
        lax.psum_scatter(dense_all[4], "shard", scatter_dimension=0, tiled=True),
        lax.psum_scatter(dense_all[5], "shard", scatter_dimension=0, tiled=True),
        lax.psum_scatter(dense_all[6], "shard", scatter_dimension=0, tiled=True),
    )
    (
        qkv_grad,
        out_weight_grad,
        gate_grad,
        const_weight_grad,
        const_vector_grad,
        norm1_grad,
        norm2_grad,
    ) = lax.psum(
        (
            dense_terms[0],
            dense_terms[1],
            dense_terms[2],
            dense_terms[3],
            dense_terms[4],
            dense_terms[5],
            dense_terms[6],
        ),
        "expert",
    )
    mix_grad = lax.psum(mix_term, ("expert", "shard"))
    expert_up_grad, expert_down_grad = (
        lax.psum_scatter(up_term[None], "shard", scatter_dimension=1, tiled=True),
        lax.psum_scatter(down_term[None], "shard", scatter_dimension=1, tiled=True),
    )
    return (
        block_out,
        tokens_grad,
        prev_grad,
        qkv_grad,
        out_weight_grad,
        gate_grad,
        const_weight_grad,
        const_vector_grad,
        norm1_grad,
        norm2_grad,
        mix_grad,
        expert_up_grad,
        expert_down_grad,
    )


MESH = pl.DeviceIdType.MESH
BF = jnp.bfloat16
F32 = jnp.float32
LANES = 128
NEG = -1e30
VMEM_BYTES = 64 * 1024 * 1024
RING = 3
HOPS = (0, 1, 3, 5, 7, 9)


def dot(a, b):
    return lax.dot_general(a, b, (((1,), (0,)), ((), ())), preferred_element_type=F32)


def dot_nt(a, b):
    return lax.dot_general(a, b, (((1,), (1,)), ((), ())), preferred_element_type=F32)


def dot_tn(a, b):
    return lax.dot_general(a, b, (((0,), (0,)), ((), ())), preferred_element_type=F32)


def iota(shape, dim):
    return lax.broadcasted_iota(jnp.int32, shape, dim)


def remote(src, dst, send_sem, recv_sem, target):
    return pltpu.make_async_remote_copy(
        src_ref=src,
        dst_ref=dst,
        send_sem=send_sem,
        recv_sem=recv_sem,
        device_id=target,
        device_id_type=MESH,
    )


def swap_halves(block):
    half = HEAD_DIM // 2
    width = block.shape[1]
    lower = (iota(block.shape, 1) % HEAD_DIM) < half
    return jnp.where(
        lower, pltpu.roll(block, width - half, 1), pltpu.roll(block, half, 1)
    )


def step_kernel(dims, scratch_names, *refs):
    (tok_rows, experts, lines, share, hidden_block, capacity, gate_cols) = dims
    names = IN_NAMES + OUT_NAMES + scratch_names
    r = dict(zip(names, refs))
    pairs = D // LANES
    layer = 2 * experts
    slots = experts * capacity
    quarter = share // 4
    chunk_cols = 3 * LANES
    out_chunks = D // chunk_cols
    chunks = out_chunks + pairs
    half_ffn = lines * 2 * hidden_block
    const_col = gate_cols
    vec_col = gate_cols + 8
    row_blocks = tok_rows // LANES

    e = lax.axis_index("expert")
    s = lax.axis_index("shard")
    z = s // 2
    x = s % 2
    core = e % 2
    half = e // 2
    facing = 2 * (1 - half) + core
    across = 2 * z + 1 - x
    twin = e + 1 - 2 * core
    mine = 2 * e + x

    def rows(index, size):
        return pl.ds(pl.multiple_of(index * size, size), size)

    barrier = pltpu.get_barrier_semaphore()
    met = 0
    for step in range(1, 2 * lines):
        pl.semaphore_signal(
            barrier, 1, device_id=(e, (s + step) % (2 * lines)), device_id_type=MESH
        )
        met += 1
    for step in range(1, experts):
        for side in range(2):
            pl.semaphore_signal(
                barrier, 1, device_id=((e + step) % experts, 2 * z + side), device_id_type=MESH
            )
            met += 1
    pl.semaphore_wait(barrier, met)

    up, down, stage = r["up"], r["down"], r["stage"]
    up_in = r["up_in"]

    def up_columns(part, jj, xx):
        return pl.ds(
            pl.multiple_of(part * FF + hidden_block * (2 * jj + xx), hidden_block), hidden_block
        )

    own_rows = rows(s, share)
    for jj in range(lines):
        for part in range(2):
            spot = pl.ds(part * hidden_block, hidden_block)
            stage[jj, :, spot] = up_in[:, up_columns(part, jj, 1 - x)]
            up[jj, own_rows, spot] = up_in[:, up_columns(part, jj, x)]
    down[z] = r["down_in"][...]

    def up_across(jj, origin_x):
        return remote(
            stage.at[jj],
            up.at[jj, rows(2 * z + origin_x, share), :],
            r["ux_send"].at[jj],
            r["ux_recv"].at[jj],
            (e, across),
        )

    def chain(kind, way, step, jj, zz):
        ref = up.at[jj, rows(zz, 2 * share), :] if kind == 0 else down.at[jj]
        target = s + 2 if way == 0 else s - 2
        return remote(
            ref,
            ref,
            r["ch_send"].at[kind, way, step, jj],
            r["ch_recv"].at[kind, way, step, jj],
            (e, target),
        )

    def chain_each(way, step, jj, zz, go):
        go(chain(0, way, step, jj, zz))

        @pl.when(zz == jj)
        def _():
            go(chain(1, way, step, jj, zz))

    def begin(copy):
        copy.start()

    def arrive(copy):
        copy.wait_recv()

    def leave(copy):
        copy.wait_send()

    def chain_own(jj):
        up_across(jj, 1 - x).wait_recv()

        @pl.when(z + 1 < lines)
        def _():
            chain_each(0, 0, jj, z, begin)

        @pl.when(z > 0)
        def _():
            chain_each(1, 0, jj, z, begin)

    def chain_pass(jj, step):
        @pl.when((z - 1 - step >= 0) & (z + 1 < lines))
        def _():
            chain_each(0, step, jj, z - 1 - step, arrive)
            chain_each(0, step + 1, jj, z - 1 - step, begin)

        @pl.when((z + 1 + step < lines) & (z > 0))
        def _():
            chain_each(1, step, jj, z + 1 + step, arrive)
            chain_each(1, step + 1, jj, z + 1 + step, begin)

    def chain_end(jj):
        for step in range(lines - 1):

            @pl.when((z - 1 - step >= 0) & (z + 1 == lines))
            def _():
                chain_each(0, step, jj, z - 1 - step, arrive)

            @pl.when((z + 1 + step < lines) & (z == 0))
            def _():
                chain_each(1, step, jj, z + 1 + step, arrive)

    def chain_sent():
        for jj in range(lines):
            for step in range(lines - 1):

                @pl.when((z - step >= 0) & (z + 1 < lines))
                def _():
                    chain_each(0, step, jj, z - step, leave)

                @pl.when((z + step < lines) & (z > 0))
                def _():
                    chain_each(1, step, jj, z + step, leave)

    passes = [(jj, step) for step in range(lines - 2) for jj in range(lines)]

    def chain_events(first, count):
        for number in range(first, min(first + count, len(passes))):
            chain_pass(*passes[number])

    for jj in range(lines):
        up_across(jj, x).start()

    weights, small = r["weights"], r["small"]
    weights[rows(s, share), 0 : 3 * D] = r["qkv_in"][...]
    weights[rows(s, share), 3 * D : 4 * D] = r["out_in"][...]
    spans = ((0, 3 * D // 2), (3 * D, D // 2))

    def slab(kind, zz, xx, cc):
        start, width = spans[kind]
        columns = pl.ds(pl.multiple_of(start + width * cc, LANES), width)
        return weights.at[rows(2 * zz + xx, share), columns]

    def dense_z(kind, way, step, zz):
        ref = slab(kind, zz, x, core)
        return remote(
            ref,
            ref,
            r["dz_send"].at[kind, way, step],
            r["d_recv"].at[kind, zz, x, core],
            (e, s + 2 if way == 0 else s - 2),
        )

    def dense_z_each(kind, step, go):
        @pl.when((z - step >= 0) & (z + 1 < lines))
        def _():
            go(dense_z(kind, 0, step, z - step))

        @pl.when((z + step < lines) & (z > 0))
        def _():
            go(dense_z(kind, 1, step, z + step))

    def dense_x(kind, zz):
        ref = slab(kind, zz, x, core)
        return remote(
            ref, ref, r["dx_send"].at[kind, zz], r["d_recv"].at[kind, zz, x, core], (e, across)
        )

    def dense_core(kind, zz, xx):
        ref = slab(kind, zz, xx, core)
        return remote(
            ref,
            ref,
            r["dc_send"].at[kind, zz, xx],
            r["d_recv"].at[kind, zz, xx, core],
            (twin, s),
        )

    def dense_arrived(kind, zz, xx, cc):
        ref = slab(kind, zz, xx, cc)
        remote(
            ref, ref, r["dx_send"].at[kind, 0], r["d_recv"].at[kind, zz, xx, cc], (e, across)
        ).wait_recv()

    def dense_start(kind):
        dense_z_each(kind, 0, lambda copy: copy.start())
        dense_x(kind, z).start()

    def dense_forward(kind, step):
        for zz, there in ((z - 1 - step, z - 1 - step >= 0), (z + 1 + step, z + 1 + step < lines)):

            @pl.when(there)
            def _():
                dense_arrived(kind, zz, x, core)

                if step + 1 < lines - 1:

                    @pl.when((zz < z) & (z + 1 < lines))
                    def _():
                        dense_z(kind, 0, step + 1, zz).start()

                    @pl.when((zz > z) & (z > 0))
                    def _():
                        dense_z(kind, 1, step + 1, zz).start()

                dense_x(kind, zz).start()
                dense_core(kind, zz, x).start()

    def dense_share(kind):
        for step in range(lines):
            zz = (z + lines - step) % lines
            dense_arrived(kind, zz, 1 - x, core)
            dense_core(kind, zz, 1 - x).start()

    def dense_finish(kind):
        for step in range(lines):
            zz = (z + lines - step) % lines
            if step > 0:
                dense_arrived(kind, zz, x, 1 - core)
            dense_arrived(kind, zz, 1 - x, 1 - core)

    def dense_sent(kind):
        for step in range(lines - 1):
            dense_z_each(kind, step, lambda copy: copy.wait_send())
        for step in range(lines):
            zz = (z + lines - step) % lines
            dense_x(kind, zz).wait_send()
            if step > 0:
                dense_core(kind, zz, x).wait_send()
            dense_core(kind, zz, 1 - x).wait_send()

    def small_copy(step, origin):
        ref = small.at[rows(origin, share), :]
        return remote(
            ref,
            ref,
            r["sm_send"].at[step],
            r["sm_recv"].at[origin],
            (e, (s + step) % (2 * lines)),
        )

    dense_start(0)
    pack = r["pack"]
    pack[...] = jnp.zeros_like(pack)
    spot = 0
    for name in ("gate_in", "const_in", "const_in", "vec_in", "one_in", "two_in"):
        height = r[name].shape[0]
        pack[spot : spot + height, 0:share] = r[name][...].astype(F32)
        spot += height
    small[rows(s, share), :] = jnp.transpose(pack[...])[0:share, :].astype(BF)
    for step in range(1, 2 * lines):
        small_copy(step, s).start()
    token_rows, token_cols = r["token_rows"], r["token_cols"]
    token_rows[...] = jnp.zeros_like(token_rows)
    token_rows[0:2, :] = r["routes_in"][...].astype(F32)
    token_rows[8 : 8 + gate_cols, :] = r["prev_in"][...]
    token_cols[...] = jnp.transpose(token_rows[...])

    tokens = r["tokens"]
    cols = r["cols"]
    for block in range(row_blocks):
        at = slice(block * LANES, (block + 1) * LANES)
        inputs = tokens[at, :].astype(F32)
        cols[at, 0:1] = lax.rsqrt(jnp.mean(inputs * inputs, axis=1, keepdims=True) + norm_eps)
    dense_forward(0, 0)
    dense_start(1)

    dense_forward(0, 1)

    length = r["length"][0]
    pair_ids = iota((2 * tok_rows, 2 * tok_rows), 0)
    pair_names = jnp.where(pair_ids < tok_rows, 2 * pair_ids, 2 * (pair_ids - tok_rows) + 1)
    is_at = jnp.where(pair_names == r["order_row"][...], 1.0, 0.0).astype(BF)
    pair_lane = iota((16, 2 * tok_rows), 1)
    pair_token = jnp.where(pair_lane < tok_rows, pair_lane, pair_lane - tok_rows)
    expert_row = iota((16, 2 * tok_rows), 0)
    route_row = jnp.concatenate([token_rows[0:1, :], token_rows[1:2, :]], axis=1)
    live = (expert_row.astype(F32) == route_row) & (expert_row < experts) & (pair_token < length)
    placed = dot(jnp.where(live, 1.0, 0.0).astype(BF), is_at)
    before = jnp.where(
        iota((2 * tok_rows, 2 * tok_rows), 0) <= iota((2 * tok_rows, 2 * tok_rows), 1), 1.0, 0.0
    ).astype(BF)
    counts = dot(placed.astype(BF), before)
    kept = jnp.where((placed > 0.5) & (counts <= capacity + 0.5), counts, 0.0)
    taken = dot_nt(kept.astype(BF), is_at)
    slot_of = jnp.sum(
        jnp.where(taken > 0.5, taken + (expert_row * capacity).astype(F32), 0.0),
        axis=0,
        keepdims=True,
    )
    slot_col = jnp.transpose(jnp.broadcast_to(slot_of, (8, 2 * tok_rows)))
    for step in range(2, lines - 1):
        dense_forward(0, step)
    for jj in range(lines):
        chain_own(jj)
    put, take = r["put"], r["take"]
    for k in range(2):
        span = slice(k * tok_rows, (k + 1) * tok_rows)
        names_down = (iota((slots, tok_rows), 0) + 1).astype(F32)
        put[k] = jnp.where(slot_of[:, span] == names_down, 1.0, 0.0).astype(BF)
        names_right = (iota((tok_rows, slots), 1) + 1).astype(F32)
        take[k] = jnp.where(slot_col[span, 0:1] == names_right, 1.0, 0.0).astype(BF)

    for step in range(1, 2 * lines):
        origin = (s + 2 * lines - step) % (2 * lines)
        small_copy(step, origin).wait_recv()
    pick = jnp.where(iota((8, LANES), 1) == iota((8, LANES), 0) + vec_col, 1.0, 0.0).astype(BF)
    named = dot_nt(pick, small[...])
    r["rows"][...] = named
    gain_one, gain_two = named[2:3, :], named[3:4, :]
    vec_zero, vec_one = named[0:1, :], named[1:2, :]
    normed = r["normed"]
    for block in range(row_blocks):
        at = slice(block * LANES, (block + 1) * LANES)
        inputs = tokens[at, :].astype(F32)
        normed[at, :] = (inputs * cols[at, 0:1] * gain_one).astype(BF)

    dense_share(0)
    dense_finish(0)

    heads = r["heads"]
    cosine, sine = r["cosine"], r["sine"]

    def project(b, turn):
        wide_block = dot(normed[...], weights[:, rows(b, 2 * LANES)])
        for part in range(2):
            block = wide_block[:, part * LANES : (part + 1) * LANES]
            if turn:
                block = block * cosine[...] + swap_halves(block) * sine[...]
            heads[2 * b + part] = block.astype(BF)

    def rotated(b, _):
        project(b, True)
        return 0

    def plain(b, _):
        project(b, False)
        return 0

    lax.fori_loop(0, pairs, rotated, 0)
    lax.fori_loop(pairs, 3 * pairs // 2, plain, 0)
    for step in range(lines - 1):
        dense_forward(1, step)
    chain_events(0, 2)

    score_scale = HEAD_DIM ** (-0.5)
    first_head = iota((tok_rows, LANES), 1) < HEAD_DIM
    mixed, log_sums = r["mixed"], r["log_sums"]

    def allowed_pairs():
        key, query = iota((tok_rows, tok_rows), 0), iota((tok_rows, tok_rows), 1)
        return (key <= query) & (key < length)

    def one_head(block, head):
        keep = first_head if head == 0 else jnp.logical_not(first_head)
        return jnp.where(keep, block, jnp.zeros_like(block))

    def attend(p, _):
        query, key, value = heads[p], heads[pairs + p], heads[2 * pairs + p]
        results = []
        for head in range(2):
            scores = dot_nt(key, one_head(query, head)) * score_scale
            scores = jnp.where(allowed_pairs(), scores, NEG)
            top = jnp.max(scores, axis=0, keepdims=True)
            expo = jnp.exp(scores - top)
            total = jnp.sum(expo, axis=0, keepdims=True)
            probs = expo * (1.0 / total)
            log_sums[p, head : head + 1, :] = top + jnp.log(total)
            results.append(dot_tn(probs.astype(BF), value))
        mixed[:, rows(p, LANES)] = jnp.where(first_head, results[0], results[1]).astype(BF)
        return 0

    lax.fori_loop(0, pairs // 2, attend, 0)
    chain_events(2, 1)
    dense_share(1)
    lax.fori_loop(pairs // 2, pairs, attend, 0)
    dense_finish(1)
    chain_events(3, 1)

    hidden, normed_low = r["hidden"], r["normed_low"]
    out_grad = r["out_grad"]
    mixer = r["mix"][...].astype(F32)
    grad_low, grad_sum, sent = r["grad_low"], r["grad_sum"], r["sent"]
    for block in range(row_blocks):
        at = slice(block * LANES, (block + 1) * LANES)
        hid = tokens[at, :].astype(F32) + dot(mixed[at, :], weights[:, 3 * D : 4 * D])
        hidden[at, :] = hid
        scale = lax.rsqrt(jnp.mean(hid * hid, axis=1, keepdims=True) + norm_eps)
        cols[at, 1:2] = scale
        low = (hid * scale * gain_two).astype(BF)
        normed_low[at, :] = low
        logits = dot(low, small[...])
        lane = iota((LANES, LANES), 1)
        extra = jnp.zeros((LANES, gate_cols), F32)
        for i in range(gate_cols):
            extra = extra + token_cols[at, 8 + i : 9 + i] * mixer[i : i + 1, :]
        routes = token_cols[at, 0:2].astype(jnp.int32)
        chosen = []
        for k in range(2):
            hot = lane == routes[:, k : k + 1]
            part = jnp.sum(jnp.where(hot, logits, 0.0), axis=1, keepdims=True)
            chosen.append(
                part
                + jnp.sum(
                    jnp.where(
                        iota((LANES, gate_cols), 1) == routes[:, k : k + 1], extra, 0.0
                    ),
                    axis=1,
                    keepdims=True,
                )
            )
        top = jnp.maximum(chosen[0], chosen[1])
        powers = [jnp.exp(c - top) for c in chosen]
        total = powers[0] + powers[1]
        gates = [w / total for w in powers]
        on_normed = sum(
            gates[k] * (routes[:, k : k + 1] == experts + 1).astype(F32) for k in range(2)
        )
        for j in range(2):
            first = logits[:, const_col + 2 * j : const_col + 2 * j + 1]
            second = logits[:, const_col + 2 * j + 1 : const_col + 2 * j + 2]
            peak = jnp.maximum(first, second)
            first, second = jnp.exp(first - peak), jnp.exp(second - peak)
            both = first + second
            first, second = first / both, second / both
            weight = sum(
                gates[k] * (routes[:, k : k + 1] == experts + 2 + j).astype(F32)
                for k in range(2)
            )
            on_normed = on_normed + first * weight
            cols[at, 6 + 4 * j : 7 + 4 * j] = first
            cols[at, 7 + 4 * j : 8 + 4 * j] = second
            cols[at, 8 + 4 * j : 9 + 4 * j] = weight
        cols[at, 2:3] = gates[0]
        cols[at, 3:4] = gates[1]
        cols[at, 4:5] = on_normed
        valid = (iota((LANES, 1), 0) + block * LANES < length).astype(F32)
        grad = out_grad[at, :].astype(F32) * valid
        after = slice(tok_rows + block * LANES, tok_rows + (block + 1) * LANES)
        grad_low[at, :] = (gates[0] * grad).astype(BF)
        grad_low[after, :] = (gates[1] * grad).astype(BF)
        grad_sum[at, :] = grad.astype(BF)

    buffer, slot_grad = r["buffer"], r["slot_grad"]

    def dispatch(which, step, side, origin):
        target = (e + step) % experts
        box = buffer if which == 0 else slot_grad
        return remote(
            sent.at[rows(which * experts + target, capacity), :],
            box.at[rows(origin, capacity), :],
            r["go_send"].at[which, step, side],
            r["go_recv"].at[which, origin],
            (target, 2 * z + side),
        )

    def dispatch_each(which, step, go):
        for flip in range(2):
            side = x if flip == 0 else 1 - x
            if step > 0 or flip == 1:
                go(dispatch(which, step, side, mine))

    for step in range(experts):
        owner = (e + step) % experts
        chosen_rows = rows(owner, capacity)
        put_zero, put_one = put[0, chosen_rows, :], put[1, chosen_rows, :]
        sent[chosen_rows, :] = dot(put_zero + put_one, normed_low[...]).astype(BF)
        dispatch_each(0, step, lambda copy: copy.start())
        sent[rows(experts + owner, capacity), :] = (
            dot(put_zero, grad_low[0:tok_rows, :])
            + dot(put_one, grad_low[tok_rows : 2 * tok_rows, :])
        ).astype(BF)
        dispatch_each(1, step, lambda copy: copy.start())
    buffer[rows(mine, capacity), :] = sent[rows(e, capacity), :]
    slot_grad[rows(mine, capacity), :] = sent[rows(experts + e, capacity), :]
    chain_events(4, len(passes))

    def others(go):
        for step in range(experts):
            other = (e + step) % experts
            for flip in range(2):
                side = x if flip == 0 else 1 - x
                if step > 0 or flip == 1:
                    go(step, other, side, 2 * other + side)

    for which in range(2):
        others(lambda step, other, side, origin: dispatch(which, step, side, origin).wait_recv())

    up_sum, down_sum = r["up_sum"], r["down_sum"]
    up_box, down_box = r["up_box"], r["down_box"]
    up_out, down_out = r["up_out"], r["down_out"]
    final_send, final_box = stage, r["final_box"]
    ffn, slot_back = r["ffn"], r["slot_back"]
    last = lines - 1

    def up_rows(jj, zz):
        return up_sum.at[jj, rows(zz, 2 * share), :]

    def up_hop(way, k, jj, dest):
        return remote(
            up_rows(jj, dest),
            up_box.at[way, k, jj],
            r["ru_send"].at[way, k, jj],
            r["ru_recv"].at[way, k, jj],
            (e, s + 2 if way == 0 else s - 2),
        )

    def down_slot(way, jj, zz):
        return jj if way == 0 else jnp.where(jj == zz, lines, jj)

    def down_hop(way, jj, zz):
        return remote(
            down_sum.at[jj],
            down_box.at[down_slot(way, jj, zz)],
            r["rd_send"].at[way, jj],
            r["rd_recv"].at[way, jj],
            (e, s + 2 if way == 0 else s - 2),
        )

    def final_hop(jj):
        return remote(
            final_send.at[jj],
            final_box.at[jj],
            r["fx_send"].at[jj],
            r["fx_recv"].at[jj],
            (e, across),
        )

    def sum_event(k, jj):
        for way in range(2):
            place = z if way == 0 else last - z
            dest = last - k + place if way == 0 else k - place
            inside = (place <= k) & (place < last)

            @pl.when((k >= 1) & (k < last) & (place >= 1) & inside)
            def _():
                up_hop(way, k - 1, jj, dest).wait_recv()
                old = up_sum[jj, rows(dest, 2 * share), :].astype(F32)
                up_sum[jj, rows(dest, 2 * share), :] = (
                    old + up_box[way, k - 1, jj].astype(F32)
                ).astype(BF)

                @pl.when(dest == jj)
                def _():
                    down_hop(way, jj, z).wait_recv()
                    down_sum[jj] = (
                        down_sum[jj].astype(F32)
                        + down_box[down_slot(way, jj, z)].astype(F32)
                    ).astype(BF)

            @pl.when((k < last) & (place >= 1) & inside)
            def _():
                up_hop(way, k, jj, dest).start()

                @pl.when(dest == jj)
                def _():
                    down_hop(way, jj, z + 1 - 2 * way).start()

        @pl.when(k == last)
        def _():
            total = slot_back.at[0 : 2 * share, 0 : 2 * hidden_block]
            total[...] = up_sum[jj, rows(z, 2 * share), :].astype(F32)

            @pl.when(z > 0)
            def _():
                up_hop(0, last - 1, jj, z).wait_recv()
                total[...] += up_box[0, last - 1, jj].astype(F32)

            @pl.when(z < last)
            def _():
                up_hop(1, last - 1, jj, z).wait_recv()
                total[...] += up_box[1, last - 1, jj].astype(F32)

            final_send[jj] = total[rows(1 - x, share), :].astype(BF)
            final_hop(jj).start()
            own = total[rows(x, share), :]
            for part in range(2):
                up_out[:, up_columns(part, jj, x)] = own[
                    :, part * hidden_block : (part + 1) * hidden_block
                ]

            @pl.when(jj == z)
            def _():
                down_out[...] = down_sum[z].astype(F32)

                @pl.when(z > 0)
                def _():
                    down_hop(0, jj, z).wait_recv()
                    down_out[...] += down_box[down_slot(0, jj, z)].astype(F32)

                @pl.when(z < last)
                def _():
                    down_hop(1, jj, z).wait_recv()
                    down_out[...] += down_box[down_slot(1, jj, z)].astype(F32)

    def sum_start(jj):
        for way in range(2):

            @pl.when(z == (0 if way == 0 else last))
            def _():
                for k in range(last):
                    dest = last - k if way == 0 else k
                    up_hop(way, k, jj, dest).start()

                    @pl.when(dest == jj)
                    def _():
                        down_hop(way, jj, z + 1 - 2 * way).start()

    def sum_next(m):
        sum_event(1 + m % last, m // last)

    sum_steps = lines * last

    def sum_sent():
        for jj in range(lines):
            for way in range(2):
                place = z if way == 0 else last - z
                for k in range(last):
                    dest = last - k + place if way == 0 else k - place

                    @pl.when((place <= k) & (place < last))
                    def _():
                        up_hop(way, k, jj, dest).wait_send()

                        @pl.when(dest == jj)
                        def _():
                            down_hop(way, jj, z + 1 - 2 * way).wait_send()

    for jj in range(lines):
        up_across(jj, x).wait_send()
    act, grad_gu = r["act"], r["grad_gu"]
    back_box = r["back_box"]
    pair_rows = 2 * capacity
    for which in range(2):
        for step in range(experts):
            dispatch_each(which, step, leave)

    def come(which, target, side, origin_e, origin_x):
        box = grad_low if which == 0 else sent
        return remote(
            box.at[rows(2 * target + side, capacity), :],
            back_box.at[which, origin_x, rows(origin_e, capacity), :],
            r["come_send"].at[which, target, side],
            r["come_recv"].at[which, origin_e, origin_x],
            (target, 2 * z + side),
        )

    def expert_chunk(jj, _):
        @pl.when(jj == last)
        def _():
            sum_next(0)

        chain_end(jj)

        def forward(b, _):
            target = (e + 1 + b) % experts
            at = rows(target, pair_rows)
            given = dot(buffer[at, :], up[jj])
            gate, lift = given[:, 0:hidden_block], given[:, hidden_block:]
            squash = 1.0 / (1.0 + jnp.exp(-gate))
            silu = gate * squash
            low = (silu * lift).astype(BF)
            act[at, :] = low
            grad_act = dot_nt(slot_grad[at, :], down[jj])
            grads = jnp.concatenate(
                [grad_act * lift * squash * (1.0 + gate * (1.0 - squash)), grad_act * silu],
                axis=1,
            ).astype(BF)
            grad_gu[at, :] = grads
            forth = dot(low, down[jj])
            back = dot_nt(grads, up[jj])

            @pl.when(jj == 0)
            def _():
                ffn[at, :] = forth
                slot_back[at, :] = back

            @pl.when((jj > 0) & (jj < last))
            def _():
                ffn[at, :] += forth
                slot_back[at, :] += back

            @pl.when(jj == last)
            def _():
                grad_low[at, :] = (ffn[at, :] + forth).astype(BF)
                sent[at, :] = (slot_back[at, :] + back).astype(BF)
                for which in range(2):
                    come(which, target, 1 - x, e, x).start()

                    @pl.when(target != e)
                    def _():
                        come(which, target, x, e, x).start()

            return 0

        lax.fori_loop(0, experts, forward, 0)
        up_sum[jj] = dot_tn(buffer[...], grad_gu[...]).astype(BF)
        down_sum[jj] = dot_tn(act[...], slot_grad[...]).astype(BF)
        sum_start(jj)
        return 0

    lax.fori_loop(0, lines, expert_chunk, 0)

    for which in range(2):
        box = grad_low if which == 0 else sent
        back_box[which, x, rows(e, capacity), :] = box[rows(mine, capacity), :]
    for m in range(1, 5):
        sum_next(m)
    for which in range(2):
        others(
            lambda step, other, side, origin: come(which, other, side, other, side).wait_recv()
        )
    for which in range(2):
        back_box[which, 0] = (
            back_box[which, 0].astype(F32) + back_box[which, 1].astype(F32)
        ).astype(BF)

    named = r["rows"][...]
    gain_one, gain_two = named[2:3, :], named[3:4, :]
    vec_zero, vec_one = named[0:1, :], named[1:2, :]
    grad_hidden, grad_attn = ffn.at[0:tok_rows, :], r["grad_attn"]
    thin, wide = r["thin"], r["wide"]
    grad_logits = r["grad_logits"]
    gain_sum = jnp.zeros((1, D), F32)
    for block in range(row_blocks):
        at = slice(block * LANES, (block + 1) * LANES)
        hid = hidden[at, :]
        scale = cols[at, 1:2]
        norm = hid * scale * gain_two
        grad = grad_sum[at, :].astype(F32)
        take_zero, take_one = take[0, at, :], take[1, at, :]
        outs = [dot(take_zero, back_box[0, 0]), dot(take_one, back_box[0, 0])]
        gates = [cols[at, 2:3], cols[at, 3:4]]
        on_normed = cols[at, 4:5]
        const = [
            (cols[at, 6 + 4 * j : 7 + 4 * j], cols[at, 7 + 4 * j : 8 + 4 * j], cols[at, 8 + 4 * j : 9 + 4 * j])
            for j in range(2)
        ]
        on_vec = [a * w for _, a, w in const]
        valid = (iota((LANES, 1), 0) + block * LANES < length).astype(F32)
        mixture = (
            gates[0] * outs[0]
            + gates[1] * outs[1]
            + on_normed * norm
            + on_vec[0] * vec_zero
            + on_vec[1] * vec_one
        )
        r["block_out"][at, :] = (valid * (hid + mixture)).astype(BF)
        routes = token_cols[at, 0:2].astype(jnp.int32)
        with_norm = jnp.sum(grad * norm, axis=1, keepdims=True)
        with_vec = [
            jnp.sum(grad * v, axis=1, keepdims=True) for v in (vec_zero, vec_one)
        ]
        gate_grads = []
        for k in range(2):
            value = jnp.sum(grad * outs[k], axis=1, keepdims=True)
            value = value + (routes[:, k : k + 1] == experts + 1).astype(F32) * with_norm
            for j in range(2):
                hit = (routes[:, k : k + 1] == experts + 2 + j).astype(F32)
                value = value + hit * (const[j][0] * with_norm + const[j][1] * with_vec[j])
            gate_grads.append(value)
        mean = gates[0] * gate_grads[0] + gates[1] * gate_grads[1]
        lane = iota((LANES, LANES), 1)
        spread = jnp.zeros((LANES, LANES), F32)
        for k in range(2):
            spread = spread + jnp.where(
                lane == routes[:, k : k + 1], gates[k] * (gate_grads[k] - mean), 0.0
            )
        grad_logits[at, :] = spread[:, 0:gate_cols]
        wide_block = jnp.zeros((LANES, LANES), F32)
        for j in range(2):
            first, second, weight = const[j]
            d_first, d_second = weight * with_norm, weight * with_vec[j]
            centre = first * d_first + second * d_second
            parts = (first * (d_first - centre), second * (d_second - centre))
            for i in range(2):
                high = parts[i].astype(BF).astype(F32)
                at_high = const_col + 2 * j + i
                spread = jnp.where(lane == at_high, high, spread)
                spread = jnp.where(lane == at_high + 4, parts[i] - high, spread)
            high = on_vec[j].astype(BF).astype(F32)
            wide_block = jnp.where(lane == j, high, wide_block)
            wide_block = jnp.where(lane == 2 + j, on_vec[j] - high, wide_block)
        thin[at, :] = spread.astype(BF)
        wide[at, :] = wide_block.astype(BF)
        grad_norm = (
            dot_nt(thin[at, :], small[...])
            + dot(take_zero + take_one, back_box[1, 0])
            + on_normed * grad
        )
        gain_sum = gain_sum + jnp.sum(grad_norm * hid * scale, axis=0, keepdims=True)
        scaled = gain_two * grad_norm
        grad = (
            grad
            + scale * scaled
            - hid * (scale * scale * scale) * jnp.mean(scaled * hid, axis=1, keepdims=True)
        )
        grad_hidden[at, :] = grad
        grad_attn[at, :] = grad.astype(BF)

    sum_next(5)

    sums = r["sums"]
    sums[z] = jnp.zeros(sums.shape[1:], F32)
    by_small = dot_tn(thin[...], normed_low[...])
    by_vec = dot_tn(wide[...], grad_sum[...])
    sums[z, 0:gate_cols, :] = by_small[0:gate_cols, :]
    sums[z, gate_cols : gate_cols + 4, :] = (
        by_small[const_col : const_col + 4, :] + by_small[const_col + 4 : const_col + 8, :]
    )
    sums[z, gate_cols + 4 : gate_cols + 6, :] = by_vec[0:2, :] + by_vec[2:4, :]
    sums[z, gate_cols + 6 : gate_cols + 7, :] = gain_sum
    mix_rows = SMALL_ROWS - 16
    sums[z, mix_rows : mix_rows + gate_cols, 0:gate_cols] = lax.dot_general(
        r["prev_in"][...],
        grad_logits[...],
        (((1,), (0,)), ((), ())),
        precision=lax.Precision.HIGHEST,
        preferred_element_type=F32,
    )
    r["prev_out"][...] = lax.dot_general(
        r["mix"][...].astype(F32),
        grad_logits[...],
        (((1,), (1,)), ((), ())),
        precision=lax.Precision.HIGHEST,
        preferred_element_type=F32,
    )

    dense, ring = r["dense"], RING
    core_box, y_box, x_box = r["core_box"], r["y_box"], r["x_box"]
    z_box, all_box = r["z_box"], r["all_box"]

    def as_chunk(block):
        return block.reshape(lines, 2, 2, 2, quarter, chunk_cols).astype(BF)

    def core_hop(ch):
        return remote(
            dense.at[ch % ring, :, :, 1 - core],
            core_box.at[ch],
            r["gc_send"].at[ch],
            r["gc_recv"].at[ch],
            (twin, s),
        )

    def y_hop(ch):
        return remote(
            core_box.at[ch, :, :, 1 - half],
            y_box.at[ch],
            r["gy_send"].at[ch],
            r["gy_recv"].at[ch],
            (facing, s),
        )

    def x_hop(ch):
        return remote(
            y_box.at[ch, :, 1 - x],
            x_box.at[ch],
            r["gx_send"].at[ch],
            r["gx_recv"].at[ch],
            (e, across),
        )

    def z_hop(ch, step, origin):
        zz = (z + step) % lines
        return remote(
            x_box.at[ch, zz],
            z_box.at[ch, origin],
            r["gz_send"].at[ch, step],
            r["gz_recv"].at[ch, origin],
            (e, 2 * zz + x),
        )

    def all_hop(ch, step, origin):
        return remote(
            all_box.at[ch, e],
            all_box.at[ch, origin],
            r["ga_send"].at[ch, step],
            r["ga_recv"].at[ch, origin],
            ((e + step) % experts, s),
        )

    def summed(first, second):
        return (first.astype(F32) + second.astype(F32)).astype(BF)

    def dense_event(it):
        def stage_of(number):
            ch = it - HOPS[number]
            return ch, (ch >= 0) & (ch < chunks)

        ch0, on0 = stage_of(0)

        @pl.when(on0)
        def _():
            core_hop(ch0).start()

        ch1, on1 = stage_of(1)

        @pl.when(on1)
        def _():
            core_hop(ch1).wait_recv()
            core_box[ch1] = summed(core_box[ch1], dense[ch1 % ring, :, :, core])
            y_hop(ch1).start()
            core_hop(ch1).wait_send()

        ch2, on2 = stage_of(2)

        @pl.when(on2)
        def _():
            y_hop(ch2).wait_recv()
            y_box[ch2] = summed(y_box[ch2], core_box[ch2, :, :, half])
            x_hop(ch2).start()

        ch3, on3 = stage_of(3)

        @pl.when(on3)
        def _():
            x_hop(ch3).wait_recv()
            x_box[ch3] = summed(x_box[ch3], y_box[ch3, :, x])
            for step in range(1, lines):
                z_hop(ch3, step, z).start()

        ch4, on4 = stage_of(4)

        @pl.when(on4)
        def _():
            total = x_box[ch4, z].astype(F32)
            for step in range(1, lines):
                origin = (z + lines - step) % lines
                z_hop(ch4, step, origin).wait_recv()
                total = total + z_box[ch4, origin].astype(F32)
            all_box[ch4, e] = total.astype(BF)
            for step in range(1, experts):
                all_hop(ch4, step, e).start()

        ch5, on5 = stage_of(5)

        @pl.when(on5)
        def _():
            for step in range(1, experts):
                origin = (e + experts - step) % experts
                all_hop(ch5, step, origin).wait_recv()
            for owner in range(experts):
                total = all_box[ch5, owner].astype(F32)
                place = (owner % 2) * 2 + owner // 2
                at = slice(place * quarter, (place + 1) * quarter)

                @pl.when(ch5 < out_chunks)
                def _():
                    r["out_w_out"][at, rows(ch5, chunk_cols)] = total

                @pl.when(ch5 >= out_chunks)
                def _():
                    for part in range(3):
                        spot = pl.ds(
                            pl.multiple_of(part * D + (ch5 - out_chunks) * LANES, LANES), LANES
                        )
                        r["qkv_out"][at, spot] = total[:, part * LANES : (part + 1) * LANES]

    def dense_events_sent():
        def one(ch, _):
            y_hop(ch).wait_send()
            x_hop(ch).wait_send()
            for step in range(1, lines):
                z_hop(ch, step, z).wait_send()
            for step in range(1, experts):
                all_hop(ch, step, e).wait_send()
            return 0

        lax.fori_loop(0, chunks, one, 0)

    grad_normed = ffn.at[tok_rows : 2 * tok_rows, :]
    grad_normed[...] = jnp.zeros_like(grad_normed)
    out_grads = dot_tn(mixed[...], grad_attn[...])
    for ch in range(out_chunks):
        dense[ch] = as_chunk(out_grads[:, ch * chunk_cols : (ch + 1) * chunk_cols])

    def attend_back(p):
        query, key, value = heads[p], heads[pairs + p], heads[2 * pairs + p]
        upper = dot_nt(grad_attn[...], weights[rows(p, LANES), 3 * D : 4 * D]).astype(BF)
        grads = []
        for head in range(2):
            scores = dot_nt(key, one_head(query, head)) * score_scale
            probs = jnp.where(
                allowed_pairs(), jnp.exp(scores - log_sums[p, head : head + 1, :]), 0.0
            )
            grad_probs = dot_nt(value, one_head(upper, head))
            delta = jnp.sum(grad_probs * probs, axis=0, keepdims=True)
            grad_scores = (probs * (grad_probs - delta)).astype(BF)
            grads.append(
                (
                    dot_tn(grad_scores, key),
                    dot(grad_scores, query),
                    dot(probs.astype(BF), upper),
                )
            )
        joined = [jnp.where(first_head, a, b) for a, b in zip(*grads)]
        parts = []
        for part in range(3):
            block = joined[part]
            if part < 2:
                block = block * score_scale
                block = block * cosine[...] - swap_halves(block) * sine[...]
            parts.append(block.astype(BF))
        total = grad_normed[...]
        for part in range(3):
            spot = pl.ds(pl.multiple_of(part * D + p * LANES, LANES), LANES)
            total = total + dot_nt(parts[part], weights[:, spot])
        grad_normed[...] = total
        dense[(out_chunks + p) % ring] = as_chunk(
            dot_tn(normed[...], jnp.concatenate(parts, axis=1))
        )

    sum_next(6)

    def back_step(it, _):
        @pl.when(it >= out_chunks)
        def _():
            attend_back(it - out_chunks)

        dense_event(it)

        @pl.when((it >= 3) & (it % 3 == 0))
        def _():
            sum_next(7 + (it - 3) // 3)

        return 0

    def tail_step(it, _):
        dense_event(it)

        @pl.when(((it - chunks) % 2 == 0) & (9 + (it - chunks) // 2 < sum_steps))
        def _():
            sum_next(9 + (it - chunks) // 2)

        return 0

    lax.fori_loop(0, chunks, back_step, 0)

    gain_sum = jnp.zeros((1, D), F32)
    for block in range(row_blocks):
        at = slice(block * LANES, (block + 1) * LANES)
        inputs = tokens[at, :].astype(F32)
        scale = cols[at, 0:1]
        grad_norm = grad_normed[at, :]
        gain_sum = gain_sum + jnp.sum(grad_norm * inputs * scale, axis=0, keepdims=True)
        scaled = gain_one * grad_norm
        r["tokens_out"][at, :] = (
            grad_hidden[at, :]
            + scale * scaled
            - inputs * (scale * scale * scale) * jnp.mean(scaled * inputs, axis=1, keepdims=True)
        )
    sums[z, gate_cols + 7 : gate_cols + 8, :] = gain_sum

    layer_sums = r["layer_sums"]

    def sums_z(step, origin):
        return remote(
            sums.at[z],
            sums.at[origin],
            r["az_send"].at[step],
            r["az_recv"].at[origin],
            (e, ((z + step) % lines) * 2 + x),
        )

    def sums_layer(step, side, origin):
        return remote(
            layer_sums.at[mine],
            layer_sums.at[origin],
            r["al_send"].at[step, side],
            r["al_recv"].at[origin],
            ((e + step) % experts, 2 * z + side),
        )

    for step in range(1, lines):
        sums_z(step, z).start()
    lax.fori_loop(chunks, chunks + 3, tail_step, 0)
    for step in range(1, lines):
        sums_z(step, (z + lines - step) % lines).wait_recv()
    total = sums[0]
    for zz in range(1, lines):
        total = total + sums[zz]
    layer_sums[mine] = total
    others(lambda step, other, side, origin: sums_layer(step, side, mine).start())
    lax.fori_loop(chunks + 3, chunks + HOPS[-1], tail_step, 0)
    others(lambda step, other, side, origin: sums_layer(step, side, origin).wait_recv())
    total = layer_sums[0]
    for other in range(1, layer):
        total = total + layer_sums[other]
    mine_only = pltpu.roll(total, (2 * lines - s) * share % D, 1)[:, 0:share]
    r["gate_out"][...] = mine_only[0:gate_cols, :]
    r["const_out"][...] = mine_only[gate_cols : gate_cols + 4, :]
    r["vec_out"][...] = mine_only[gate_cols + 4 : gate_cols + 6, :]
    r["two_out"][...] = mine_only[gate_cols + 6 : gate_cols + 7, :]
    r["one_out"][...] = mine_only[gate_cols + 7 : gate_cols + 8, :]
    r["mix_out"][...] = total[mix_rows : mix_rows + gate_cols, 0:gate_cols]

    for jj in range(lines):
        final_hop(jj).wait_recv()
        for part in range(2):
            up_out[:, up_columns(part, jj, 1 - x)] = final_box[
                jj, :, part * hidden_block : (part + 1) * hidden_block
            ].astype(F32)

    for kind in range(2):
        dense_sent(kind)
    chain_sent()
    for step in range(1, 2 * lines):
        small_copy(step, s).wait_send()
    for which in range(2):
        others(lambda step, other, side, origin: come(which, other, side, e, x).wait_send())
    sum_sent()
    for jj in range(lines):
        final_hop(jj).wait_send()
    dense_events_sent()
    for step in range(1, lines):
        sums_z(step, z).wait_send()
    others(lambda step, other, side, origin: sums_layer(step, side, mine).wait_send())

SMALL_ROWS = 32
IN_NAMES = (
    "length", "tokens", "out_grad", "routes_in", "order_row", "prev_in", "mix",
    "cosine", "sine", "qkv_in", "out_in", "gate_in", "const_in", "vec_in", "one_in", "two_in",
    "up_in", "down_in",
)
OUT_NAMES = (
    "block_out", "tokens_out", "prev_out", "qkv_out", "out_w_out", "gate_out", "const_out",
    "vec_out", "one_out", "two_out", "mix_out", "up_out", "down_out",
)


def scratch_list(dims):
    tok_rows, experts, lines, share, hidden_block, capacity, gate_cols = dims
    pairs = D // LANES
    chunk_cols = 3 * LANES
    chunks = D // chunk_cols + pairs
    slots = experts * capacity
    gathered = 2 * experts * capacity
    quarter = share // 4
    last = lines - 1
    wide = 2 * hidden_block
    vmem = {
        "weights": ((D, 4 * D), BF),
        "small": ((D, LANES), BF),
        "up": ((lines, D, wide), BF),
        "down": ((lines, hidden_block, D), BF),
        "stage": ((lines, share, wide), BF),
        "put": ((2, slots, tok_rows), BF),
        "take": ((2, tok_rows, slots), BF),
        "rows": ((8, D), F32),
        "cols": ((tok_rows, 16), F32),
        "normed": ((tok_rows, D), BF),
        "heads": ((3 * pairs, tok_rows, LANES), BF),
        "mixed": ((tok_rows, D), BF),
        "log_sums": ((pairs, 8, tok_rows), F32),
        "hidden": ((tok_rows, D), F32),
        "normed_low": ((tok_rows, D), BF),
        "grad_low": ((2 * tok_rows, D), BF),
        "grad_sum": ((tok_rows, D), BF),
        "sent": ((gathered, D), BF),
        "buffer": ((gathered, D), BF),
        "slot_grad": ((gathered, D), BF),
        "up_sum": ((lines, D, wide), BF),
        "down_sum": ((lines, hidden_block, D), BF),
        "up_box": ((2, last, lines, 2 * share, wide), BF),
        "down_box": ((lines + 1, hidden_block, D), BF),
        "final_box": ((lines, share, wide), BF),
        "ffn": ((gathered, D), F32),
        "slot_back": ((gathered, D), F32),
        "act": ((gathered, hidden_block), BF),
        "grad_gu": ((gathered, wide), BF),
        "back_box": ((2, 2, slots, D), BF),
        "grad_attn": ((tok_rows, D), BF),
        "thin": ((tok_rows, LANES), BF),
        "wide": ((tok_rows, LANES), BF),
        "grad_logits": ((tok_rows, gate_cols), F32),
        "sums": ((lines, SMALL_ROWS, D), F32),
        "layer_sums": ((2 * experts, SMALL_ROWS, D), F32),
        "dense": ((RING, lines, 2, 2, 2, quarter, chunk_cols), BF),
        "core_box": ((chunks, lines, 2, 2, quarter, chunk_cols), BF),
        "y_box": ((chunks, lines, 2, quarter, chunk_cols), BF),
        "x_box": ((chunks, lines, quarter, chunk_cols), BF),
        "z_box": ((chunks, lines, quarter, chunk_cols), BF),
        "all_box": ((chunks, experts, quarter, chunk_cols), BF),
        "pack": ((LANES, LANES), F32),
        "token_rows": ((16, tok_rows), F32),
        "token_cols": ((tok_rows, 16), F32),
    }
    sems = {
        "dz_send": (2, 2, last),
        "dx_send": (2, lines),
        "dc_send": (2, lines, 2),
        "d_recv": (2, lines, 2, 2),
        "sm_send": (2 * lines,),
        "sm_recv": (2 * lines,),
        "ux_send": (lines,),
        "ux_recv": (lines,),
        "ch_send": (2, 2, last, lines),
        "ch_recv": (2, 2, last, lines),
        "go_send": (2, experts, 2),
        "go_recv": (2, 2 * experts),
        "come_send": (2, experts, 2),
        "come_recv": (2, experts, 2),
        "ru_send": (2, last, lines),
        "ru_recv": (2, last, lines),
        "rd_send": (2, lines),
        "rd_recv": (2, lines),
        "fx_send": (lines,),
        "fx_recv": (lines,),
        "gc_send": (chunks,),
        "gc_recv": (chunks,),
        "gy_send": (chunks,),
        "gy_recv": (chunks,),
        "gx_send": (chunks,),
        "gx_recv": (chunks,),
        "gz_send": (chunks, lines),
        "gz_recv": (chunks, lines),
        "ga_send": (chunks, experts),
        "ga_recv": (chunks, experts),
        "az_send": (lines,),
        "az_recv": (lines,),
        "al_send": (experts, 2),
        "al_recv": (2 * experts,),
    }
    names = tuple(vmem) + tuple(sems)
    shapes = [pltpu.VMEM(*spec) for spec in vmem.values()]
    shapes += [pltpu.SemaphoreType.DMA(shape) for shape in sems.values()]
    return names, shapes


def kernel_body(
    tokens,
    seq_lengths,
    routes,
    pair_order,
    prev_logits,
    out_grad,
    qkv_weight,
    out_weight,
    gate_weight,
    const_weight,
    const_vector,
    norm1_gain,
    norm2_gain,
    gate_mix,
    expert_up,
    expert_down,
):
    tok_rows = tokens.shape[0]
    experts = lax.axis_size("expert")
    shards = lax.axis_size("shard")
    share = qkv_weight.shape[0]
    gate_cols = gate_weight.shape[1]
    hidden_block = expert_down.shape[1]
    capacity = 2 * tok_rows // (experts + 4)
    dims = (tok_rows, experts, shards // 2, share, hidden_block, capacity, gate_cols)
    cosine, sine_table = turn_tables(tok_rows)
    args = (
        seq_lengths,
        tokens,
        out_grad,
        routes.T,
        pair_order,
        prev_logits.T,
        gate_mix,
        cosine,
        sine_table,
        qkv_weight,
        out_weight,
        gate_weight.T,
        const_weight.T,
        const_vector.T,
        norm1_gain[None],
        norm2_gain[None],
        expert_up[0],
        expert_down[0],
    )
    names, shapes = scratch_list(dims)
    vmem = pl.BlockSpec(memory_space=pltpu.VMEM)
    outs = pl.pallas_call(
        functools.partial(step_kernel, dims, names),
        out_shape=(
            jax.ShapeDtypeStruct((tok_rows, D), BF),
            jax.ShapeDtypeStruct((tok_rows, D), F32),
            jax.ShapeDtypeStruct((gate_cols, tok_rows), F32),
            jax.ShapeDtypeStruct((share, 3 * D), F32),
            jax.ShapeDtypeStruct((share, D), F32),
            jax.ShapeDtypeStruct((gate_cols, share), F32),
            jax.ShapeDtypeStruct((4, share), F32),
            jax.ShapeDtypeStruct((2, share), F32),
            jax.ShapeDtypeStruct((1, share), F32),
            jax.ShapeDtypeStruct((1, share), F32),
            jax.ShapeDtypeStruct((gate_cols, gate_cols), F32),
            jax.ShapeDtypeStruct((share, 2 * FF), F32),
            jax.ShapeDtypeStruct((hidden_block, D), F32),
        ),
        in_specs=[pl.BlockSpec(memory_space=pltpu.SMEM)] + [vmem] * (len(args) - 1),
        out_specs=(vmem,) * len(OUT_NAMES),
        scratch_shapes=shapes,
        compiler_params=pltpu.CompilerParams(
            collective_id=0, has_side_effects=True, vmem_limit_bytes=VMEM_BYTES
        ),
        name="step",
    )(*args)
    (
        block_out,
        tokens_grad,
        prev_grad,
        qkv_grad,
        out_w_grad,
        gate_grad,
        const_grad,
        vec_grad,
        one_grad,
        two_grad,
        mix_grad,
        up_grad,
        down_grad,
    ) = hand_over(outs)
    return (
        block_out,
        tokens_grad,
        prev_grad.T,
        qkv_grad,
        out_w_grad,
        gate_grad.T,
        const_grad.T,
        vec_grad.T,
        one_grad[0],
        two_grad[0],
        mix_grad,
        up_grad[None],
        down_grad[None],
    )


def copy_kernel(count, *refs):
    held = refs[2 * count : 3 * count]
    in_sems, out_sems = refs[3 * count :]
    reads = [pltpu.make_async_copy(refs[i], held[i], in_sems.at[i]) for i in range(count)]
    writes = [
        pltpu.make_async_copy(held[i], refs[count + i], out_sems.at[i]) for i in range(count)
    ]
    for copy in reads:
        copy.start()
    for read, write in zip(reads, writes):
        read.wait()
        write.start()
    for copy in writes:
        copy.wait()


def hand_over(arrays):
    count = len(arrays)
    anywhere = pl.BlockSpec(memory_space=pl.ANY)
    return pl.pallas_call(
        functools.partial(copy_kernel, count),
        out_shape=tuple(jax.ShapeDtypeStruct(a.shape, a.dtype) for a in arrays),
        in_specs=[anywhere] * count,
        out_specs=(anywhere,) * count,
        scratch_shapes=[pltpu.VMEM(a.shape, a.dtype) for a in arrays]
        + [pltpu.SemaphoreType.DMA((count,))] * 2,
        name="hand_over",
    )(*arrays)


def turn_tables(tok_rows):
    half_dim = HEAD_DIM // 2
    steps = np.arange(half_dim, dtype=np.float32) * np.float32(2.0 / HEAD_DIM)
    frequency = np.power(np.float32(rotary_base), -steps).astype(np.float32)
    angles = np.arange(tok_rows, dtype=np.float32)[:, None] * frequency[None, :]
    cosine = np.cos(angles.astype(np.float64)).astype(np.float32)
    sine = np.sin(angles.astype(np.float64)).astype(np.float32)
    cosine = np.tile(cosine, (1, LANES // half_dim))
    sine = np.tile(np.concatenate([-sine, sine], axis=1), (1, LANES // HEAD_DIM))
    return jnp.asarray(cosine), jnp.asarray(sine)


def fits_kernel(mesh):
    experts, shards = mesh.shape["expert"], mesh.shape["shard"]
    share, hidden_block = D // shards, FF // shards
    return (
        experts == 4
        and shards % 2 == 0
        and share % 32 == 0
        and hidden_block % LANES == 0
    )


def solution(mesh):
    placed = (
        P(("expert", "shard"), None),
        P(("expert", "shard")),
        P(("expert", "shard"), None),
        P(("expert", "shard"), None),
        P(("expert", "shard"), None),
        P(("expert", "shard"), None),
        P("shard", None),
        P("shard", None),
        P("shard", None),
        P("shard", None),
        P("shard", None),
        P("shard"),
        P("shard"),
        P(),
        P("expert", "shard", None),
        P("expert", "shard", None),
    )
    return jax.shard_map(
        kernel_body if fits_kernel(mesh) else body,
        mesh=mesh,
        in_specs=placed,
        out_specs=(
            P(("expert", "shard"), None),
            P(("expert", "shard"), None),
            P(("expert", "shard"), None),
            P("shard", None),
            P("shard", None),
            P("shard", None),
            P("shard", None),
            P("shard", None),
            P("shard"),
            P("shard"),
            P(),
            P("expert", "shard", None),
            P("expert", "shard", None),
        ),
        check_vma=False,
    )
```

```python
import functools

import jax
import jax.numpy as jnp
import numpy as np
from jax import lax
from jax.experimental import pallas as pl
from jax.experimental.pallas import tpu as pltpu
from jax.sharding import PartitionSpec as P

D = 768
FF = 2048
HEADS = 12
HEAD_DIM = 64


norm_eps = 1e-06
rotary_base = 10000.0
highest = lax.Precision.HIGHEST


def tables(tok_rows, head_dim):
    half_dim = head_dim // 2
    frequency = rotary_base ** (-(jnp.arange(half_dim, dtype=jnp.float32) * 2.0 / head_dim))
    angles = jnp.arange(tok_rows, dtype=jnp.float32)[:, None] * frequency[None, :]
    return (jnp.cos(angles)[:, None, :], jnp.sin(angles)[:, None, :])


def rotate(field, cosine, sine_table):
    half_dim = field.shape[-1] // 2
    first_half = field[..., :half_dim]
    second_half = field[..., half_dim:]
    return jnp.concatenate(
        [
            first_half * cosine - second_half * sine_table,
            second_half * cosine + first_half * sine_table,
        ],
        axis=-1,
    )


def place_pairs(route_rows, order, length, experts_ffn, capacity):
    tok_rows = route_rows.shape[0]
    token_ids = jnp.arange(tok_rows, dtype=jnp.int32)
    pair_valid = jnp.repeat(token_ids < length, 2)
    expert_flat = route_rows.reshape(-1)
    placed_expert = expert_flat[order]
    placed_live = pair_valid[order] & (placed_expert < experts_ffn)
    one_hot = (
        placed_expert[:, None] == jnp.arange(experts_ffn, dtype=jnp.int32)[None, :]
    ) & placed_live[:, None]
    counts = jnp.cumsum(one_hot.astype(jnp.int32), axis=0)
    slot_index = jnp.sum(jnp.where(one_hot, counts - 1, 0), axis=1)
    kept_pairs = placed_live & (slot_index < capacity)
    dest_placed = jnp.where(
        kept_pairs, placed_expert * capacity + slot_index, experts_ffn * capacity
    )
    pair_dest = jnp.zeros((2 * tok_rows,), jnp.int32).at[order].set(dest_placed)
    slot_pair = (
        jnp.full((experts_ffn * capacity,), 2 * tok_rows, jnp.int32)
        .at[dest_placed]
        .set(order, mode="drop")
    )
    return (pair_dest, slot_pair)


def attend_head(head, allowed, score_scale):
    query, keys_rot, values = head
    scores = jnp.dot(query, keys_rot.T, preferred_element_type=jnp.float32) * score_scale
    scores = jnp.where(allowed, scores, -1e30)
    top_score = jnp.max(scores, axis=1, keepdims=True)
    expo = jnp.exp(scores - top_score)
    total = jnp.sum(expo, axis=1, keepdims=True)
    probs = expo / total
    mixed = jnp.dot(probs.astype(jnp.bfloat16), values, preferred_element_type=jnp.float32).astype(
        jnp.bfloat16
    )
    return (mixed, top_score + jnp.log(total))


def attend_back(head, allowed, score_scale):
    query, keys_rot, values, grad_mixed, log_total = head
    scores = jnp.dot(query, keys_rot.T, preferred_element_type=jnp.float32) * score_scale
    scores = jnp.where(allowed, scores, -1e30)
    probs = jnp.where(allowed, jnp.exp(scores - log_total), 0.0)
    grad_probs = jnp.dot(grad_mixed, values.T, preferred_element_type=jnp.float32)
    delta = jnp.sum(grad_probs * probs, axis=1, keepdims=True)
    grad_scores = (probs * (grad_probs - delta)).astype(jnp.bfloat16)
    grad_query = jnp.dot(grad_scores, keys_rot, preferred_element_type=jnp.float32) * score_scale
    grad_key = jnp.dot(grad_scores.T, query, preferred_element_type=jnp.float32) * score_scale
    grad_value = jnp.dot(
        probs.astype(jnp.bfloat16).T, grad_mixed, preferred_element_type=jnp.float32
    )
    return (grad_query, grad_key, grad_value)


def body(
    tokens,
    seq_lengths,
    routes,
    pair_order,
    prev_logits,
    out_grad,
    qkv_weight,
    out_weight,
    gate_weight,
    const_weight,
    const_vector,
    norm1_gain,
    norm2_gain,
    gate_mix,
    expert_up,
    expert_down,
):
    tok_rows = tokens.shape[0]
    experts_ffn = lax.axis_size("expert")
    capacity = 2 * tok_rows // (experts_ffn + 4)
    length = seq_lengths[0]
    order = pair_order[0]
    score_scale = HEAD_DIM ** (-0.5)
    dense_shards = (
        qkv_weight,
        out_weight,
        gate_weight,
        const_weight,
        const_vector,
        norm1_gain,
        norm2_gain,
    )
    weight_qkv, weight_out, weight_gate, weight_const, vector_const, gain_one, gain_two = (
        lax.all_gather(dense_shards[0], "shard", axis=0, tiled=True),
        lax.all_gather(dense_shards[1], "shard", axis=0, tiled=True),
        lax.all_gather(dense_shards[2], "shard", axis=0, tiled=True),
        lax.all_gather(dense_shards[3], "shard", axis=0, tiled=True),
        lax.all_gather(dense_shards[4], "shard", axis=0, tiled=True),
        lax.all_gather(dense_shards[5], "shard", axis=0, tiled=True),
        lax.all_gather(dense_shards[6], "shard", axis=0, tiled=True),
    )
    weight_up, weight_down = (
        lax.all_gather(expert_up, "shard", axis=1, tiled=True),
        lax.all_gather(expert_down, "shard", axis=1, tiled=True),
    )
    weight_up = weight_up[0]
    weight_down = weight_down[0]
    inputs = tokens.astype(jnp.float32)
    token_ids = jnp.arange(tok_rows, dtype=jnp.int32)
    valid_mask = (token_ids < length).astype(jnp.float32)[:, None]
    gain_first = gain_one.astype(jnp.float32)
    gain_second = gain_two.astype(jnp.float32)
    scale_one = lax.rsqrt(jnp.mean(inputs * inputs, axis=1, keepdims=True) + norm_eps)
    normed = (inputs * scale_one * gain_first).astype(jnp.bfloat16)
    qkv_all = jnp.dot(normed, weight_qkv, preferred_element_type=jnp.float32)
    cosine, sine_table = tables(tok_rows, HEAD_DIM)

    def heads_first(block):
        return jnp.transpose(block, (1, 0, 2)).astype(jnp.bfloat16)

    query = heads_first(
        rotate(qkv_all[:, :D].reshape(tok_rows, HEADS, HEAD_DIM), cosine, sine_table)
    )
    keys_rot = heads_first(
        rotate(qkv_all[:, D : 2 * D].reshape(tok_rows, HEADS, HEAD_DIM), cosine, sine_table)
    )
    values = heads_first(qkv_all[:, 2 * D :].reshape(tok_rows, HEADS, HEAD_DIM))
    allowed = (token_ids[None, :] <= token_ids[:, None]) & (token_ids[None, :] < length)
    mixed_heads, log_totals = lax.map(
        lambda head: attend_head(head, allowed, score_scale), (query, keys_rot, values)
    )
    mixed = jnp.transpose(mixed_heads, (1, 0, 2)).reshape(tok_rows, D)
    hidden = inputs + jnp.dot(mixed, weight_out, preferred_element_type=jnp.float32)
    scale_two = lax.rsqrt(jnp.mean(hidden * hidden, axis=1, keepdims=True) + norm_eps)
    normed_two = hidden * scale_two * gain_second
    normed_low = normed_two.astype(jnp.bfloat16)
    mixer = gate_mix.astype(jnp.float32)
    logits = jnp.dot(normed_low, weight_gate, preferred_element_type=jnp.float32) + jnp.dot(
        prev_logits, mixer, precision=highest
    )
    chosen = jnp.take_along_axis(logits, routes, axis=1)
    gate_exp = jnp.exp(chosen - jnp.max(chosen, axis=1, keepdims=True))
    gates = gate_exp / jnp.sum(gate_exp, axis=1, keepdims=True)
    pair_dest, slot_pair = place_pairs(routes, order, length, experts_ffn, capacity)
    padded = jnp.concatenate([normed_low, jnp.zeros((1, D), jnp.bfloat16)], axis=0)
    send_rows = padded[slot_pair // 2].reshape(experts_ffn, capacity, D)
    received = lax.all_to_all(send_rows, "expert", split_axis=0, concat_axis=0, tiled=True)
    lead_shape = received.shape[:2]
    flat_rows = received.reshape(-1, D)
    gate_up = jnp.dot(flat_rows, weight_up, preferred_element_type=jnp.float32)
    activated = (jax.nn.silu(gate_up[:, :FF]) * gate_up[:, FF:]).astype(jnp.bfloat16)
    expert_out = jnp.dot(activated, weight_down, preferred_element_type=jnp.float32).astype(
        jnp.bfloat16
    )
    received, gate_up, activated, expert_out = (
        received,
        gate_up.reshape(lead_shape + (2 * FF,)),
        activated.reshape(lead_shape + (FF,)),
        expert_out.reshape(received.shape),
    )
    returned = lax.all_to_all(expert_out, "expert", split_axis=0, concat_axis=0, tiled=True)
    returned_pad = jnp.concatenate(
        [returned.reshape(-1, D), jnp.zeros((1, D), jnp.bfloat16)], axis=0
    )
    pair_ffn = returned_pad[pair_dest].astype(jnp.float32).reshape(tok_rows, 2, D)
    vector_float = vector_const.astype(jnp.float32)
    const_logits = jnp.dot(normed_low, weight_const, preferred_element_type=jnp.float32).reshape(
        tok_rows, 2, 2
    )
    const_exp = jnp.exp(const_logits - jnp.max(const_logits, axis=2, keepdims=True))
    coefs = const_exp / jnp.sum(const_exp, axis=2, keepdims=True)
    const_out = (
        coefs[..., 0:1] * normed_two[:, None, :] + coefs[..., 1:2] * vector_float.T[None, :, :]
    )
    const_select = (
        routes[:, :, None] == experts_ffn + 2 + jnp.arange(2, dtype=jnp.int32)[None, None, :]
    ).astype(jnp.float32)
    copy_select = (routes == experts_ffn + 1).astype(jnp.float32)[:, :, None]
    pair_out = (
        pair_ffn
        + copy_select * normed_two[:, None, :]
        + jnp.einsum("tkc,tcd->tkd", const_select, const_out, precision=highest)
    )
    mixture = jnp.sum(gates[:, :, None] * pair_out, axis=1)
    block_out = (valid_mask * (hidden + mixture)).astype(jnp.bfloat16)
    back_dense = (
        lax.all_gather(dense_shards[0], "shard", axis=0, tiled=True),
        lax.all_gather(dense_shards[1], "shard", axis=0, tiled=True),
        lax.all_gather(dense_shards[2], "shard", axis=0, tiled=True),
        lax.all_gather(dense_shards[3], "shard", axis=0, tiled=True),
        lax.all_gather(dense_shards[4], "shard", axis=0, tiled=True),
        lax.all_gather(dense_shards[5], "shard", axis=0, tiled=True),
        lax.all_gather(dense_shards[6], "shard", axis=0, tiled=True),
    )
    back_up, back_down = (
        lax.all_gather(expert_up, "shard", axis=1, tiled=True),
        lax.all_gather(expert_down, "shard", axis=1, tiled=True),
    )
    back_up = back_up[0]
    back_down = back_down[0]
    back_qkv, back_out, back_gate, back_const = (
        back_dense[0],
        back_dense[1],
        back_dense[2],
        back_dense[3],
    )
    grad_rows = out_grad.astype(jnp.float32) * valid_mask
    grad_gates = jnp.sum(grad_rows[:, None, :] * pair_out, axis=2)
    grad_pairs = gates[:, :, None] * grad_rows[:, None, :]
    grad_chosen = gates * (grad_gates - jnp.sum(gates * grad_gates, axis=1, keepdims=True))
    route_hot = (
        routes[:, :, None] == jnp.arange(experts_ffn + 4, dtype=jnp.int32)[None, None, :]
    ).astype(jnp.float32)
    grad_logits = jnp.sum(route_hot * grad_chosen[:, :, None], axis=1)
    prev_grad = jnp.dot(grad_logits, mixer.T, precision=highest)
    mix_term = jnp.dot(prev_logits.T, grad_logits, precision=highest)
    logit_low = grad_logits.astype(jnp.bfloat16)
    gate_term = jnp.dot(normed_low.T, logit_low, preferred_element_type=jnp.float32)
    grad_normed = jnp.dot(logit_low, back_gate.T, preferred_element_type=jnp.float32)
    grad_flat = jnp.concatenate(
        [grad_pairs.reshape(2 * tok_rows, D).astype(jnp.bfloat16), jnp.zeros((1, D), jnp.bfloat16)],
        axis=0,
    )
    grad_send = grad_flat[slot_pair].reshape(experts_ffn, capacity, D)
    grad_recv = lax.all_to_all(grad_send, "expert", split_axis=0, concat_axis=0, tiled=True)
    grad_slots = grad_recv.reshape(-1, D)
    down_term = jnp.dot(activated.reshape(-1, FF).T, grad_slots, preferred_element_type=jnp.float32)
    grad_act = jnp.dot(grad_slots, back_down.T, preferred_element_type=jnp.float32)
    gate_part = gate_up[..., :FF].reshape(-1, FF)
    up_part = gate_up[..., FF:].reshape(-1, FF)
    sigmoid_gate = jax.nn.sigmoid(gate_part)
    grad_gate_up = jnp.concatenate(
        [
            grad_act * up_part * sigmoid_gate * (1.0 + gate_part * (1.0 - sigmoid_gate)),
            grad_act * gate_part * sigmoid_gate,
        ],
        axis=1,
    ).astype(jnp.bfloat16)
    up_term = jnp.dot(received.reshape(-1, D).T, grad_gate_up, preferred_element_type=jnp.float32)
    grad_input = (
        jnp.dot(grad_gate_up, back_up.T, preferred_element_type=jnp.float32)
        .astype(jnp.bfloat16)
        .reshape(received.shape)
    )
    grad_back = lax.all_to_all(grad_input, "expert", split_axis=0, concat_axis=0, tiled=True)
    back_pad = jnp.concatenate([grad_back.reshape(-1, D), jnp.zeros((1, D), jnp.bfloat16)], axis=0)
    grad_normed = grad_normed + jnp.sum(
        back_pad[pair_dest].astype(jnp.float32).reshape(tok_rows, 2, D), axis=1
    )
    grad_normed = grad_normed + jnp.sum(copy_select * grad_pairs, axis=1)
    grad_const_out = jnp.einsum("tkc,tkd->tcd", const_select, grad_pairs, precision=highest)
    grad_first = jnp.sum(grad_const_out * normed_two[:, None, :], axis=2)
    grad_second = jnp.sum(grad_const_out * vector_float.T[None, :, :], axis=2)
    grad_coefs = jnp.stack([grad_first, grad_second], axis=2)
    grad_const_logits = (
        coefs * (grad_coefs - jnp.sum(coefs * grad_coefs, axis=2, keepdims=True))
    ).reshape(tok_rows, 4)
    grad_normed = grad_normed + jnp.sum(coefs[..., 0:1] * grad_const_out, axis=1)
    grad_normed = grad_normed + jnp.dot(
        grad_const_logits, back_const.astype(jnp.float32).T, precision=highest
    )
    vector_term = jnp.einsum("tc,tcd->dc", coefs[..., 1], grad_const_out, precision=highest)
    const_term = jnp.dot(normed_low.astype(jnp.float32).T, grad_const_logits, precision=highest)
    second_gain_term = jnp.sum(grad_normed * hidden * scale_two, axis=0)
    scaled_two = gain_second * grad_normed
    grad_hidden = (
        grad_rows
        + scale_two * scaled_two
        - hidden * scale_two**3 * jnp.mean(scaled_two * hidden, axis=1, keepdims=True)
    )
    grad_attn_low = grad_hidden.astype(jnp.bfloat16)
    out_term = jnp.dot(mixed.T, grad_attn_low, preferred_element_type=jnp.float32)
    grad_mixed = jnp.dot(grad_attn_low, back_out.T, preferred_element_type=jnp.float32).astype(
        jnp.bfloat16
    )
    grad_mixed_heads = jnp.transpose(grad_mixed.reshape(tok_rows, HEADS, HEAD_DIM), (1, 0, 2))
    grad_query, grad_key, grad_value = lax.map(
        lambda head: attend_back(head, allowed, score_scale),
        (query, keys_rot, values, grad_mixed_heads, log_totals),
    )
    grad_query = rotate(jnp.transpose(grad_query, (1, 0, 2)), cosine, -sine_table).reshape(
        tok_rows, D
    )
    grad_key = rotate(jnp.transpose(grad_key, (1, 0, 2)), cosine, -sine_table).reshape(tok_rows, D)
    grad_value = jnp.transpose(grad_value, (1, 0, 2)).reshape(tok_rows, D)
    grad_qkv = jnp.concatenate([grad_query, grad_key, grad_value], axis=1).astype(jnp.bfloat16)
    qkv_term = jnp.dot(normed.T, grad_qkv, preferred_element_type=jnp.float32)
    grad_first_norm = jnp.dot(grad_qkv, back_qkv.T, preferred_element_type=jnp.float32)
    first_gain_term = jnp.sum(grad_first_norm * inputs * scale_one, axis=0)
    scaled_one = gain_first * grad_first_norm
    tokens_grad = (
        grad_hidden
        + scale_one * scaled_one
        - inputs * scale_one**3 * jnp.mean(scaled_one * inputs, axis=1, keepdims=True)
    )
    dense_all = (
        qkv_term,
        out_term,
        gate_term,
        const_term,
        vector_term,
        first_gain_term,
        second_gain_term,
    )
    dense_terms = (
        lax.psum_scatter(dense_all[0], "shard", scatter_dimension=0, tiled=True),
        lax.psum_scatter(dense_all[1], "shard", scatter_dimension=0, tiled=True),
        lax.psum_scatter(dense_all[2], "shard", scatter_dimension=0, tiled=True),
        lax.psum_scatter(dense_all[3], "shard", scatter_dimension=0, tiled=True),
        lax.psum_scatter(dense_all[4], "shard", scatter_dimension=0, tiled=True),
        lax.psum_scatter(dense_all[5], "shard", scatter_dimension=0, tiled=True),
        lax.psum_scatter(dense_all[6], "shard", scatter_dimension=0, tiled=True),
    )
    (
        qkv_grad,
        out_weight_grad,
        gate_grad,
        const_weight_grad,
        const_vector_grad,
        norm1_grad,
        norm2_grad,
    ) = lax.psum(
        (
            dense_terms[0],
            dense_terms[1],
            dense_terms[2],
            dense_terms[3],
            dense_terms[4],
            dense_terms[5],
            dense_terms[6],
        ),
        "expert",
    )
    mix_grad = lax.psum(mix_term, ("expert", "shard"))
    expert_up_grad, expert_down_grad = (
        lax.psum_scatter(up_term[None], "shard", scatter_dimension=1, tiled=True),
        lax.psum_scatter(down_term[None], "shard", scatter_dimension=1, tiled=True),
    )
    return (
        block_out,
        tokens_grad,
        prev_grad,
        qkv_grad,
        out_weight_grad,
        gate_grad,
        const_weight_grad,
        const_vector_grad,
        norm1_grad,
        norm2_grad,
        mix_grad,
        expert_up_grad,
        expert_down_grad,
    )


MESH = pl.DeviceIdType.MESH
BF = jnp.bfloat16
F32 = jnp.float32
LANES = 128
NEG = -1e30
VMEM_BYTES = 64 * 1024 * 1024
RING = 3
HOPS = (0, 1, 3, 5)
PARTS = 2
BATCHES = 2


def dot(a, b):
    return lax.dot_general(a, b, (((1,), (0,)), ((), ())), preferred_element_type=F32)


def dot_nt(a, b):
    return lax.dot_general(a, b, (((1,), (1,)), ((), ())), preferred_element_type=F32)


def dot_tn(a, b):
    return lax.dot_general(a, b, (((0,), (0,)), ((), ())), preferred_element_type=F32)


def iota(shape, dim):
    return lax.broadcasted_iota(jnp.int32, shape, dim)


def remote(src, dst, send_sem, recv_sem, target):
    return pltpu.make_async_remote_copy(
        src_ref=src,
        dst_ref=dst,
        send_sem=send_sem,
        recv_sem=recv_sem,
        device_id=target,
        device_id_type=MESH,
    )


def swap_halves(block):
    half = HEAD_DIM // 2
    width = block.shape[1]
    lower = (iota(block.shape, 1) % HEAD_DIM) < half
    return jnp.where(
        lower, pltpu.roll(block, width - half, 1), pltpu.roll(block, half, 1)
    )


def step_kernel(dims, scratch_names, *refs):
    (tok_rows, experts, lines, share, hidden_block, capacity, gate_cols) = dims
    names = IN_NAMES + OUT_NAMES + scratch_names
    r = dict(zip(names, refs))
    pairs = D // LANES
    layer = 2 * experts
    slots = experts * capacity
    quarter = share // 4
    chunk_cols = 3 * LANES
    out_chunks = D // chunk_cols
    chunks = out_chunks + pairs
    half_ffn = lines * 2 * hidden_block
    const_col = gate_cols
    vec_col = gate_cols + 8
    row_blocks = tok_rows // LANES

    e = lax.axis_index("expert")
    s = lax.axis_index("shard")
    z = s // 2
    x = s % 2
    core = e % 2
    half = e // 2
    facing = 2 * (1 - half) + core
    across = 2 * z + 1 - x
    twin = e + 1 - 2 * core
    mine = 2 * e + x

    def rows(index, size):
        return pl.ds(pl.multiple_of(index * size, size), size)

    weights, small = r["weights"], r["small"]
    up, down, stage = r["up"], r["down"], r["stage"]
    own_rows = rows(s, share)

    def up_columns(part, jj, xx):
        return pl.ds(
            pl.multiple_of(part * FF + hidden_block * (2 * jj + xx), hidden_block), hidden_block
        )

    def up_load(jj, part, to):
        spot = pl.ds(part * hidden_block, hidden_block)
        box = stage.at[jj, :, spot] if to == 0 else up.at[jj, own_rows, spot]
        xx = 1 - x if to == 0 else x
        return pltpu.make_async_copy(
            r["up_in"].at[:, up_columns(part, jj, xx)], box, r["up_sem"].at[to, jj, part]
        )

    direct = {
        "qkv_in": weights.at[own_rows, pl.ds(0, 3 * D)],
        "out_in": weights.at[own_rows, pl.ds(3 * D, D)],
        "down_in": down.at[z],
    }

    def load(name):
        box = direct[name] if name in direct else r["own_" + name]
        return pltpu.make_async_copy(r[name], box, r["in_sem"].at[LOADED.index(name)])

    def store(name):
        return pltpu.make_async_copy(
            r["own_" + name], r[name], r["out_sem"].at[OUT_NAMES.index(name)]
        )

    load("qkv_in").start()
    for jj in range(lines):
        for part in range(2):
            up_load(jj, part, 0).start()
    for name in LOADED[1:]:
        load(name).start()
    for jj in range(lines):
        for part in range(2):
            up_load(jj, part, 1).start()

    barrier = pltpu.get_barrier_semaphore()
    met = 0
    for step in range(1, 2 * lines):
        pl.semaphore_signal(
            barrier, 1, device_id=(e, (s + step) % (2 * lines)), device_id_type=MESH
        )
        met += 1
    for step in range(1, experts):
        for side in range(2):
            pl.semaphore_signal(
                barrier, 1, device_id=((e + step) % experts, 2 * z + side), device_id_type=MESH
            )
            met += 1
    pl.semaphore_wait(barrier, met)

    def down_part(ref, index, part):
        height = hidden_block // PARTS
        return ref.at[index, pl.ds(part * height, height), :]

    def up_across(jj, origin_x):
        return remote(
            stage.at[jj],
            up.at[jj, rows(2 * z + origin_x, share), :],
            r["ux_send"].at[jj],
            r["ux_recv"].at[jj],
            (e, across),
        )

    def chain(kind, way, step, jj, zz):
        ref = up.at[jj, rows(zz, 2 * share), :] if kind == 0 else down_part(down, jj, kind - 1)
        target = s + 2 if way == 0 else s - 2
        return remote(
            ref,
            ref,
            r["ch_send"].at[kind, way, step, jj],
            r["ch_recv"].at[kind, way, step, jj],
            (e, target),
        )

    def chain_each(way, step, jj, zz, go):
        go(0, way, step, jj, zz)

        @pl.when(zz == jj)
        def _():
            for part in range(PARTS):
                go(1 + part, way, step, jj, zz)

    def begin(*which):
        chain(*which).start()

    def arrive(*which):
        chain(*which).wait_recv()

    def leave(*which):
        chain(*which).wait_send()

    def hand_on(kind, way, step, jj, zz):
        chain(kind, way, step, jj, zz).wait_recv()
        chain(kind, way, step + 1, jj, zz).start()

    def chain_own(jj):
        for part in range(2):
            up_load(jj, part, 1).wait()
        up_across(jj, 1 - x).wait_recv()

        @pl.when(z + 1 < lines)
        def _():
            chain_each(0, 0, jj, z, begin)

        @pl.when(z > 0)
        def _():
            chain_each(1, 0, jj, z, begin)

    def chain_pass(jj, step):
        @pl.when((z - 1 - step >= 0) & (z + 1 < lines))
        def _():
            chain_each(0, step, jj, z - 1 - step, hand_on)

        @pl.when((z + 1 + step < lines) & (z > 0))
        def _():
            chain_each(1, step, jj, z + 1 + step, hand_on)

    def chain_end(jj):
        for step in range(lines - 1):

            @pl.when((z - 1 - step >= 0) & (z + 1 == lines))
            def _():
                chain_each(0, step, jj, z - 1 - step, arrive)

            @pl.when((z + 1 + step < lines) & (z == 0))
            def _():
                chain_each(1, step, jj, z + 1 + step, arrive)

    def chain_sent():
        for jj in range(lines):
            for step in range(lines - 1):

                @pl.when((z - step >= 0) & (z + 1 < lines))
                def _():
                    chain_each(0, step, jj, z - step, leave)

                @pl.when((z + step < lines) & (z > 0))
                def _():
                    chain_each(1, step, jj, z + step, leave)

    passes = [(jj, step) for step in range(lines - 2) for jj in range(lines)]

    def chain_events(first, count):
        for number in range(first, min(first + count, len(passes))):
            chain_pass(*passes[number])

    for jj in range(lines):
        for part in range(2):
            up_load(jj, part, 0).wait()
    up_across(0, x).start()

    spans = ((0, 3 * D // 2), (3 * D, D // 2))

    third = share // 3

    def part_of(kind, zz, xx, cc, first, height):
        start, width = spans[kind]
        columns = pl.ds(pl.multiple_of(start + width * cc, LANES), width)
        spot = pl.ds(pl.multiple_of((2 * zz + xx) * share + first, third), height)
        return weights.at[spot, columns]

    def slab(kind, zz, xx, cc):
        return part_of(kind, zz, xx, cc, third * half, 2 * third)

    def dense_z(kind, way, step, zz):
        ref = slab(kind, zz, x, core)
        return remote(
            ref,
            ref,
            r["dz_send"].at[kind, way, step],
            r["d_recv"].at[kind, zz, x, core],
            (e, s + 2 if way == 0 else s - 2),
        )

    def dense_z_each(kind, step, go):
        @pl.when((z - step >= 0) & (z + 1 < lines))
        def _():
            go(dense_z(kind, 0, step, z - step))

        @pl.when((z + step < lines) & (z > 0))
        def _():
            go(dense_z(kind, 1, step, z + step))

    def dense_x(kind, zz):
        ref = slab(kind, zz, x, core)
        return remote(
            ref, ref, r["dx_send"].at[kind, zz], r["d_recv"].at[kind, zz, x, core], (e, across)
        )

    def dense_core(kind, zz, xx):
        ref = slab(kind, zz, xx, core)
        return remote(
            ref,
            ref,
            r["dc_send"].at[kind, zz, xx],
            r["d_recv"].at[kind, zz, xx, core],
            (twin, s),
        )

    def dense_y(kind, zz, xx):
        ref = part_of(kind, zz, xx, core, 2 * third * half, third)
        return remote(
            ref,
            ref,
            r["dy_send"].at[kind, zz, xx],
            r["dy_recv"].at[kind, zz, xx, core],
            (facing, s),
        )

    def rest_core(kind, zz, xx, cc):
        ref = part_of(kind, zz, xx, cc, 2 * third * (1 - half), third)
        return remote(
            ref,
            ref,
            r["dr_send"].at[kind, zz, xx],
            r["dy_recv"].at[kind, zz, xx, cc],
            (twin, s),
        )

    def dense_arrived(kind, zz, xx, cc):
        ref = slab(kind, zz, xx, cc)
        remote(
            ref, ref, r["dx_send"].at[kind, 0], r["d_recv"].at[kind, zz, xx, cc], (e, across)
        ).wait_recv()

    def dense_start(kind):
        dense_z_each(kind, 0, lambda copy: copy.start())
        dense_x(kind, z).start()

    def dense_forward(kind, step):
        for zz, there in ((z - 1 - step, z - 1 - step >= 0), (z + 1 + step, z + 1 + step < lines)):

            @pl.when(there)
            def _():
                dense_arrived(kind, zz, x, core)

                if step + 1 < lines - 1:

                    @pl.when((zz < z) & (z + 1 < lines))
                    def _():
                        dense_z(kind, 0, step + 1, zz).start()

                    @pl.when((zz > z) & (z > 0))
                    def _():
                        dense_z(kind, 1, step + 1, zz).start()

                dense_x(kind, zz).start()
                dense_core(kind, zz, x).start()
                dense_y(kind, zz, x).start()

    def dense_share(kind):
        for step in range(lines):
            zz = (z + lines - step) % lines
            dense_arrived(kind, zz, 1 - x, core)
            dense_core(kind, zz, 1 - x).start()
            dense_y(kind, zz, 1 - x).start()

    def dense_cross(kind):
        for step in range(lines):
            zz = (z + lines - step) % lines
            for xx in (x, 1 - x) if step > 0 else (1 - x,):
                rest_core(kind, zz, xx, core).wait_recv()
                rest_core(kind, zz, xx, core).start()

    def dense_finish(kind):
        for step in range(lines):
            zz = (z + lines - step) % lines
            for xx in (x, 1 - x) if step > 0 else (1 - x,):
                dense_arrived(kind, zz, xx, 1 - core)
                rest_core(kind, zz, xx, 1 - core).wait_recv()

    def dense_sent(kind):
        for step in range(lines - 1):
            dense_z_each(kind, step, lambda copy: copy.wait_send())
        for step in range(lines):
            zz = (z + lines - step) % lines
            dense_x(kind, zz).wait_send()
            for xx in (x, 1 - x) if step > 0 else (1 - x,):
                dense_core(kind, zz, xx).wait_send()
                dense_y(kind, zz, xx).wait_send()
                rest_core(kind, zz, xx, core).wait_send()

    def small_copy(step, origin):
        ref = small.at[rows(origin, share), :]
        return remote(
            ref,
            ref,
            r["sm_send"].at[step],
            r["sm_recv"].at[origin],
            (e, (s + step) % (2 * lines)),
        )

    load("qkv_in").wait()
    dense_start(0)
    for name in LOADED[1:]:
        load(name).wait()
    dense_start(1)
    pack = r["pack"]
    pack[...] = jnp.zeros_like(pack)
    spot = 0
    for name in ("gate_in", "const_in", "const_in", "vec_in", "one_in", "two_in"):
        height = r[name].shape[0]
        pack[spot : spot + height, 0:share] = r["own_" + name][...].astype(F32)
        spot += height
    small[rows(s, share), :] = jnp.transpose(pack[...])[0:share, :].astype(BF)
    for step in range(1, 2 * lines):
        small_copy(step, s).start()
    token_rows, token_cols = r["token_rows"], r["token_cols"]
    token_rows[...] = jnp.zeros_like(token_rows)
    token_rows[0:2, :] = r["own_routes_in"][...].astype(F32)
    token_rows[8 : 8 + gate_cols, :] = r["own_prev_in"][...]
    token_cols[...] = jnp.transpose(token_rows[...])

    tokens = r["own_tokens"]
    cols = r["cols"]
    for block in range(row_blocks):
        at = slice(block * LANES, (block + 1) * LANES)
        inputs = tokens[at, :].astype(F32)
        cols[at, 0:1] = lax.rsqrt(jnp.mean(inputs * inputs, axis=1, keepdims=True) + norm_eps)
    dense_forward(0, 0)

    dense_forward(0, 1)
    dense_forward(1, 0)

    length = r["length"][0]
    pair_ids = iota((2 * tok_rows, 2 * tok_rows), 0)
    pair_names = jnp.where(pair_ids < tok_rows, 2 * pair_ids, 2 * (pair_ids - tok_rows) + 1)
    is_at = jnp.where(pair_names == r["own_order_row"][...], 1.0, 0.0).astype(BF)
    pair_lane = iota((16, 2 * tok_rows), 1)
    pair_token = jnp.where(pair_lane < tok_rows, pair_lane, pair_lane - tok_rows)
    expert_row = iota((16, 2 * tok_rows), 0)
    route_row = jnp.concatenate([token_rows[0:1, :], token_rows[1:2, :]], axis=1)
    live = (expert_row.astype(F32) == route_row) & (expert_row < experts) & (pair_token < length)
    placed = dot(jnp.where(live, 1.0, 0.0).astype(BF), is_at)
    before = jnp.where(
        iota((2 * tok_rows, 2 * tok_rows), 0) <= iota((2 * tok_rows, 2 * tok_rows), 1), 1.0, 0.0
    ).astype(BF)
    counts = dot(placed.astype(BF), before)
    kept = jnp.where((placed > 0.5) & (counts <= capacity + 0.5), counts, 0.0)
    taken = dot_nt(kept.astype(BF), is_at)
    slot_of = jnp.sum(
        jnp.where(taken > 0.5, taken + (expert_row * capacity).astype(F32), 0.0),
        axis=0,
        keepdims=True,
    )
    slot_col = jnp.transpose(jnp.broadcast_to(slot_of, (8, 2 * tok_rows)))
    for step in range(2, lines - 1):
        dense_forward(0, step)
    for step in range(1, lines - 1):
        dense_forward(1, step)
    for jj in range(1, lines):
        up_across(jj, x).start()
    chain_own(0)
    put, take = r["put"], r["take"]
    for k in range(2):
        span = slice(k * tok_rows, (k + 1) * tok_rows)
        names_down = (iota((slots, tok_rows), 0) + 1).astype(F32)
        put[k] = jnp.where(slot_of[:, span] == names_down, 1.0, 0.0).astype(BF)
        names_right = (iota((tok_rows, slots), 1) + 1).astype(F32)
        take[k] = jnp.where(slot_col[span, 0:1] == names_right, 1.0, 0.0).astype(BF)

    for step in range(1, 2 * lines):
        origin = (s + 2 * lines - step) % (2 * lines)
        small_copy(step, origin).wait_recv()
    pick = jnp.where(iota((8, LANES), 1) == iota((8, LANES), 0) + vec_col, 1.0, 0.0).astype(BF)
    named = dot_nt(pick, small[...])
    r["rows"][...] = named
    gain_one, gain_two = named[2:3, :], named[3:4, :]
    vec_zero, vec_one = named[0:1, :], named[1:2, :]
    normed = r["normed"]
    for block in range(row_blocks):
        at = slice(block * LANES, (block + 1) * LANES)
        inputs = tokens[at, :].astype(F32)
        normed[at, :] = (inputs * cols[at, 0:1] * gain_one).astype(BF)

    dense_share(0)
    dense_cross(0)
    for jj in range(1, lines):
        chain_own(jj)
    dense_finish(0)

    heads = r["heads"]
    cosine, sine = r["own_cosine"], r["own_sine"]

    def project(b, turn):
        wide_block = dot(normed[...], weights[:, rows(b, 2 * LANES)])
        for part in range(2):
            block = wide_block[:, part * LANES : (part + 1) * LANES]
            if turn:
                block = block * cosine[...] + swap_halves(block) * sine[...]
            heads[2 * b + part] = block.astype(BF)

    def rotated(b, _):
        project(b, True)
        return 0

    def plain(b, _):
        project(b, False)
        return 0

    lax.fori_loop(0, pairs, rotated, 0)
    lax.fori_loop(pairs, 3 * pairs // 2, plain, 0)
    chain_events(0, 2)

    score_scale = HEAD_DIM ** (-0.5)
    first_head = iota((tok_rows, LANES), 1) < HEAD_DIM
    mixed, log_sums = r["mixed"], r["log_sums"]

    def allowed_pairs():
        key, query = iota((tok_rows, tok_rows), 0), iota((tok_rows, tok_rows), 1)
        return (key <= query) & (key < length)

    def one_head(block, head):
        keep = first_head if head == 0 else jnp.logical_not(first_head)
        return jnp.where(keep, block, jnp.zeros_like(block))

    def attend(p, _):
        query, key, value = heads[p], heads[pairs + p], heads[2 * pairs + p]
        results = []
        for head in range(2):
            scores = dot_nt(key, one_head(query, head)) * score_scale
            scores = jnp.where(allowed_pairs(), scores, NEG)
            top = jnp.max(scores, axis=0, keepdims=True)
            expo = jnp.exp(scores - top)
            total = jnp.sum(expo, axis=0, keepdims=True)
            probs = expo * (1.0 / total)
            log_sums[p, head : head + 1, :] = top + jnp.log(total)
            results.append(dot_tn(probs.astype(BF), value))
        mixed[:, rows(p, LANES)] = jnp.where(first_head, results[0], results[1]).astype(BF)
        return 0

    lax.fori_loop(0, pairs // 2, attend, 0)
    chain_events(2, 1)
    dense_share(1)
    dense_cross(1)
    lax.fori_loop(pairs // 2, pairs, attend, 0)
    dense_finish(1)
    chain_events(3, 1)

    hidden, normed_low = r["hidden"], r["normed_low"]
    out_grad = r["own_out_grad"]
    mixer = r["own_mix"][...].astype(F32)
    grad_low, grad_sum, sent = r["grad_low"], r["grad_sum"], r["sent"]
    for block in range(row_blocks):
        at = slice(block * LANES, (block + 1) * LANES)
        hid = tokens[at, :].astype(F32) + dot(mixed[at, :], weights[:, 3 * D : 4 * D])
        hidden[at, :] = hid
        scale = lax.rsqrt(jnp.mean(hid * hid, axis=1, keepdims=True) + norm_eps)
        cols[at, 1:2] = scale
        low = (hid * scale * gain_two).astype(BF)
        normed_low[at, :] = low
        logits = dot(low, small[...])
        lane = iota((LANES, LANES), 1)
        extra = jnp.zeros((LANES, gate_cols), F32)
        for i in range(gate_cols):
            extra = extra + token_cols[at, 8 + i : 9 + i] * mixer[i : i + 1, :]
        routes = token_cols[at, 0:2].astype(jnp.int32)
        chosen = []
        for k in range(2):
            hot = lane == routes[:, k : k + 1]
            part = jnp.sum(jnp.where(hot, logits, 0.0), axis=1, keepdims=True)
            chosen.append(
                part
                + jnp.sum(
                    jnp.where(
                        iota((LANES, gate_cols), 1) == routes[:, k : k + 1], extra, 0.0
                    ),
                    axis=1,
                    keepdims=True,
                )
            )
        top = jnp.maximum(chosen[0], chosen[1])
        powers = [jnp.exp(c - top) for c in chosen]
        total = powers[0] + powers[1]
        gates = [w / total for w in powers]
        on_normed = sum(
            gates[k] * (routes[:, k : k + 1] == experts + 1).astype(F32) for k in range(2)
        )
        for j in range(2):
            first = logits[:, const_col + 2 * j : const_col + 2 * j + 1]
            second = logits[:, const_col + 2 * j + 1 : const_col + 2 * j + 2]
            peak = jnp.maximum(first, second)
            first, second = jnp.exp(first - peak), jnp.exp(second - peak)
            both = first + second
            first, second = first / both, second / both
            weight = sum(
                gates[k] * (routes[:, k : k + 1] == experts + 2 + j).astype(F32)
                for k in range(2)
            )
            on_normed = on_normed + first * weight
            cols[at, 6 + 4 * j : 7 + 4 * j] = first
            cols[at, 7 + 4 * j : 8 + 4 * j] = second
            cols[at, 8 + 4 * j : 9 + 4 * j] = weight
        cols[at, 2:3] = gates[0]
        cols[at, 3:4] = gates[1]
        cols[at, 4:5] = on_normed
        valid = (iota((LANES, 1), 0) + block * LANES < length).astype(F32)
        grad = out_grad[at, :].astype(F32) * valid
        after = slice(tok_rows + block * LANES, tok_rows + (block + 1) * LANES)
        grad_low[at, :] = (gates[0] * grad).astype(BF)
        grad_low[after, :] = (gates[1] * grad).astype(BF)
        grad_sum[at, :] = grad.astype(BF)

    buffer, slot_grad = r["buffer"], r["slot_grad"]

    def dispatch(which, step, side, origin):
        target = (e + step) % experts
        box = buffer if which == 0 else slot_grad
        return remote(
            sent.at[rows(which * experts + target, capacity), :],
            box.at[rows(origin, capacity), :],
            r["go_send"].at[which, step, side],
            r["go_recv"].at[which, origin],
            (target, 2 * z + side),
        )

    def dispatch_each(which, step, go):
        for flip in range(2):
            side = x if flip == 0 else 1 - x
            if step > 0 or flip == 1:
                go(dispatch(which, step, side, mine))

    for step in range(experts):
        owner = (e + step) % experts
        chosen_rows = rows(owner, capacity)
        put_zero, put_one = put[0, chosen_rows, :], put[1, chosen_rows, :]
        sent[chosen_rows, :] = dot(put_zero + put_one, normed_low[...]).astype(BF)
        dispatch_each(0, step, lambda copy: copy.start())
        sent[rows(experts + owner, capacity), :] = (
            dot(put_zero, grad_low[0:tok_rows, :])
            + dot(put_one, grad_low[tok_rows : 2 * tok_rows, :])
        ).astype(BF)
        dispatch_each(1, step, lambda copy: copy.start())
    buffer[rows(mine, capacity), :] = sent[rows(e, capacity), :]
    slot_grad[rows(mine, capacity), :] = sent[rows(experts + e, capacity), :]
    chain_events(4, len(passes))

    def others(go):
        for step in range(experts):
            other = (e + step) % experts
            for flip in range(2):
                side = x if flip == 0 else 1 - x
                if step > 0 or flip == 1:
                    go(step, other, side, 2 * other + side)

    for which in range(2):
        others(lambda step, other, side, origin: dispatch(which, step, side, origin).wait_recv())

    up_sum, down_sum = r["up_sum"], r["down_sum"]
    up_box, down_box = r["up_box"], r["down_box"]
    up_out, down_out = r["own_up_out"], r["own_down_out"]
    final_send, final_box = stage, r["final_box"]
    ffn, slot_back = r["ffn"], r["slot_back"]
    last = lines - 1

    def summed(first, second):
        return (first.astype(F32) + second.astype(F32)).astype(BF)

    def up_rows(jj, zz):
        return up_sum.at[jj, rows(zz, 2 * share), :]

    def up_hop(way, k, jj, dest):
        return remote(
            up_rows(jj, dest),
            up_box.at[way, k, jj],
            r["ru_send"].at[way, k, jj],
            r["ru_recv"].at[way, k, jj],
            (e, s + 2 if way == 0 else s - 2),
        )

    def down_slot(way, jj, zz):
        return jj if way == 0 else jnp.where(jj == zz, lines, jj)

    def down_hop(way, jj, zz, part):
        return remote(
            down_part(down_sum, jj, part),
            down_part(down_box, down_slot(way, jj, zz), part),
            r["rd_send"].at[way, jj, part],
            r["rd_recv"].at[way, jj, part],
            (e, s + 2 if way == 0 else s - 2),
        )

    def final_hop(jj):
        return remote(
            final_send.at[jj],
            final_box.at[jj],
            r["fx_send"].at[jj],
            r["fx_recv"].at[jj],
            (e, across),
        )

    def sum_pass(jj, k):
        for way in range(2):
            place = z if way == 0 else last - z
            dest = last - k + place if way == 0 else k - place

            @pl.when((place >= 1) & (place <= k) & (place < last))
            def _():
                up_hop(way, k - 1, jj, dest).wait_recv()
                spot = rows(dest, 2 * share)
                up_sum[jj, spot, :] = summed(up_sum[jj, spot, :], up_box[way, k - 1, jj])
                up_hop(way, k, jj, dest).start()

                @pl.when(dest == jj)
                def _():
                    for part in range(PARTS):
                        down_hop(way, jj, z, part).wait_recv()
                        own = down_part(down_sum, jj, part)
                        own[...] = summed(
                            own[...], down_part(down_box, down_slot(way, jj, z), part)[...]
                        )
                        down_hop(way, jj, z + 1 - 2 * way, part).start()

    def sum_final(jj):
        total = slot_back.at[0 : 2 * share, 0 : 2 * hidden_block]
        total[...] = up_sum[jj, rows(z, 2 * share), :].astype(F32)
        for way, there in ((0, z > 0), (1, z < last)):

            @pl.when(there)
            def _():
                up_hop(way, last - 1, jj, z).wait_recv()
                total[...] += up_box[way, last - 1, jj].astype(F32)

        final_send[jj] = total[rows(1 - x, share), :].astype(BF)
        final_hop(jj).start()
        own = total[rows(x, share), :]
        for part in range(2):
            up_out[:, up_columns(part, jj, x)] = own[
                :, part * hidden_block : (part + 1) * hidden_block
            ]

        @pl.when(jj == z)
        def _():
            down_out[...] = down_sum[z].astype(F32)
            for way, there in ((0, z > 0), (1, z < last)):

                @pl.when(there)
                def _():
                    for part in range(PARTS):
                        down_hop(way, jj, z, part).wait_recv()
                    down_out[...] += down_box[down_slot(way, jj, z)].astype(F32)

    def sum_start(jj):
        for way in range(2):

            @pl.when(z == (0 if way == 0 else last))
            def _():
                for k in range(last):
                    dest = last - k if way == 0 else k
                    up_hop(way, k, jj, dest).start()

                    @pl.when(dest == jj)
                    def _():
                        for part in range(PARTS):
                            down_hop(way, jj, z + 1 - 2 * way, part).start()

    sum_passes = [(jj, k) for jj in range(lines) for k in range(1, last)]

    def sum_passed(first, count):
        for number in range(first, min(first + count, len(sum_passes))):
            sum_pass(*sum_passes[number])

    def sum_sent():
        for jj in range(lines):
            for way in range(2):
                place = z if way == 0 else last - z
                for k in range(last):
                    dest = last - k + place if way == 0 else k - place

                    @pl.when((place <= k) & (place < last))
                    def _():
                        up_hop(way, k, jj, dest).wait_send()

                        @pl.when(dest == jj)
                        def _():
                            for part in range(PARTS):
                                down_hop(way, jj, z + 1 - 2 * way, part).wait_send()

    for jj in range(lines):
        up_across(jj, x).wait_send()
    act, grad_gu = r["act"], r["grad_gu"]
    back_box = r["back_box"]
    side_rows = 4 * capacity
    for which in range(2):
        for step in range(experts):
            dispatch_each(which, step, lambda copy: copy.wait_send())

    def come(which, target, side, origin_e, origin_x):
        box = grad_low if which == 0 else sent
        return remote(
            box.at[rows(2 * target + side, capacity), :],
            back_box.at[which, origin_x, rows(origin_e, capacity), :],
            r["come_send"].at[which, target, side],
            r["come_recv"].at[which, origin_e, origin_x],
            (target, 2 * z + side),
        )

    def expert_chunk(jj, _):
        chain_end(jj)

        def forward(b, _):
            group = (half + 1 + b) % 2
            at = rows(group, side_rows)
            given = dot(buffer[at, :], up[jj])
            gate, lift = given[:, 0:hidden_block], given[:, hidden_block:]
            squash = 1.0 / (1.0 + jnp.exp(-gate))
            silu = gate * squash
            low = (silu * lift).astype(BF)
            act[at, :] = low
            grad_act = dot_nt(slot_grad[at, :], down[jj])
            grads = jnp.concatenate(
                [grad_act * lift * squash * (1.0 + gate * (1.0 - squash)), grad_act * silu],
                axis=1,
            ).astype(BF)
            grad_gu[at, :] = grads
            forth = dot(low, down[jj])
            back = dot_nt(grads, up[jj])

            @pl.when(jj == 0)
            def _():
                ffn[at, :] = forth
                slot_back[at, :] = back

            @pl.when((jj > 0) & (jj < last))
            def _():
                ffn[at, :] += forth
                slot_back[at, :] += back

            @pl.when(jj == last)
            def _():
                grad_low[at, :] = (ffn[at, :] + forth).astype(BF)
                sent[at, :] = (slot_back[at, :] + back).astype(BF)
                for other in range(2):
                    target = 2 * group + other
                    for which in range(2):
                        come(which, target, 1 - x, e, x).start()

                        @pl.when(target != e)
                        def _():
                            come(which, target, x, e, x).start()

            return 0

        lax.fori_loop(0, 2, forward, 0)
        up_sum[jj] = dot_tn(buffer[...], grad_gu[...]).astype(BF)
        down_sum[jj] = dot_tn(act[...], slot_grad[...]).astype(BF)
        sum_start(jj)
        return 0

    lax.fori_loop(0, lines, expert_chunk, 0)

    for which in range(2):
        box = grad_low if which == 0 else sent
        back_box[which, x, rows(e, capacity), :] = box[rows(mine, capacity), :]
    sum_passed(0, 3)
    for which in range(2):
        others(
            lambda step, other, side, origin: come(which, other, side, other, side).wait_recv()
        )
    for which in range(2):
        back_box[which, 0] = (
            back_box[which, 0].astype(F32) + back_box[which, 1].astype(F32)
        ).astype(BF)

    named = r["rows"][...]
    gain_one, gain_two = named[2:3, :], named[3:4, :]
    vec_zero, vec_one = named[0:1, :], named[1:2, :]
    grad_hidden, grad_attn = ffn.at[0:tok_rows, :], r["grad_attn"]
    thin, wide = r["thin"], r["wide"]
    grad_logits = r["grad_logits"]
    gain_sum = jnp.zeros((1, D), F32)
    for block in range(row_blocks):
        at = slice(block * LANES, (block + 1) * LANES)
        hid = hidden[at, :]
        scale = cols[at, 1:2]
        norm = hid * scale * gain_two
        grad = grad_sum[at, :].astype(F32)
        take_zero, take_one = take[0, at, :], take[1, at, :]
        outs = [dot(take_zero, back_box[0, 0]), dot(take_one, back_box[0, 0])]
        gates = [cols[at, 2:3], cols[at, 3:4]]
        on_normed = cols[at, 4:5]
        const = [
            (cols[at, 6 + 4 * j : 7 + 4 * j], cols[at, 7 + 4 * j : 8 + 4 * j], cols[at, 8 + 4 * j : 9 + 4 * j])
            for j in range(2)
        ]
        on_vec = [a * w for _, a, w in const]
        valid = (iota((LANES, 1), 0) + block * LANES < length).astype(F32)
        mixture = (
            gates[0] * outs[0]
            + gates[1] * outs[1]
            + on_normed * norm
            + on_vec[0] * vec_zero
            + on_vec[1] * vec_one
        )
        r["own_block_out"][at, :] = (valid * (hid + mixture)).astype(BF)
        routes = token_cols[at, 0:2].astype(jnp.int32)
        with_norm = jnp.sum(grad * norm, axis=1, keepdims=True)
        with_vec = [
            jnp.sum(grad * v, axis=1, keepdims=True) for v in (vec_zero, vec_one)
        ]
        gate_grads = []
        for k in range(2):
            value = jnp.sum(grad * outs[k], axis=1, keepdims=True)
            value = value + (routes[:, k : k + 1] == experts + 1).astype(F32) * with_norm
            for j in range(2):
                hit = (routes[:, k : k + 1] == experts + 2 + j).astype(F32)
                value = value + hit * (const[j][0] * with_norm + const[j][1] * with_vec[j])
            gate_grads.append(value)
        mean = gates[0] * gate_grads[0] + gates[1] * gate_grads[1]
        lane = iota((LANES, LANES), 1)
        spread = jnp.zeros((LANES, LANES), F32)
        for k in range(2):
            spread = spread + jnp.where(
                lane == routes[:, k : k + 1], gates[k] * (gate_grads[k] - mean), 0.0
            )
        grad_logits[at, :] = spread[:, 0:gate_cols]
        wide_block = jnp.zeros((LANES, LANES), F32)
        for j in range(2):
            first, second, weight = const[j]
            d_first, d_second = weight * with_norm, weight * with_vec[j]
            centre = first * d_first + second * d_second
            parts = (first * (d_first - centre), second * (d_second - centre))
            for i in range(2):
                high = parts[i].astype(BF).astype(F32)
                at_high = const_col + 2 * j + i
                spread = jnp.where(lane == at_high, high, spread)
                spread = jnp.where(lane == at_high + 4, parts[i] - high, spread)
            high = on_vec[j].astype(BF).astype(F32)
            wide_block = jnp.where(lane == j, high, wide_block)
            wide_block = jnp.where(lane == 2 + j, on_vec[j] - high, wide_block)
        thin[at, :] = spread.astype(BF)
        wide[at, :] = wide_block.astype(BF)
        grad_norm = (
            dot_nt(thin[at, :], small[...])
            + dot(take_zero + take_one, back_box[1, 0])
            + on_normed * grad
        )
        gain_sum = gain_sum + jnp.sum(grad_norm * hid * scale, axis=0, keepdims=True)
        scaled = gain_two * grad_norm
        grad = (
            grad
            + scale * scaled
            - hid * (scale * scale * scale) * jnp.mean(scaled * hid, axis=1, keepdims=True)
        )
        grad_hidden[at, :] = grad
        grad_attn[at, :] = grad.astype(BF)

    sum_passed(3, 2)

    sums = r["sums"]
    own_sums = r["own_sums"]
    own_sums[...] = jnp.zeros_like(own_sums)
    by_small = dot_tn(thin[...], normed_low[...])
    by_vec = dot_tn(wide[...], grad_sum[...])
    own_sums[0:gate_cols, :] = by_small[0:gate_cols, :]
    own_sums[gate_cols : gate_cols + 4, :] = (
        by_small[const_col : const_col + 4, :] + by_small[const_col + 4 : const_col + 8, :]
    )
    own_sums[gate_cols + 4 : gate_cols + 6, :] = by_vec[0:2, :] + by_vec[2:4, :]
    own_sums[gate_cols + 6 : gate_cols + 7, :] = gain_sum
    mix_rows = SMALL_ROWS - 8
    own_sums[mix_rows : mix_rows + gate_cols, 0:gate_cols] = lax.dot_general(
        r["own_prev_in"][...],
        grad_logits[...],
        (((1,), (0,)), ((), ())),
        precision=lax.Precision.HIGHEST,
        preferred_element_type=F32,
    )
    r["own_prev_out"][...] = lax.dot_general(
        r["own_mix"][...].astype(F32),
        grad_logits[...],
        (((1,), (1,)), ((), ())),
        precision=lax.Precision.HIGHEST,
        preferred_element_type=F32,
    )

    store("block_out").start()
    store("prev_out").start()

    dense, ring = r["dense"], RING
    core_box, y_box, x_box = r["core_box"], r["y_box"], r["x_box"]
    z_box, all_box = r["z_box"], r["all_box"]

    def as_chunk(block):
        return block.reshape(lines, 2, 2, 2, quarter, chunk_cols).astype(BF)

    def core_hop(ch):
        return remote(
            dense.at[ch % ring, :, :, 1 - core],
            core_box.at[ch],
            r["gc_send"].at[ch],
            r["gc_recv"].at[ch],
            (twin, s),
        )

    def y_hop(ch):
        return remote(
            core_box.at[ch, :, :, 1 - half],
            y_box.at[ch],
            r["gy_send"].at[ch],
            r["gy_recv"].at[ch],
            (facing, s),
        )

    def x_hop(ch):
        return remote(
            y_box.at[ch, :, 1 - x],
            x_box.at[ch],
            r["gx_send"].at[ch],
            r["gx_recv"].at[ch],
            (e, across),
        )

    batch = chunks // BATCHES

    def z_hop(group, step, origin):
        zz = (z + step) % lines
        span = pl.ds(group * batch, batch)
        return remote(
            x_box.at[span, zz],
            z_box.at[origin, span],
            r["gz_send"].at[group, step],
            r["gz_recv"].at[group, origin],
            (e, 2 * zz + x),
        )

    def all_hop(group, step, origin):
        span = pl.ds(group * batch, batch)
        return remote(
            all_box.at[e, span],
            all_box.at[origin, span],
            r["ga_send"].at[group, step],
            r["ga_recv"].at[group, origin],
            ((e + step) % experts, s),
        )

    def dense_event(it):
        def stage_of(number):
            ch = it - HOPS[number]
            return ch, (ch >= 0) & (ch < chunks)

        ch0, on0 = stage_of(0)

        @pl.when(on0)
        def _():
            core_hop(ch0).start()

        ch1, on1 = stage_of(1)

        @pl.when(on1)
        def _():
            core_hop(ch1).wait_recv()
            core_box[ch1] = summed(core_box[ch1], dense[ch1 % ring, :, :, core])
            y_hop(ch1).start()
            core_hop(ch1).wait_send()

        ch2, on2 = stage_of(2)

        @pl.when(on2)
        def _():
            y_hop(ch2).wait_recv()
            y_box[ch2] = summed(y_box[ch2], core_box[ch2, :, :, half])
            x_hop(ch2).start()

        ch3, on3 = stage_of(3)

        @pl.when(on3)
        def _():
            x_hop(ch3).wait_recv()
            x_box[ch3] = summed(x_box[ch3], y_box[ch3, :, x])

            @pl.when(ch3 % batch == batch - 1)
            def _():
                for step in range(1, lines):
                    z_hop(ch3 // batch, step, z).start()

    def dense_meet(group):
        span = pl.ds(group * batch, batch)
        total = x_box[span, z].astype(F32)
        for step in range(1, lines):
            origin = (z + lines - step) % lines
            z_hop(group, step, origin).wait_recv()
            total = total + z_box[origin, span].astype(F32)
        all_box[e, span] = total.astype(BF)
        for step in range(1, experts):
            all_hop(group, step, e).start()

    def dense_write(group):
        for step in range(1, experts):
            all_hop(group, step, (e + experts - step) % experts).wait_recv()
        for owner in range(experts):
            place = (owner % 2) * 2 + owner // 2
            at = slice(place * quarter, (place + 1) * quarter)
            for ch in range(group * batch, (group + 1) * batch):
                total = all_box[owner, ch].astype(F32)
                if ch < out_chunks:
                    spot = slice(ch * chunk_cols, (ch + 1) * chunk_cols)
                    r["own_out_w_out"][at, spot] = total
                else:
                    for part in range(3):
                        begin_at = part * D + (ch - out_chunks) * LANES
                        r["own_qkv_out"][at, begin_at : begin_at + LANES] = total[
                            :, part * LANES : (part + 1) * LANES
                        ]

    def dense_events_sent():
        def one(ch, _):
            y_hop(ch).wait_send()
            x_hop(ch).wait_send()
            return 0

        lax.fori_loop(0, chunks, one, 0)
        for group in range(BATCHES):
            for step in range(1, lines):
                z_hop(group, step, z).wait_send()
            for step in range(1, experts):
                all_hop(group, step, e).wait_send()

    grad_normed = ffn.at[tok_rows : 2 * tok_rows, :]
    grad_normed[...] = jnp.zeros_like(grad_normed)
    out_grads = dot_tn(mixed[...], grad_attn[...])
    for ch in range(out_chunks):
        dense[ch] = as_chunk(out_grads[:, ch * chunk_cols : (ch + 1) * chunk_cols])

    def attend_back(p):
        query, key, value = heads[p], heads[pairs + p], heads[2 * pairs + p]
        upper = dot_nt(grad_attn[...], weights[rows(p, LANES), 3 * D : 4 * D]).astype(BF)
        grads = []
        for head in range(2):
            scores = dot_nt(key, one_head(query, head)) * score_scale
            probs = jnp.where(
                allowed_pairs(), jnp.exp(scores - log_sums[p, head : head + 1, :]), 0.0
            )
            grad_probs = dot_nt(value, one_head(upper, head))
            delta = jnp.sum(grad_probs * probs, axis=0, keepdims=True)
            grad_scores = (probs * (grad_probs - delta)).astype(BF)
            grads.append(
                (
                    dot_tn(grad_scores, key),
                    dot(grad_scores, query),
                    dot(probs.astype(BF), upper),
                )
            )
        joined = [jnp.where(first_head, a, b) for a, b in zip(*grads)]
        parts = []
        for part in range(3):
            block = joined[part]
            if part < 2:
                block = block * score_scale
                block = block * cosine[...] - swap_halves(block) * sine[...]
            parts.append(block.astype(BF))
        total = grad_normed[...]
        for part in range(3):
            spot = pl.ds(pl.multiple_of(part * D + p * LANES, LANES), LANES)
            total = total + dot_nt(parts[part], weights[:, spot])
        grad_normed[...] = total
        dense[(out_chunks + p) % ring] = as_chunk(
            dot_tn(normed[...], jnp.concatenate(parts, axis=1))
        )

    def back_step(it, _):
        @pl.when(it >= out_chunks)
        def _():
            attend_back(it - out_chunks)

        dense_event(it)

        @pl.when(it == out_chunks + 3)
        def _():
            sum_passed(5, 1)

        return 0

    def tail_step(it, _):
        dense_event(it)

        return 0

    lax.fori_loop(0, chunks, back_step, 0)

    gain_sum = jnp.zeros((1, D), F32)
    for block in range(row_blocks):
        at = slice(block * LANES, (block + 1) * LANES)
        inputs = tokens[at, :].astype(F32)
        scale = cols[at, 0:1]
        grad_norm = grad_normed[at, :]
        gain_sum = gain_sum + jnp.sum(grad_norm * inputs * scale, axis=0, keepdims=True)
        scaled = gain_one * grad_norm
        r["own_tokens_out"][at, :] = (
            grad_hidden[at, :]
            + scale * scaled
            - inputs * (scale * scale * scale) * jnp.mean(scaled * inputs, axis=1, keepdims=True)
        )
    own_sums[gate_cols + 7 : gate_cols + 8, :] = gain_sum

    store("tokens_out").start()

    layer_sums = r["layer_sums"]

    def final_step(jj, _):
        sum_final(jj)
        return 0

    def sums_z(step, origin):
        return remote(
            sums.at[z],
            sums.at[origin],
            r["az_send"].at[step],
            r["az_recv"].at[origin],
            (e, ((z + step) % lines) * 2 + x),
        )

    def sums_layer(step, side, origin):
        return remote(
            layer_sums.at[mine],
            layer_sums.at[origin],
            r["al_send"].at[step, side],
            r["al_recv"].at[origin],
            ((e + step) % experts, 2 * z + side),
        )

    sums[z] = own_sums[...].astype(BF)
    for step in range(1, lines):
        sums_z(step, z).start()
    lax.fori_loop(chunks, chunks + HOPS[3], tail_step, 0)
    lax.fori_loop(0, lines - 1, final_step, 0)
    for step in range(1, lines):
        sums_z(step, (z + lines - step) % lines).wait_recv()
    total = sums[0].astype(F32)
    for zz in range(1, lines):
        total = total + sums[zz].astype(F32)
    layer_sums[mine] = total
    others(lambda step, other, side, origin: sums_layer(step, side, mine).start())
    sum_passed(6, len(sum_passes))
    for group in range(BATCHES):
        dense_meet(group)
    lax.fori_loop(lines - 1, lines, final_step, 0)
    for group in range(BATCHES):
        dense_write(group)
    others(lambda step, other, side, origin: sums_layer(step, side, origin).wait_recv())
    total = layer_sums[0]
    for other in range(1, layer):
        total = total + layer_sums[other]
    mine_only = pltpu.roll(total, (2 * lines - s) * share % D, 1)[:, 0:share]
    r["own_gate_out"][...] = mine_only[0:gate_cols, :]
    r["own_const_out"][...] = mine_only[gate_cols : gate_cols + 4, :]
    r["own_vec_out"][...] = mine_only[gate_cols + 4 : gate_cols + 6, :]
    r["own_two_out"][...] = mine_only[gate_cols + 6 : gate_cols + 7, :]
    r["own_one_out"][...] = mine_only[gate_cols + 7 : gate_cols + 8, :]
    r["own_mix_out"][...] = total[mix_rows : mix_rows + gate_cols, 0:gate_cols]

    for jj in range(lines):
        final_hop(jj).wait_recv()
        for part in range(2):
            up_out[:, up_columns(part, jj, 1 - x)] = final_box[
                jj, :, part * hidden_block : (part + 1) * hidden_block
            ].astype(F32)

    for name in OUT_NAMES:
        if name not in ("block_out", "prev_out", "tokens_out"):
            store(name).start()

    for kind in range(2):
        dense_sent(kind)
    chain_sent()
    for step in range(1, 2 * lines):
        small_copy(step, s).wait_send()
    for which in range(2):
        others(lambda step, other, side, origin: come(which, other, side, e, x).wait_send())
    sum_sent()
    for jj in range(lines):
        final_hop(jj).wait_send()
    dense_events_sent()
    for step in range(1, lines):
        sums_z(step, z).wait_send()
    others(lambda step, other, side, origin: sums_layer(step, side, mine).wait_send())
    for name in OUT_NAMES:
        store(name).wait()

SMALL_ROWS = 24
IN_NAMES = (
    "length", "tokens", "out_grad", "routes_in", "order_row", "prev_in", "mix",
    "cosine", "sine", "qkv_in", "out_in", "gate_in", "const_in", "vec_in", "one_in", "two_in",
    "up_in", "down_in",
)
LOADED = (
    "qkv_in", "gate_in", "const_in", "vec_in", "one_in", "two_in", "routes_in", "prev_in",
    "order_row", "tokens", "out_in", "down_in", "mix", "cosine", "sine", "out_grad",
)
OUT_NAMES = (
    "block_out", "tokens_out", "prev_out", "qkv_out", "out_w_out", "gate_out", "const_out",
    "vec_out", "one_out", "two_out", "mix_out", "up_out", "down_out",
)


def scratch_list(dims, held):
    tok_rows, experts, lines, share, hidden_block, capacity, gate_cols = dims
    pairs = D // LANES
    chunk_cols = 3 * LANES
    chunks = D // chunk_cols + pairs
    slots = experts * capacity
    gathered = 2 * experts * capacity
    quarter = share // 4
    last = lines - 1
    wide = 2 * hidden_block
    vmem = {
        "weights": ((D, 4 * D), BF),
        "small": ((D, LANES), BF),
        "up": ((lines, D, wide), BF),
        "down": ((lines, hidden_block, D), BF),
        "stage": ((lines, share, wide), BF),
        "put": ((2, slots, tok_rows), BF),
        "take": ((2, tok_rows, slots), BF),
        "rows": ((8, D), F32),
        "cols": ((tok_rows, 16), F32),
        "normed": ((tok_rows, D), BF),
        "heads": ((3 * pairs, tok_rows, LANES), BF),
        "mixed": ((tok_rows, D), BF),
        "log_sums": ((pairs, 8, tok_rows), F32),
        "hidden": ((tok_rows, D), F32),
        "normed_low": ((tok_rows, D), BF),
        "grad_low": ((2 * tok_rows, D), BF),
        "grad_sum": ((tok_rows, D), BF),
        "sent": ((gathered, D), BF),
        "buffer": ((gathered, D), BF),
        "slot_grad": ((gathered, D), BF),
        "up_sum": ((lines, D, wide), BF),
        "down_sum": ((lines, hidden_block, D), BF),
        "up_box": ((2, last, lines, 2 * share, wide), BF),
        "down_box": ((lines + 1, hidden_block, D), BF),
        "final_box": ((lines, share, wide), BF),
        "ffn": ((gathered, D), F32),
        "slot_back": ((gathered, D), F32),
        "act": ((gathered, hidden_block), BF),
        "grad_gu": ((gathered, wide), BF),
        "back_box": ((2, 2, slots, D), BF),
        "grad_attn": ((tok_rows, D), BF),
        "thin": ((tok_rows, LANES), BF),
        "wide": ((tok_rows, LANES), BF),
        "grad_logits": ((tok_rows, gate_cols), F32),
        "sums": ((lines, SMALL_ROWS, D), BF),
        "own_sums": ((SMALL_ROWS, D), F32),
        "layer_sums": ((2 * experts, SMALL_ROWS, D), F32),
        "dense": ((RING, lines, 2, 2, 2, quarter, chunk_cols), BF),
        "core_box": ((chunks, lines, 2, 2, quarter, chunk_cols), BF),
        "y_box": ((chunks, lines, 2, quarter, chunk_cols), BF),
        "x_box": ((chunks, lines, quarter, chunk_cols), BF),
        "z_box": ((lines, chunks, quarter, chunk_cols), BF),
        "all_box": ((experts, chunks, quarter, chunk_cols), BF),
        "pack": ((LANES, LANES), F32),
        "token_rows": ((16, tok_rows), F32),
        "token_cols": ((tok_rows, 16), F32),
    }
    vmem.update(held)
    sems = {
        "in_sem": (len(LOADED),),
        "out_sem": (len(OUT_NAMES),),
        "up_sem": (2, lines, 2),
        "dz_send": (2, 2, last),
        "dx_send": (2, lines),
        "dc_send": (2, lines, 2),
        "d_recv": (2, lines, 2, 2),
        "dy_send": (2, lines, 2),
        "dr_send": (2, lines, 2),
        "dy_recv": (2, lines, 2, 2),
        "sm_send": (2 * lines,),
        "sm_recv": (2 * lines,),
        "ux_send": (lines,),
        "ux_recv": (lines,),
        "ch_send": (1 + PARTS, 2, last, lines),
        "ch_recv": (1 + PARTS, 2, last, lines),
        "go_send": (2, experts, 2),
        "go_recv": (2, 2 * experts),
        "come_send": (2, experts, 2),
        "come_recv": (2, experts, 2),
        "ru_send": (2, last, lines),
        "ru_recv": (2, last, lines),
        "rd_send": (2, lines, PARTS),
        "rd_recv": (2, lines, PARTS),
        "fx_send": (lines,),
        "fx_recv": (lines,),
        "gc_send": (chunks,),
        "gc_recv": (chunks,),
        "gy_send": (chunks,),
        "gy_recv": (chunks,),
        "gx_send": (chunks,),
        "gx_recv": (chunks,),
        "gz_send": (BATCHES, lines),
        "gz_recv": (BATCHES, lines),
        "ga_send": (BATCHES, experts),
        "ga_recv": (BATCHES, experts),
        "az_send": (lines,),
        "az_recv": (lines,),
        "al_send": (experts, 2),
        "al_recv": (2 * experts,),
    }
    names = tuple(vmem) + tuple(sems)
    shapes = [pltpu.VMEM(*spec) for spec in vmem.values()]
    shapes += [pltpu.SemaphoreType.DMA(shape) for shape in sems.values()]
    return names, shapes


def kernel_body(
    tokens,
    seq_lengths,
    routes,
    pair_order,
    prev_logits,
    out_grad,
    qkv_weight,
    out_weight,
    gate_weight,
    const_weight,
    const_vector,
    norm1_gain,
    norm2_gain,
    gate_mix,
    expert_up,
    expert_down,
):
    tok_rows = tokens.shape[0]
    experts = lax.axis_size("expert")
    shards = lax.axis_size("shard")
    share = qkv_weight.shape[0]
    gate_cols = gate_weight.shape[1]
    hidden_block = expert_down.shape[1]
    capacity = 2 * tok_rows // (experts + 4)
    dims = (tok_rows, experts, shards // 2, share, hidden_block, capacity, gate_cols)
    cosine, sine_table = turn_tables(tok_rows)
    args = (
        seq_lengths,
        tokens,
        out_grad,
        routes.T,
        pair_order,
        prev_logits.T,
        gate_mix,
        cosine,
        sine_table,
        qkv_weight,
        out_weight,
        gate_weight.T,
        const_weight.T,
        const_vector.T,
        norm1_gain[None],
        norm2_gain[None],
        expert_up[0],
        expert_down[0],
    )
    results = (
        ((tok_rows, D), BF),
        ((tok_rows, D), F32),
        ((gate_cols, tok_rows), F32),
        ((share, 3 * D), F32),
        ((share, D), F32),
        ((gate_cols, share), F32),
        ((4, share), F32),
        ((2, share), F32),
        ((1, share), F32),
        ((1, share), F32),
        ((gate_cols, gate_cols), F32),
        ((share, 2 * FF), F32),
        ((hidden_block, D), F32),
    )
    held = {
        "own_" + name: (arg.shape, arg.dtype)
        for name, arg in zip(IN_NAMES, args)
        if name in LOADED and name not in ("qkv_in", "out_in", "down_in")
    }
    held.update({"own_" + name: spec for name, spec in zip(OUT_NAMES, results)})
    names, shapes = scratch_list(dims, held)
    anywhere = pl.BlockSpec(memory_space=pl.ANY)
    outs = pl.pallas_call(
        functools.partial(step_kernel, dims, names),
        out_shape=tuple(jax.ShapeDtypeStruct(*spec) for spec in results),
        in_specs=[pl.BlockSpec(memory_space=pltpu.SMEM)] + [anywhere] * (len(args) - 1),
        out_specs=(anywhere,) * len(OUT_NAMES),
        scratch_shapes=shapes,
        compiler_params=pltpu.CompilerParams(
            collective_id=0, has_side_effects=True, vmem_limit_bytes=VMEM_BYTES
        ),
        name="step",
    )(*args)
    (
        block_out,
        tokens_grad,
        prev_grad,
        qkv_grad,
        out_w_grad,
        gate_grad,
        const_grad,
        vec_grad,
        one_grad,
        two_grad,
        mix_grad,
        up_grad,
        down_grad,
    ) = hand_over(outs)
    return (
        block_out,
        tokens_grad,
        prev_grad.T,
        qkv_grad,
        out_w_grad,
        gate_grad.T,
        const_grad.T,
        vec_grad.T,
        one_grad[0],
        two_grad[0],
        mix_grad,
        up_grad[None],
        down_grad[None],
    )


def copy_kernel(count, *refs):
    held = refs[2 * count : 3 * count]
    in_sems, out_sems = refs[3 * count :]
    reads = [pltpu.make_async_copy(refs[i], held[i], in_sems.at[i]) for i in range(count)]
    writes = [
        pltpu.make_async_copy(held[i], refs[count + i], out_sems.at[i]) for i in range(count)
    ]
    for copy in reads:
        copy.start()
    for read, write in zip(reads, writes):
        read.wait()
        write.start()
    for copy in writes:
        copy.wait()


def hand_over(arrays):
    count = len(arrays)
    anywhere = pl.BlockSpec(memory_space=pl.ANY)
    return pl.pallas_call(
        functools.partial(copy_kernel, count),
        out_shape=tuple(jax.ShapeDtypeStruct(a.shape, a.dtype) for a in arrays),
        in_specs=[anywhere] * count,
        out_specs=(anywhere,) * count,
        scratch_shapes=[pltpu.VMEM(a.shape, a.dtype) for a in arrays]
        + [pltpu.SemaphoreType.DMA((count,))] * 2,
        name="hand_over",
    )(*arrays)


def turn_tables(tok_rows):
    half_dim = HEAD_DIM // 2
    steps = np.arange(half_dim, dtype=np.float32) * np.float32(2.0 / HEAD_DIM)
    frequency = np.power(np.float32(rotary_base), -steps).astype(np.float32)
    angles = np.arange(tok_rows, dtype=np.float32)[:, None] * frequency[None, :]
    cosine = np.cos(angles.astype(np.float64)).astype(np.float32)
    sine = np.sin(angles.astype(np.float64)).astype(np.float32)
    cosine = np.tile(cosine, (1, LANES // half_dim))
    sine = np.tile(np.concatenate([-sine, sine], axis=1), (1, LANES // HEAD_DIM))
    return jnp.asarray(cosine), jnp.asarray(sine)


def fits_kernel(mesh):
    experts, shards = mesh.shape["expert"], mesh.shape["shard"]
    share, hidden_block = D // shards, FF // shards
    return (
        experts == 4
        and shards % 2 == 0
        and share % 96 == 0
        and hidden_block % LANES == 0
    )


def solution(mesh):
    placed = (
        P(("expert", "shard"), None),
        P(("expert", "shard")),
        P(("expert", "shard"), None),
        P(("expert", "shard"), None),
        P(("expert", "shard"), None),
        P(("expert", "shard"), None),
        P("shard", None),
        P("shard", None),
        P("shard", None),
        P("shard", None),
        P("shard", None),
        P("shard"),
        P("shard"),
        P(),
        P("expert", "shard", None),
        P("expert", "shard", None),
    )
    return jax.shard_map(
        kernel_body if fits_kernel(mesh) else body,
        mesh=mesh,
        in_specs=placed,
        out_specs=(
            P(("expert", "shard"), None),
            P(("expert", "shard"), None),
            P(("expert", "shard"), None),
            P("shard", None),
            P("shard", None),
            P("shard", None),
            P("shard", None),
            P("shard", None),
            P("shard"),
            P("shard"),
            P(),
            P("expert", "shard", None),
            P("expert", "shard", None),
        ),
        check_vma=False,
    )
```

```python
import functools

import jax
import jax.numpy as jnp
import numpy as np
from jax import lax
from jax.experimental import pallas as pl
from jax.experimental.pallas import tpu as pltpu
from jax.sharding import PartitionSpec as P

D = 768
FF = 2048
HEADS = 12
HEAD_DIM = 64


norm_eps = 1e-06
rotary_base = 10000.0
highest = lax.Precision.HIGHEST


def tables(tok_rows, head_dim):
    half_dim = head_dim // 2
    frequency = rotary_base ** (-(jnp.arange(half_dim, dtype=jnp.float32) * 2.0 / head_dim))
    angles = jnp.arange(tok_rows, dtype=jnp.float32)[:, None] * frequency[None, :]
    return (jnp.cos(angles)[:, None, :], jnp.sin(angles)[:, None, :])


def rotate(field, cosine, sine_table):
    half_dim = field.shape[-1] // 2
    first_half = field[..., :half_dim]
    second_half = field[..., half_dim:]
    return jnp.concatenate(
        [
            first_half * cosine - second_half * sine_table,
            second_half * cosine + first_half * sine_table,
        ],
        axis=-1,
    )


def place_pairs(route_rows, order, length, experts_ffn, capacity):
    tok_rows = route_rows.shape[0]
    token_ids = jnp.arange(tok_rows, dtype=jnp.int32)
    pair_valid = jnp.repeat(token_ids < length, 2)
    expert_flat = route_rows.reshape(-1)
    placed_expert = expert_flat[order]
    placed_live = pair_valid[order] & (placed_expert < experts_ffn)
    one_hot = (
        placed_expert[:, None] == jnp.arange(experts_ffn, dtype=jnp.int32)[None, :]
    ) & placed_live[:, None]
    counts = jnp.cumsum(one_hot.astype(jnp.int32), axis=0)
    slot_index = jnp.sum(jnp.where(one_hot, counts - 1, 0), axis=1)
    kept_pairs = placed_live & (slot_index < capacity)
    dest_placed = jnp.where(
        kept_pairs, placed_expert * capacity + slot_index, experts_ffn * capacity
    )
    pair_dest = jnp.zeros((2 * tok_rows,), jnp.int32).at[order].set(dest_placed)
    slot_pair = (
        jnp.full((experts_ffn * capacity,), 2 * tok_rows, jnp.int32)
        .at[dest_placed]
        .set(order, mode="drop")
    )
    return (pair_dest, slot_pair)


def attend_head(head, allowed, score_scale):
    query, keys_rot, values = head
    scores = jnp.dot(query, keys_rot.T, preferred_element_type=jnp.float32) * score_scale
    scores = jnp.where(allowed, scores, -1e30)
    top_score = jnp.max(scores, axis=1, keepdims=True)
    expo = jnp.exp(scores - top_score)
    total = jnp.sum(expo, axis=1, keepdims=True)
    probs = expo / total
    mixed = jnp.dot(probs.astype(jnp.bfloat16), values, preferred_element_type=jnp.float32).astype(
        jnp.bfloat16
    )
    return (mixed, top_score + jnp.log(total))


def attend_back(head, allowed, score_scale):
    query, keys_rot, values, grad_mixed, log_total = head
    scores = jnp.dot(query, keys_rot.T, preferred_element_type=jnp.float32) * score_scale
    scores = jnp.where(allowed, scores, -1e30)
    probs = jnp.where(allowed, jnp.exp(scores - log_total), 0.0)
    grad_probs = jnp.dot(grad_mixed, values.T, preferred_element_type=jnp.float32)
    delta = jnp.sum(grad_probs * probs, axis=1, keepdims=True)
    grad_scores = (probs * (grad_probs - delta)).astype(jnp.bfloat16)
    grad_query = jnp.dot(grad_scores, keys_rot, preferred_element_type=jnp.float32) * score_scale
    grad_key = jnp.dot(grad_scores.T, query, preferred_element_type=jnp.float32) * score_scale
    grad_value = jnp.dot(
        probs.astype(jnp.bfloat16).T, grad_mixed, preferred_element_type=jnp.float32
    )
    return (grad_query, grad_key, grad_value)


def body(
    tokens,
    seq_lengths,
    routes,
    pair_order,
    prev_logits,
    out_grad,
    qkv_weight,
    out_weight,
    gate_weight,
    const_weight,
    const_vector,
    norm1_gain,
    norm2_gain,
    gate_mix,
    expert_up,
    expert_down,
):
    tok_rows = tokens.shape[0]
    experts_ffn = lax.axis_size("expert")
    capacity = 2 * tok_rows // (experts_ffn + 4)
    length = seq_lengths[0]
    order = pair_order[0]
    score_scale = HEAD_DIM ** (-0.5)
    dense_shards = (
        qkv_weight,
        out_weight,
        gate_weight,
        const_weight,
        const_vector,
        norm1_gain,
        norm2_gain,
    )
    weight_qkv, weight_out, weight_gate, weight_const, vector_const, gain_one, gain_two = (
        lax.all_gather(dense_shards[0], "shard", axis=0, tiled=True),
        lax.all_gather(dense_shards[1], "shard", axis=0, tiled=True),
        lax.all_gather(dense_shards[2], "shard", axis=0, tiled=True),
        lax.all_gather(dense_shards[3], "shard", axis=0, tiled=True),
        lax.all_gather(dense_shards[4], "shard", axis=0, tiled=True),
        lax.all_gather(dense_shards[5], "shard", axis=0, tiled=True),
        lax.all_gather(dense_shards[6], "shard", axis=0, tiled=True),
    )
    weight_up, weight_down = (
        lax.all_gather(expert_up, "shard", axis=1, tiled=True),
        lax.all_gather(expert_down, "shard", axis=1, tiled=True),
    )
    weight_up = weight_up[0]
    weight_down = weight_down[0]
    inputs = tokens.astype(jnp.float32)
    token_ids = jnp.arange(tok_rows, dtype=jnp.int32)
    valid_mask = (token_ids < length).astype(jnp.float32)[:, None]
    gain_first = gain_one.astype(jnp.float32)
    gain_second = gain_two.astype(jnp.float32)
    scale_one = lax.rsqrt(jnp.mean(inputs * inputs, axis=1, keepdims=True) + norm_eps)
    normed = (inputs * scale_one * gain_first).astype(jnp.bfloat16)
    qkv_all = jnp.dot(normed, weight_qkv, preferred_element_type=jnp.float32)
    cosine, sine_table = tables(tok_rows, HEAD_DIM)

    def heads_first(block):
        return jnp.transpose(block, (1, 0, 2)).astype(jnp.bfloat16)

    query = heads_first(
        rotate(qkv_all[:, :D].reshape(tok_rows, HEADS, HEAD_DIM), cosine, sine_table)
    )
    keys_rot = heads_first(
        rotate(qkv_all[:, D : 2 * D].reshape(tok_rows, HEADS, HEAD_DIM), cosine, sine_table)
    )
    values = heads_first(qkv_all[:, 2 * D :].reshape(tok_rows, HEADS, HEAD_DIM))
    allowed = (token_ids[None, :] <= token_ids[:, None]) & (token_ids[None, :] < length)
    mixed_heads, log_totals = lax.map(
        lambda head: attend_head(head, allowed, score_scale), (query, keys_rot, values)
    )
    mixed = jnp.transpose(mixed_heads, (1, 0, 2)).reshape(tok_rows, D)
    hidden = inputs + jnp.dot(mixed, weight_out, preferred_element_type=jnp.float32)
    scale_two = lax.rsqrt(jnp.mean(hidden * hidden, axis=1, keepdims=True) + norm_eps)
    normed_two = hidden * scale_two * gain_second
    normed_low = normed_two.astype(jnp.bfloat16)
    mixer = gate_mix.astype(jnp.float32)
    logits = jnp.dot(normed_low, weight_gate, preferred_element_type=jnp.float32) + jnp.dot(
        prev_logits, mixer, precision=highest
    )
    chosen = jnp.take_along_axis(logits, routes, axis=1)
    gate_exp = jnp.exp(chosen - jnp.max(chosen, axis=1, keepdims=True))
    gates = gate_exp / jnp.sum(gate_exp, axis=1, keepdims=True)
    pair_dest, slot_pair = place_pairs(routes, order, length, experts_ffn, capacity)
    padded = jnp.concatenate([normed_low, jnp.zeros((1, D), jnp.bfloat16)], axis=0)
    send_rows = padded[slot_pair // 2].reshape(experts_ffn, capacity, D)
    received = lax.all_to_all(send_rows, "expert", split_axis=0, concat_axis=0, tiled=True)
    lead_shape = received.shape[:2]
    flat_rows = received.reshape(-1, D)
    gate_up = jnp.dot(flat_rows, weight_up, preferred_element_type=jnp.float32)
    activated = (jax.nn.silu(gate_up[:, :FF]) * gate_up[:, FF:]).astype(jnp.bfloat16)
    expert_out = jnp.dot(activated, weight_down, preferred_element_type=jnp.float32).astype(
        jnp.bfloat16
    )
    received, gate_up, activated, expert_out = (
        received,
        gate_up.reshape(lead_shape + (2 * FF,)),
        activated.reshape(lead_shape + (FF,)),
        expert_out.reshape(received.shape),
    )
    returned = lax.all_to_all(expert_out, "expert", split_axis=0, concat_axis=0, tiled=True)
    returned_pad = jnp.concatenate(
        [returned.reshape(-1, D), jnp.zeros((1, D), jnp.bfloat16)], axis=0
    )
    pair_ffn = returned_pad[pair_dest].astype(jnp.float32).reshape(tok_rows, 2, D)
    vector_float = vector_const.astype(jnp.float32)
    const_logits = jnp.dot(normed_low, weight_const, preferred_element_type=jnp.float32).reshape(
        tok_rows, 2, 2
    )
    const_exp = jnp.exp(const_logits - jnp.max(const_logits, axis=2, keepdims=True))
    coefs = const_exp / jnp.sum(const_exp, axis=2, keepdims=True)
    const_out = (
        coefs[..., 0:1] * normed_two[:, None, :] + coefs[..., 1:2] * vector_float.T[None, :, :]
    )
    const_select = (
        routes[:, :, None] == experts_ffn + 2 + jnp.arange(2, dtype=jnp.int32)[None, None, :]
    ).astype(jnp.float32)
    copy_select = (routes == experts_ffn + 1).astype(jnp.float32)[:, :, None]
    pair_out = (
        pair_ffn
        + copy_select * normed_two[:, None, :]
        + jnp.einsum("tkc,tcd->tkd", const_select, const_out, precision=highest)
    )
    mixture = jnp.sum(gates[:, :, None] * pair_out, axis=1)
    block_out = (valid_mask * (hidden + mixture)).astype(jnp.bfloat16)
    back_dense = (
        lax.all_gather(dense_shards[0], "shard", axis=0, tiled=True),
        lax.all_gather(dense_shards[1], "shard", axis=0, tiled=True),
        lax.all_gather(dense_shards[2], "shard", axis=0, tiled=True),
        lax.all_gather(dense_shards[3], "shard", axis=0, tiled=True),
        lax.all_gather(dense_shards[4], "shard", axis=0, tiled=True),
        lax.all_gather(dense_shards[5], "shard", axis=0, tiled=True),
        lax.all_gather(dense_shards[6], "shard", axis=0, tiled=True),
    )
    back_up, back_down = (
        lax.all_gather(expert_up, "shard", axis=1, tiled=True),
        lax.all_gather(expert_down, "shard", axis=1, tiled=True),
    )
    back_up = back_up[0]
    back_down = back_down[0]
    back_qkv, back_out, back_gate, back_const = (
        back_dense[0],
        back_dense[1],
        back_dense[2],
        back_dense[3],
    )
    grad_rows = out_grad.astype(jnp.float32) * valid_mask
    grad_gates = jnp.sum(grad_rows[:, None, :] * pair_out, axis=2)
    grad_pairs = gates[:, :, None] * grad_rows[:, None, :]
    grad_chosen = gates * (grad_gates - jnp.sum(gates * grad_gates, axis=1, keepdims=True))
    route_hot = (
        routes[:, :, None] == jnp.arange(experts_ffn + 4, dtype=jnp.int32)[None, None, :]
    ).astype(jnp.float32)
    grad_logits = jnp.sum(route_hot * grad_chosen[:, :, None], axis=1)
    prev_grad = jnp.dot(grad_logits, mixer.T, precision=highest)
    mix_term = jnp.dot(prev_logits.T, grad_logits, precision=highest)
    logit_low = grad_logits.astype(jnp.bfloat16)
    gate_term = jnp.dot(normed_low.T, logit_low, preferred_element_type=jnp.float32)
    grad_normed = jnp.dot(logit_low, back_gate.T, preferred_element_type=jnp.float32)
    grad_flat = jnp.concatenate(
        [grad_pairs.reshape(2 * tok_rows, D).astype(jnp.bfloat16), jnp.zeros((1, D), jnp.bfloat16)],
        axis=0,
    )
    grad_send = grad_flat[slot_pair].reshape(experts_ffn, capacity, D)
    grad_recv = lax.all_to_all(grad_send, "expert", split_axis=0, concat_axis=0, tiled=True)
    grad_slots = grad_recv.reshape(-1, D)
    down_term = jnp.dot(activated.reshape(-1, FF).T, grad_slots, preferred_element_type=jnp.float32)
    grad_act = jnp.dot(grad_slots, back_down.T, preferred_element_type=jnp.float32)
    gate_part = gate_up[..., :FF].reshape(-1, FF)
    up_part = gate_up[..., FF:].reshape(-1, FF)
    sigmoid_gate = jax.nn.sigmoid(gate_part)
    grad_gate_up = jnp.concatenate(
        [
            grad_act * up_part * sigmoid_gate * (1.0 + gate_part * (1.0 - sigmoid_gate)),
            grad_act * gate_part * sigmoid_gate,
        ],
        axis=1,
    ).astype(jnp.bfloat16)
    up_term = jnp.dot(received.reshape(-1, D).T, grad_gate_up, preferred_element_type=jnp.float32)
    grad_input = (
        jnp.dot(grad_gate_up, back_up.T, preferred_element_type=jnp.float32)
        .astype(jnp.bfloat16)
        .reshape(received.shape)
    )
    grad_back = lax.all_to_all(grad_input, "expert", split_axis=0, concat_axis=0, tiled=True)
    back_pad = jnp.concatenate([grad_back.reshape(-1, D), jnp.zeros((1, D), jnp.bfloat16)], axis=0)
    grad_normed = grad_normed + jnp.sum(
        back_pad[pair_dest].astype(jnp.float32).reshape(tok_rows, 2, D), axis=1
    )
    grad_normed = grad_normed + jnp.sum(copy_select * grad_pairs, axis=1)
    grad_const_out = jnp.einsum("tkc,tkd->tcd", const_select, grad_pairs, precision=highest)
    grad_first = jnp.sum(grad_const_out * normed_two[:, None, :], axis=2)
    grad_second = jnp.sum(grad_const_out * vector_float.T[None, :, :], axis=2)
    grad_coefs = jnp.stack([grad_first, grad_second], axis=2)
    grad_const_logits = (
        coefs * (grad_coefs - jnp.sum(coefs * grad_coefs, axis=2, keepdims=True))
    ).reshape(tok_rows, 4)
    grad_normed = grad_normed + jnp.sum(coefs[..., 0:1] * grad_const_out, axis=1)
    grad_normed = grad_normed + jnp.dot(
        grad_const_logits, back_const.astype(jnp.float32).T, precision=highest
    )
    vector_term = jnp.einsum("tc,tcd->dc", coefs[..., 1], grad_const_out, precision=highest)
    const_term = jnp.dot(normed_low.astype(jnp.float32).T, grad_const_logits, precision=highest)
    second_gain_term = jnp.sum(grad_normed * hidden * scale_two, axis=0)
    scaled_two = gain_second * grad_normed
    grad_hidden = (
        grad_rows
        + scale_two * scaled_two
        - hidden * scale_two**3 * jnp.mean(scaled_two * hidden, axis=1, keepdims=True)
    )
    grad_attn_low = grad_hidden.astype(jnp.bfloat16)
    out_term = jnp.dot(mixed.T, grad_attn_low, preferred_element_type=jnp.float32)
    grad_mixed = jnp.dot(grad_attn_low, back_out.T, preferred_element_type=jnp.float32).astype(
        jnp.bfloat16
    )
    grad_mixed_heads = jnp.transpose(grad_mixed.reshape(tok_rows, HEADS, HEAD_DIM), (1, 0, 2))
    grad_query, grad_key, grad_value = lax.map(
        lambda head: attend_back(head, allowed, score_scale),
        (query, keys_rot, values, grad_mixed_heads, log_totals),
    )
    grad_query = rotate(jnp.transpose(grad_query, (1, 0, 2)), cosine, -sine_table).reshape(
        tok_rows, D
    )
    grad_key = rotate(jnp.transpose(grad_key, (1, 0, 2)), cosine, -sine_table).reshape(tok_rows, D)
    grad_value = jnp.transpose(grad_value, (1, 0, 2)).reshape(tok_rows, D)
    grad_qkv = jnp.concatenate([grad_query, grad_key, grad_value], axis=1).astype(jnp.bfloat16)
    qkv_term = jnp.dot(normed.T, grad_qkv, preferred_element_type=jnp.float32)
    grad_first_norm = jnp.dot(grad_qkv, back_qkv.T, preferred_element_type=jnp.float32)
    first_gain_term = jnp.sum(grad_first_norm * inputs * scale_one, axis=0)
    scaled_one = gain_first * grad_first_norm
    tokens_grad = (
        grad_hidden
        + scale_one * scaled_one
        - inputs * scale_one**3 * jnp.mean(scaled_one * inputs, axis=1, keepdims=True)
    )
    dense_all = (
        qkv_term,
        out_term,
        gate_term,
        const_term,
        vector_term,
        first_gain_term,
        second_gain_term,
    )
    dense_terms = (
        lax.psum_scatter(dense_all[0], "shard", scatter_dimension=0, tiled=True),
        lax.psum_scatter(dense_all[1], "shard", scatter_dimension=0, tiled=True),
        lax.psum_scatter(dense_all[2], "shard", scatter_dimension=0, tiled=True),
        lax.psum_scatter(dense_all[3], "shard", scatter_dimension=0, tiled=True),
        lax.psum_scatter(dense_all[4], "shard", scatter_dimension=0, tiled=True),
        lax.psum_scatter(dense_all[5], "shard", scatter_dimension=0, tiled=True),
        lax.psum_scatter(dense_all[6], "shard", scatter_dimension=0, tiled=True),
    )
    (
        qkv_grad,
        out_weight_grad,
        gate_grad,
        const_weight_grad,
        const_vector_grad,
        norm1_grad,
        norm2_grad,
    ) = lax.psum(
        (
            dense_terms[0],
            dense_terms[1],
            dense_terms[2],
            dense_terms[3],
            dense_terms[4],
            dense_terms[5],
            dense_terms[6],
        ),
        "expert",
    )
    mix_grad = lax.psum(mix_term, ("expert", "shard"))
    expert_up_grad, expert_down_grad = (
        lax.psum_scatter(up_term[None], "shard", scatter_dimension=1, tiled=True),
        lax.psum_scatter(down_term[None], "shard", scatter_dimension=1, tiled=True),
    )
    return (
        block_out,
        tokens_grad,
        prev_grad,
        qkv_grad,
        out_weight_grad,
        gate_grad,
        const_weight_grad,
        const_vector_grad,
        norm1_grad,
        norm2_grad,
        mix_grad,
        expert_up_grad,
        expert_down_grad,
    )


MESH = pl.DeviceIdType.MESH
BF = jnp.bfloat16
F32 = jnp.float32
LANES = 128
NEG = -1e30
VMEM_BYTES = 64 * 1024 * 1024
RING = 3
HOPS = (0, 1, 3, 5)
PARTS = 2
BATCHES = 2


def dot(a, b):
    return lax.dot_general(a, b, (((1,), (0,)), ((), ())), preferred_element_type=F32)


def dot_nt(a, b):
    return lax.dot_general(a, b, (((1,), (1,)), ((), ())), preferred_element_type=F32)


def dot_tn(a, b):
    return lax.dot_general(a, b, (((0,), (0,)), ((), ())), preferred_element_type=F32)


def iota(shape, dim):
    return lax.broadcasted_iota(jnp.int32, shape, dim)


def remote(src, dst, send_sem, recv_sem, target):
    return pltpu.make_async_remote_copy(
        src_ref=src,
        dst_ref=dst,
        send_sem=send_sem,
        recv_sem=recv_sem,
        device_id=target,
        device_id_type=MESH,
    )


def swap_halves(block):
    half = HEAD_DIM // 2
    width = block.shape[1]
    lower = (iota(block.shape, 1) % HEAD_DIM) < half
    return jnp.where(
        lower, pltpu.roll(block, width - half, 1), pltpu.roll(block, half, 1)
    )


def step_kernel(dims, scratch_names, *refs):
    (tok_rows, experts, lines, share, hidden_block, capacity, gate_cols) = dims
    names = IN_NAMES + OUT_NAMES + scratch_names
    r = dict(zip(names, refs))
    pairs = D // LANES
    layer = 2 * experts
    slots = experts * capacity
    quarter = share // 4
    chunk_cols = 3 * LANES
    out_chunks = D // chunk_cols
    chunks = out_chunks + pairs
    half_ffn = lines * 2 * hidden_block
    const_col = gate_cols
    vec_col = gate_cols + 8
    row_blocks = tok_rows // LANES

    e = lax.axis_index("expert")
    s = lax.axis_index("shard")
    z = s // 2
    x = s % 2
    core = e % 2
    half = e // 2
    facing = 2 * (1 - half) + core
    across = 2 * z + 1 - x
    twin = e + 1 - 2 * core
    mine = 2 * e + x

    def rows(index, size):
        return pl.ds(pl.multiple_of(index * size, size), size)

    weights, small = r["weights"], r["small"]
    up, down, stage = r["up"], r["down"], r["stage"]
    own_rows = rows(s, share)

    def up_columns(part, jj, xx):
        return pl.ds(
            pl.multiple_of(part * FF + hidden_block * (2 * jj + xx), hidden_block), hidden_block
        )

    def up_load(jj, part, to):
        spot = pl.ds(part * hidden_block, hidden_block)
        box = stage.at[jj, :, spot] if to == 0 else up.at[jj, own_rows, spot]
        xx = 1 - x if to == 0 else x
        return pltpu.make_async_copy(
            r["up_in"].at[:, up_columns(part, jj, xx)], box, r["up_sem"].at[to, jj, part]
        )

    direct = {
        "qkv_in": weights.at[own_rows, pl.ds(0, 3 * D)],
        "out_in": weights.at[own_rows, pl.ds(3 * D, D)],
        "down_in": down.at[z],
    }

    def load(name):
        box = direct[name] if name in direct else r["own_" + name]
        return pltpu.make_async_copy(r[name], box, r["in_sem"].at[LOADED.index(name)])

    def store(name):
        held = r["ffn"].at[0:tok_rows, :] if name == "tokens_out" else r["own_" + name]
        return pltpu.make_async_copy(held, r[name], r["out_sem"].at[OUT_NAMES.index(name)])

    load("qkv_in").start()
    for jj in range(lines):
        for part in range(2):
            up_load(jj, part, 0).start()
    for name in LOADED[1:]:
        load(name).start()
    for jj in range(lines):
        for part in range(2):
            up_load(jj, part, 1).start()

    barrier = pltpu.get_barrier_semaphore()
    met = 0
    for step in range(1, 2 * lines):
        pl.semaphore_signal(
            barrier, 1, device_id=(e, (s + step) % (2 * lines)), device_id_type=MESH
        )
        met += 1
    for step in range(1, experts):
        for side in range(2):
            pl.semaphore_signal(
                barrier, 1, device_id=((e + step) % experts, 2 * z + side), device_id_type=MESH
            )
            met += 1
    pl.semaphore_wait(barrier, met)

    def down_part(ref, index, part):
        height = hidden_block // PARTS
        return ref.at[index, pl.ds(part * height, height), :]

    def up_across(jj, origin_x):
        return remote(
            stage.at[jj],
            up.at[jj, rows(2 * z + origin_x, share), :],
            r["ux_send"].at[jj],
            r["ux_recv"].at[jj],
            (e, across),
        )

    def chain(kind, way, step, jj, zz):
        ref = up.at[jj, rows(zz, 2 * share), :] if kind == 0 else down_part(down, jj, kind - 1)
        target = s + 2 if way == 0 else s - 2
        return remote(
            ref,
            ref,
            r["ch_send"].at[kind, way, step, jj],
            r["ch_recv"].at[kind, way, step, jj],
            (e, target),
        )

    def chain_each(way, step, jj, zz, go):
        go(0, way, step, jj, zz)

        @pl.when(zz == jj)
        def _():
            for part in range(PARTS):
                go(1 + part, way, step, jj, zz)

    def begin(*which):
        chain(*which).start()

    def arrive(*which):
        chain(*which).wait_recv()

    def leave(*which):
        chain(*which).wait_send()

    def hand_on(kind, way, step, jj, zz):
        chain(kind, way, step, jj, zz).wait_recv()
        chain(kind, way, step + 1, jj, zz).start()

    def turn(index):
        return (index + 1) % lines

    def chain_ready(jj):
        for part in range(2):
            up_load(jj, part, 1).wait()
        up_across(jj, 1 - x).wait_recv()

    def chain_own(kinds, jj):
        for way, there in ((0, z + 1 < lines), (1, z > 0)):

            @pl.when(there)
            def _():
                for kind in kinds:
                    begin(kind, way, 0, jj, z)

    def chain_pass(index, step):
        @pl.when((z - 1 - step >= 0) & (z + 1 < lines))
        def _():
            chain_each(0, step, turn(index), z - 1 - step, hand_on)

        @pl.when((z + 1 + step < lines) & (z > 0))
        def _():
            chain_each(1, step, turn(index), z + 1 + step, hand_on)

    def chain_end(jj):
        for step in range(lines - 1):

            @pl.when((z - 1 - step >= 0) & (z + 1 == lines))
            def _():
                chain_each(0, step, jj, z - 1 - step, arrive)

            @pl.when((z + 1 + step < lines) & (z == 0))
            def _():
                chain_each(1, step, jj, z + 1 + step, arrive)

    def chain_sent():
        for jj in range(lines):
            for step in range(lines - 1):

                @pl.when((z - step >= 0) & (z + 1 < lines))
                def _():
                    chain_each(0, step, jj, z - step, leave)

                @pl.when((z + step < lines) & (z > 0))
                def _():
                    chain_each(1, step, jj, z + step, leave)

    passes = [(jj, step) for step in range(lines - 2) for jj in range(lines)]

    def chain_events(first, count):
        for number in range(first, min(first + count, len(passes))):
            chain_pass(*passes[number])

    for jj in range(lines):
        for part in range(2):
            up_load(jj, part, 0).wait()
    up_across(1, x).start()

    spans = ((0, 3 * D // 2), (3 * D, D // 2))

    third = share // 3

    def part_of(kind, zz, xx, cc, first, height):
        start, width = spans[kind]
        columns = pl.ds(pl.multiple_of(start + width * cc, LANES), width)
        spot = pl.ds(pl.multiple_of((2 * zz + xx) * share + first, third), height)
        return weights.at[spot, columns]

    def slab(kind, zz, xx, cc):
        return part_of(kind, zz, xx, cc, third * half, 2 * third)

    def dense_z(kind, way, step, zz):
        ref = slab(kind, zz, x, core)
        return remote(
            ref,
            ref,
            r["dz_send"].at[kind, way, step],
            r["d_recv"].at[kind, zz, x, core],
            (e, s + 2 if way == 0 else s - 2),
        )

    def dense_z_each(kind, step, go):
        @pl.when((z - step >= 0) & (z + 1 < lines))
        def _():
            go(dense_z(kind, 0, step, z - step))

        @pl.when((z + step < lines) & (z > 0))
        def _():
            go(dense_z(kind, 1, step, z + step))

    def dense_x(kind, zz):
        ref = slab(kind, zz, x, core)
        return remote(
            ref, ref, r["dx_send"].at[kind, zz], r["d_recv"].at[kind, zz, x, core], (e, across)
        )

    def dense_core(kind, zz, xx):
        ref = slab(kind, zz, xx, core)
        return remote(
            ref,
            ref,
            r["dc_send"].at[kind, zz, xx],
            r["d_recv"].at[kind, zz, xx, core],
            (twin, s),
        )

    def dense_y(kind, zz, xx):
        ref = part_of(kind, zz, xx, core, 2 * third * half, third)
        return remote(
            ref,
            ref,
            r["dy_send"].at[kind, zz, xx],
            r["dy_recv"].at[kind, zz, xx, core],
            (facing, s),
        )

    def rest_core(kind, zz, xx, cc):
        ref = part_of(kind, zz, xx, cc, 2 * third * (1 - half), third)
        return remote(
            ref,
            ref,
            r["dr_send"].at[kind, zz, xx],
            r["dy_recv"].at[kind, zz, xx, cc],
            (twin, s),
        )

    def dense_arrived(kind, zz, xx, cc):
        ref = slab(kind, zz, xx, cc)
        remote(
            ref, ref, r["dx_send"].at[kind, 0], r["d_recv"].at[kind, zz, xx, cc], (e, across)
        ).wait_recv()

    def dense_start(kind):
        dense_z_each(kind, 0, lambda copy: copy.start())
        dense_x(kind, z).start()

    def dense_forward(kind, step):
        for zz, there in ((z - 1 - step, z - 1 - step >= 0), (z + 1 + step, z + 1 + step < lines)):

            @pl.when(there)
            def _():
                dense_arrived(kind, zz, x, core)

                if step + 1 < lines - 1:

                    @pl.when((zz < z) & (z + 1 < lines))
                    def _():
                        dense_z(kind, 0, step + 1, zz).start()

                    @pl.when((zz > z) & (z > 0))
                    def _():
                        dense_z(kind, 1, step + 1, zz).start()

                dense_x(kind, zz).start()
                dense_core(kind, zz, x).start()
                dense_y(kind, zz, x).start()

    def dense_share(kind):
        for step in range(lines):
            zz = (z + lines - step) % lines
            dense_arrived(kind, zz, 1 - x, core)
            dense_core(kind, zz, 1 - x).start()
            dense_y(kind, zz, 1 - x).start()

    def dense_cross(kind):
        for step in range(lines):
            zz = (z + lines - step) % lines
            for xx in (x, 1 - x) if step > 0 else (1 - x,):
                rest_core(kind, zz, xx, core).wait_recv()
                rest_core(kind, zz, xx, core).start()

    def dense_finish(kind):
        for step in range(lines):
            zz = (z + lines - step) % lines
            for xx in (x, 1 - x) if step > 0 else (1 - x,):
                dense_arrived(kind, zz, xx, 1 - core)
                rest_core(kind, zz, xx, 1 - core).wait_recv()

    def dense_sent(kind):
        for step in range(lines - 1):
            dense_z_each(kind, step, lambda copy: copy.wait_send())
        for step in range(lines):
            zz = (z + lines - step) % lines
            dense_x(kind, zz).wait_send()
            for xx in (x, 1 - x) if step > 0 else (1 - x,):
                dense_core(kind, zz, xx).wait_send()
                dense_y(kind, zz, xx).wait_send()
                rest_core(kind, zz, xx, core).wait_send()

    def small_copy(step, origin):
        ref = small.at[rows(origin, share), :]
        return remote(
            ref,
            ref,
            r["sm_send"].at[step],
            r["sm_recv"].at[origin],
            (e, (s + step) % (2 * lines)),
        )

    load("qkv_in").wait()
    dense_start(0)
    for name in LOADED[1:]:
        load(name).wait()
    dense_start(1)
    pack = r["pack"]
    pack[...] = jnp.zeros_like(pack)
    spot = 0
    for name in ("gate_in", "const_in", "const_in", "vec_in", "one_in", "two_in"):
        height = r[name].shape[0]
        pack[spot : spot + height, 0:share] = r["own_" + name][...].astype(F32)
        spot += height
    small[rows(s, share), :] = jnp.transpose(pack[...])[0:share, :].astype(BF)
    for step in range(1, 2 * lines):
        small_copy(step, s).start()
    token_rows, token_cols = r["token_rows"], r["token_cols"]
    token_rows[...] = jnp.zeros_like(token_rows)
    token_rows[0:2, :] = r["own_routes_in"][...].astype(F32)
    token_rows[8 : 8 + gate_cols, :] = r["own_prev_in"][...]
    token_cols[...] = jnp.transpose(token_rows[...])

    tokens = r["own_tokens"]
    cols = r["cols"]
    for block in range(row_blocks):
        at = slice(block * LANES, (block + 1) * LANES)
        inputs = tokens[at, :].astype(F32)
        cols[at, 0:1] = lax.rsqrt(jnp.mean(inputs * inputs, axis=1, keepdims=True) + norm_eps)
    dense_forward(0, 0)

    dense_forward(0, 1)
    dense_forward(1, 0)

    length = r["length"][0]
    pair_ids = iota((2 * tok_rows, 2 * tok_rows), 0)
    pair_names = jnp.where(pair_ids < tok_rows, 2 * pair_ids, 2 * (pair_ids - tok_rows) + 1)
    is_at = jnp.where(pair_names == r["own_order_row"][...], 1.0, 0.0).astype(BF)
    pair_lane = iota((16, 2 * tok_rows), 1)
    pair_token = jnp.where(pair_lane < tok_rows, pair_lane, pair_lane - tok_rows)
    expert_row = iota((16, 2 * tok_rows), 0)
    route_row = jnp.concatenate([token_rows[0:1, :], token_rows[1:2, :]], axis=1)
    live = (expert_row.astype(F32) == route_row) & (expert_row < experts) & (pair_token < length)
    placed = dot(jnp.where(live, 1.0, 0.0).astype(BF), is_at)
    before = jnp.where(
        iota((2 * tok_rows, 2 * tok_rows), 0) <= iota((2 * tok_rows, 2 * tok_rows), 1), 1.0, 0.0
    ).astype(BF)
    counts = dot(placed.astype(BF), before)
    kept = jnp.where((placed > 0.5) & (counts <= capacity + 0.5), counts, 0.0)
    taken = dot_nt(kept.astype(BF), is_at)
    slot_of = jnp.sum(
        jnp.where(taken > 0.5, taken + (expert_row * capacity).astype(F32), 0.0),
        axis=0,
        keepdims=True,
    )
    slot_col = jnp.transpose(jnp.broadcast_to(slot_of, (8, 2 * tok_rows)))
    for step in range(2, lines - 1):
        dense_forward(0, step)
    for step in range(1, lines - 1):
        dense_forward(1, step)
    for index in range(1, lines):
        up_across((index + 1) % lines, x).start()
    chain_ready(1)
    chain_own((0,), 1)
    chain_own(tuple(range(1, 1 + PARTS)), z)
    put, take = r["put"], r["take"]
    for k in range(2):
        span = slice(k * tok_rows, (k + 1) * tok_rows)
        names_down = (iota((slots, tok_rows), 0) + 1).astype(F32)
        put[k] = jnp.where(slot_of[:, span] == names_down, 1.0, 0.0).astype(BF)
        names_right = (iota((tok_rows, slots), 1) + 1).astype(F32)
        take[k] = jnp.where(slot_col[span, 0:1] == names_right, 1.0, 0.0).astype(BF)

    buffer, slot_grad = r["buffer"], r["slot_grad"]
    sent, sent_wide = r["sent"], r["sent_wide"]

    def dispatch(which, step, side, origin):
        target = (e + step) % experts
        box = buffer if which == 0 else slot_grad
        source = sent_wide if which == 0 else sent
        return remote(
            source.at[rows(target, capacity), :],
            box.at[rows(origin, capacity), :],
            r["go_send"].at[which, step, side],
            r["go_recv"].at[which, origin],
            (target, 2 * z + side),
        )

    def dispatch_each(which, step, go):
        for flip in range(2):
            side = x if flip == 0 else 1 - x
            if step > 0 or flip == 1:
                go(dispatch(which, step, side, mine))

    for step in range(experts):
        chosen_rows = rows((e + step) % experts, capacity)
        sent[chosen_rows, :] = dot(
            put[0, chosen_rows, :] + put[1, chosen_rows, :], r["own_out_grad"][...]
        ).astype(BF)
    slot_grad[rows(mine, capacity), :] = sent[rows(e, capacity), :]

    for step in range(1, 2 * lines):
        origin = (s + 2 * lines - step) % (2 * lines)
        small_copy(step, origin).wait_recv()
    pick = jnp.where(iota((8, LANES), 1) == iota((8, LANES), 0) + vec_col, 1.0, 0.0).astype(BF)
    named = dot_nt(pick, small[...])
    r["rows"][...] = named
    gain_one, gain_two = named[2:3, :], named[3:4, :]
    vec_zero, vec_one = named[0:1, :], named[1:2, :]
    normed = r["normed"]
    for block in range(row_blocks):
        at = slice(block * LANES, (block + 1) * LANES)
        inputs = tokens[at, :].astype(F32)
        normed[at, :] = (inputs * cols[at, 0:1] * gain_one).astype(BF)

    dense_share(0)
    dense_cross(0)
    for index in range(1, lines):
        chain_ready((index + 1) % lines)
        chain_own((0,), (index + 1) % lines)
    dense_finish(0)
    for step in range(experts):
        dispatch_each(1, step, lambda copy: copy.start())

    heads = r["heads"]
    cosine, sine = r["own_cosine"], r["own_sine"]

    def project(b, turn):
        wide_block = dot(normed[...], weights[:, rows(b, 2 * LANES)])
        for part in range(2):
            block = wide_block[:, part * LANES : (part + 1) * LANES]
            if turn:
                block = block * cosine[...] + swap_halves(block) * sine[...]
            heads[2 * b + part] = block.astype(BF)

    def rotated(b, _):
        project(b, True)
        return 0

    def plain(b, _):
        project(b, False)
        return 0

    lax.fori_loop(0, pairs, rotated, 0)
    lax.fori_loop(pairs, 3 * pairs // 2, plain, 0)
    chain_events(0, 2)

    score_scale = HEAD_DIM ** (-0.5)
    first_head = iota((tok_rows, LANES), 1) < HEAD_DIM
    mixed, log_sums = r["mixed"], r["log_sums"]

    def allowed_pairs():
        key, query = iota((tok_rows, tok_rows), 0), iota((tok_rows, tok_rows), 1)
        return (key <= query) & (key < length)

    def one_head(block, head):
        keep = first_head if head == 0 else jnp.logical_not(first_head)
        return jnp.where(keep, block, jnp.zeros_like(block))

    def attend(p, _):
        query, key, value = heads[p], heads[pairs + p], heads[2 * pairs + p]
        results = []
        for head in range(2):
            scores = dot_nt(key, one_head(query, head)) * score_scale
            scores = jnp.where(allowed_pairs(), scores, NEG)
            top = jnp.max(scores, axis=0, keepdims=True)
            expo = jnp.exp(scores - top)
            total = jnp.sum(expo, axis=0, keepdims=True)
            probs = expo * (1.0 / total)
            log_sums[p, head : head + 1, :] = top + jnp.log(total)
            results.append(dot_tn(probs.astype(BF), value))
        mixed[:, rows(p, LANES)] = jnp.where(first_head, results[0], results[1]).astype(BF)
        return 0

    lax.fori_loop(0, pairs // 2, attend, 0)
    chain_events(2, 1)
    dense_share(1)
    dense_cross(1)
    lax.fori_loop(pairs // 2, pairs, attend, 0)
    dense_finish(1)
    chain_events(3, 1)

    hidden, normed_low = r["hidden"], r["normed_low"]
    out_grad = r["own_out_grad"]
    mixer = r["own_mix"][...].astype(F32)
    grad_low, grad_sum, gate_parts = r["grad_low"], r["own_out_grad"], r["gate_parts"]
    for block in range(row_blocks):
        at = slice(block * LANES, (block + 1) * LANES)
        hid = tokens[at, :].astype(F32) + dot(mixed[at, :], weights[:, 3 * D : 4 * D])
        hidden[at, :] = hid
        scale = lax.rsqrt(jnp.mean(hid * hid, axis=1, keepdims=True) + norm_eps)
        cols[at, 1:2] = scale
        low = (hid * scale * gain_two).astype(BF)
        normed_low[at, :] = low
        logits = dot(low, small[...])
        lane = iota((LANES, LANES), 1)
        extra = jnp.zeros((LANES, gate_cols), F32)
        for i in range(gate_cols):
            extra = extra + token_cols[at, 8 + i : 9 + i] * mixer[i : i + 1, :]
        routes = token_cols[at, 0:2].astype(jnp.int32)
        chosen = []
        for k in range(2):
            hot = lane == routes[:, k : k + 1]
            part = jnp.sum(jnp.where(hot, logits, 0.0), axis=1, keepdims=True)
            chosen.append(
                part
                + jnp.sum(
                    jnp.where(
                        iota((LANES, gate_cols), 1) == routes[:, k : k + 1], extra, 0.0
                    ),
                    axis=1,
                    keepdims=True,
                )
            )
        top = jnp.maximum(chosen[0], chosen[1])
        powers = [jnp.exp(c - top) for c in chosen]
        total = powers[0] + powers[1]
        gates = [w / total for w in powers]
        on_normed = sum(
            gates[k] * (routes[:, k : k + 1] == experts + 1).astype(F32) for k in range(2)
        )
        for j in range(2):
            first = logits[:, const_col + 2 * j : const_col + 2 * j + 1]
            second = logits[:, const_col + 2 * j + 1 : const_col + 2 * j + 2]
            peak = jnp.maximum(first, second)
            first, second = jnp.exp(first - peak), jnp.exp(second - peak)
            both = first + second
            first, second = first / both, second / both
            weight = sum(
                gates[k] * (routes[:, k : k + 1] == experts + 2 + j).astype(F32)
                for k in range(2)
            )
            on_normed = on_normed + first * weight
            cols[at, 6 + 4 * j : 7 + 4 * j] = first
            cols[at, 7 + 4 * j : 8 + 4 * j] = second
            cols[at, 8 + 4 * j : 9 + 4 * j] = weight
        cols[at, 2:3] = gates[0]
        cols[at, 3:4] = gates[1]
        cols[at, 4:5] = on_normed
        valid = (iota((LANES, 1), 0) + block * LANES < length).astype(F32)
        grad = out_grad[at, :].astype(F32) * valid
        for k in range(2):
            high = gates[k].astype(BF).astype(F32)
            middle = (gates[k] - high).astype(BF).astype(F32)
            parts = jnp.where(lane == 0, high, 0.0)
            parts = jnp.where(lane == 1, middle, parts)
            gate_parts[k, at, :] = jnp.where(lane == 2, gates[k] - high - middle, parts).astype(BF)
        grad_sum[at, :] = grad.astype(BF)


    for step in range(experts):
        chosen_rows = rows((e + step) % experts, capacity)
        put_zero, put_one = put[0, chosen_rows, :], put[1, chosen_rows, :]
        sent_wide[chosen_rows, 0:D] = dot(put_zero + put_one, normed_low[...]).astype(BF)
        sent_wide[chosen_rows, D : D + LANES] = (
            dot(put_zero, gate_parts[0]) + dot(put_one, gate_parts[1])
        ).astype(BF)
        dispatch_each(0, step, lambda copy: copy.start())
    buffer[rows(mine, capacity), :] = sent_wide[rows(e, capacity), :]
    chain_events(4, len(passes))

    def others(go):
        for step in range(experts):
            other = (e + step) % experts
            for flip in range(2):
                side = x if flip == 0 else 1 - x
                if step > 0 or flip == 1:
                    go(step, other, side, 2 * other + side)

    for which in range(2):
        others(lambda step, other, side, origin: dispatch(which, step, side, origin).wait_recv())
    for block in range(2 * experts * capacity // LANES):
        at = slice(block * LANES, (block + 1) * LANES)
        shares = buffer[at, D : D + LANES].astype(F32)
        gate = shares[:, 0:1] + shares[:, 1:2] + shares[:, 2:3]
        slot_grad[at, :] = (gate * slot_grad[at, :].astype(F32)).astype(BF)

    up_sum, down_sum = r["up_sum"], r["down_sum"]
    up_box, down_box = r["up_box"], r["down_box"]
    up_out, down_out = r["own_up_out"], r["own_down_out"]
    final_send, final_box = stage, r["final_box"]
    ffn, slot_back = r["ffn"], r["slot_back"]
    last = lines - 1

    def summed(first, second):
        return (first.astype(F32) + second.astype(F32)).astype(BF)

    def up_rows(jj, zz):
        return up_sum.at[jj, rows(zz, 2 * share), :]

    def up_hop(way, k, jj, dest):
        return remote(
            up_rows(jj, dest),
            up_box.at[way, k, jj],
            r["ru_send"].at[way, k, jj],
            r["ru_recv"].at[way, k, jj],
            (e, s + 2 if way == 0 else s - 2),
        )

    def down_slot(way, jj, zz):
        return jj if way == 0 else jnp.where(jj == zz, lines, jj)

    def down_hop(way, jj, zz, part):
        return remote(
            down_part(down_sum, jj, part),
            down_part(down_box, down_slot(way, jj, zz), part),
            r["rd_send"].at[way, jj, part],
            r["rd_recv"].at[way, jj, part],
            (e, s + 2 if way == 0 else s - 2),
        )

    def final_hop(jj):
        return remote(
            final_send.at[jj],
            final_box.at[jj],
            r["fx_send"].at[jj],
            r["fx_recv"].at[jj],
            (e, across),
        )

    def sum_pass(index, k):
        for way in range(2):
            jj = turn(index)
            place = z if way == 0 else last - z
            dest = last - k + place if way == 0 else k - place

            @pl.when((place >= 1) & (place <= k) & (place < last))
            def _():
                up_hop(way, k - 1, jj, dest).wait_recv()
                spot = rows(dest, 2 * share)
                up_sum[jj, spot, :] = summed(up_sum[jj, spot, :], up_box[way, k - 1, jj])
                up_hop(way, k, jj, dest).start()

                @pl.when(dest == jj)
                def _():
                    for part in range(PARTS):
                        down_hop(way, jj, z, part).wait_recv()
                        own = down_part(down_sum, jj, part)
                        own[...] = summed(
                            own[...], down_part(down_box, down_slot(way, jj, z), part)[...]
                        )
                        down_hop(way, jj, z + 1 - 2 * way, part).start()

    def sum_final(jj):
        total = slot_back.at[0 : 2 * share, 0 : 2 * hidden_block]
        total[...] = up_sum[jj, rows(z, 2 * share), :].astype(F32)
        for way, there in ((0, z > 0), (1, z < last)):

            @pl.when(there)
            def _():
                up_hop(way, last - 1, jj, z).wait_recv()
                total[...] += up_box[way, last - 1, jj].astype(F32)

        final_send[jj] = total[rows(1 - x, share), :].astype(BF)
        final_hop(jj).start()
        own = total[rows(x, share), :]
        for part in range(2):
            up_out[:, up_columns(part, jj, x)] = own[
                :, part * hidden_block : (part + 1) * hidden_block
            ]

        @pl.when(jj == z)
        def _():
            down_out[...] = down_sum[z].astype(F32)
            for way, there in ((0, z > 0), (1, z < last)):

                @pl.when(there)
                def _():
                    for part in range(PARTS):
                        down_hop(way, jj, z, part).wait_recv()
                    down_out[...] += down_box[down_slot(way, jj, z)].astype(F32)

    def sum_start(jj):
        for way in range(2):

            @pl.when(z == (0 if way == 0 else last))
            def _():
                for k in range(last):
                    dest = last - k if way == 0 else k
                    up_hop(way, k, jj, dest).start()

                    @pl.when(dest == jj)
                    def _():
                        for part in range(PARTS):
                            down_hop(way, jj, z + 1 - 2 * way, part).start()

    sum_passes = [(jj, k) for jj in range(lines) for k in range(1, last)]

    def sum_passed(first, count):
        for number in range(first, min(first + count, len(sum_passes))):
            sum_pass(*sum_passes[number])

    def sum_sent():
        for jj in range(lines):
            for way in range(2):
                place = z if way == 0 else last - z
                for k in range(last):
                    dest = last - k + place if way == 0 else k - place

                    @pl.when((place <= k) & (place < last))
                    def _():
                        up_hop(way, k, jj, dest).wait_send()

                        @pl.when(dest == jj)
                        def _():
                            for part in range(PARTS):
                                down_hop(way, jj, z + 1 - 2 * way, part).wait_send()

    for jj in range(lines):
        up_across(jj, x).wait_send()
    act, grad_gu = r["act"], r["grad_gu"]
    back_box = r["back_box"]
    side_rows = 4 * capacity
    for which in range(2):
        for step in range(experts):
            dispatch_each(which, step, lambda copy: copy.wait_send())

    def come(which, target, side, origin_e, origin_x):
        box = grad_low if which == 0 else sent
        return remote(
            box.at[rows(2 * target + side, capacity), :],
            back_box.at[which, origin_x, rows(origin_e, capacity), :],
            r["come_send"].at[which, target, side],
            r["come_recv"].at[which, origin_e, origin_x],
            (target, 2 * z + side),
        )

    def expert_chunk(index, _):
        jj = turn(index)
        chain_end(jj)

        def forward(b, _):
            group = (half + 1 + b) % 2
            at = rows(group, side_rows)
            given = dot(buffer[at, 0:D], up[jj])
            gate, lift = given[:, 0:hidden_block], given[:, hidden_block:]
            squash = 1.0 / (1.0 + jnp.exp(-gate))
            silu = gate * squash
            low = (silu * lift).astype(BF)
            act[at, :] = low
            grad_act = dot_nt(slot_grad[at, :], down[jj])
            grads = jnp.concatenate(
                [grad_act * lift * squash * (1.0 + gate * (1.0 - squash)), grad_act * silu],
                axis=1,
            ).astype(BF)
            grad_gu[at, :] = grads
            forth = dot(low, down[jj])
            back = dot_nt(grads, up[jj])

            @pl.when(index == 0)
            def _():
                ffn[at, :] = forth
                slot_back[at, :] = back

            @pl.when((index > 0) & (index < last))
            def _():
                ffn[at, :] += forth
                slot_back[at, :] += back

            @pl.when(index == last)
            def _():
                grad_low[at, :] = (ffn[at, :] + forth).astype(BF)
                sent[at, :] = (slot_back[at, :] + back).astype(BF)
                for other in range(2):
                    target = 2 * group + other
                    for which in range(2):
                        come(which, target, 1 - x, e, x).start()

                        @pl.when(target != e)
                        def _():
                            come(which, target, x, e, x).start()

            return 0

        lax.fori_loop(0, 2, forward, 0)
        up_sum[jj] = dot_tn(buffer[:, 0:D], grad_gu[...]).astype(BF)
        down_sum[jj] = dot_tn(act[...], slot_grad[...]).astype(BF)
        sum_start(jj)
        return 0

    lax.fori_loop(0, lines, expert_chunk, 0)

    for which in range(2):
        box = grad_low if which == 0 else sent
        back_box[which, x, rows(e, capacity), :] = box[rows(mine, capacity), :]
    sum_passed(0, 3)
    for which in range(2):
        others(
            lambda step, other, side, origin: come(which, other, side, other, side).wait_recv()
        )
    for which in range(2):
        back_box[which, 0] = (
            back_box[which, 0].astype(F32) + back_box[which, 1].astype(F32)
        ).astype(BF)

    named = r["rows"][...]
    gain_one, gain_two = named[2:3, :], named[3:4, :]
    vec_zero, vec_one = named[0:1, :], named[1:2, :]
    grad_hidden, grad_attn = ffn.at[0:tok_rows, :], r["grad_attn"]
    thin, wide = r["thin"], r["wide"]
    grad_logits = r["grad_logits"]
    gain_sum = jnp.zeros((1, D), F32)
    for block in range(row_blocks):
        at = slice(block * LANES, (block + 1) * LANES)
        hid = hidden[at, :]
        scale = cols[at, 1:2]
        norm = hid * scale * gain_two
        grad = grad_sum[at, :].astype(F32)
        take_zero, take_one = take[0, at, :], take[1, at, :]
        outs = [dot(take_zero, back_box[0, 0]), dot(take_one, back_box[0, 0])]
        gates = [cols[at, 2:3], cols[at, 3:4]]
        on_normed = cols[at, 4:5]
        const = [
            (cols[at, 6 + 4 * j : 7 + 4 * j], cols[at, 7 + 4 * j : 8 + 4 * j], cols[at, 8 + 4 * j : 9 + 4 * j])
            for j in range(2)
        ]
        on_vec = [a * w for _, a, w in const]
        valid = (iota((LANES, 1), 0) + block * LANES < length).astype(F32)
        mixture = (
            gates[0] * outs[0]
            + gates[1] * outs[1]
            + on_normed * norm
            + on_vec[0] * vec_zero
            + on_vec[1] * vec_one
        )
        r["own_block_out"][at, :] = (valid * (hid + mixture)).astype(BF)
        routes = token_cols[at, 0:2].astype(jnp.int32)
        with_norm = jnp.sum(grad * norm, axis=1, keepdims=True)
        with_vec = [
            jnp.sum(grad * v, axis=1, keepdims=True) for v in (vec_zero, vec_one)
        ]
        gate_grads = []
        for k in range(2):
            value = jnp.sum(grad * outs[k], axis=1, keepdims=True)
            value = value + (routes[:, k : k + 1] == experts + 1).astype(F32) * with_norm
            for j in range(2):
                hit = (routes[:, k : k + 1] == experts + 2 + j).astype(F32)
                value = value + hit * (const[j][0] * with_norm + const[j][1] * with_vec[j])
            gate_grads.append(value)
        mean = gates[0] * gate_grads[0] + gates[1] * gate_grads[1]
        lane = iota((LANES, LANES), 1)
        spread = jnp.zeros((LANES, LANES), F32)
        for k in range(2):
            spread = spread + jnp.where(
                lane == routes[:, k : k + 1], gates[k] * (gate_grads[k] - mean), 0.0
            )
        grad_logits[at, :] = spread[:, 0:gate_cols]
        wide_block = jnp.zeros((LANES, LANES), F32)
        for j in range(2):
            first, second, weight = const[j]
            d_first, d_second = weight * with_norm, weight * with_vec[j]
            centre = first * d_first + second * d_second
            parts = (first * (d_first - centre), second * (d_second - centre))
            for i in range(2):
                high = parts[i].astype(BF).astype(F32)
                at_high = const_col + 2 * j + i
                spread = jnp.where(lane == at_high, high, spread)
                spread = jnp.where(lane == at_high + 4, parts[i] - high, spread)
            high = on_vec[j].astype(BF).astype(F32)
            wide_block = jnp.where(lane == j, high, wide_block)
            wide_block = jnp.where(lane == 2 + j, on_vec[j] - high, wide_block)
        thin[at, :] = spread.astype(BF)
        wide[at, :] = wide_block.astype(BF)
        grad_norm = (
            dot_nt(thin[at, :], small[...])
            + dot(take_zero + take_one, back_box[1, 0])
            + on_normed * grad
        )
        gain_sum = gain_sum + jnp.sum(grad_norm * hid * scale, axis=0, keepdims=True)
        scaled = gain_two * grad_norm
        grad = (
            grad
            + scale * scaled
            - hid * (scale * scale * scale) * jnp.mean(scaled * hid, axis=1, keepdims=True)
        )
        grad_hidden[at, :] = grad
        grad_attn[at, :] = grad.astype(BF)

    sum_passed(3, 1)

    sums = r["sums"]
    own_sums = r["own_sums"]
    own_sums[...] = jnp.zeros_like(own_sums)
    by_small = dot_tn(thin[...], normed_low[...])
    by_vec = dot_tn(wide[...], grad_sum[...])
    own_sums[0:gate_cols, :] = by_small[0:gate_cols, :]
    own_sums[gate_cols : gate_cols + 4, :] = (
        by_small[const_col : const_col + 4, :] + by_small[const_col + 4 : const_col + 8, :]
    )
    own_sums[gate_cols + 4 : gate_cols + 6, :] = by_vec[0:2, :] + by_vec[2:4, :]
    own_sums[gate_cols + 6 : gate_cols + 7, :] = gain_sum
    mix_rows = SMALL_ROWS - 8
    own_sums[mix_rows : mix_rows + gate_cols, 0:gate_cols] = lax.dot_general(
        r["own_prev_in"][...],
        grad_logits[...],
        (((1,), (0,)), ((), ())),
        precision=lax.Precision.HIGHEST,
        preferred_element_type=F32,
    )
    r["own_prev_out"][...] = lax.dot_general(
        r["own_mix"][...].astype(F32),
        grad_logits[...],
        (((1,), (1,)), ((), ())),
        precision=lax.Precision.HIGHEST,
        preferred_element_type=F32,
    )

    store("block_out").start()
    store("prev_out").start()

    dense, ring = r["dense"], RING
    core_box, y_box, x_box = r["core_box"], r["y_box"], r["x_box"]
    z_box, all_box = r["z_box"], r["all_box"]

    def as_chunk(block):
        return block.reshape(lines, 2, 2, 2, quarter, chunk_cols).astype(BF)

    def core_hop(ch):
        return remote(
            dense.at[ch % ring, :, :, 1 - core],
            core_box.at[ch],
            r["gc_send"].at[ch],
            r["gc_recv"].at[ch],
            (twin, s),
        )

    def y_hop(ch):
        return remote(
            core_box.at[ch, :, :, 1 - half],
            y_box.at[ch],
            r["gy_send"].at[ch],
            r["gy_recv"].at[ch],
            (facing, s),
        )

    def x_hop(ch):
        return remote(
            y_box.at[ch, :, 1 - x],
            x_box.at[ch],
            r["gx_send"].at[ch],
            r["gx_recv"].at[ch],
            (e, across),
        )

    batch = chunks // BATCHES

    def z_hop(group, step, origin):
        zz = (z + step) % lines
        span = pl.ds(group * batch, batch)
        return remote(
            x_box.at[span, zz],
            z_box.at[origin, span],
            r["gz_send"].at[group, step],
            r["gz_recv"].at[group, origin],
            (e, 2 * zz + x),
        )

    def all_hop(group, step, origin):
        span = pl.ds(group * batch, batch)
        return remote(
            all_box.at[e, span],
            all_box.at[origin, span],
            r["ga_send"].at[group, step],
            r["ga_recv"].at[group, origin],
            ((e + step) % experts, s),
        )

    def dense_event(it):
        def stage_of(number):
            ch = it - HOPS[number]
            return ch, (ch >= 0) & (ch < chunks)

        ch0, on0 = stage_of(0)

        @pl.when(on0)
        def _():
            core_hop(ch0).start()

        ch1, on1 = stage_of(1)

        @pl.when(on1)
        def _():
            core_hop(ch1).wait_recv()
            core_box[ch1] = summed(core_box[ch1], dense[ch1 % ring, :, :, core])
            y_hop(ch1).start()
            core_hop(ch1).wait_send()

        ch2, on2 = stage_of(2)

        @pl.when(on2)
        def _():
            y_hop(ch2).wait_recv()
            y_box[ch2] = summed(y_box[ch2], core_box[ch2, :, :, half])
            x_hop(ch2).start()

        ch3, on3 = stage_of(3)

        @pl.when(on3)
        def _():
            x_hop(ch3).wait_recv()
            x_box[ch3] = summed(x_box[ch3], y_box[ch3, :, x])

            @pl.when(ch3 % batch == batch - 1)
            def _():
                for step in range(1, lines):
                    z_hop(ch3 // batch, step, z).start()

    def dense_meet(group):
        span = pl.ds(group * batch, batch)
        total = x_box[span, z].astype(F32)
        for step in range(1, lines):
            origin = (z + lines - step) % lines
            z_hop(group, step, origin).wait_recv()
            total = total + z_box[origin, span].astype(F32)
        all_box[e, span] = total.astype(BF)
        for step in range(1, experts):
            all_hop(group, step, e).start()

    def dense_write(group):
        for step in range(1, experts):
            all_hop(group, step, (e + experts - step) % experts).wait_recv()
        for owner in range(experts):
            place = (owner % 2) * 2 + owner // 2
            at = slice(place * quarter, (place + 1) * quarter)
            for ch in range(group * batch, (group + 1) * batch):
                total = all_box[owner, ch].astype(F32)
                if ch < out_chunks:
                    spot = slice(ch * chunk_cols, (ch + 1) * chunk_cols)
                    r["own_out_w_out"][at, spot] = total
                else:
                    for part in range(3):
                        begin_at = part * D + (ch - out_chunks) * LANES
                        r["own_qkv_out"][at, begin_at : begin_at + LANES] = total[
                            :, part * LANES : (part + 1) * LANES
                        ]

    def dense_events_sent():
        def one(ch, _):
            y_hop(ch).wait_send()
            x_hop(ch).wait_send()
            return 0

        lax.fori_loop(0, chunks, one, 0)
        for group in range(BATCHES):
            for step in range(1, lines):
                z_hop(group, step, z).wait_send()
            for step in range(1, experts):
                all_hop(group, step, e).wait_send()

    grad_normed = ffn.at[tok_rows : 2 * tok_rows, :]
    grad_normed[...] = jnp.zeros_like(grad_normed)
    out_grads = dot_tn(mixed[...], grad_attn[...])
    for ch in range(out_chunks):
        dense[ch] = as_chunk(out_grads[:, ch * chunk_cols : (ch + 1) * chunk_cols])

    def attend_back(p):
        query, key, value = heads[p], heads[pairs + p], heads[2 * pairs + p]
        upper = dot_nt(grad_attn[...], weights[rows(p, LANES), 3 * D : 4 * D]).astype(BF)
        grads = []
        for head in range(2):
            scores = dot_nt(key, one_head(query, head)) * score_scale
            probs = jnp.where(
                allowed_pairs(), jnp.exp(scores - log_sums[p, head : head + 1, :]), 0.0
            )
            grad_probs = dot_nt(value, one_head(upper, head))
            delta = jnp.sum(grad_probs * probs, axis=0, keepdims=True)
            grad_scores = (probs * (grad_probs - delta)).astype(BF)
            grads.append(
                (
                    dot_tn(grad_scores, key),
                    dot(grad_scores, query),
                    dot(probs.astype(BF), upper),
                )
            )
        joined = [jnp.where(first_head, a, b) for a, b in zip(*grads)]
        parts = []
        for part in range(3):
            block = joined[part]
            if part < 2:
                block = block * score_scale
                block = block * cosine[...] - swap_halves(block) * sine[...]
            parts.append(block.astype(BF))
        total = grad_normed[...]
        for part in range(3):
            spot = pl.ds(pl.multiple_of(part * D + p * LANES, LANES), LANES)
            total = total + dot_nt(parts[part], weights[:, spot])
        grad_normed[...] = total
        dense[(out_chunks + p) % ring] = as_chunk(
            dot_tn(normed[...], jnp.concatenate(parts, axis=1))
        )

    def back_step(it, _):
        @pl.when(it >= out_chunks)
        def _():
            attend_back(it - out_chunks)

        dense_event(it)

        @pl.when(it == out_chunks + 2)
        def _():
            sum_passed(4, 1)

        @pl.when(it == out_chunks + 5)
        def _():
            sum_passed(5, 1)

        return 0

    def tail_step(it, _):
        dense_event(it)

        return 0

    lax.fori_loop(0, chunks, back_step, 0)

    gain_sum = jnp.zeros((1, D), F32)
    for block in range(row_blocks):
        at = slice(block * LANES, (block + 1) * LANES)
        inputs = tokens[at, :].astype(F32)
        scale = cols[at, 0:1]
        grad_norm = grad_normed[at, :]
        gain_sum = gain_sum + jnp.sum(grad_norm * inputs * scale, axis=0, keepdims=True)
        scaled = gain_one * grad_norm
        grad_hidden[at, :] = (
            grad_hidden[at, :]
            + scale * scaled
            - inputs * (scale * scale * scale) * jnp.mean(scaled * inputs, axis=1, keepdims=True)
        )
    own_sums[gate_cols + 7 : gate_cols + 8, :] = gain_sum

    store("tokens_out").start()

    layer_sums = r["layer_sums"]

    def final_step(index, _):
        sum_final(turn(index))
        return 0

    def sums_z(step, origin):
        return remote(
            sums.at[z],
            sums.at[origin],
            r["az_send"].at[step],
            r["az_recv"].at[origin],
            (e, ((z + step) % lines) * 2 + x),
        )

    def sums_layer(step, side, origin):
        return remote(
            layer_sums.at[mine],
            layer_sums.at[origin],
            r["al_send"].at[step, side],
            r["al_recv"].at[origin],
            ((e + step) % experts, 2 * z + side),
        )

    sums[z] = own_sums[...].astype(BF)
    for step in range(1, lines):
        sums_z(step, z).start()
    lax.fori_loop(chunks, chunks + HOPS[3], tail_step, 0)
    lax.fori_loop(0, lines - 1, final_step, 0)
    for step in range(1, lines):
        sums_z(step, (z + lines - step) % lines).wait_recv()
    total = sums[0].astype(F32)
    for zz in range(1, lines):
        total = total + sums[zz].astype(F32)
    layer_sums[mine] = total
    others(lambda step, other, side, origin: sums_layer(step, side, mine).start())
    sum_passed(6, len(sum_passes))
    for group in range(BATCHES):
        dense_meet(group)
    final_step(lines - 1, 0)
    for group in range(BATCHES):
        dense_write(group)
    others(lambda step, other, side, origin: sums_layer(step, side, origin).wait_recv())
    total = layer_sums[0]
    for other in range(1, layer):
        total = total + layer_sums[other]
    mine_only = pltpu.roll(total, (2 * lines - s) * share % D, 1)[:, 0:share]
    r["own_gate_out"][...] = mine_only[0:gate_cols, :]
    r["own_const_out"][...] = mine_only[gate_cols : gate_cols + 4, :]
    r["own_vec_out"][...] = mine_only[gate_cols + 4 : gate_cols + 6, :]
    r["own_two_out"][...] = mine_only[gate_cols + 6 : gate_cols + 7, :]
    r["own_one_out"][...] = mine_only[gate_cols + 7 : gate_cols + 8, :]
    r["own_mix_out"][...] = total[mix_rows : mix_rows + gate_cols, 0:gate_cols]

    for jj in range(lines):
        final_hop(jj).wait_recv()
        for part in range(2):
            up_out[:, up_columns(part, jj, 1 - x)] = final_box[
                jj, :, part * hidden_block : (part + 1) * hidden_block
            ].astype(F32)

    for name in OUT_NAMES:
        if name not in ("block_out", "prev_out", "tokens_out"):
            store(name).start()

    for kind in range(2):
        dense_sent(kind)
    chain_sent()
    for step in range(1, 2 * lines):
        small_copy(step, s).wait_send()
    for which in range(2):
        others(lambda step, other, side, origin: come(which, other, side, e, x).wait_send())
    sum_sent()
    for jj in range(lines):
        final_hop(jj).wait_send()
    dense_events_sent()
    for step in range(1, lines):
        sums_z(step, z).wait_send()
    others(lambda step, other, side, origin: sums_layer(step, side, mine).wait_send())
    for name in OUT_NAMES:
        store(name).wait()

SMALL_ROWS = 24
IN_NAMES = (
    "length", "tokens", "out_grad", "routes_in", "order_row", "prev_in", "mix",
    "cosine", "sine", "qkv_in", "out_in", "gate_in", "const_in", "vec_in", "one_in", "two_in",
    "up_in", "down_in",
)
LOADED = (
    "qkv_in", "gate_in", "const_in", "vec_in", "one_in", "two_in", "routes_in", "prev_in",
    "order_row", "tokens", "out_in", "down_in", "mix", "cosine", "sine", "out_grad",
)
OUT_NAMES = (
    "block_out", "tokens_out", "prev_out", "qkv_out", "out_w_out", "gate_out", "const_out",
    "vec_out", "one_out", "two_out", "mix_out", "up_out", "down_out",
)


def scratch_list(dims, held):
    tok_rows, experts, lines, share, hidden_block, capacity, gate_cols = dims
    pairs = D // LANES
    chunk_cols = 3 * LANES
    chunks = D // chunk_cols + pairs
    slots = experts * capacity
    gathered = 2 * experts * capacity
    quarter = share // 4
    last = lines - 1
    wide = 2 * hidden_block
    vmem = {
        "weights": ((D, 4 * D), BF),
        "small": ((D, LANES), BF),
        "up": ((lines, D, wide), BF),
        "down": ((lines, hidden_block, D), BF),
        "stage": ((lines, share, wide), BF),
        "put": ((2, slots, tok_rows), BF),
        "take": ((2, tok_rows, slots), BF),
        "rows": ((8, D), F32),
        "cols": ((tok_rows, 16), F32),
        "normed": ((tok_rows, D), BF),
        "heads": ((3 * pairs, tok_rows, LANES), BF),
        "mixed": ((tok_rows, D), BF),
        "log_sums": ((pairs, 8, tok_rows), F32),
        "hidden": ((tok_rows, D), F32),
        "normed_low": ((tok_rows, D), BF),
        "grad_low": ((2 * tok_rows, D), BF),
        "sent": ((gathered, D), BF),
        "sent_wide": ((slots, D + LANES), BF),
        "gate_parts": ((2, tok_rows, LANES), BF),
        "buffer": ((gathered, D + LANES), BF),
        "slot_grad": ((gathered, D), BF),
        "up_sum": ((lines, D, wide), BF),
        "down_sum": ((lines, hidden_block, D), BF),
        "up_box": ((2, last, lines, 2 * share, wide), BF),
        "down_box": ((lines + 1, hidden_block, D), BF),
        "final_box": ((lines, share, wide), BF),
        "ffn": ((gathered, D), F32),
        "slot_back": ((gathered, D), F32),
        "act": ((gathered, hidden_block), BF),
        "grad_gu": ((gathered, wide), BF),
        "back_box": ((2, 2, slots, D), BF),
        "grad_attn": ((tok_rows, D), BF),
        "thin": ((tok_rows, LANES), BF),
        "wide": ((tok_rows, LANES), BF),
        "grad_logits": ((tok_rows, gate_cols), F32),
        "sums": ((lines, SMALL_ROWS, D), BF),
        "own_sums": ((SMALL_ROWS, D), F32),
        "layer_sums": ((2 * experts, SMALL_ROWS, D), F32),
        "dense": ((RING, lines, 2, 2, 2, quarter, chunk_cols), BF),
        "core_box": ((chunks, lines, 2, 2, quarter, chunk_cols), BF),
        "y_box": ((chunks, lines, 2, quarter, chunk_cols), BF),
        "x_box": ((chunks, lines, quarter, chunk_cols), BF),
        "z_box": ((lines, chunks, quarter, chunk_cols), BF),
        "all_box": ((experts, chunks, quarter, chunk_cols), BF),
        "pack": ((LANES, LANES), F32),
        "token_rows": ((16, tok_rows), F32),
        "token_cols": ((tok_rows, 16), F32),
    }
    vmem.update(held)
    sems = {
        "in_sem": (len(LOADED),),
        "out_sem": (len(OUT_NAMES),),
        "up_sem": (2, lines, 2),
        "dz_send": (2, 2, last),
        "dx_send": (2, lines),
        "dc_send": (2, lines, 2),
        "d_recv": (2, lines, 2, 2),
        "dy_send": (2, lines, 2),
        "dr_send": (2, lines, 2),
        "dy_recv": (2, lines, 2, 2),
        "sm_send": (2 * lines,),
        "sm_recv": (2 * lines,),
        "ux_send": (lines,),
        "ux_recv": (lines,),
        "ch_send": (1 + PARTS, 2, last, lines),
        "ch_recv": (1 + PARTS, 2, last, lines),
        "go_send": (2, experts, 2),
        "go_recv": (2, 2 * experts),
        "come_send": (2, experts, 2),
        "come_recv": (2, experts, 2),
        "ru_send": (2, last, lines),
        "ru_recv": (2, last, lines),
        "rd_send": (2, lines, PARTS),
        "rd_recv": (2, lines, PARTS),
        "fx_send": (lines,),
        "fx_recv": (lines,),
        "gc_send": (chunks,),
        "gc_recv": (chunks,),
        "gy_send": (chunks,),
        "gy_recv": (chunks,),
        "gx_send": (chunks,),
        "gx_recv": (chunks,),
        "gz_send": (BATCHES, lines),
        "gz_recv": (BATCHES, lines),
        "ga_send": (BATCHES, experts),
        "ga_recv": (BATCHES, experts),
        "az_send": (lines,),
        "az_recv": (lines,),
        "al_send": (experts, 2),
        "al_recv": (2 * experts,),
    }
    names = tuple(vmem) + tuple(sems)
    shapes = [pltpu.VMEM(*spec) for spec in vmem.values()]
    shapes += [pltpu.SemaphoreType.DMA(shape) for shape in sems.values()]
    return names, shapes


def kernel_body(
    tokens,
    seq_lengths,
    routes,
    pair_order,
    prev_logits,
    out_grad,
    qkv_weight,
    out_weight,
    gate_weight,
    const_weight,
    const_vector,
    norm1_gain,
    norm2_gain,
    gate_mix,
    expert_up,
    expert_down,
):
    tok_rows = tokens.shape[0]
    experts = lax.axis_size("expert")
    shards = lax.axis_size("shard")
    share = qkv_weight.shape[0]
    gate_cols = gate_weight.shape[1]
    hidden_block = expert_down.shape[1]
    capacity = 2 * tok_rows // (experts + 4)
    dims = (tok_rows, experts, shards // 2, share, hidden_block, capacity, gate_cols)
    cosine, sine_table = turn_tables(tok_rows)
    args = (
        seq_lengths,
        tokens,
        out_grad,
        routes.T,
        pair_order,
        prev_logits.T,
        gate_mix,
        cosine,
        sine_table,
        qkv_weight,
        out_weight,
        gate_weight.T,
        const_weight.T,
        const_vector.T,
        norm1_gain[None],
        norm2_gain[None],
        expert_up[0],
        expert_down[0],
    )
    results = (
        ((tok_rows, D), BF),
        ((tok_rows, D), F32),
        ((gate_cols, tok_rows), F32),
        ((share, 3 * D), F32),
        ((share, D), F32),
        ((gate_cols, share), F32),
        ((4, share), F32),
        ((2, share), F32),
        ((1, share), F32),
        ((1, share), F32),
        ((gate_cols, gate_cols), F32),
        ((share, 2 * FF), F32),
        ((hidden_block, D), F32),
    )
    held = {
        "own_" + name: (arg.shape, arg.dtype)
        for name, arg in zip(IN_NAMES, args)
        if name in LOADED and name not in ("qkv_in", "out_in", "down_in")
    }
    held.update(
        {"own_" + name: spec for name, spec in zip(OUT_NAMES, results) if name != "tokens_out"}
    )
    names, shapes = scratch_list(dims, held)
    anywhere = pl.BlockSpec(memory_space=pl.ANY)
    outs = pl.pallas_call(
        functools.partial(step_kernel, dims, names),
        out_shape=tuple(jax.ShapeDtypeStruct(*spec) for spec in results),
        in_specs=[pl.BlockSpec(memory_space=pltpu.SMEM)] + [anywhere] * (len(args) - 1),
        out_specs=(anywhere,) * len(OUT_NAMES),
        scratch_shapes=shapes,
        compiler_params=pltpu.CompilerParams(
            collective_id=0, has_side_effects=True, vmem_limit_bytes=VMEM_BYTES
        ),
        name="step",
    )(*args)
    (
        block_out,
        tokens_grad,
        prev_grad,
        qkv_grad,
        out_w_grad,
        gate_grad,
        const_grad,
        vec_grad,
        one_grad,
        two_grad,
        mix_grad,
        up_grad,
        down_grad,
    ) = hand_over(outs)
    return (
        block_out,
        tokens_grad,
        prev_grad.T,
        qkv_grad,
        out_w_grad,
        gate_grad.T,
        const_grad.T,
        vec_grad.T,
        one_grad[0],
        two_grad[0],
        mix_grad,
        up_grad[None],
        down_grad[None],
    )


def copy_kernel(count, *refs):
    held = refs[2 * count : 3 * count]
    in_sems, out_sems = refs[3 * count :]
    reads = [pltpu.make_async_copy(refs[i], held[i], in_sems.at[i]) for i in range(count)]
    writes = [
        pltpu.make_async_copy(held[i], refs[count + i], out_sems.at[i]) for i in range(count)
    ]
    for copy in reads:
        copy.start()
    for read, write in zip(reads, writes):
        read.wait()
        write.start()
    for copy in writes:
        copy.wait()


def hand_over(arrays):
    count = len(arrays)
    anywhere = pl.BlockSpec(memory_space=pl.ANY)
    return pl.pallas_call(
        functools.partial(copy_kernel, count),
        out_shape=tuple(jax.ShapeDtypeStruct(a.shape, a.dtype) for a in arrays),
        in_specs=[anywhere] * count,
        out_specs=(anywhere,) * count,
        scratch_shapes=[pltpu.VMEM(a.shape, a.dtype) for a in arrays]
        + [pltpu.SemaphoreType.DMA((count,))] * 2,
        name="hand_over",
    )(*arrays)


def turn_tables(tok_rows):
    half_dim = HEAD_DIM // 2
    steps = np.arange(half_dim, dtype=np.float32) * np.float32(2.0 / HEAD_DIM)
    frequency = np.power(np.float32(rotary_base), -steps).astype(np.float32)
    angles = np.arange(tok_rows, dtype=np.float32)[:, None] * frequency[None, :]
    cosine = np.cos(angles.astype(np.float64)).astype(np.float32)
    sine = np.sin(angles.astype(np.float64)).astype(np.float32)
    cosine = np.tile(cosine, (1, LANES // half_dim))
    sine = np.tile(np.concatenate([-sine, sine], axis=1), (1, LANES // HEAD_DIM))
    return jnp.asarray(cosine), jnp.asarray(sine)


def fits_kernel(mesh):
    experts, shards = mesh.shape["expert"], mesh.shape["shard"]
    share, hidden_block = D // shards, FF // shards
    return (
        experts == 4
        and shards % 2 == 0
        and share % 96 == 0
        and hidden_block % LANES == 0
    )


def solution(mesh):
    placed = (
        P(("expert", "shard"), None),
        P(("expert", "shard")),
        P(("expert", "shard"), None),
        P(("expert", "shard"), None),
        P(("expert", "shard"), None),
        P(("expert", "shard"), None),
        P("shard", None),
        P("shard", None),
        P("shard", None),
        P("shard", None),
        P("shard", None),
        P("shard"),
        P("shard"),
        P(),
        P("expert", "shard", None),
        P("expert", "shard", None),
    )
    return jax.shard_map(
        kernel_body if fits_kernel(mesh) else body,
        mesh=mesh,
        in_specs=placed,
        out_specs=(
            P(("expert", "shard"), None),
            P(("expert", "shard"), None),
            P(("expert", "shard"), None),
            P("shard", None),
            P("shard", None),
            P("shard", None),
            P("shard", None),
            P("shard", None),
            P("shard"),
            P("shard"),
            P(),
            P("expert", "shard", None),
            P("expert", "shard", None),
        ),
        check_vma=False,
    )
```

```python
import functools

import jax
import jax.numpy as jnp
import numpy as np
from jax import lax
from jax.experimental import pallas as pl
from jax.experimental.pallas import tpu as pltpu
from jax.sharding import PartitionSpec as P

D = 768
FF = 2048
HEADS = 12
HEAD_DIM = 64


norm_eps = 1e-06
rotary_base = 10000.0
highest = lax.Precision.HIGHEST


def tables(tok_rows, head_dim):
    half_dim = head_dim // 2
    frequency = rotary_base ** (-(jnp.arange(half_dim, dtype=jnp.float32) * 2.0 / head_dim))
    angles = jnp.arange(tok_rows, dtype=jnp.float32)[:, None] * frequency[None, :]
    return (jnp.cos(angles)[:, None, :], jnp.sin(angles)[:, None, :])


def rotate(field, cosine, sine_table):
    half_dim = field.shape[-1] // 2
    first_half = field[..., :half_dim]
    second_half = field[..., half_dim:]
    return jnp.concatenate(
        [
            first_half * cosine - second_half * sine_table,
            second_half * cosine + first_half * sine_table,
        ],
        axis=-1,
    )


def place_pairs(route_rows, order, length, experts_ffn, capacity):
    tok_rows = route_rows.shape[0]
    token_ids = jnp.arange(tok_rows, dtype=jnp.int32)
    pair_valid = jnp.repeat(token_ids < length, 2)
    expert_flat = route_rows.reshape(-1)
    placed_expert = expert_flat[order]
    placed_live = pair_valid[order] & (placed_expert < experts_ffn)
    one_hot = (
        placed_expert[:, None] == jnp.arange(experts_ffn, dtype=jnp.int32)[None, :]
    ) & placed_live[:, None]
    counts = jnp.cumsum(one_hot.astype(jnp.int32), axis=0)
    slot_index = jnp.sum(jnp.where(one_hot, counts - 1, 0), axis=1)
    kept_pairs = placed_live & (slot_index < capacity)
    dest_placed = jnp.where(
        kept_pairs, placed_expert * capacity + slot_index, experts_ffn * capacity
    )
    pair_dest = jnp.zeros((2 * tok_rows,), jnp.int32).at[order].set(dest_placed)
    slot_pair = (
        jnp.full((experts_ffn * capacity,), 2 * tok_rows, jnp.int32)
        .at[dest_placed]
        .set(order, mode="drop")
    )
    return (pair_dest, slot_pair)


def attend_head(head, allowed, score_scale):
    query, keys_rot, values = head
    scores = jnp.dot(query, keys_rot.T, preferred_element_type=jnp.float32) * score_scale
    scores = jnp.where(allowed, scores, -1e30)
    top_score = jnp.max(scores, axis=1, keepdims=True)
    expo = jnp.exp(scores - top_score)
    total = jnp.sum(expo, axis=1, keepdims=True)
    probs = expo / total
    mixed = jnp.dot(probs.astype(jnp.bfloat16), values, preferred_element_type=jnp.float32).astype(
        jnp.bfloat16
    )
    return (mixed, top_score + jnp.log(total))


def attend_back(head, allowed, score_scale):
    query, keys_rot, values, grad_mixed, log_total = head
    scores = jnp.dot(query, keys_rot.T, preferred_element_type=jnp.float32) * score_scale
    scores = jnp.where(allowed, scores, -1e30)
    probs = jnp.where(allowed, jnp.exp(scores - log_total), 0.0)
    grad_probs = jnp.dot(grad_mixed, values.T, preferred_element_type=jnp.float32)
    delta = jnp.sum(grad_probs * probs, axis=1, keepdims=True)
    grad_scores = (probs * (grad_probs - delta)).astype(jnp.bfloat16)
    grad_query = jnp.dot(grad_scores, keys_rot, preferred_element_type=jnp.float32) * score_scale
    grad_key = jnp.dot(grad_scores.T, query, preferred_element_type=jnp.float32) * score_scale
    grad_value = jnp.dot(
        probs.astype(jnp.bfloat16).T, grad_mixed, preferred_element_type=jnp.float32
    )
    return (grad_query, grad_key, grad_value)


def body(
    tokens,
    seq_lengths,
    routes,
    pair_order,
    prev_logits,
    out_grad,
    qkv_weight,
    out_weight,
    gate_weight,
    const_weight,
    const_vector,
    norm1_gain,
    norm2_gain,
    gate_mix,
    expert_up,
    expert_down,
):
    tok_rows = tokens.shape[0]
    experts_ffn = lax.axis_size("expert")
    capacity = 2 * tok_rows // (experts_ffn + 4)
    length = seq_lengths[0]
    order = pair_order[0]
    score_scale = HEAD_DIM ** (-0.5)
    dense_shards = (
        qkv_weight,
        out_weight,
        gate_weight,
        const_weight,
        const_vector,
        norm1_gain,
        norm2_gain,
    )
    weight_qkv, weight_out, weight_gate, weight_const, vector_const, gain_one, gain_two = (
        lax.all_gather(dense_shards[0], "shard", axis=0, tiled=True),
        lax.all_gather(dense_shards[1], "shard", axis=0, tiled=True),
        lax.all_gather(dense_shards[2], "shard", axis=0, tiled=True),
        lax.all_gather(dense_shards[3], "shard", axis=0, tiled=True),
        lax.all_gather(dense_shards[4], "shard", axis=0, tiled=True),
        lax.all_gather(dense_shards[5], "shard", axis=0, tiled=True),
        lax.all_gather(dense_shards[6], "shard", axis=0, tiled=True),
    )
    weight_up, weight_down = (
        lax.all_gather(expert_up, "shard", axis=1, tiled=True),
        lax.all_gather(expert_down, "shard", axis=1, tiled=True),
    )
    weight_up = weight_up[0]
    weight_down = weight_down[0]
    inputs = tokens.astype(jnp.float32)
    token_ids = jnp.arange(tok_rows, dtype=jnp.int32)
    valid_mask = (token_ids < length).astype(jnp.float32)[:, None]
    gain_first = gain_one.astype(jnp.float32)
    gain_second = gain_two.astype(jnp.float32)
    scale_one = lax.rsqrt(jnp.mean(inputs * inputs, axis=1, keepdims=True) + norm_eps)
    normed = (inputs * scale_one * gain_first).astype(jnp.bfloat16)
    qkv_all = jnp.dot(normed, weight_qkv, preferred_element_type=jnp.float32)
    cosine, sine_table = tables(tok_rows, HEAD_DIM)

    def heads_first(block):
        return jnp.transpose(block, (1, 0, 2)).astype(jnp.bfloat16)

    query = heads_first(
        rotate(qkv_all[:, :D].reshape(tok_rows, HEADS, HEAD_DIM), cosine, sine_table)
    )
    keys_rot = heads_first(
        rotate(qkv_all[:, D : 2 * D].reshape(tok_rows, HEADS, HEAD_DIM), cosine, sine_table)
    )
    values = heads_first(qkv_all[:, 2 * D :].reshape(tok_rows, HEADS, HEAD_DIM))
    allowed = (token_ids[None, :] <= token_ids[:, None]) & (token_ids[None, :] < length)
    mixed_heads, log_totals = lax.map(
        lambda head: attend_head(head, allowed, score_scale), (query, keys_rot, values)
    )
    mixed = jnp.transpose(mixed_heads, (1, 0, 2)).reshape(tok_rows, D)
    hidden = inputs + jnp.dot(mixed, weight_out, preferred_element_type=jnp.float32)
    scale_two = lax.rsqrt(jnp.mean(hidden * hidden, axis=1, keepdims=True) + norm_eps)
    normed_two = hidden * scale_two * gain_second
    normed_low = normed_two.astype(jnp.bfloat16)
    mixer = gate_mix.astype(jnp.float32)
    logits = jnp.dot(normed_low, weight_gate, preferred_element_type=jnp.float32) + jnp.dot(
        prev_logits, mixer, precision=highest
    )
    chosen = jnp.take_along_axis(logits, routes, axis=1)
    gate_exp = jnp.exp(chosen - jnp.max(chosen, axis=1, keepdims=True))
    gates = gate_exp / jnp.sum(gate_exp, axis=1, keepdims=True)
    pair_dest, slot_pair = place_pairs(routes, order, length, experts_ffn, capacity)
    padded = jnp.concatenate([normed_low, jnp.zeros((1, D), jnp.bfloat16)], axis=0)
    send_rows = padded[slot_pair // 2].reshape(experts_ffn, capacity, D)
    received = lax.all_to_all(send_rows, "expert", split_axis=0, concat_axis=0, tiled=True)
    lead_shape = received.shape[:2]
    flat_rows = received.reshape(-1, D)
    gate_up = jnp.dot(flat_rows, weight_up, preferred_element_type=jnp.float32)
    activated = (jax.nn.silu(gate_up[:, :FF]) * gate_up[:, FF:]).astype(jnp.bfloat16)
    expert_out = jnp.dot(activated, weight_down, preferred_element_type=jnp.float32).astype(
        jnp.bfloat16
    )
    received, gate_up, activated, expert_out = (
        received,
        gate_up.reshape(lead_shape + (2 * FF,)),
        activated.reshape(lead_shape + (FF,)),
        expert_out.reshape(received.shape),
    )
    returned = lax.all_to_all(expert_out, "expert", split_axis=0, concat_axis=0, tiled=True)
    returned_pad = jnp.concatenate(
        [returned.reshape(-1, D), jnp.zeros((1, D), jnp.bfloat16)], axis=0
    )
    pair_ffn = returned_pad[pair_dest].astype(jnp.float32).reshape(tok_rows, 2, D)
    vector_float = vector_const.astype(jnp.float32)
    const_logits = jnp.dot(normed_low, weight_const, preferred_element_type=jnp.float32).reshape(
        tok_rows, 2, 2
    )
    const_exp = jnp.exp(const_logits - jnp.max(const_logits, axis=2, keepdims=True))
    coefs = const_exp / jnp.sum(const_exp, axis=2, keepdims=True)
    const_out = (
        coefs[..., 0:1] * normed_two[:, None, :] + coefs[..., 1:2] * vector_float.T[None, :, :]
    )
    const_select = (
        routes[:, :, None] == experts_ffn + 2 + jnp.arange(2, dtype=jnp.int32)[None, None, :]
    ).astype(jnp.float32)
    copy_select = (routes == experts_ffn + 1).astype(jnp.float32)[:, :, None]
    pair_out = (
        pair_ffn
        + copy_select * normed_two[:, None, :]
        + jnp.einsum("tkc,tcd->tkd", const_select, const_out, precision=highest)
    )
    mixture = jnp.sum(gates[:, :, None] * pair_out, axis=1)
    block_out = (valid_mask * (hidden + mixture)).astype(jnp.bfloat16)
    back_dense = (
        lax.all_gather(dense_shards[0], "shard", axis=0, tiled=True),
        lax.all_gather(dense_shards[1], "shard", axis=0, tiled=True),
        lax.all_gather(dense_shards[2], "shard", axis=0, tiled=True),
        lax.all_gather(dense_shards[3], "shard", axis=0, tiled=True),
        lax.all_gather(dense_shards[4], "shard", axis=0, tiled=True),
        lax.all_gather(dense_shards[5], "shard", axis=0, tiled=True),
        lax.all_gather(dense_shards[6], "shard", axis=0, tiled=True),
    )
    back_up, back_down = (
        lax.all_gather(expert_up, "shard", axis=1, tiled=True),
        lax.all_gather(expert_down, "shard", axis=1, tiled=True),
    )
    back_up = back_up[0]
    back_down = back_down[0]
    back_qkv, back_out, back_gate, back_const = (
        back_dense[0],
        back_dense[1],
        back_dense[2],
        back_dense[3],
    )
    grad_rows = out_grad.astype(jnp.float32) * valid_mask
    grad_gates = jnp.sum(grad_rows[:, None, :] * pair_out, axis=2)
    grad_pairs = gates[:, :, None] * grad_rows[:, None, :]
    grad_chosen = gates * (grad_gates - jnp.sum(gates * grad_gates, axis=1, keepdims=True))
    route_hot = (
        routes[:, :, None] == jnp.arange(experts_ffn + 4, dtype=jnp.int32)[None, None, :]
    ).astype(jnp.float32)
    grad_logits = jnp.sum(route_hot * grad_chosen[:, :, None], axis=1)
    prev_grad = jnp.dot(grad_logits, mixer.T, precision=highest)
    mix_term = jnp.dot(prev_logits.T, grad_logits, precision=highest)
    logit_low = grad_logits.astype(jnp.bfloat16)
    gate_term = jnp.dot(normed_low.T, logit_low, preferred_element_type=jnp.float32)
    grad_normed = jnp.dot(logit_low, back_gate.T, preferred_element_type=jnp.float32)
    grad_flat = jnp.concatenate(
        [grad_pairs.reshape(2 * tok_rows, D).astype(jnp.bfloat16), jnp.zeros((1, D), jnp.bfloat16)],
        axis=0,
    )
    grad_send = grad_flat[slot_pair].reshape(experts_ffn, capacity, D)
    grad_recv = lax.all_to_all(grad_send, "expert", split_axis=0, concat_axis=0, tiled=True)
    grad_slots = grad_recv.reshape(-1, D)
    down_term = jnp.dot(activated.reshape(-1, FF).T, grad_slots, preferred_element_type=jnp.float32)
    grad_act = jnp.dot(grad_slots, back_down.T, preferred_element_type=jnp.float32)
    gate_part = gate_up[..., :FF].reshape(-1, FF)
    up_part = gate_up[..., FF:].reshape(-1, FF)
    sigmoid_gate = jax.nn.sigmoid(gate_part)
    grad_gate_up = jnp.concatenate(
        [
            grad_act * up_part * sigmoid_gate * (1.0 + gate_part * (1.0 - sigmoid_gate)),
            grad_act * gate_part * sigmoid_gate,
        ],
        axis=1,
    ).astype(jnp.bfloat16)
    up_term = jnp.dot(received.reshape(-1, D).T, grad_gate_up, preferred_element_type=jnp.float32)
    grad_input = (
        jnp.dot(grad_gate_up, back_up.T, preferred_element_type=jnp.float32)
        .astype(jnp.bfloat16)
        .reshape(received.shape)
    )
    grad_back = lax.all_to_all(grad_input, "expert", split_axis=0, concat_axis=0, tiled=True)
    back_pad = jnp.concatenate([grad_back.reshape(-1, D), jnp.zeros((1, D), jnp.bfloat16)], axis=0)
    grad_normed = grad_normed + jnp.sum(
        back_pad[pair_dest].astype(jnp.float32).reshape(tok_rows, 2, D), axis=1
    )
    grad_normed = grad_normed + jnp.sum(copy_select * grad_pairs, axis=1)
    grad_const_out = jnp.einsum("tkc,tkd->tcd", const_select, grad_pairs, precision=highest)
    grad_first = jnp.sum(grad_const_out * normed_two[:, None, :], axis=2)
    grad_second = jnp.sum(grad_const_out * vector_float.T[None, :, :], axis=2)
    grad_coefs = jnp.stack([grad_first, grad_second], axis=2)
    grad_const_logits = (
        coefs * (grad_coefs - jnp.sum(coefs * grad_coefs, axis=2, keepdims=True))
    ).reshape(tok_rows, 4)
    grad_normed = grad_normed + jnp.sum(coefs[..., 0:1] * grad_const_out, axis=1)
    grad_normed = grad_normed + jnp.dot(
        grad_const_logits, back_const.astype(jnp.float32).T, precision=highest
    )
    vector_term = jnp.einsum("tc,tcd->dc", coefs[..., 1], grad_const_out, precision=highest)
    const_term = jnp.dot(normed_low.astype(jnp.float32).T, grad_const_logits, precision=highest)
    second_gain_term = jnp.sum(grad_normed * hidden * scale_two, axis=0)
    scaled_two = gain_second * grad_normed
    grad_hidden = (
        grad_rows
        + scale_two * scaled_two
        - hidden * scale_two**3 * jnp.mean(scaled_two * hidden, axis=1, keepdims=True)
    )
    grad_attn_low = grad_hidden.astype(jnp.bfloat16)
    out_term = jnp.dot(mixed.T, grad_attn_low, preferred_element_type=jnp.float32)
    grad_mixed = jnp.dot(grad_attn_low, back_out.T, preferred_element_type=jnp.float32).astype(
        jnp.bfloat16
    )
    grad_mixed_heads = jnp.transpose(grad_mixed.reshape(tok_rows, HEADS, HEAD_DIM), (1, 0, 2))
    grad_query, grad_key, grad_value = lax.map(
        lambda head: attend_back(head, allowed, score_scale),
        (query, keys_rot, values, grad_mixed_heads, log_totals),
    )
    grad_query = rotate(jnp.transpose(grad_query, (1, 0, 2)), cosine, -sine_table).reshape(
        tok_rows, D
    )
    grad_key = rotate(jnp.transpose(grad_key, (1, 0, 2)), cosine, -sine_table).reshape(tok_rows, D)
    grad_value = jnp.transpose(grad_value, (1, 0, 2)).reshape(tok_rows, D)
    grad_qkv = jnp.concatenate([grad_query, grad_key, grad_value], axis=1).astype(jnp.bfloat16)
    qkv_term = jnp.dot(normed.T, grad_qkv, preferred_element_type=jnp.float32)
    grad_first_norm = jnp.dot(grad_qkv, back_qkv.T, preferred_element_type=jnp.float32)
    first_gain_term = jnp.sum(grad_first_norm * inputs * scale_one, axis=0)
    scaled_one = gain_first * grad_first_norm
    tokens_grad = (
        grad_hidden
        + scale_one * scaled_one
        - inputs * scale_one**3 * jnp.mean(scaled_one * inputs, axis=1, keepdims=True)
    )
    dense_all = (
        qkv_term,
        out_term,
        gate_term,
        const_term,
        vector_term,
        first_gain_term,
        second_gain_term,
    )
    dense_terms = (
        lax.psum_scatter(dense_all[0], "shard", scatter_dimension=0, tiled=True),
        lax.psum_scatter(dense_all[1], "shard", scatter_dimension=0, tiled=True),
        lax.psum_scatter(dense_all[2], "shard", scatter_dimension=0, tiled=True),
        lax.psum_scatter(dense_all[3], "shard", scatter_dimension=0, tiled=True),
        lax.psum_scatter(dense_all[4], "shard", scatter_dimension=0, tiled=True),
        lax.psum_scatter(dense_all[5], "shard", scatter_dimension=0, tiled=True),
        lax.psum_scatter(dense_all[6], "shard", scatter_dimension=0, tiled=True),
    )
    (
        qkv_grad,
        out_weight_grad,
        gate_grad,
        const_weight_grad,
        const_vector_grad,
        norm1_grad,
        norm2_grad,
    ) = lax.psum(
        (
            dense_terms[0],
            dense_terms[1],
            dense_terms[2],
            dense_terms[3],
            dense_terms[4],
            dense_terms[5],
            dense_terms[6],
        ),
        "expert",
    )
    mix_grad = lax.psum(mix_term, ("expert", "shard"))
    expert_up_grad, expert_down_grad = (
        lax.psum_scatter(up_term[None], "shard", scatter_dimension=1, tiled=True),
        lax.psum_scatter(down_term[None], "shard", scatter_dimension=1, tiled=True),
    )
    return (
        block_out,
        tokens_grad,
        prev_grad,
        qkv_grad,
        out_weight_grad,
        gate_grad,
        const_weight_grad,
        const_vector_grad,
        norm1_grad,
        norm2_grad,
        mix_grad,
        expert_up_grad,
        expert_down_grad,
    )


MESH = pl.DeviceIdType.MESH
BF = jnp.bfloat16
F32 = jnp.float32
LANES = 128
NEG = -1e30
VMEM_BYTES = 64 * 1024 * 1024
RING = 3
HOPS = (0, 1, 3, 5)
PARTS = 2
BATCHES = 2


def dot(a, b):
    return lax.dot_general(a, b, (((1,), (0,)), ((), ())), preferred_element_type=F32)


def dot_nt(a, b):
    return lax.dot_general(a, b, (((1,), (1,)), ((), ())), preferred_element_type=F32)


def dot_tn(a, b):
    return lax.dot_general(a, b, (((0,), (0,)), ((), ())), preferred_element_type=F32)


def iota(shape, dim):
    return lax.broadcasted_iota(jnp.int32, shape, dim)


def remote(src, dst, send_sem, recv_sem, target):
    return pltpu.make_async_remote_copy(
        src_ref=src,
        dst_ref=dst,
        send_sem=send_sem,
        recv_sem=recv_sem,
        device_id=target,
        device_id_type=MESH,
    )


def swap_halves(block):
    half = HEAD_DIM // 2
    width = block.shape[1]
    lower = (iota(block.shape, 1) % HEAD_DIM) < half
    return jnp.where(
        lower, pltpu.roll(block, width - half, 1), pltpu.roll(block, half, 1)
    )


def step_kernel(dims, scratch_names, *refs):
    (tok_rows, experts, lines, share, hidden_block, capacity, gate_cols) = dims
    names = IN_NAMES + OUT_NAMES + scratch_names
    r = dict(zip(names, refs))
    pairs = D // LANES
    layer = 2 * experts
    slots = experts * capacity
    quarter = share // 4
    chunk_cols = 3 * LANES
    out_chunks = D // chunk_cols
    chunks = out_chunks + pairs
    half_ffn = lines * 2 * hidden_block
    const_col = gate_cols
    vec_col = gate_cols + 8
    row_blocks = tok_rows // LANES

    e = lax.axis_index("expert")
    s = lax.axis_index("shard")
    z = s // 2
    x = s % 2
    core = e % 2
    half = e // 2
    facing = 2 * (1 - half) + core
    across = 2 * z + 1 - x
    twin = e + 1 - 2 * core
    mine = 2 * e + x

    def rows(index, size):
        return pl.ds(pl.multiple_of(index * size, size), size)

    weights, small = r["weights"], r["small"]
    up, down, stage = r["up"], r["down"], r["stage"]
    own_rows = rows(s, share)

    def up_columns(part, jj, xx):
        return pl.ds(
            pl.multiple_of(part * FF + hidden_block * (2 * jj + xx), hidden_block), hidden_block
        )

    def up_load(jj, part, to):
        spot = pl.ds(part * hidden_block, hidden_block)
        box = stage.at[jj, :, spot] if to == 0 else up.at[jj, own_rows, spot]
        xx = 1 - x if to == 0 else x
        return pltpu.make_async_copy(
            r["up_in"].at[:, up_columns(part, jj, xx)], box, r["up_sem"].at[to, jj, part]
        )

    direct = {
        "qkv_in": weights.at[own_rows, pl.ds(0, 3 * D)],
        "out_in": weights.at[own_rows, pl.ds(3 * D, D)],
        "down_in": down.at[z],
    }

    def load(name):
        box = direct[name] if name in direct else r["own_" + name]
        return pltpu.make_async_copy(r[name], box, r["in_sem"].at[LOADED.index(name)])

    def store(name):
        held = r["ffn"].at[0:tok_rows, :] if name == "tokens_out" else r["own_" + name]
        return pltpu.make_async_copy(held, r[name], r["out_sem"].at[OUT_NAMES.index(name)])

    load("qkv_in").start()
    for jj in range(lines):
        for part in range(2):
            up_load(jj, part, 0).start()
    for name in LOADED[1:]:
        load(name).start()
    for jj in range(lines):
        for part in range(2):
            up_load(jj, part, 1).start()

    barrier = pltpu.get_barrier_semaphore()
    met = 0
    for step in range(1, 2 * lines):
        pl.semaphore_signal(
            barrier, 1, device_id=(e, (s + step) % (2 * lines)), device_id_type=MESH
        )
        met += 1
    for step in range(1, experts):
        for side in range(2):
            pl.semaphore_signal(
                barrier, 1, device_id=((e + step) % experts, 2 * z + side), device_id_type=MESH
            )
            met += 1
    pl.semaphore_wait(barrier, met)

    def down_part(ref, index, part):
        height = hidden_block // PARTS
        return ref.at[index, pl.ds(part * height, height), :]

    def up_across(jj, origin_x):
        return remote(
            stage.at[jj],
            up.at[jj, rows(2 * z + origin_x, share), :],
            r["ux_send"].at[jj],
            r["ux_recv"].at[jj],
            (e, across),
        )

    def chain(kind, way, step, jj, zz):
        ref = up.at[jj, rows(zz, 2 * share), :] if kind == 0 else down_part(down, jj, kind - 1)
        target = s + 2 if way == 0 else s - 2
        return remote(
            ref,
            ref,
            r["ch_send"].at[kind, way, step, jj],
            r["ch_recv"].at[kind, way, step, jj],
            (e, target),
        )

    def chain_each(way, step, jj, zz, go):
        go(0, way, step, jj, zz)

        @pl.when(zz == jj)
        def _():
            for part in range(PARTS):
                go(1 + part, way, step, jj, zz)

    def begin(*which):
        chain(*which).start()

    def arrive(*which):
        chain(*which).wait_recv()

    def leave(*which):
        chain(*which).wait_send()

    def hand_on(kind, way, step, jj, zz):
        chain(kind, way, step, jj, zz).wait_recv()
        chain(kind, way, step + 1, jj, zz).start()

    def turn(index):
        return (2 * index + 1) % (lines + 1)

    def chain_ready(jj):
        for part in range(2):
            up_load(jj, part, 1).wait()
        up_across(jj, 1 - x).wait_recv()

    def chain_own(kinds, jj):
        for way, there in ((0, z + 1 < lines), (1, z > 0)):

            @pl.when(there)
            def _():
                for kind in kinds:
                    begin(kind, way, 0, jj, z)

    def chain_pass(index, step):
        @pl.when((z - 1 - step >= 0) & (z + 1 < lines))
        def _():
            chain_each(0, step, turn(index), z - 1 - step, hand_on)

        @pl.when((z + 1 + step < lines) & (z > 0))
        def _():
            chain_each(1, step, turn(index), z + 1 + step, hand_on)

    def chain_end(jj):
        for step in range(lines - 1):

            @pl.when((z - 1 - step >= 0) & (z + 1 == lines))
            def _():
                chain_each(0, step, jj, z - 1 - step, arrive)

            @pl.when((z + 1 + step < lines) & (z == 0))
            def _():
                chain_each(1, step, jj, z + 1 + step, arrive)

    def chain_sent():
        for jj in range(lines):
            for step in range(lines - 1):

                @pl.when((z - step >= 0) & (z + 1 < lines))
                def _():
                    chain_each(0, step, jj, z - step, leave)

                @pl.when((z + step < lines) & (z > 0))
                def _():
                    chain_each(1, step, jj, z + step, leave)

    passes = [(jj, step) for step in range(lines - 2) for jj in range(lines)]

    def chain_events(first, count):
        for number in range(first, min(first + count, len(passes))):
            chain_pass(*passes[number])

    for jj in range(lines):
        for part in range(2):
            up_load(jj, part, 0).wait()
    up_across(1, x).start()

    spans = ((0, 3 * D // 2), (3 * D, D // 2))

    third = share // 3

    def part_of(kind, zz, xx, cc, first, height):
        start, width = spans[kind]
        columns = pl.ds(pl.multiple_of(start + width * cc, LANES), width)
        spot = pl.ds(pl.multiple_of((2 * zz + xx) * share + first, third), height)
        return weights.at[spot, columns]

    def slab(kind, zz, xx, cc):
        return part_of(kind, zz, xx, cc, third * half, 2 * third)

    def dense_z(kind, way, step, zz):
        ref = slab(kind, zz, x, core)
        return remote(
            ref,
            ref,
            r["dz_send"].at[kind, way, step],
            r["d_recv"].at[kind, zz, x, core],
            (e, s + 2 if way == 0 else s - 2),
        )

    def dense_z_each(kind, step, go):
        @pl.when((z - step >= 0) & (z + 1 < lines))
        def _():
            go(dense_z(kind, 0, step, z - step))

        @pl.when((z + step < lines) & (z > 0))
        def _():
            go(dense_z(kind, 1, step, z + step))

    def dense_x(kind, zz):
        ref = slab(kind, zz, x, core)
        return remote(
            ref, ref, r["dx_send"].at[kind, zz], r["d_recv"].at[kind, zz, x, core], (e, across)
        )

    def dense_core(kind, zz, xx):
        ref = slab(kind, zz, xx, core)
        return remote(
            ref,
            ref,
            r["dc_send"].at[kind, zz, xx],
            r["d_recv"].at[kind, zz, xx, core],
            (twin, s),
        )

    def dense_y(kind, zz, xx):
        ref = part_of(kind, zz, xx, core, 2 * third * half, third)
        return remote(
            ref,
            ref,
            r["dy_send"].at[kind, zz, xx],
            r["dy_recv"].at[kind, zz, xx, core],
            (facing, s),
        )

    def rest_core(kind, zz, xx, cc):
        ref = part_of(kind, zz, xx, cc, 2 * third * (1 - half), third)
        return remote(
            ref,
            ref,
            r["dr_send"].at[kind, zz, xx],
            r["dy_recv"].at[kind, zz, xx, cc],
            (twin, s),
        )

    def dense_arrived(kind, zz, xx, cc):
        ref = slab(kind, zz, xx, cc)
        remote(
            ref, ref, r["dx_send"].at[kind, 0], r["d_recv"].at[kind, zz, xx, cc], (e, across)
        ).wait_recv()

    def dense_start(kind):
        dense_z_each(kind, 0, lambda copy: copy.start())
        dense_x(kind, z).start()

    def dense_forward(kind, step):
        for zz, there in ((z - 1 - step, z - 1 - step >= 0), (z + 1 + step, z + 1 + step < lines)):

            @pl.when(there)
            def _():
                dense_arrived(kind, zz, x, core)

                if step + 1 < lines - 1:

                    @pl.when((zz < z) & (z + 1 < lines))
                    def _():
                        dense_z(kind, 0, step + 1, zz).start()

                    @pl.when((zz > z) & (z > 0))
                    def _():
                        dense_z(kind, 1, step + 1, zz).start()

                dense_x(kind, zz).start()
                dense_core(kind, zz, x).start()
                dense_y(kind, zz, x).start()

    def dense_share(kind):
        for step in range(lines):
            zz = (z + lines - step) % lines
            dense_arrived(kind, zz, 1 - x, core)
            dense_core(kind, zz, 1 - x).start()
            dense_y(kind, zz, 1 - x).start()

    def dense_cross(kind):
        for step in range(lines):
            zz = (z + lines - step) % lines
            for xx in (x, 1 - x) if step > 0 else (1 - x,):
                rest_core(kind, zz, xx, core).wait_recv()
                rest_core(kind, zz, xx, core).start()

    def dense_finish(kind):
        for step in range(lines):
            zz = (z + lines - step) % lines
            for xx in (x, 1 - x) if step > 0 else (1 - x,):
                dense_arrived(kind, zz, xx, 1 - core)
                rest_core(kind, zz, xx, 1 - core).wait_recv()

    def dense_sent(kind):
        for step in range(lines - 1):
            dense_z_each(kind, step, lambda copy: copy.wait_send())
        for step in range(lines):
            zz = (z + lines - step) % lines
            dense_x(kind, zz).wait_send()
            for xx in (x, 1 - x) if step > 0 else (1 - x,):
                dense_core(kind, zz, xx).wait_send()
                dense_y(kind, zz, xx).wait_send()
                rest_core(kind, zz, xx, core).wait_send()

    def small_copy(step, origin):
        ref = small.at[rows(origin, share), :]
        return remote(
            ref,
            ref,
            r["sm_send"].at[step],
            r["sm_recv"].at[origin],
            (e, (s + step) % (2 * lines)),
        )

    load("qkv_in").wait()
    dense_start(0)
    for name in LOADED[1:]:
        load(name).wait()
    dense_start(1)
    pack = r["pack"]
    pack[...] = jnp.zeros_like(pack)
    spot = 0
    for name in ("gate_in", "const_in", "const_in", "vec_in", "one_in", "two_in"):
        height = r[name].shape[0]
        pack[spot : spot + height, 0:share] = r["own_" + name][...].astype(F32)
        spot += height
    small[rows(s, share), :] = jnp.transpose(pack[...])[0:share, :].astype(BF)
    for step in range(1, 2 * lines):
        small_copy(step, s).start()
    token_rows, token_cols = r["token_rows"], r["token_cols"]
    token_rows[...] = jnp.zeros_like(token_rows)
    token_rows[0:2, :] = r["own_routes_in"][...].astype(F32)
    token_rows[8 : 8 + gate_cols, :] = r["own_prev_in"][...]
    token_cols[...] = jnp.transpose(token_rows[...])

    tokens = r["own_tokens"]
    cols = r["cols"]
    for block in range(row_blocks):
        at = slice(block * LANES, (block + 1) * LANES)
        inputs = tokens[at, :].astype(F32)
        cols[at, 0:1] = lax.rsqrt(jnp.mean(inputs * inputs, axis=1, keepdims=True) + norm_eps)
    dense_forward(0, 0)

    dense_forward(0, 1)
    dense_forward(1, 0)

    length = r["length"][0]
    pair_ids = iota((2 * tok_rows, 2 * tok_rows), 0)
    pair_names = jnp.where(pair_ids < tok_rows, 2 * pair_ids, 2 * (pair_ids - tok_rows) + 1)
    is_at = jnp.where(pair_names == r["own_order_row"][...], 1.0, 0.0).astype(BF)
    pair_lane = iota((16, 2 * tok_rows), 1)
    pair_token = jnp.where(pair_lane < tok_rows, pair_lane, pair_lane - tok_rows)
    expert_row = iota((16, 2 * tok_rows), 0)
    route_row = jnp.concatenate([token_rows[0:1, :], token_rows[1:2, :]], axis=1)
    live = (expert_row.astype(F32) == route_row) & (expert_row < experts) & (pair_token < length)
    placed = dot(jnp.where(live, 1.0, 0.0).astype(BF), is_at)
    before = jnp.where(
        iota((2 * tok_rows, 2 * tok_rows), 0) <= iota((2 * tok_rows, 2 * tok_rows), 1), 1.0, 0.0
    ).astype(BF)
    counts = dot(placed.astype(BF), before)
    kept = jnp.where((placed > 0.5) & (counts <= capacity + 0.5), counts, 0.0)
    taken = dot_nt(kept.astype(BF), is_at)
    slot_of = jnp.sum(
        jnp.where(taken > 0.5, taken + (expert_row * capacity).astype(F32), 0.0),
        axis=0,
        keepdims=True,
    )
    slot_col = jnp.transpose(jnp.broadcast_to(slot_of, (8, 2 * tok_rows)))
    for step in range(2, lines - 1):
        dense_forward(0, step)
    for step in range(1, lines - 1):
        dense_forward(1, step)
    for index in range(1, lines):
        up_across(turn(index), x).start()
    chain_ready(1)
    chain_own((0,), 1)
    chain_own(tuple(range(1, 1 + PARTS)), z)
    put, take = r["put"], r["take"]
    for k in range(2):
        span = slice(k * tok_rows, (k + 1) * tok_rows)
        names_down = (iota((slots, tok_rows), 0) + 1).astype(F32)
        put[k] = jnp.where(slot_of[:, span] == names_down, 1.0, 0.0).astype(BF)
        names_right = (iota((tok_rows, slots), 1) + 1).astype(F32)
        take[k] = jnp.where(slot_col[span, 0:1] == names_right, 1.0, 0.0).astype(BF)

    buffer, slot_grad = r["buffer"], r["slot_grad"]
    sent, sent_wide = r["sent"], r["sent_wide"]

    def dispatch(which, step, side, origin):
        target = (e + step) % experts
        box = buffer if which == 0 else slot_grad
        source = sent_wide if which == 0 else sent
        return remote(
            source.at[rows(target, capacity), :],
            box.at[rows(origin, capacity), :],
            r["go_send"].at[which, step, side],
            r["go_recv"].at[which, origin],
            (target, 2 * z + side),
        )

    def dispatch_each(which, step, go):
        for flip in range(2):
            side = x if flip == 0 else 1 - x
            if step > 0 or flip == 1:
                go(dispatch(which, step, side, mine))

    for step in range(experts):
        chosen_rows = rows((e + step) % experts, capacity)
        sent[chosen_rows, :] = dot(
            put[0, chosen_rows, :] + put[1, chosen_rows, :], r["own_out_grad"][...]
        ).astype(BF)
    slot_grad[rows(mine, capacity), :] = sent[rows(e, capacity), :]

    for step in range(1, 2 * lines):
        origin = (s + 2 * lines - step) % (2 * lines)
        small_copy(step, origin).wait_recv()
    pick = jnp.where(iota((8, LANES), 1) == iota((8, LANES), 0) + vec_col, 1.0, 0.0).astype(BF)
    named = dot_nt(pick, small[...])
    r["rows"][...] = named
    gain_one, gain_two = named[2:3, :], named[3:4, :]
    vec_zero, vec_one = named[0:1, :], named[1:2, :]
    normed = r["normed"]
    for block in range(row_blocks):
        at = slice(block * LANES, (block + 1) * LANES)
        inputs = tokens[at, :].astype(F32)
        normed[at, :] = (inputs * cols[at, 0:1] * gain_one).astype(BF)

    dense_share(0)
    dense_cross(0)
    for index in range(1, lines):
        chain_ready(turn(index))
        chain_own((0,), turn(index))
    dense_finish(0)

    heads = r["heads"]
    cosine, sine = r["own_cosine"], r["own_sine"]

    def project(b, turn):
        wide_block = dot(normed[...], weights[:, rows(b, 2 * LANES)])
        for part in range(2):
            block = wide_block[:, part * LANES : (part + 1) * LANES]
            if turn:
                block = block * cosine[...] + swap_halves(block) * sine[...]
            heads[2 * b + part] = block.astype(BF)

    def rotated(b, _):
        project(b, True)
        return 0

    def plain(b, _):
        project(b, False)
        return 0

    lax.fori_loop(0, pairs, rotated, 0)
    lax.fori_loop(pairs, 3 * pairs // 2, plain, 0)
    dense_share(1)
    for step in range(experts):
        dispatch_each(1, step, lambda copy: copy.start())
    chain_events(0, 2)

    score_scale = HEAD_DIM ** (-0.5)
    first_head = iota((tok_rows, LANES), 1) < HEAD_DIM
    mixed, log_sums = r["mixed"], r["log_sums"]

    def allowed_pairs():
        key, query = iota((tok_rows, tok_rows), 0), iota((tok_rows, tok_rows), 1)
        return (key <= query) & (key < length)

    def one_head(block, head):
        keep = first_head if head == 0 else jnp.logical_not(first_head)
        return jnp.where(keep, block, jnp.zeros_like(block))

    def attend(p, _):
        query, key, value = heads[p], heads[pairs + p], heads[2 * pairs + p]
        results = []
        for head in range(2):
            scores = dot_nt(key, one_head(query, head)) * score_scale
            scores = jnp.where(allowed_pairs(), scores, NEG)
            top = jnp.max(scores, axis=0, keepdims=True)
            expo = jnp.exp(scores - top)
            total = jnp.sum(expo, axis=0, keepdims=True)
            probs = expo * (1.0 / total)
            log_sums[p, head : head + 1, :] = top + jnp.log(total)
            results.append(dot_tn(probs.astype(BF), value))
        mixed[:, rows(p, LANES)] = jnp.where(first_head, results[0], results[1]).astype(BF)
        return 0

    lax.fori_loop(0, pairs // 2, attend, 0)
    chain_events(2, 1)
    dense_cross(1)
    lax.fori_loop(pairs // 2, pairs, attend, 0)
    dense_finish(1)
    chain_events(3, 1)

    hidden, normed_low = r["hidden"], r["normed_low"]
    out_grad = r["own_out_grad"]
    mixer = r["own_mix"][...].astype(F32)
    grad_low, grad_sum, gate_parts = r["grad_low"], r["own_out_grad"], r["gate_parts"]
    for block in range(row_blocks):
        at = slice(block * LANES, (block + 1) * LANES)
        hid = tokens[at, :].astype(F32) + dot(mixed[at, :], weights[:, 3 * D : 4 * D])
        hidden[at, :] = hid
        scale = lax.rsqrt(jnp.mean(hid * hid, axis=1, keepdims=True) + norm_eps)
        cols[at, 1:2] = scale
        low = (hid * scale * gain_two).astype(BF)
        normed_low[at, :] = low
        logits = dot(low, small[...])
        lane = iota((LANES, LANES), 1)
        extra = jnp.zeros((LANES, gate_cols), F32)
        for i in range(gate_cols):
            extra = extra + token_cols[at, 8 + i : 9 + i] * mixer[i : i + 1, :]
        routes = token_cols[at, 0:2].astype(jnp.int32)
        chosen = []
        for k in range(2):
            hot = lane == routes[:, k : k + 1]
            part = jnp.sum(jnp.where(hot, logits, 0.0), axis=1, keepdims=True)
            chosen.append(
                part
                + jnp.sum(
                    jnp.where(
                        iota((LANES, gate_cols), 1) == routes[:, k : k + 1], extra, 0.0
                    ),
                    axis=1,
                    keepdims=True,
                )
            )
        top = jnp.maximum(chosen[0], chosen[1])
        powers = [jnp.exp(c - top) for c in chosen]
        total = powers[0] + powers[1]
        gates = [w / total for w in powers]
        on_normed = sum(
            gates[k] * (routes[:, k : k + 1] == experts + 1).astype(F32) for k in range(2)
        )
        for j in range(2):
            first = logits[:, const_col + 2 * j : const_col + 2 * j + 1]
            second = logits[:, const_col + 2 * j + 1 : const_col + 2 * j + 2]
            peak = jnp.maximum(first, second)
            first, second = jnp.exp(first - peak), jnp.exp(second - peak)
            both = first + second
            first, second = first / both, second / both
            weight = sum(
                gates[k] * (routes[:, k : k + 1] == experts + 2 + j).astype(F32)
                for k in range(2)
            )
            on_normed = on_normed + first * weight
            cols[at, 6 + 4 * j : 7 + 4 * j] = first
            cols[at, 7 + 4 * j : 8 + 4 * j] = second
            cols[at, 8 + 4 * j : 9 + 4 * j] = weight
        cols[at, 2:3] = gates[0]
        cols[at, 3:4] = gates[1]
        cols[at, 4:5] = on_normed
        valid = (iota((LANES, 1), 0) + block * LANES < length).astype(F32)
        grad = out_grad[at, :].astype(F32) * valid
        for k in range(2):
            high = gates[k].astype(BF).astype(F32)
            middle = (gates[k] - high).astype(BF).astype(F32)
            parts = jnp.where(lane == 0, high, 0.0)
            parts = jnp.where(lane == 1, middle, parts)
            gate_parts[k, at, :] = jnp.where(lane == 2, gates[k] - high - middle, parts).astype(BF)
        grad_sum[at, :] = grad.astype(BF)


    for step in range(experts):
        chosen_rows = rows((e + step) % experts, capacity)
        put_zero, put_one = put[0, chosen_rows, :], put[1, chosen_rows, :]
        sent_wide[chosen_rows, 0:D] = dot(put_zero + put_one, normed_low[...]).astype(BF)
        sent_wide[chosen_rows, D : D + LANES] = (
            dot(put_zero, gate_parts[0]) + dot(put_one, gate_parts[1])
        ).astype(BF)
        dispatch_each(0, step, lambda copy: copy.start())
    buffer[rows(mine, capacity), :] = sent_wide[rows(e, capacity), :]
    chain_events(4, len(passes))

    def others(go):
        for step in range(experts):
            other = (e + step) % experts
            for flip in range(2):
                side = x if flip == 0 else 1 - x
                if step > 0 or flip == 1:
                    go(step, other, side, 2 * other + side)

    for which in range(2):
        others(lambda step, other, side, origin: dispatch(which, step, side, origin).wait_recv())
    for block in range(2 * experts * capacity // LANES):
        at = slice(block * LANES, (block + 1) * LANES)
        shares = buffer[at, D : D + LANES].astype(F32)
        gate = shares[:, 0:1] + shares[:, 1:2] + shares[:, 2:3]
        slot_grad[at, :] = (gate * slot_grad[at, :].astype(F32)).astype(BF)

    up_sum, down_sum = r["up_sum"], r["down_sum"]
    up_box, down_box = r["up_box"], r["down_box"]
    up_out, down_out = r["own_up_out"], r["own_down_out"]
    final_send, final_box = stage, r["final_box"]
    ffn, slot_back = r["ffn"], r["slot_back"]
    last = lines - 1

    def summed(first, second):
        return (first.astype(F32) + second.astype(F32)).astype(BF)

    def up_rows(jj, zz):
        return up_sum.at[jj, rows(zz, 2 * share), :]

    def up_hop(way, k, jj, dest):
        return remote(
            up_rows(jj, dest),
            up_box.at[way, k, jj],
            r["ru_send"].at[way, k, jj],
            r["ru_recv"].at[way, k, jj],
            (e, s + 2 if way == 0 else s - 2),
        )

    def down_slot(way, jj, zz):
        return jj if way == 0 else jnp.where(jj == zz, lines, jj)

    def down_hop(way, jj, zz, part):
        return remote(
            down_part(down_sum, jj, part),
            down_part(down_box, down_slot(way, jj, zz), part),
            r["rd_send"].at[way, jj, part],
            r["rd_recv"].at[way, jj, part],
            (e, s + 2 if way == 0 else s - 2),
        )

    def final_hop(jj):
        return remote(
            final_send.at[jj],
            final_box.at[jj],
            r["fx_send"].at[jj],
            r["fx_recv"].at[jj],
            (e, across),
        )

    def sum_pass(index, k):
        for way in range(2):
            jj = turn(index)
            place = z if way == 0 else last - z
            dest = last - k + place if way == 0 else k - place

            @pl.when((place >= 1) & (place <= k) & (place < last))
            def _():
                up_hop(way, k - 1, jj, dest).wait_recv()
                spot = rows(dest, 2 * share)
                up_sum[jj, spot, :] = summed(up_sum[jj, spot, :], up_box[way, k - 1, jj])
                up_hop(way, k, jj, dest).start()

                @pl.when(dest == jj)
                def _():
                    for part in range(PARTS):
                        down_hop(way, jj, z, part).wait_recv()
                        own = down_part(down_sum, jj, part)
                        own[...] = summed(
                            own[...], down_part(down_box, down_slot(way, jj, z), part)[...]
                        )
                        down_hop(way, jj, z + 1 - 2 * way, part).start()

    def sum_final(jj):
        total = slot_back.at[0 : 2 * share, 0 : 2 * hidden_block]
        total[...] = up_sum[jj, rows(z, 2 * share), :].astype(F32)
        for way, there in ((0, z > 0), (1, z < last)):

            @pl.when(there)
            def _():
                up_hop(way, last - 1, jj, z).wait_recv()
                total[...] += up_box[way, last - 1, jj].astype(F32)

        final_send[jj] = total[rows(1 - x, share), :].astype(BF)
        final_hop(jj).start()
        own = total[rows(x, share), :]
        for part in range(2):
            up_out[:, up_columns(part, jj, x)] = own[
                :, part * hidden_block : (part + 1) * hidden_block
            ]

        @pl.when(jj == z)
        def _():
            down_out[...] = down_sum[z].astype(F32)
            for way, there in ((0, z > 0), (1, z < last)):

                @pl.when(there)
                def _():
                    for part in range(PARTS):
                        down_hop(way, jj, z, part).wait_recv()
                    down_out[...] += down_box[down_slot(way, jj, z)].astype(F32)

    def sum_start(jj):
        for way in range(2):

            @pl.when(z == (0 if way == 0 else last))
            def _():
                for k in range(last):
                    dest = last - k if way == 0 else k
                    up_hop(way, k, jj, dest).start()

                    @pl.when(dest == jj)
                    def _():
                        for part in range(PARTS):
                            down_hop(way, jj, z + 1 - 2 * way, part).start()

    sum_passes = [(jj, k) for jj in range(lines) for k in range(1, last)]

    def sum_passed(first, count):
        for number in range(first, min(first + count, len(sum_passes))):
            sum_pass(*sum_passes[number])

    def sum_sent():
        for jj in range(lines):
            for way in range(2):
                place = z if way == 0 else last - z
                for k in range(last):
                    dest = last - k + place if way == 0 else k - place

                    @pl.when((place <= k) & (place < last))
                    def _():
                        up_hop(way, k, jj, dest).wait_send()

                        @pl.when(dest == jj)
                        def _():
                            for part in range(PARTS):
                                down_hop(way, jj, z + 1 - 2 * way, part).wait_send()

    for jj in range(lines):
        up_across(jj, x).wait_send()
    act, grad_gu = r["act"], r["grad_gu"]
    back_box = r["back_box"]
    side_rows = 4 * capacity
    for which in range(2):
        for step in range(experts):
            dispatch_each(which, step, lambda copy: copy.wait_send())

    def come(which, target, side, origin_e, origin_x):
        box = grad_low if which == 0 else sent
        return remote(
            box.at[rows(2 * target + side, capacity), :],
            back_box.at[which, origin_x, rows(origin_e, capacity), :],
            r["come_send"].at[which, target, side],
            r["come_recv"].at[which, origin_e, origin_x],
            (target, 2 * z + side),
        )

    def expert_chunk(index, _):
        jj = turn(index)
        chain_end(jj)

        def forward(b, _):
            group = (half + 1 + b) % 2
            at = rows(group, side_rows)
            given = dot(buffer[at, 0:D], up[jj])
            gate, lift = given[:, 0:hidden_block], given[:, hidden_block:]
            squash = 1.0 / (1.0 + jnp.exp(-gate))
            silu = gate * squash
            low = (silu * lift).astype(BF)
            act[at, :] = low
            grad_act = dot_nt(slot_grad[at, :], down[jj])
            grads = jnp.concatenate(
                [grad_act * lift * squash * (1.0 + gate * (1.0 - squash)), grad_act * silu],
                axis=1,
            ).astype(BF)
            grad_gu[at, :] = grads
            forth = dot(low, down[jj])
            back = dot_nt(grads, up[jj])

            @pl.when(index == 0)
            def _():
                ffn[at, :] = forth
                slot_back[at, :] = back

            @pl.when((index > 0) & (index < last))
            def _():
                ffn[at, :] += forth
                slot_back[at, :] += back

            @pl.when(index == last)
            def _():
                grad_low[at, :] = (ffn[at, :] + forth).astype(BF)
                sent[at, :] = (slot_back[at, :] + back).astype(BF)
                for other in range(2):
                    target = 2 * group + other
                    for which in range(2):
                        come(which, target, 1 - x, e, x).start()

                        @pl.when(target != e)
                        def _():
                            come(which, target, x, e, x).start()

            return 0

        lax.fori_loop(0, 2, forward, 0)
        up_sum[jj] = dot_tn(buffer[:, 0:D], grad_gu[...]).astype(BF)
        down_sum[jj] = dot_tn(act[...], slot_grad[...]).astype(BF)
        sum_start(jj)
        return 0

    lax.fori_loop(0, lines, expert_chunk, 0)

    for which in range(2):
        box = grad_low if which == 0 else sent
        back_box[which, x, rows(e, capacity), :] = box[rows(mine, capacity), :]
    sum_passed(0, 3)
    for which in range(2):
        others(
            lambda step, other, side, origin: come(which, other, side, other, side).wait_recv()
        )
    for which in range(2):
        back_box[which, 0] = (
            back_box[which, 0].astype(F32) + back_box[which, 1].astype(F32)
        ).astype(BF)

    named = r["rows"][...]
    gain_one, gain_two = named[2:3, :], named[3:4, :]
    vec_zero, vec_one = named[0:1, :], named[1:2, :]
    grad_hidden, grad_attn = ffn.at[0:tok_rows, :], r["grad_attn"]
    thin, wide = r["thin"], r["wide"]
    grad_logits = r["grad_logits"]
    gain_sum = jnp.zeros((1, D), F32)
    for block in range(row_blocks):
        at = slice(block * LANES, (block + 1) * LANES)
        hid = hidden[at, :]
        scale = cols[at, 1:2]
        norm = hid * scale * gain_two
        grad = grad_sum[at, :].astype(F32)
        take_zero, take_one = take[0, at, :], take[1, at, :]
        outs = [dot(take_zero, back_box[0, 0]), dot(take_one, back_box[0, 0])]
        gates = [cols[at, 2:3], cols[at, 3:4]]
        on_normed = cols[at, 4:5]
        const = [
            (cols[at, 6 + 4 * j : 7 + 4 * j], cols[at, 7 + 4 * j : 8 + 4 * j], cols[at, 8 + 4 * j : 9 + 4 * j])
            for j in range(2)
        ]
        on_vec = [a * w for _, a, w in const]
        valid = (iota((LANES, 1), 0) + block * LANES < length).astype(F32)
        mixture = (
            gates[0] * outs[0]
            + gates[1] * outs[1]
            + on_normed * norm
            + on_vec[0] * vec_zero
            + on_vec[1] * vec_one
        )
        r["own_block_out"][at, :] = (valid * (hid + mixture)).astype(BF)
        routes = token_cols[at, 0:2].astype(jnp.int32)
        with_norm = jnp.sum(grad * norm, axis=1, keepdims=True)
        with_vec = [
            jnp.sum(grad * v, axis=1, keepdims=True) for v in (vec_zero, vec_one)
        ]
        gate_grads = []
        for k in range(2):
            value = jnp.sum(grad * outs[k], axis=1, keepdims=True)
            value = value + (routes[:, k : k + 1] == experts + 1).astype(F32) * with_norm
            for j in range(2):
                hit = (routes[:, k : k + 1] == experts + 2 + j).astype(F32)
                value = value + hit * (const[j][0] * with_norm + const[j][1] * with_vec[j])
            gate_grads.append(value)
        mean = gates[0] * gate_grads[0] + gates[1] * gate_grads[1]
        lane = iota((LANES, LANES), 1)
        spread = jnp.zeros((LANES, LANES), F32)
        for k in range(2):
            spread = spread + jnp.where(
                lane == routes[:, k : k + 1], gates[k] * (gate_grads[k] - mean), 0.0
            )
        grad_logits[at, :] = spread[:, 0:gate_cols]
        wide_block = jnp.zeros((LANES, LANES), F32)
        for j in range(2):
            first, second, weight = const[j]
            d_first, d_second = weight * with_norm, weight * with_vec[j]
            centre = first * d_first + second * d_second
            parts = (first * (d_first - centre), second * (d_second - centre))
            for i in range(2):
                high = parts[i].astype(BF).astype(F32)
                at_high = const_col + 2 * j + i
                spread = jnp.where(lane == at_high, high, spread)
                spread = jnp.where(lane == at_high + 4, parts[i] - high, spread)
            high = on_vec[j].astype(BF).astype(F32)
            wide_block = jnp.where(lane == j, high, wide_block)
            wide_block = jnp.where(lane == 2 + j, on_vec[j] - high, wide_block)
        thin[at, :] = spread.astype(BF)
        wide[at, :] = wide_block.astype(BF)
        grad_norm = (
            dot_nt(thin[at, :], small[...])
            + dot(take_zero + take_one, back_box[1, 0])
            + on_normed * grad
        )
        gain_sum = gain_sum + jnp.sum(grad_norm * hid * scale, axis=0, keepdims=True)
        scaled = gain_two * grad_norm
        grad = (
            grad
            + scale * scaled
            - hid * (scale * scale * scale) * jnp.mean(scaled * hid, axis=1, keepdims=True)
        )
        grad_hidden[at, :] = grad
        grad_attn[at, :] = grad.astype(BF)

    sum_passed(3, 1)

    sums = r["sums"]
    own_sums = r["own_sums"]
    own_sums[...] = jnp.zeros_like(own_sums)
    by_small = dot_tn(thin[...], normed_low[...])
    by_vec = dot_tn(wide[...], grad_sum[...])
    own_sums[0:gate_cols, :] = by_small[0:gate_cols, :]
    own_sums[gate_cols : gate_cols + 4, :] = (
        by_small[const_col : const_col + 4, :] + by_small[const_col + 4 : const_col + 8, :]
    )
    own_sums[gate_cols + 4 : gate_cols + 6, :] = by_vec[0:2, :] + by_vec[2:4, :]
    own_sums[gate_cols + 6 : gate_cols + 7, :] = gain_sum
    mix_rows = SMALL_ROWS - 8
    own_sums[mix_rows : mix_rows + gate_cols, 0:gate_cols] = lax.dot_general(
        r["own_prev_in"][...],
        grad_logits[...],
        (((1,), (0,)), ((), ())),
        precision=lax.Precision.HIGHEST,
        preferred_element_type=F32,
    )
    r["own_prev_out"][...] = lax.dot_general(
        r["own_mix"][...].astype(F32),
        grad_logits[...],
        (((1,), (1,)), ((), ())),
        precision=lax.Precision.HIGHEST,
        preferred_element_type=F32,
    )

    store("block_out").start()
    store("prev_out").start()

    dense, ring = r["dense"], RING
    core_box, y_box, x_box = r["core_box"], r["y_box"], r["x_box"]
    z_box, all_box = r["z_box"], r["all_box"]

    def as_chunk(block):
        return block.reshape(lines, 2, 2, 2, quarter, chunk_cols).astype(BF)

    def core_hop(ch):
        return remote(
            dense.at[ch % ring, :, :, 1 - core],
            core_box.at[ch],
            r["gc_send"].at[ch],
            r["gc_recv"].at[ch],
            (twin, s),
        )

    def y_hop(ch):
        return remote(
            core_box.at[ch, :, :, 1 - half],
            y_box.at[ch],
            r["gy_send"].at[ch],
            r["gy_recv"].at[ch],
            (facing, s),
        )

    def x_hop(ch):
        return remote(
            y_box.at[ch, :, 1 - x],
            x_box.at[ch],
            r["gx_send"].at[ch],
            r["gx_recv"].at[ch],
            (e, across),
        )

    batch = chunks // BATCHES

    def z_hop(group, step, origin):
        zz = (z + step) % lines
        span = pl.ds(group * batch, batch)
        return remote(
            x_box.at[span, zz],
            z_box.at[origin, span],
            r["gz_send"].at[group, step],
            r["gz_recv"].at[group, origin],
            (e, 2 * zz + x),
        )

    def all_hop(group, step, origin):
        span = pl.ds(group * batch, batch)
        return remote(
            all_box.at[e, span],
            all_box.at[origin, span],
            r["ga_send"].at[group, step],
            r["ga_recv"].at[group, origin],
            ((e + step) % experts, s),
        )

    def dense_event(it):
        def stage_of(number):
            ch = it - HOPS[number]
            return ch, (ch >= 0) & (ch < chunks)

        ch0, on0 = stage_of(0)

        @pl.when(on0)
        def _():
            core_hop(ch0).start()

        ch1, on1 = stage_of(1)

        @pl.when(on1)
        def _():
            core_hop(ch1).wait_recv()
            core_box[ch1] = summed(core_box[ch1], dense[ch1 % ring, :, :, core])
            y_hop(ch1).start()
            core_hop(ch1).wait_send()

        ch2, on2 = stage_of(2)

        @pl.when(on2)
        def _():
            y_hop(ch2).wait_recv()
            y_box[ch2] = summed(y_box[ch2], core_box[ch2, :, :, half])
            x_hop(ch2).start()

        ch3, on3 = stage_of(3)

        @pl.when(on3)
        def _():
            x_hop(ch3).wait_recv()
            x_box[ch3] = summed(x_box[ch3], y_box[ch3, :, x])

            @pl.when(ch3 % batch == batch - 1)
            def _():
                for step in range(1, lines):
                    z_hop(ch3 // batch, step, z).start()

    def dense_meet(group):
        span = pl.ds(group * batch, batch)
        total = x_box[span, z].astype(F32)
        for step in range(1, lines):
            origin = (z + lines - step) % lines
            z_hop(group, step, origin).wait_recv()
            total = total + z_box[origin, span].astype(F32)
        all_box[e, span] = total.astype(BF)
        for step in range(1, experts):
            all_hop(group, step, e).start()

    def dense_write(group):
        for step in range(1, experts):
            all_hop(group, step, (e + experts - step) % experts).wait_recv()
        for owner in range(experts):
            place = (owner % 2) * 2 + owner // 2
            at = slice(place * quarter, (place + 1) * quarter)
            for ch in range(group * batch, (group + 1) * batch):
                total = all_box[owner, ch].astype(F32)
                if ch < out_chunks:
                    spot = slice(ch * chunk_cols, (ch + 1) * chunk_cols)
                    r["own_out_w_out"][at, spot] = total
                else:
                    for part in range(3):
                        begin_at = part * D + (ch - out_chunks) * LANES
                        r["own_qkv_out"][at, begin_at : begin_at + LANES] = total[
                            :, part * LANES : (part + 1) * LANES
                        ]

    def dense_events_sent():
        def one(ch, _):
            y_hop(ch).wait_send()
            x_hop(ch).wait_send()
            return 0

        lax.fori_loop(0, chunks, one, 0)
        for group in range(BATCHES):
            for step in range(1, lines):
                z_hop(group, step, z).wait_send()
            for step in range(1, experts):
                all_hop(group, step, e).wait_send()

    grad_normed = ffn.at[tok_rows : 2 * tok_rows, :]
    grad_normed[...] = jnp.zeros_like(grad_normed)
    out_grads = dot_tn(mixed[...], grad_attn[...])
    for ch in range(out_chunks):
        dense[ch] = as_chunk(out_grads[:, ch * chunk_cols : (ch + 1) * chunk_cols])

    def attend_back(p):
        query, key, value = heads[p], heads[pairs + p], heads[2 * pairs + p]
        upper = dot_nt(grad_attn[...], weights[rows(p, LANES), 3 * D : 4 * D]).astype(BF)
        grads = []
        for head in range(2):
            scores = dot_nt(key, one_head(query, head)) * score_scale
            probs = jnp.where(
                allowed_pairs(), jnp.exp(scores - log_sums[p, head : head + 1, :]), 0.0
            )
            grad_probs = dot_nt(value, one_head(upper, head))
            delta = jnp.sum(grad_probs * probs, axis=0, keepdims=True)
            grad_scores = (probs * (grad_probs - delta)).astype(BF)
            grads.append(
                (
                    dot_tn(grad_scores, key),
                    dot(grad_scores, query),
                    dot(probs.astype(BF), upper),
                )
            )
        joined = [jnp.where(first_head, a, b) for a, b in zip(*grads)]
        parts = []
        for part in range(3):
            block = joined[part]
            if part < 2:
                block = block * score_scale
                block = block * cosine[...] - swap_halves(block) * sine[...]
            parts.append(block.astype(BF))
        total = grad_normed[...]
        for part in range(3):
            spot = pl.ds(pl.multiple_of(part * D + p * LANES, LANES), LANES)
            total = total + dot_nt(parts[part], weights[:, spot])
        grad_normed[...] = total
        dense[(out_chunks + p) % ring] = as_chunk(
            dot_tn(normed[...], jnp.concatenate(parts, axis=1))
        )

    def back_step(it, _):
        @pl.when(it >= out_chunks)
        def _():
            attend_back(it - out_chunks)

        dense_event(it)

        @pl.when(it == out_chunks + 2)
        def _():
            sum_passed(4, 1)

        @pl.when(it == out_chunks + 5)
        def _():
            sum_passed(5, 1)

        return 0

    def tail_step(it, _):
        dense_event(it)

        return 0

    lax.fori_loop(0, chunks, back_step, 0)

    gain_sum = jnp.zeros((1, D), F32)
    for block in range(row_blocks):
        at = slice(block * LANES, (block + 1) * LANES)
        inputs = tokens[at, :].astype(F32)
        scale = cols[at, 0:1]
        grad_norm = grad_normed[at, :]
        gain_sum = gain_sum + jnp.sum(grad_norm * inputs * scale, axis=0, keepdims=True)
        scaled = gain_one * grad_norm
        grad_hidden[at, :] = (
            grad_hidden[at, :]
            + scale * scaled
            - inputs * (scale * scale * scale) * jnp.mean(scaled * inputs, axis=1, keepdims=True)
        )
    own_sums[gate_cols + 7 : gate_cols + 8, :] = gain_sum

    store("tokens_out").start()

    layer_sums = r["layer_sums"]

    def final_step(index, _):
        sum_final(turn(index))
        return 0

    def sums_z(step, origin):
        return remote(
            sums.at[z],
            sums.at[origin],
            r["az_send"].at[step],
            r["az_recv"].at[origin],
            (e, ((z + step) % lines) * 2 + x),
        )

    def sums_layer(step, side, origin):
        return remote(
            layer_sums.at[mine],
            layer_sums.at[origin],
            r["al_send"].at[step, side],
            r["al_recv"].at[origin],
            ((e + step) % experts, 2 * z + side),
        )

    sums[z] = own_sums[...].astype(BF)
    for step in range(1, lines):
        sums_z(step, z).start()
    lax.fori_loop(chunks, chunks + HOPS[3], tail_step, 0)
    lax.fori_loop(0, lines - 1, final_step, 0)
    for step in range(1, lines):
        sums_z(step, (z + lines - step) % lines).wait_recv()
    total = sums[0].astype(F32)
    for zz in range(1, lines):
        total = total + sums[zz].astype(F32)
    layer_sums[mine] = total
    others(lambda step, other, side, origin: sums_layer(step, side, mine).start())
    sum_passed(6, len(sum_passes))
    for group in range(BATCHES):
        dense_meet(group)
    final_step(lines - 1, 0)
    for group in range(BATCHES):
        dense_write(group)
    others(lambda step, other, side, origin: sums_layer(step, side, origin).wait_recv())
    total = layer_sums[0]
    for other in range(1, layer):
        total = total + layer_sums[other]
    mine_only = pltpu.roll(total, (2 * lines - s) * share % D, 1)[:, 0:share]
    r["own_gate_out"][...] = mine_only[0:gate_cols, :]
    r["own_const_out"][...] = mine_only[gate_cols : gate_cols + 4, :]
    r["own_vec_out"][...] = mine_only[gate_cols + 4 : gate_cols + 6, :]
    r["own_two_out"][...] = mine_only[gate_cols + 6 : gate_cols + 7, :]
    r["own_one_out"][...] = mine_only[gate_cols + 7 : gate_cols + 8, :]
    r["own_mix_out"][...] = total[mix_rows : mix_rows + gate_cols, 0:gate_cols]

    for jj in range(lines):
        final_hop(jj).wait_recv()
        for part in range(2):
            up_out[:, up_columns(part, jj, 1 - x)] = final_box[
                jj, :, part * hidden_block : (part + 1) * hidden_block
            ].astype(F32)

    for name in OUT_NAMES:
        if name not in ("block_out", "prev_out", "tokens_out"):
            store(name).start()

    for kind in range(2):
        dense_sent(kind)
    chain_sent()
    for step in range(1, 2 * lines):
        small_copy(step, s).wait_send()
    for which in range(2):
        others(lambda step, other, side, origin: come(which, other, side, e, x).wait_send())
    sum_sent()
    for jj in range(lines):
        final_hop(jj).wait_send()
    dense_events_sent()
    for step in range(1, lines):
        sums_z(step, z).wait_send()
    others(lambda step, other, side, origin: sums_layer(step, side, mine).wait_send())
    for name in OUT_NAMES:
        store(name).wait()

SMALL_ROWS = 24
IN_NAMES = (
    "length", "tokens", "out_grad", "routes_in", "order_row", "prev_in", "mix",
    "cosine", "sine", "qkv_in", "out_in", "gate_in", "const_in", "vec_in", "one_in", "two_in",
    "up_in", "down_in",
)
LOADED = (
    "qkv_in", "gate_in", "const_in", "vec_in", "one_in", "two_in", "routes_in", "prev_in",
    "order_row", "tokens", "out_in", "down_in", "mix", "cosine", "sine", "out_grad",
)
OUT_NAMES = (
    "block_out", "tokens_out", "prev_out", "qkv_out", "out_w_out", "gate_out", "const_out",
    "vec_out", "one_out", "two_out", "mix_out", "up_out", "down_out",
)


def scratch_list(dims, held):
    tok_rows, experts, lines, share, hidden_block, capacity, gate_cols = dims
    pairs = D // LANES
    chunk_cols = 3 * LANES
    chunks = D // chunk_cols + pairs
    slots = experts * capacity
    gathered = 2 * experts * capacity
    quarter = share // 4
    last = lines - 1
    wide = 2 * hidden_block
    vmem = {
        "weights": ((D, 4 * D), BF),
        "small": ((D, LANES), BF),
        "up": ((lines, D, wide), BF),
        "down": ((lines, hidden_block, D), BF),
        "stage": ((lines, share, wide), BF),
        "put": ((2, slots, tok_rows), BF),
        "take": ((2, tok_rows, slots), BF),
        "rows": ((8, D), F32),
        "cols": ((tok_rows, 16), F32),
        "normed": ((tok_rows, D), BF),
        "heads": ((3 * pairs, tok_rows, LANES), BF),
        "mixed": ((tok_rows, D), BF),
        "log_sums": ((pairs, 8, tok_rows), F32),
        "hidden": ((tok_rows, D), F32),
        "normed_low": ((tok_rows, D), BF),
        "grad_low": ((2 * tok_rows, D), BF),
        "sent": ((gathered, D), BF),
        "sent_wide": ((slots, D + LANES), BF),
        "gate_parts": ((2, tok_rows, LANES), BF),
        "buffer": ((gathered, D + LANES), BF),
        "slot_grad": ((gathered, D), BF),
        "up_sum": ((lines, D, wide), BF),
        "down_sum": ((lines, hidden_block, D), BF),
        "up_box": ((2, last, lines, 2 * share, wide), BF),
        "down_box": ((lines + 1, hidden_block, D), BF),
        "final_box": ((lines, share, wide), BF),
        "ffn": ((gathered, D), F32),
        "slot_back": ((gathered, D), F32),
        "act": ((gathered, hidden_block), BF),
        "grad_gu": ((gathered, wide), BF),
        "back_box": ((2, 2, slots, D), BF),
        "grad_attn": ((tok_rows, D), BF),
        "thin": ((tok_rows, LANES), BF),
        "wide": ((tok_rows, LANES), BF),
        "grad_logits": ((tok_rows, gate_cols), F32),
        "sums": ((lines, SMALL_ROWS, D), BF),
        "own_sums": ((SMALL_ROWS, D), F32),
        "layer_sums": ((2 * experts, SMALL_ROWS, D), F32),
        "dense": ((RING, lines, 2, 2, 2, quarter, chunk_cols), BF),
        "core_box": ((chunks, lines, 2, 2, quarter, chunk_cols), BF),
        "y_box": ((chunks, lines, 2, quarter, chunk_cols), BF),
        "x_box": ((chunks, lines, quarter, chunk_cols), BF),
        "z_box": ((lines, chunks, quarter, chunk_cols), BF),
        "all_box": ((experts, chunks, quarter, chunk_cols), BF),
        "pack": ((LANES, LANES), F32),
        "token_rows": ((16, tok_rows), F32),
        "token_cols": ((tok_rows, 16), F32),
    }
    vmem.update(held)
    sems = {
        "in_sem": (len(LOADED),),
        "out_sem": (len(OUT_NAMES),),
        "up_sem": (2, lines, 2),
        "dz_send": (2, 2, last),
        "dx_send": (2, lines),
        "dc_send": (2, lines, 2),
        "d_recv": (2, lines, 2, 2),
        "dy_send": (2, lines, 2),
        "dr_send": (2, lines, 2),
        "dy_recv": (2, lines, 2, 2),
        "sm_send": (2 * lines,),
        "sm_recv": (2 * lines,),
        "ux_send": (lines,),
        "ux_recv": (lines,),
        "ch_send": (1 + PARTS, 2, last, lines),
        "ch_recv": (1 + PARTS, 2, last, lines),
        "go_send": (2, experts, 2),
        "go_recv": (2, 2 * experts),
        "come_send": (2, experts, 2),
        "come_recv": (2, experts, 2),
        "ru_send": (2, last, lines),
        "ru_recv": (2, last, lines),
        "rd_send": (2, lines, PARTS),
        "rd_recv": (2, lines, PARTS),
        "fx_send": (lines,),
        "fx_recv": (lines,),
        "gc_send": (chunks,),
        "gc_recv": (chunks,),
        "gy_send": (chunks,),
        "gy_recv": (chunks,),
        "gx_send": (chunks,),
        "gx_recv": (chunks,),
        "gz_send": (BATCHES, lines),
        "gz_recv": (BATCHES, lines),
        "ga_send": (BATCHES, experts),
        "ga_recv": (BATCHES, experts),
        "az_send": (lines,),
        "az_recv": (lines,),
        "al_send": (experts, 2),
        "al_recv": (2 * experts,),
    }
    names = tuple(vmem) + tuple(sems)
    shapes = [pltpu.VMEM(*spec) for spec in vmem.values()]
    shapes += [pltpu.SemaphoreType.DMA(shape) for shape in sems.values()]
    return names, shapes


def kernel_body(
    tokens,
    seq_lengths,
    routes,
    pair_order,
    prev_logits,
    out_grad,
    qkv_weight,
    out_weight,
    gate_weight,
    const_weight,
    const_vector,
    norm1_gain,
    norm2_gain,
    gate_mix,
    expert_up,
    expert_down,
):
    tok_rows = tokens.shape[0]
    experts = lax.axis_size("expert")
    shards = lax.axis_size("shard")
    share = qkv_weight.shape[0]
    gate_cols = gate_weight.shape[1]
    hidden_block = expert_down.shape[1]
    capacity = 2 * tok_rows // (experts + 4)
    dims = (tok_rows, experts, shards // 2, share, hidden_block, capacity, gate_cols)
    cosine, sine_table = turn_tables(tok_rows)
    args = (
        seq_lengths,
        tokens,
        out_grad,
        routes.T,
        pair_order,
        prev_logits.T,
        gate_mix,
        cosine,
        sine_table,
        qkv_weight,
        out_weight,
        gate_weight.T,
        const_weight.T,
        const_vector.T,
        norm1_gain[None],
        norm2_gain[None],
        expert_up[0],
        expert_down[0],
    )
    results = (
        ((tok_rows, D), BF),
        ((tok_rows, D), F32),
        ((gate_cols, tok_rows), F32),
        ((share, 3 * D), F32),
        ((share, D), F32),
        ((gate_cols, share), F32),
        ((4, share), F32),
        ((2, share), F32),
        ((1, share), F32),
        ((1, share), F32),
        ((gate_cols, gate_cols), F32),
        ((share, 2 * FF), F32),
        ((hidden_block, D), F32),
    )
    held = {
        "own_" + name: (arg.shape, arg.dtype)
        for name, arg in zip(IN_NAMES, args)
        if name in LOADED and name not in ("qkv_in", "out_in", "down_in")
    }
    held.update(
        {"own_" + name: spec for name, spec in zip(OUT_NAMES, results) if name != "tokens_out"}
    )
    names, shapes = scratch_list(dims, held)
    anywhere = pl.BlockSpec(memory_space=pl.ANY)
    outs = pl.pallas_call(
        functools.partial(step_kernel, dims, names),
        out_shape=tuple(jax.ShapeDtypeStruct(*spec) for spec in results),
        in_specs=[pl.BlockSpec(memory_space=pltpu.SMEM)] + [anywhere] * (len(args) - 1),
        out_specs=(anywhere,) * len(OUT_NAMES),
        scratch_shapes=shapes,
        compiler_params=pltpu.CompilerParams(
            collective_id=0, has_side_effects=True, vmem_limit_bytes=VMEM_BYTES
        ),
        name="step",
    )(*args)
    (
        block_out,
        tokens_grad,
        prev_grad,
        qkv_grad,
        out_w_grad,
        gate_grad,
        const_grad,
        vec_grad,
        one_grad,
        two_grad,
        mix_grad,
        up_grad,
        down_grad,
    ) = hand_over(outs)
    return (
        block_out,
        tokens_grad,
        prev_grad.T,
        qkv_grad,
        out_w_grad,
        gate_grad.T,
        const_grad.T,
        vec_grad.T,
        one_grad[0],
        two_grad[0],
        mix_grad,
        up_grad[None],
        down_grad[None],
    )


def copy_kernel(count, *refs):
    held = refs[2 * count : 3 * count]
    in_sems, out_sems = refs[3 * count :]
    reads = [pltpu.make_async_copy(refs[i], held[i], in_sems.at[i]) for i in range(count)]
    writes = [
        pltpu.make_async_copy(held[i], refs[count + i], out_sems.at[i]) for i in range(count)
    ]
    for copy in reads:
        copy.start()
    for read, write in zip(reads, writes):
        read.wait()
        write.start()
    for copy in writes:
        copy.wait()


def hand_over(arrays):
    count = len(arrays)
    anywhere = pl.BlockSpec(memory_space=pl.ANY)
    return pl.pallas_call(
        functools.partial(copy_kernel, count),
        out_shape=tuple(jax.ShapeDtypeStruct(a.shape, a.dtype) for a in arrays),
        in_specs=[anywhere] * count,
        out_specs=(anywhere,) * count,
        scratch_shapes=[pltpu.VMEM(a.shape, a.dtype) for a in arrays]
        + [pltpu.SemaphoreType.DMA((count,))] * 2,
        name="hand_over",
    )(*arrays)


def turn_tables(tok_rows):
    half_dim = HEAD_DIM // 2
    steps = np.arange(half_dim, dtype=np.float32) * np.float32(2.0 / HEAD_DIM)
    frequency = np.power(np.float32(rotary_base), -steps).astype(np.float32)
    angles = np.arange(tok_rows, dtype=np.float32)[:, None] * frequency[None, :]
    cosine = np.cos(angles.astype(np.float64)).astype(np.float32)
    sine = np.sin(angles.astype(np.float64)).astype(np.float32)
    cosine = np.tile(cosine, (1, LANES // half_dim))
    sine = np.tile(np.concatenate([-sine, sine], axis=1), (1, LANES // HEAD_DIM))
    return jnp.asarray(cosine), jnp.asarray(sine)


def fits_kernel(mesh):
    experts, shards = mesh.shape["expert"], mesh.shape["shard"]
    share, hidden_block = D // shards, FF // shards
    return (
        experts == 4
        and shards % 2 == 0
        and share % 96 == 0
        and hidden_block % LANES == 0
    )


def solution(mesh):
    placed = (
        P(("expert", "shard"), None),
        P(("expert", "shard")),
        P(("expert", "shard"), None),
        P(("expert", "shard"), None),
        P(("expert", "shard"), None),
        P(("expert", "shard"), None),
        P("shard", None),
        P("shard", None),
        P("shard", None),
        P("shard", None),
        P("shard", None),
        P("shard"),
        P("shard"),
        P(),
        P("expert", "shard", None),
        P("expert", "shard", None),
    )
    return jax.shard_map(
        kernel_body if fits_kernel(mesh) else body,
        mesh=mesh,
        in_specs=placed,
        out_specs=(
            P(("expert", "shard"), None),
            P(("expert", "shard"), None),
            P(("expert", "shard"), None),
            P("shard", None),
            P("shard", None),
            P("shard", None),
            P("shard", None),
            P("shard", None),
            P("shard"),
            P("shard"),
            P(),
            P("expert", "shard", None),
            P("expert", "shard", None),
        ),
        check_vma=False,
    )
```

```python
import functools

import jax
import jax.numpy as jnp
import numpy as np
from jax import lax
from jax.experimental import pallas as pl
from jax.experimental.pallas import tpu as pltpu
from jax.sharding import PartitionSpec as P

D = 768
FF = 2048
HEADS = 12
HEAD_DIM = 64


norm_eps = 1e-06
rotary_base = 10000.0
highest = lax.Precision.HIGHEST


def tables(tok_rows, head_dim):
    half_dim = head_dim // 2
    frequency = rotary_base ** (-(jnp.arange(half_dim, dtype=jnp.float32) * 2.0 / head_dim))
    angles = jnp.arange(tok_rows, dtype=jnp.float32)[:, None] * frequency[None, :]
    return (jnp.cos(angles)[:, None, :], jnp.sin(angles)[:, None, :])


def rotate(field, cosine, sine_table):
    half_dim = field.shape[-1] // 2
    first_half = field[..., :half_dim]
    second_half = field[..., half_dim:]
    return jnp.concatenate(
        [
            first_half * cosine - second_half * sine_table,
            second_half * cosine + first_half * sine_table,
        ],
        axis=-1,
    )


def place_pairs(route_rows, order, length, experts_ffn, capacity):
    tok_rows = route_rows.shape[0]
    token_ids = jnp.arange(tok_rows, dtype=jnp.int32)
    pair_valid = jnp.repeat(token_ids < length, 2)
    expert_flat = route_rows.reshape(-1)
    placed_expert = expert_flat[order]
    placed_live = pair_valid[order] & (placed_expert < experts_ffn)
    one_hot = (
        placed_expert[:, None] == jnp.arange(experts_ffn, dtype=jnp.int32)[None, :]
    ) & placed_live[:, None]
    counts = jnp.cumsum(one_hot.astype(jnp.int32), axis=0)
    slot_index = jnp.sum(jnp.where(one_hot, counts - 1, 0), axis=1)
    kept_pairs = placed_live & (slot_index < capacity)
    dest_placed = jnp.where(
        kept_pairs, placed_expert * capacity + slot_index, experts_ffn * capacity
    )
    pair_dest = jnp.zeros((2 * tok_rows,), jnp.int32).at[order].set(dest_placed)
    slot_pair = (
        jnp.full((experts_ffn * capacity,), 2 * tok_rows, jnp.int32)
        .at[dest_placed]
        .set(order, mode="drop")
    )
    return (pair_dest, slot_pair)


def attend_head(head, allowed, score_scale):
    query, keys_rot, values = head
    scores = jnp.dot(query, keys_rot.T, preferred_element_type=jnp.float32) * score_scale
    scores = jnp.where(allowed, scores, -1e30)
    top_score = jnp.max(scores, axis=1, keepdims=True)
    expo = jnp.exp(scores - top_score)
    total = jnp.sum(expo, axis=1, keepdims=True)
    probs = expo / total
    mixed = jnp.dot(probs.astype(jnp.bfloat16), values, preferred_element_type=jnp.float32).astype(
        jnp.bfloat16
    )
    return (mixed, top_score + jnp.log(total))


def attend_back(head, allowed, score_scale):
    query, keys_rot, values, grad_mixed, log_total = head
    scores = jnp.dot(query, keys_rot.T, preferred_element_type=jnp.float32) * score_scale
    scores = jnp.where(allowed, scores, -1e30)
    probs = jnp.where(allowed, jnp.exp(scores - log_total), 0.0)
    grad_probs = jnp.dot(grad_mixed, values.T, preferred_element_type=jnp.float32)
    delta = jnp.sum(grad_probs * probs, axis=1, keepdims=True)
    grad_scores = (probs * (grad_probs - delta)).astype(jnp.bfloat16)
    grad_query = jnp.dot(grad_scores, keys_rot, preferred_element_type=jnp.float32) * score_scale
    grad_key = jnp.dot(grad_scores.T, query, preferred_element_type=jnp.float32) * score_scale
    grad_value = jnp.dot(
        probs.astype(jnp.bfloat16).T, grad_mixed, preferred_element_type=jnp.float32
    )
    return (grad_query, grad_key, grad_value)


def body(
    tokens,
    seq_lengths,
    routes,
    pair_order,
    prev_logits,
    out_grad,
    qkv_weight,
    out_weight,
    gate_weight,
    const_weight,
    const_vector,
    norm1_gain,
    norm2_gain,
    gate_mix,
    expert_up,
    expert_down,
):
    tok_rows = tokens.shape[0]
    experts_ffn = lax.axis_size("expert")
    capacity = 2 * tok_rows // (experts_ffn + 4)
    length = seq_lengths[0]
    order = pair_order[0]
    score_scale = HEAD_DIM ** (-0.5)
    dense_shards = (
        qkv_weight,
        out_weight,
        gate_weight,
        const_weight,
        const_vector,
        norm1_gain,
        norm2_gain,
    )
    weight_qkv, weight_out, weight_gate, weight_const, vector_const, gain_one, gain_two = (
        lax.all_gather(dense_shards[0], "shard", axis=0, tiled=True),
        lax.all_gather(dense_shards[1], "shard", axis=0, tiled=True),
        lax.all_gather(dense_shards[2], "shard", axis=0, tiled=True),
        lax.all_gather(dense_shards[3], "shard", axis=0, tiled=True),
        lax.all_gather(dense_shards[4], "shard", axis=0, tiled=True),
        lax.all_gather(dense_shards[5], "shard", axis=0, tiled=True),
        lax.all_gather(dense_shards[6], "shard", axis=0, tiled=True),
    )
    weight_up, weight_down = (
        lax.all_gather(expert_up, "shard", axis=1, tiled=True),
        lax.all_gather(expert_down, "shard", axis=1, tiled=True),
    )
    weight_up = weight_up[0]
    weight_down = weight_down[0]
    inputs = tokens.astype(jnp.float32)
    token_ids = jnp.arange(tok_rows, dtype=jnp.int32)
    valid_mask = (token_ids < length).astype(jnp.float32)[:, None]
    gain_first = gain_one.astype(jnp.float32)
    gain_second = gain_two.astype(jnp.float32)
    scale_one = lax.rsqrt(jnp.mean(inputs * inputs, axis=1, keepdims=True) + norm_eps)
    normed = (inputs * scale_one * gain_first).astype(jnp.bfloat16)
    qkv_all = jnp.dot(normed, weight_qkv, preferred_element_type=jnp.float32)
    cosine, sine_table = tables(tok_rows, HEAD_DIM)

    def heads_first(block):
        return jnp.transpose(block, (1, 0, 2)).astype(jnp.bfloat16)

    query = heads_first(
        rotate(qkv_all[:, :D].reshape(tok_rows, HEADS, HEAD_DIM), cosine, sine_table)
    )
    keys_rot = heads_first(
        rotate(qkv_all[:, D : 2 * D].reshape(tok_rows, HEADS, HEAD_DIM), cosine, sine_table)
    )
    values = heads_first(qkv_all[:, 2 * D :].reshape(tok_rows, HEADS, HEAD_DIM))
    allowed = (token_ids[None, :] <= token_ids[:, None]) & (token_ids[None, :] < length)
    mixed_heads, log_totals = lax.map(
        lambda head: attend_head(head, allowed, score_scale), (query, keys_rot, values)
    )
    mixed = jnp.transpose(mixed_heads, (1, 0, 2)).reshape(tok_rows, D)
    hidden = inputs + jnp.dot(mixed, weight_out, preferred_element_type=jnp.float32)
    scale_two = lax.rsqrt(jnp.mean(hidden * hidden, axis=1, keepdims=True) + norm_eps)
    normed_two = hidden * scale_two * gain_second
    normed_low = normed_two.astype(jnp.bfloat16)
    mixer = gate_mix.astype(jnp.float32)
    logits = jnp.dot(normed_low, weight_gate, preferred_element_type=jnp.float32) + jnp.dot(
        prev_logits, mixer, precision=highest
    )
    chosen = jnp.take_along_axis(logits, routes, axis=1)
    gate_exp = jnp.exp(chosen - jnp.max(chosen, axis=1, keepdims=True))
    gates = gate_exp / jnp.sum(gate_exp, axis=1, keepdims=True)
    pair_dest, slot_pair = place_pairs(routes, order, length, experts_ffn, capacity)
    padded = jnp.concatenate([normed_low, jnp.zeros((1, D), jnp.bfloat16)], axis=0)
    send_rows = padded[slot_pair // 2].reshape(experts_ffn, capacity, D)
    received = lax.all_to_all(send_rows, "expert", split_axis=0, concat_axis=0, tiled=True)
    lead_shape = received.shape[:2]
    flat_rows = received.reshape(-1, D)
    gate_up = jnp.dot(flat_rows, weight_up, preferred_element_type=jnp.float32)
    activated = (jax.nn.silu(gate_up[:, :FF]) * gate_up[:, FF:]).astype(jnp.bfloat16)
    expert_out = jnp.dot(activated, weight_down, preferred_element_type=jnp.float32).astype(
        jnp.bfloat16
    )
    received, gate_up, activated, expert_out = (
        received,
        gate_up.reshape(lead_shape + (2 * FF,)),
        activated.reshape(lead_shape + (FF,)),
        expert_out.reshape(received.shape),
    )
    returned = lax.all_to_all(expert_out, "expert", split_axis=0, concat_axis=0, tiled=True)
    returned_pad = jnp.concatenate(
        [returned.reshape(-1, D), jnp.zeros((1, D), jnp.bfloat16)], axis=0
    )
    pair_ffn = returned_pad[pair_dest].astype(jnp.float32).reshape(tok_rows, 2, D)
    vector_float = vector_const.astype(jnp.float32)
    const_logits = jnp.dot(normed_low, weight_const, preferred_element_type=jnp.float32).reshape(
        tok_rows, 2, 2
    )
    const_exp = jnp.exp(const_logits - jnp.max(const_logits, axis=2, keepdims=True))
    coefs = const_exp / jnp.sum(const_exp, axis=2, keepdims=True)
    const_out = (
        coefs[..., 0:1] * normed_two[:, None, :] + coefs[..., 1:2] * vector_float.T[None, :, :]
    )
    const_select = (
        routes[:, :, None] == experts_ffn + 2 + jnp.arange(2, dtype=jnp.int32)[None, None, :]
    ).astype(jnp.float32)
    copy_select = (routes == experts_ffn + 1).astype(jnp.float32)[:, :, None]
    pair_out = (
        pair_ffn
        + copy_select * normed_two[:, None, :]
        + jnp.einsum("tkc,tcd->tkd", const_select, const_out, precision=highest)
    )
    mixture = jnp.sum(gates[:, :, None] * pair_out, axis=1)
    block_out = (valid_mask * (hidden + mixture)).astype(jnp.bfloat16)
    back_dense = (
        lax.all_gather(dense_shards[0], "shard", axis=0, tiled=True),
        lax.all_gather(dense_shards[1], "shard", axis=0, tiled=True),
        lax.all_gather(dense_shards[2], "shard", axis=0, tiled=True),
        lax.all_gather(dense_shards[3], "shard", axis=0, tiled=True),
        lax.all_gather(dense_shards[4], "shard", axis=0, tiled=True),
        lax.all_gather(dense_shards[5], "shard", axis=0, tiled=True),
        lax.all_gather(dense_shards[6], "shard", axis=0, tiled=True),
    )
    back_up, back_down = (
        lax.all_gather(expert_up, "shard", axis=1, tiled=True),
        lax.all_gather(expert_down, "shard", axis=1, tiled=True),
    )
    back_up = back_up[0]
    back_down = back_down[0]
    back_qkv, back_out, back_gate, back_const = (
        back_dense[0],
        back_dense[1],
        back_dense[2],
        back_dense[3],
    )
    grad_rows = out_grad.astype(jnp.float32) * valid_mask
    grad_gates = jnp.sum(grad_rows[:, None, :] * pair_out, axis=2)
    grad_pairs = gates[:, :, None] * grad_rows[:, None, :]
    grad_chosen = gates * (grad_gates - jnp.sum(gates * grad_gates, axis=1, keepdims=True))
    route_hot = (
        routes[:, :, None] == jnp.arange(experts_ffn + 4, dtype=jnp.int32)[None, None, :]
    ).astype(jnp.float32)
    grad_logits = jnp.sum(route_hot * grad_chosen[:, :, None], axis=1)
    prev_grad = jnp.dot(grad_logits, mixer.T, precision=highest)
    mix_term = jnp.dot(prev_logits.T, grad_logits, precision=highest)
    logit_low = grad_logits.astype(jnp.bfloat16)
    gate_term = jnp.dot(normed_low.T, logit_low, preferred_element_type=jnp.float32)
    grad_normed = jnp.dot(logit_low, back_gate.T, preferred_element_type=jnp.float32)
    grad_flat = jnp.concatenate(
        [grad_pairs.reshape(2 * tok_rows, D).astype(jnp.bfloat16), jnp.zeros((1, D), jnp.bfloat16)],
        axis=0,
    )
    grad_send = grad_flat[slot_pair].reshape(experts_ffn, capacity, D)
    grad_recv = lax.all_to_all(grad_send, "expert", split_axis=0, concat_axis=0, tiled=True)
    grad_slots = grad_recv.reshape(-1, D)
    down_term = jnp.dot(activated.reshape(-1, FF).T, grad_slots, preferred_element_type=jnp.float32)
    grad_act = jnp.dot(grad_slots, back_down.T, preferred_element_type=jnp.float32)
    gate_part = gate_up[..., :FF].reshape(-1, FF)
    up_part = gate_up[..., FF:].reshape(-1, FF)
    sigmoid_gate = jax.nn.sigmoid(gate_part)
    grad_gate_up = jnp.concatenate(
        [
            grad_act * up_part * sigmoid_gate * (1.0 + gate_part * (1.0 - sigmoid_gate)),
            grad_act * gate_part * sigmoid_gate,
        ],
        axis=1,
    ).astype(jnp.bfloat16)
    up_term = jnp.dot(received.reshape(-1, D).T, grad_gate_up, preferred_element_type=jnp.float32)
    grad_input = (
        jnp.dot(grad_gate_up, back_up.T, preferred_element_type=jnp.float32)
        .astype(jnp.bfloat16)
        .reshape(received.shape)
    )
    grad_back = lax.all_to_all(grad_input, "expert", split_axis=0, concat_axis=0, tiled=True)
    back_pad = jnp.concatenate([grad_back.reshape(-1, D), jnp.zeros((1, D), jnp.bfloat16)], axis=0)
    grad_normed = grad_normed + jnp.sum(
        back_pad[pair_dest].astype(jnp.float32).reshape(tok_rows, 2, D), axis=1
    )
    grad_normed = grad_normed + jnp.sum(copy_select * grad_pairs, axis=1)
    grad_const_out = jnp.einsum("tkc,tkd->tcd", const_select, grad_pairs, precision=highest)
    grad_first = jnp.sum(grad_const_out * normed_two[:, None, :], axis=2)
    grad_second = jnp.sum(grad_const_out * vector_float.T[None, :, :], axis=2)
    grad_coefs = jnp.stack([grad_first, grad_second], axis=2)
    grad_const_logits = (
        coefs * (grad_coefs - jnp.sum(coefs * grad_coefs, axis=2, keepdims=True))
    ).reshape(tok_rows, 4)
    grad_normed = grad_normed + jnp.sum(coefs[..., 0:1] * grad_const_out, axis=1)
    grad_normed = grad_normed + jnp.dot(
        grad_const_logits, back_const.astype(jnp.float32).T, precision=highest
    )
    vector_term = jnp.einsum("tc,tcd->dc", coefs[..., 1], grad_const_out, precision=highest)
    const_term = jnp.dot(normed_low.astype(jnp.float32).T, grad_const_logits, precision=highest)
    second_gain_term = jnp.sum(grad_normed * hidden * scale_two, axis=0)
    scaled_two = gain_second * grad_normed
    grad_hidden = (
        grad_rows
        + scale_two * scaled_two
        - hidden * scale_two**3 * jnp.mean(scaled_two * hidden, axis=1, keepdims=True)
    )
    grad_attn_low = grad_hidden.astype(jnp.bfloat16)
    out_term = jnp.dot(mixed.T, grad_attn_low, preferred_element_type=jnp.float32)
    grad_mixed = jnp.dot(grad_attn_low, back_out.T, preferred_element_type=jnp.float32).astype(
        jnp.bfloat16
    )
    grad_mixed_heads = jnp.transpose(grad_mixed.reshape(tok_rows, HEADS, HEAD_DIM), (1, 0, 2))
    grad_query, grad_key, grad_value = lax.map(
        lambda head: attend_back(head, allowed, score_scale),
        (query, keys_rot, values, grad_mixed_heads, log_totals),
    )
    grad_query = rotate(jnp.transpose(grad_query, (1, 0, 2)), cosine, -sine_table).reshape(
        tok_rows, D
    )
    grad_key = rotate(jnp.transpose(grad_key, (1, 0, 2)), cosine, -sine_table).reshape(tok_rows, D)
    grad_value = jnp.transpose(grad_value, (1, 0, 2)).reshape(tok_rows, D)
    grad_qkv = jnp.concatenate([grad_query, grad_key, grad_value], axis=1).astype(jnp.bfloat16)
    qkv_term = jnp.dot(normed.T, grad_qkv, preferred_element_type=jnp.float32)
    grad_first_norm = jnp.dot(grad_qkv, back_qkv.T, preferred_element_type=jnp.float32)
    first_gain_term = jnp.sum(grad_first_norm * inputs * scale_one, axis=0)
    scaled_one = gain_first * grad_first_norm
    tokens_grad = (
        grad_hidden
        + scale_one * scaled_one
        - inputs * scale_one**3 * jnp.mean(scaled_one * inputs, axis=1, keepdims=True)
    )
    dense_all = (
        qkv_term,
        out_term,
        gate_term,
        const_term,
        vector_term,
        first_gain_term,
        second_gain_term,
    )
    dense_terms = (
        lax.psum_scatter(dense_all[0], "shard", scatter_dimension=0, tiled=True),
        lax.psum_scatter(dense_all[1], "shard", scatter_dimension=0, tiled=True),
        lax.psum_scatter(dense_all[2], "shard", scatter_dimension=0, tiled=True),
        lax.psum_scatter(dense_all[3], "shard", scatter_dimension=0, tiled=True),
        lax.psum_scatter(dense_all[4], "shard", scatter_dimension=0, tiled=True),
        lax.psum_scatter(dense_all[5], "shard", scatter_dimension=0, tiled=True),
        lax.psum_scatter(dense_all[6], "shard", scatter_dimension=0, tiled=True),
    )
    (
        qkv_grad,
        out_weight_grad,
        gate_grad,
        const_weight_grad,
        const_vector_grad,
        norm1_grad,
        norm2_grad,
    ) = lax.psum(
        (
            dense_terms[0],
            dense_terms[1],
            dense_terms[2],
            dense_terms[3],
            dense_terms[4],
            dense_terms[5],
            dense_terms[6],
        ),
        "expert",
    )
    mix_grad = lax.psum(mix_term, ("expert", "shard"))
    expert_up_grad, expert_down_grad = (
        lax.psum_scatter(up_term[None], "shard", scatter_dimension=1, tiled=True),
        lax.psum_scatter(down_term[None], "shard", scatter_dimension=1, tiled=True),
    )
    return (
        block_out,
        tokens_grad,
        prev_grad,
        qkv_grad,
        out_weight_grad,
        gate_grad,
        const_weight_grad,
        const_vector_grad,
        norm1_grad,
        norm2_grad,
        mix_grad,
        expert_up_grad,
        expert_down_grad,
    )


MESH = pl.DeviceIdType.MESH
BF = jnp.bfloat16
F32 = jnp.float32
LANES = 128
NEG = -1e30
VMEM_BYTES = 64 * 1024 * 1024
RING = 3
HOPS = (0, 2, 4, 6)
PARTS = 2
BATCHES = 2


def dot(a, b):
    return lax.dot_general(a, b, (((1,), (0,)), ((), ())), preferred_element_type=F32)


def dot_nt(a, b):
    return lax.dot_general(a, b, (((1,), (1,)), ((), ())), preferred_element_type=F32)


def dot_tn(a, b):
    return lax.dot_general(a, b, (((0,), (0,)), ((), ())), preferred_element_type=F32)


def iota(shape, dim):
    return lax.broadcasted_iota(jnp.int32, shape, dim)


def remote(src, dst, send_sem, recv_sem, target):
    return pltpu.make_async_remote_copy(
        src_ref=src,
        dst_ref=dst,
        send_sem=send_sem,
        recv_sem=recv_sem,
        device_id=target,
        device_id_type=MESH,
    )


def swap_halves(block):
    half = HEAD_DIM // 2
    width = block.shape[1]
    lower = (iota(block.shape, 1) % HEAD_DIM) < half
    return jnp.where(
        lower, pltpu.roll(block, width - half, 1), pltpu.roll(block, half, 1)
    )


def step_kernel(dims, scratch_names, *refs):
    (tok_rows, experts, lines, share, hidden_block, capacity, gate_cols) = dims
    names = IN_NAMES + OUT_NAMES + scratch_names
    r = dict(zip(names, refs))
    pairs = D // LANES
    layer = 2 * experts
    slots = experts * capacity
    quarter = share // 4
    chunk_cols = 3 * LANES
    out_chunks = D // chunk_cols
    chunks = out_chunks + pairs
    half_ffn = lines * 2 * hidden_block
    const_col = gate_cols
    vec_col = gate_cols + 8
    row_blocks = tok_rows // LANES

    e = lax.axis_index("expert")
    s = lax.axis_index("shard")
    z = s // 2
    x = s % 2
    core = e % 2
    half = e // 2
    facing = 2 * (1 - half) + core
    across = 2 * z + 1 - x
    twin = e + 1 - 2 * core
    mine = 2 * e + x

    def rows(index, size):
        return pl.ds(pl.multiple_of(index * size, size), size)

    weights, small = r["weights"], r["small"]
    up, down, stage = r["up"], r["down"], r["stage"]
    own_rows = rows(s, share)

    def up_columns(part, jj, xx):
        return pl.ds(
            pl.multiple_of(part * FF + hidden_block * (2 * jj + xx), hidden_block), hidden_block
        )

    def up_load(jj, part, to):
        spot = pl.ds(part * hidden_block, hidden_block)
        box = stage.at[jj, :, spot] if to == 0 else up.at[jj, own_rows, spot]
        xx = 1 - x if to == 0 else x
        return pltpu.make_async_copy(
            r["up_in"].at[:, up_columns(part, jj, xx)], box, r["up_sem"].at[to, jj, part]
        )

    direct = {
        "qkv_in": weights.at[own_rows, pl.ds(0, 3 * D)],
        "out_in": weights.at[own_rows, pl.ds(3 * D, D)],
        "down_in": down.at[z],
    }

    def load(name):
        box = direct[name] if name in direct else r["own_" + name]
        return pltpu.make_async_copy(r[name], box, r["in_sem"].at[LOADED.index(name)])

    def store(name):
        held = r["ffn"].at[0:tok_rows, :] if name == "tokens_out" else r["own_" + name]
        return pltpu.make_async_copy(held, r[name], r["out_sem"].at[OUT_NAMES.index(name)])

    load("qkv_in").start()
    for jj in range(lines):
        for part in range(2):
            up_load(jj, part, 0).start()
    for name in LOADED[1:]:
        load(name).start()
    for jj in range(lines):
        for part in range(2):
            up_load(jj, part, 1).start()

    barrier = pltpu.get_barrier_semaphore()
    met = 0
    for step in range(1, 2 * lines):
        pl.semaphore_signal(
            barrier, 1, device_id=(e, (s + step) % (2 * lines)), device_id_type=MESH
        )
        met += 1
    for step in range(1, experts):
        for side in range(2):
            pl.semaphore_signal(
                barrier, 1, device_id=((e + step) % experts, 2 * z + side), device_id_type=MESH
            )
            met += 1
    pl.semaphore_wait(barrier, met)

    def down_part(ref, index, part):
        height = hidden_block // PARTS
        return ref.at[index, pl.ds(part * height, height), :]

    def up_across(jj, origin_x):
        return remote(
            stage.at[jj],
            up.at[jj, rows(2 * z + origin_x, share), :],
            r["ux_send"].at[jj],
            r["ux_recv"].at[jj],
            (e, across),
        )

    def chain(kind, way, step, jj, zz):
        ref = up.at[jj, rows(zz, 2 * share), :] if kind == 0 else down_part(down, jj, kind - 1)
        target = s + 2 if way == 0 else s - 2
        return remote(
            ref,
            ref,
            r["ch_send"].at[kind, way, step, jj],
            r["ch_recv"].at[kind, way, step, jj],
            (e, target),
        )

    def chain_each(way, step, jj, zz, go):
        go(0, way, step, jj, zz)

        @pl.when(zz == jj)
        def _():
            for part in range(PARTS):
                go(1 + part, way, step, jj, zz)

    def begin(*which):
        chain(*which).start()

    def arrive(*which):
        chain(*which).wait_recv()

    def leave(*which):
        chain(*which).wait_send()

    def hand_on(kind, way, step, jj, zz):
        chain(kind, way, step, jj, zz).wait_recv()
        chain(kind, way, step + 1, jj, zz).start()

    def turn(index):
        return (2 * index + 1) % (lines + 1)

    def chain_ready(jj):
        for part in range(2):
            up_load(jj, part, 1).wait()
        up_across(jj, 1 - x).wait_recv()

    def chain_own(kinds, jj):
        for way, there in ((0, z + 1 < lines), (1, z > 0)):

            @pl.when(there)
            def _():
                for kind in kinds:
                    begin(kind, way, 0, jj, z)

    def chain_pass(index, step):
        @pl.when((z - 1 - step >= 0) & (z + 1 < lines))
        def _():
            chain_each(0, step, turn(index), z - 1 - step, hand_on)

        @pl.when((z + 1 + step < lines) & (z > 0))
        def _():
            chain_each(1, step, turn(index), z + 1 + step, hand_on)

    def chain_end(jj):
        for step in range(lines - 1):

            @pl.when((z - 1 - step >= 0) & (z + 1 == lines))
            def _():
                chain_each(0, step, jj, z - 1 - step, arrive)

            @pl.when((z + 1 + step < lines) & (z == 0))
            def _():
                chain_each(1, step, jj, z + 1 + step, arrive)

    def chain_sent():
        for jj in range(lines):
            for step in range(lines - 1):

                @pl.when((z - step >= 0) & (z + 1 < lines))
                def _():
                    chain_each(0, step, jj, z - step, leave)

                @pl.when((z + step < lines) & (z > 0))
                def _():
                    chain_each(1, step, jj, z + step, leave)

    passes = [(jj, step) for step in range(lines - 2) for jj in range(lines)]

    def chain_events(first, count):
        for number in range(first, min(first + count, len(passes))):
            chain_pass(*passes[number])

    for jj in range(lines):
        for part in range(2):
            up_load(jj, part, 0).wait()
    up_across(1, x).start()

    spans = ((0, 3 * D // 2), (3 * D, D // 2))

    third = share // 3

    def part_of(kind, zz, xx, cc, first, height):
        start, width = spans[kind]
        columns = pl.ds(pl.multiple_of(start + width * cc, LANES), width)
        spot = pl.ds(pl.multiple_of((2 * zz + xx) * share + first, third), height)
        return weights.at[spot, columns]

    def slab(kind, zz, xx, cc):
        return part_of(kind, zz, xx, cc, third * half, 2 * third)

    def dense_z(kind, way, step, zz):
        ref = slab(kind, zz, x, core)
        return remote(
            ref,
            ref,
            r["dz_send"].at[kind, way, step],
            r["d_recv"].at[kind, zz, x, core],
            (e, s + 2 if way == 0 else s - 2),
        )

    def dense_z_each(kind, step, go):
        @pl.when((z - step >= 0) & (z + 1 < lines))
        def _():
            go(dense_z(kind, 0, step, z - step))

        @pl.when((z + step < lines) & (z > 0))
        def _():
            go(dense_z(kind, 1, step, z + step))

    def dense_x(kind, zz):
        ref = slab(kind, zz, x, core)
        return remote(
            ref, ref, r["dx_send"].at[kind, zz], r["d_recv"].at[kind, zz, x, core], (e, across)
        )

    def dense_core(kind, zz, xx):
        ref = slab(kind, zz, xx, core)
        return remote(
            ref,
            ref,
            r["dc_send"].at[kind, zz, xx],
            r["d_recv"].at[kind, zz, xx, core],
            (twin, s),
        )

    def dense_y(kind, zz, xx):
        ref = part_of(kind, zz, xx, core, 2 * third * half, third)
        return remote(
            ref,
            ref,
            r["dy_send"].at[kind, zz, xx],
            r["dy_recv"].at[kind, zz, xx, core],
            (facing, s),
        )

    def rest_core(kind, zz, xx, cc):
        ref = part_of(kind, zz, xx, cc, 2 * third * (1 - half), third)
        return remote(
            ref,
            ref,
            r["dr_send"].at[kind, zz, xx],
            r["dy_recv"].at[kind, zz, xx, cc],
            (twin, s),
        )

    def dense_arrived(kind, zz, xx, cc):
        ref = slab(kind, zz, xx, cc)
        remote(
            ref, ref, r["dx_send"].at[kind, 0], r["d_recv"].at[kind, zz, xx, cc], (e, across)
        ).wait_recv()

    def dense_start(kind):
        dense_z_each(kind, 0, lambda copy: copy.start())
        dense_x(kind, z).start()

    def dense_forward(kind, step):
        for zz, there in ((z - 1 - step, z - 1 - step >= 0), (z + 1 + step, z + 1 + step < lines)):

            @pl.when(there)
            def _():
                dense_arrived(kind, zz, x, core)

                if step + 1 < lines - 1:

                    @pl.when((zz < z) & (z + 1 < lines))
                    def _():
                        dense_z(kind, 0, step + 1, zz).start()

                    @pl.when((zz > z) & (z > 0))
                    def _():
                        dense_z(kind, 1, step + 1, zz).start()

                dense_x(kind, zz).start()
                dense_core(kind, zz, x).start()
                dense_y(kind, zz, x).start()

    def dense_share(kind):
        for step in range(lines):
            zz = (z + lines - step) % lines
            dense_arrived(kind, zz, 1 - x, core)
            dense_core(kind, zz, 1 - x).start()
            dense_y(kind, zz, 1 - x).start()

    def dense_cross(kind):
        for step in range(lines):
            zz = (z + lines - step) % lines
            for xx in (x, 1 - x) if step > 0 else (1 - x,):
                rest_core(kind, zz, xx, core).wait_recv()
                rest_core(kind, zz, xx, core).start()

    def dense_finish(kind):
        for step in range(lines):
            zz = (z + lines - step) % lines
            for xx in (x, 1 - x) if step > 0 else (1 - x,):
                dense_arrived(kind, zz, xx, 1 - core)
                rest_core(kind, zz, xx, 1 - core).wait_recv()

    def dense_sent(kind):
        for step in range(lines - 1):
            dense_z_each(kind, step, lambda copy: copy.wait_send())
        for step in range(lines):
            zz = (z + lines - step) % lines
            dense_x(kind, zz).wait_send()
            for xx in (x, 1 - x) if step > 0 else (1 - x,):
                dense_core(kind, zz, xx).wait_send()
                dense_y(kind, zz, xx).wait_send()
                rest_core(kind, zz, xx, core).wait_send()

    def small_copy(step, origin):
        ref = small.at[rows(origin, share), :]
        return remote(
            ref,
            ref,
            r["sm_send"].at[step],
            r["sm_recv"].at[origin],
            (e, (s + step) % (2 * lines)),
        )

    load("qkv_in").wait()
    dense_start(0)
    for name in LOADED[1:]:
        load(name).wait()
    dense_start(1)
    pack = r["pack"]
    pack[...] = jnp.zeros_like(pack)
    spot = 0
    for name in ("gate_in", "const_in", "const_in", "vec_in", "one_in", "two_in"):
        height = r[name].shape[0]
        pack[spot : spot + height, 0:share] = r["own_" + name][...].astype(F32)
        spot += height
    small[rows(s, share), :] = jnp.transpose(pack[...])[0:share, :].astype(BF)
    for step in range(1, 2 * lines):
        small_copy(step, s).start()
    token_rows, token_cols = r["token_rows"], r["token_cols"]
    token_rows[...] = jnp.zeros_like(token_rows)
    token_rows[0:2, :] = r["own_routes_in"][...].astype(F32)
    token_rows[8 : 8 + gate_cols, :] = r["own_prev_in"][...]
    token_cols[...] = jnp.transpose(token_rows[...])

    tokens = r["own_tokens"]
    cols = r["cols"]
    for block in range(row_blocks):
        at = slice(block * LANES, (block + 1) * LANES)
        inputs = tokens[at, :].astype(F32)
        cols[at, 0:1] = lax.rsqrt(jnp.mean(inputs * inputs, axis=1, keepdims=True) + norm_eps)
    dense_forward(0, 0)

    dense_forward(0, 1)
    dense_forward(1, 0)

    length = r["length"][0]
    pair_ids = iota((2 * tok_rows, 2 * tok_rows), 0)
    pair_names = jnp.where(pair_ids < tok_rows, 2 * pair_ids, 2 * (pair_ids - tok_rows) + 1)
    is_at = jnp.where(pair_names == r["own_order_row"][...], 1.0, 0.0).astype(BF)
    pair_lane = iota((16, 2 * tok_rows), 1)
    pair_token = jnp.where(pair_lane < tok_rows, pair_lane, pair_lane - tok_rows)
    expert_row = iota((16, 2 * tok_rows), 0)
    route_row = jnp.concatenate([token_rows[0:1, :], token_rows[1:2, :]], axis=1)
    live = (expert_row.astype(F32) == route_row) & (expert_row < experts) & (pair_token < length)
    placed = dot(jnp.where(live, 1.0, 0.0).astype(BF), is_at)
    before = jnp.where(
        iota((2 * tok_rows, 2 * tok_rows), 0) <= iota((2 * tok_rows, 2 * tok_rows), 1), 1.0, 0.0
    ).astype(BF)
    counts = dot(placed.astype(BF), before)
    kept = jnp.where((placed > 0.5) & (counts <= capacity + 0.5), counts, 0.0)
    taken = dot_nt(kept.astype(BF), is_at)
    slot_of = jnp.sum(
        jnp.where(taken > 0.5, taken + (expert_row * capacity).astype(F32), 0.0),
        axis=0,
        keepdims=True,
    )
    slot_col = jnp.transpose(jnp.broadcast_to(slot_of, (8, 2 * tok_rows)))
    for step in range(2, lines - 1):
        dense_forward(0, step)
    for step in range(1, lines - 1):
        dense_forward(1, step)
    for index in range(1, lines):
        up_across(turn(index), x).start()
    chain_ready(1)
    chain_own((0,), 1)
    chain_own(tuple(range(1, 1 + PARTS)), z)
    put, take = r["put"], r["take"]
    for k in range(2):
        span = slice(k * tok_rows, (k + 1) * tok_rows)
        names_down = (iota((slots, tok_rows), 0) + 1).astype(F32)
        put[k] = jnp.where(slot_of[:, span] == names_down, 1.0, 0.0).astype(BF)
        names_right = (iota((tok_rows, slots), 1) + 1).astype(F32)
        take[k] = jnp.where(slot_col[span, 0:1] == names_right, 1.0, 0.0).astype(BF)

    buffer, slot_grad = r["buffer"], r["slot_grad"]
    sent, sent_wide = r["sent"], r["sent_wide"]

    def dispatch(which, step, side, origin):
        target = (e + step) % experts
        box = buffer if which == 0 else slot_grad
        source = sent_wide if which == 0 else sent
        return remote(
            source.at[rows(target, capacity), :],
            box.at[rows(origin, capacity), :],
            r["go_send"].at[which, step, side],
            r["go_recv"].at[which, origin],
            (target, 2 * z + side),
        )

    def dispatch_each(which, step, go):
        for flip in range(2):
            side = x if flip == 0 else 1 - x
            if step > 0 or flip == 1:
                go(dispatch(which, step, side, mine))

    for step in range(experts):
        chosen_rows = rows((e + step) % experts, capacity)
        sent[chosen_rows, :] = dot(
            put[0, chosen_rows, :] + put[1, chosen_rows, :], r["own_out_grad"][...]
        ).astype(BF)
    slot_grad[rows(mine, capacity), :] = sent[rows(e, capacity), :]

    for step in range(1, 2 * lines):
        origin = (s + 2 * lines - step) % (2 * lines)
        small_copy(step, origin).wait_recv()
    pick = jnp.where(iota((8, LANES), 1) == iota((8, LANES), 0) + vec_col, 1.0, 0.0).astype(BF)
    named = dot_nt(pick, small[...])
    r["rows"][...] = named
    gain_one, gain_two = named[2:3, :], named[3:4, :]
    vec_zero, vec_one = named[0:1, :], named[1:2, :]
    normed = r["normed"]
    for block in range(row_blocks):
        at = slice(block * LANES, (block + 1) * LANES)
        inputs = tokens[at, :].astype(F32)
        normed[at, :] = (inputs * cols[at, 0:1] * gain_one).astype(BF)

    dense_share(0)
    for index in range(1, lines):
        chain_ready(turn(index))
        chain_own((0,), turn(index))
    dense_cross(0)
    dense_finish(0)

    heads = r["heads"]
    cosine, sine = r["own_cosine"], r["own_sine"]

    def project(b, turn):
        wide_block = dot(normed[...], weights[:, rows(b, 2 * LANES)])
        for part in range(2):
            block = wide_block[:, part * LANES : (part + 1) * LANES]
            if turn:
                block = block * cosine[...] + swap_halves(block) * sine[...]
            heads[2 * b + part] = block.astype(BF)

    def rotated(b, _):
        project(b, True)
        return 0

    def plain(b, _):
        project(b, False)
        return 0

    lax.fori_loop(0, pairs, rotated, 0)
    lax.fori_loop(pairs, 3 * pairs // 2, plain, 0)
    dense_share(1)
    for step in range(experts):
        dispatch_each(1, step, lambda copy: copy.start())

    score_scale = HEAD_DIM ** (-0.5)
    first_head = iota((tok_rows, LANES), 1) < HEAD_DIM
    mixed, log_sums = r["mixed"], r["log_sums"]

    def allowed_pairs():
        key, query = iota((tok_rows, tok_rows), 0), iota((tok_rows, tok_rows), 1)
        return (key <= query) & (key < length)

    def one_head(block, head):
        keep = first_head if head == 0 else jnp.logical_not(first_head)
        return jnp.where(keep, block, jnp.zeros_like(block))

    def attend(p, _):
        query, key, value = heads[p], heads[pairs + p], heads[2 * pairs + p]
        results = []
        for head in range(2):
            scores = dot_nt(key, one_head(query, head)) * score_scale
            scores = jnp.where(allowed_pairs(), scores, NEG)
            top = jnp.max(scores, axis=0, keepdims=True)
            expo = jnp.exp(scores - top)
            total = jnp.sum(expo, axis=0, keepdims=True)
            probs = expo * (1.0 / total)
            log_sums[p, head : head + 1, :] = top + jnp.log(total)
            results.append(dot_tn(probs.astype(BF), value))
        mixed[:, rows(p, LANES)] = jnp.where(first_head, results[0], results[1]).astype(BF)
        return 0

    lax.fori_loop(0, pairs // 2, attend, 0)
    chain_events(0, 2)
    dense_cross(1)
    lax.fori_loop(pairs // 2, pairs, attend, 0)
    dense_finish(1)
    chain_events(2, 2)

    hidden, normed_low = r["hidden"], r["normed_low"]
    out_grad = r["own_out_grad"]
    mixer = r["own_mix"][...].astype(F32)
    grad_low, grad_sum, gate_parts = r["grad_low"], r["own_out_grad"], r["gate_parts"]
    for block in range(row_blocks):
        at = slice(block * LANES, (block + 1) * LANES)
        hid = tokens[at, :].astype(F32) + dot(mixed[at, :], weights[:, 3 * D : 4 * D])
        hidden[at, :] = hid
        scale = lax.rsqrt(jnp.mean(hid * hid, axis=1, keepdims=True) + norm_eps)
        cols[at, 1:2] = scale
        low = (hid * scale * gain_two).astype(BF)
        normed_low[at, :] = low
        logits = dot(low, small[...])
        lane = iota((LANES, LANES), 1)
        extra = jnp.zeros((LANES, gate_cols), F32)
        for i in range(gate_cols):
            extra = extra + token_cols[at, 8 + i : 9 + i] * mixer[i : i + 1, :]
        routes = token_cols[at, 0:2].astype(jnp.int32)
        chosen = []
        for k in range(2):
            hot = lane == routes[:, k : k + 1]
            part = jnp.sum(jnp.where(hot, logits, 0.0), axis=1, keepdims=True)
            chosen.append(
                part
                + jnp.sum(
                    jnp.where(
                        iota((LANES, gate_cols), 1) == routes[:, k : k + 1], extra, 0.0
                    ),
                    axis=1,
                    keepdims=True,
                )
            )
        top = jnp.maximum(chosen[0], chosen[1])
        powers = [jnp.exp(c - top) for c in chosen]
        total = powers[0] + powers[1]
        gates = [w / total for w in powers]
        on_normed = sum(
            gates[k] * (routes[:, k : k + 1] == experts + 1).astype(F32) for k in range(2)
        )
        for j in range(2):
            first = logits[:, const_col + 2 * j : const_col + 2 * j + 1]
            second = logits[:, const_col + 2 * j + 1 : const_col + 2 * j + 2]
            peak = jnp.maximum(first, second)
            first, second = jnp.exp(first - peak), jnp.exp(second - peak)
            both = first + second
            first, second = first / both, second / both
            weight = sum(
                gates[k] * (routes[:, k : k + 1] == experts + 2 + j).astype(F32)
                for k in range(2)
            )
            on_normed = on_normed + first * weight
            cols[at, 6 + 4 * j : 7 + 4 * j] = first
            cols[at, 7 + 4 * j : 8 + 4 * j] = second
            cols[at, 8 + 4 * j : 9 + 4 * j] = weight
        cols[at, 2:3] = gates[0]
        cols[at, 3:4] = gates[1]
        cols[at, 4:5] = on_normed
        valid = (iota((LANES, 1), 0) + block * LANES < length).astype(F32)
        grad = out_grad[at, :].astype(F32) * valid
        for k in range(2):
            high = gates[k].astype(BF).astype(F32)
            middle = (gates[k] - high).astype(BF).astype(F32)
            parts = jnp.where(lane == 0, high, 0.0)
            parts = jnp.where(lane == 1, middle, parts)
            gate_parts[k, at, :] = jnp.where(lane == 2, gates[k] - high - middle, parts).astype(BF)
        grad_sum[at, :] = grad.astype(BF)


    for step in range(experts):
        chosen_rows = rows((e + step) % experts, capacity)
        put_zero, put_one = put[0, chosen_rows, :], put[1, chosen_rows, :]
        sent_wide[chosen_rows, 0:D] = dot(put_zero + put_one, normed_low[...]).astype(BF)
        sent_wide[chosen_rows, D : D + LANES] = (
            dot(put_zero, gate_parts[0]) + dot(put_one, gate_parts[1])
        ).astype(BF)
        dispatch_each(0, step, lambda copy: copy.start())
    buffer[rows(mine, capacity), :] = sent_wide[rows(e, capacity), :]
    chain_events(4, len(passes))

    def others(go):
        for step in range(experts):
            other = (e + step) % experts
            for flip in range(2):
                side = x if flip == 0 else 1 - x
                if step > 0 or flip == 1:
                    go(step, other, side, 2 * other + side)

    for which in range(2):
        others(lambda step, other, side, origin: dispatch(which, step, side, origin).wait_recv())
    for block in range(2 * experts * capacity // LANES):
        at = slice(block * LANES, (block + 1) * LANES)
        shares = buffer[at, D : D + LANES].astype(F32)
        gate = shares[:, 0:1] + shares[:, 1:2] + shares[:, 2:3]
        slot_grad[at, :] = (gate * slot_grad[at, :].astype(F32)).astype(BF)

    up_sum, down_sum = r["up_sum"], r["down_sum"]
    up_box, down_box = r["up_box"], r["down_box"]
    up_out, down_out = r["own_up_out"], r["own_down_out"]
    final_send, final_box = stage, r["final_box"]
    ffn, slot_back = r["ffn"], r["slot_back"]
    last = lines - 1

    def summed(first, second):
        return (first.astype(F32) + second.astype(F32)).astype(BF)

    def up_rows(jj, zz):
        return up_sum.at[jj, rows(zz, 2 * share), :]

    def up_hop(way, k, jj, dest):
        return remote(
            up_rows(jj, dest),
            up_box.at[way, k, jj],
            r["ru_send"].at[way, k, jj],
            r["ru_recv"].at[way, k, jj],
            (e, s + 2 if way == 0 else s - 2),
        )

    def down_slot(way, jj, zz):
        return jj if way == 0 else jnp.where(jj == zz, lines, jj)

    def down_hop(way, jj, zz, part):
        return remote(
            down_part(down_sum, jj, part),
            down_part(down_box, down_slot(way, jj, zz), part),
            r["rd_send"].at[way, jj, part],
            r["rd_recv"].at[way, jj, part],
            (e, s + 2 if way == 0 else s - 2),
        )

    def final_hop(jj):
        return remote(
            final_send.at[jj],
            final_box.at[jj],
            r["fx_send"].at[jj],
            r["fx_recv"].at[jj],
            (e, across),
        )

    def sum_pass(index, k):
        for way in range(2):
            jj = turn(index)
            place = z if way == 0 else last - z
            dest = last - k + place if way == 0 else k - place

            @pl.when((place >= 1) & (place <= k) & (place < last))
            def _():
                up_hop(way, k - 1, jj, dest).wait_recv()
                spot = rows(dest, 2 * share)
                up_sum[jj, spot, :] = summed(up_sum[jj, spot, :], up_box[way, k - 1, jj])
                up_hop(way, k, jj, dest).start()

                @pl.when(dest == jj)
                def _():
                    for part in range(PARTS):
                        down_hop(way, jj, z, part).wait_recv()
                        own = down_part(down_sum, jj, part)
                        own[...] = summed(
                            own[...], down_part(down_box, down_slot(way, jj, z), part)[...]
                        )
                        down_hop(way, jj, z + 1 - 2 * way, part).start()

    def sum_final(jj):
        total = slot_back.at[0 : 2 * share, 0 : 2 * hidden_block]
        total[...] = up_sum[jj, rows(z, 2 * share), :].astype(F32)
        for way, there in ((0, z > 0), (1, z < last)):

            @pl.when(there)
            def _():
                up_hop(way, last - 1, jj, z).wait_recv()
                total[...] += up_box[way, last - 1, jj].astype(F32)

        final_send[jj] = total[rows(1 - x, share), :].astype(BF)
        final_hop(jj).start()
        own = total[rows(x, share), :]
        for part in range(2):
            up_out[:, up_columns(part, jj, x)] = own[
                :, part * hidden_block : (part + 1) * hidden_block
            ]

        @pl.when(jj == z)
        def _():
            down_out[...] = down_sum[z].astype(F32)
            for way, there in ((0, z > 0), (1, z < last)):

                @pl.when(there)
                def _():
                    for part in range(PARTS):
                        down_hop(way, jj, z, part).wait_recv()
                    down_out[...] += down_box[down_slot(way, jj, z)].astype(F32)

    def sum_start(jj):
        for way in range(2):

            @pl.when(z == (0 if way == 0 else last))
            def _():
                for k in range(last):
                    dest = last - k if way == 0 else k
                    up_hop(way, k, jj, dest).start()

                    @pl.when(dest == jj)
                    def _():
                        for part in range(PARTS):
                            down_hop(way, jj, z + 1 - 2 * way, part).start()

    sum_passes = [(jj, k) for jj in range(lines) for k in range(1, last)]

    def sum_passed(first, count):
        for number in range(first, min(first + count, len(sum_passes))):
            sum_pass(*sum_passes[number])

    def sum_sent():
        for jj in range(lines):
            for way in range(2):
                place = z if way == 0 else last - z
                for k in range(last):
                    dest = last - k + place if way == 0 else k - place

                    @pl.when((place <= k) & (place < last))
                    def _():
                        up_hop(way, k, jj, dest).wait_send()

                        @pl.when(dest == jj)
                        def _():
                            for part in range(PARTS):
                                down_hop(way, jj, z + 1 - 2 * way, part).wait_send()

    for jj in range(lines):
        up_across(jj, x).wait_send()
    act, grad_gu = r["act"], r["grad_gu"]
    back_box = r["back_box"]
    side_rows = 4 * capacity
    for which in range(2):
        for step in range(experts):
            dispatch_each(which, step, lambda copy: copy.wait_send())

    def come(which, target, side, origin_e, origin_x):
        box = grad_low if which == 0 else sent
        return remote(
            box.at[rows(2 * target + side, capacity), :],
            back_box.at[which, origin_x, rows(origin_e, capacity), :],
            r["come_send"].at[which, target, side],
            r["come_recv"].at[which, origin_e, origin_x],
            (target, 2 * z + side),
        )

    def expert_chunk(index, _):
        jj = turn(index)
        chain_end(jj)

        def forward(b, _):
            group = (half + 1 + b) % 2
            at = rows(group, side_rows)
            given = dot(buffer[at, 0:D], up[jj])
            gate, lift = given[:, 0:hidden_block], given[:, hidden_block:]
            squash = 1.0 / (1.0 + jnp.exp(-gate))
            silu = gate * squash
            low = (silu * lift).astype(BF)
            act[at, :] = low
            grad_act = dot_nt(slot_grad[at, :], down[jj])
            grads = jnp.concatenate(
                [grad_act * lift * squash * (1.0 + gate * (1.0 - squash)), grad_act * silu],
                axis=1,
            ).astype(BF)
            grad_gu[at, :] = grads
            forth = dot(low, down[jj])
            back = dot_nt(grads, up[jj])

            @pl.when(index == 0)
            def _():
                ffn[at, :] = forth
                slot_back[at, :] = back

            @pl.when((index > 0) & (index < last))
            def _():
                ffn[at, :] += forth
                slot_back[at, :] += back

            @pl.when(index == last)
            def _():
                grad_low[at, :] = (ffn[at, :] + forth).astype(BF)
                sent[at, :] = (slot_back[at, :] + back).astype(BF)
                for other in range(2):
                    target = 2 * group + other
                    for which in range(2):
                        come(which, target, 1 - x, e, x).start()

                        @pl.when(target != e)
                        def _():
                            come(which, target, x, e, x).start()

            return 0

        lax.fori_loop(0, 2, forward, 0)
        up_sum[jj] = dot_tn(buffer[:, 0:D], grad_gu[...]).astype(BF)
        down_sum[jj] = dot_tn(act[...], slot_grad[...]).astype(BF)
        sum_start(jj)
        return 0

    lax.fori_loop(0, lines, expert_chunk, 0)

    for which in range(2):
        box = grad_low if which == 0 else sent
        back_box[which, x, rows(e, capacity), :] = box[rows(mine, capacity), :]
    sum_passed(0, 3)
    for which in range(2):
        others(
            lambda step, other, side, origin: come(which, other, side, other, side).wait_recv()
        )
    for which in range(2):
        back_box[which, 0] = (
            back_box[which, 0].astype(F32) + back_box[which, 1].astype(F32)
        ).astype(BF)

    named = r["rows"][...]
    gain_one, gain_two = named[2:3, :], named[3:4, :]
    vec_zero, vec_one = named[0:1, :], named[1:2, :]
    grad_hidden, grad_attn = ffn.at[0:tok_rows, :], r["grad_attn"]
    thin, wide = r["thin"], r["wide"]
    grad_logits = r["grad_logits"]
    gain_sum = jnp.zeros((1, D), F32)
    for block in range(row_blocks):
        at = slice(block * LANES, (block + 1) * LANES)
        hid = hidden[at, :]
        scale = cols[at, 1:2]
        norm = hid * scale * gain_two
        grad = grad_sum[at, :].astype(F32)
        take_zero, take_one = take[0, at, :], take[1, at, :]
        outs = [dot(take_zero, back_box[0, 0]), dot(take_one, back_box[0, 0])]
        gates = [cols[at, 2:3], cols[at, 3:4]]
        on_normed = cols[at, 4:5]
        const = [
            (cols[at, 6 + 4 * j : 7 + 4 * j], cols[at, 7 + 4 * j : 8 + 4 * j], cols[at, 8 + 4 * j : 9 + 4 * j])
            for j in range(2)
        ]
        on_vec = [a * w for _, a, w in const]
        valid = (iota((LANES, 1), 0) + block * LANES < length).astype(F32)
        mixture = (
            gates[0] * outs[0]
            + gates[1] * outs[1]
            + on_normed * norm
            + on_vec[0] * vec_zero
            + on_vec[1] * vec_one
        )
        r["own_block_out"][at, :] = (valid * (hid + mixture)).astype(BF)
        routes = token_cols[at, 0:2].astype(jnp.int32)
        with_norm = jnp.sum(grad * norm, axis=1, keepdims=True)
        with_vec = [
            jnp.sum(grad * v, axis=1, keepdims=True) for v in (vec_zero, vec_one)
        ]
        gate_grads = []
        for k in range(2):
            value = jnp.sum(grad * outs[k], axis=1, keepdims=True)
            value = value + (routes[:, k : k + 1] == experts + 1).astype(F32) * with_norm
            for j in range(2):
                hit = (routes[:, k : k + 1] == experts + 2 + j).astype(F32)
                value = value + hit * (const[j][0] * with_norm + const[j][1] * with_vec[j])
            gate_grads.append(value)
        mean = gates[0] * gate_grads[0] + gates[1] * gate_grads[1]
        lane = iota((LANES, LANES), 1)
        spread = jnp.zeros((LANES, LANES), F32)
        for k in range(2):
            spread = spread + jnp.where(
                lane == routes[:, k : k + 1], gates[k] * (gate_grads[k] - mean), 0.0
            )
        grad_logits[at, :] = spread[:, 0:gate_cols]
        wide_block = jnp.zeros((LANES, LANES), F32)
        for j in range(2):
            first, second, weight = const[j]
            d_first, d_second = weight * with_norm, weight * with_vec[j]
            centre = first * d_first + second * d_second
            parts = (first * (d_first - centre), second * (d_second - centre))
            for i in range(2):
                high = parts[i].astype(BF).astype(F32)
                at_high = const_col + 2 * j + i
                spread = jnp.where(lane == at_high, high, spread)
                spread = jnp.where(lane == at_high + 4, parts[i] - high, spread)
            high = on_vec[j].astype(BF).astype(F32)
            wide_block = jnp.where(lane == j, high, wide_block)
            wide_block = jnp.where(lane == 2 + j, on_vec[j] - high, wide_block)
        thin[at, :] = spread.astype(BF)
        wide[at, :] = wide_block.astype(BF)
        grad_norm = (
            dot_nt(thin[at, :], small[...])
            + dot(take_zero + take_one, back_box[1, 0])
            + on_normed * grad
        )
        gain_sum = gain_sum + jnp.sum(grad_norm * hid * scale, axis=0, keepdims=True)
        scaled = gain_two * grad_norm
        grad = (
            grad
            + scale * scaled
            - hid * (scale * scale * scale) * jnp.mean(scaled * hid, axis=1, keepdims=True)
        )
        grad_hidden[at, :] = grad
        grad_attn[at, :] = grad.astype(BF)

    sum_passed(3, 1)

    sums = r["sums"]
    own_sums = r["own_sums"]
    own_sums[...] = jnp.zeros_like(own_sums)
    by_small = dot_tn(thin[...], normed_low[...])
    by_vec = dot_tn(wide[...], grad_sum[...])
    own_sums[0:gate_cols, :] = by_small[0:gate_cols, :]
    own_sums[gate_cols : gate_cols + 4, :] = (
        by_small[const_col : const_col + 4, :] + by_small[const_col + 4 : const_col + 8, :]
    )
    own_sums[gate_cols + 4 : gate_cols + 6, :] = by_vec[0:2, :] + by_vec[2:4, :]
    own_sums[gate_cols + 6 : gate_cols + 7, :] = gain_sum
    mix_rows = SMALL_ROWS - 8
    own_sums[mix_rows : mix_rows + gate_cols, 0:gate_cols] = lax.dot_general(
        r["own_prev_in"][...],
        grad_logits[...],
        (((1,), (0,)), ((), ())),
        precision=lax.Precision.HIGHEST,
        preferred_element_type=F32,
    )
    r["own_prev_out"][...] = lax.dot_general(
        r["own_mix"][...].astype(F32),
        grad_logits[...],
        (((1,), (1,)), ((), ())),
        precision=lax.Precision.HIGHEST,
        preferred_element_type=F32,
    )

    store("block_out").start()
    store("prev_out").start()

    dense, ring = r["dense"], RING
    core_box, y_box, x_box = r["core_box"], r["y_box"], r["x_box"]
    z_box, all_box = r["z_box"], r["all_box"]

    def as_chunk(block):
        return block.reshape(lines, 2, 2, 2, quarter, chunk_cols).astype(BF)

    def core_hop(ch):
        return remote(
            dense.at[ch % ring, :, :, 1 - core],
            core_box.at[ch],
            r["gc_send"].at[ch],
            r["gc_recv"].at[ch],
            (twin, s),
        )

    def y_hop(ch):
        return remote(
            core_box.at[ch, :, :, 1 - half],
            y_box.at[ch],
            r["gy_send"].at[ch],
            r["gy_recv"].at[ch],
            (facing, s),
        )

    def x_hop(ch):
        return remote(
            y_box.at[ch, :, 1 - x],
            x_box.at[ch],
            r["gx_send"].at[ch],
            r["gx_recv"].at[ch],
            (e, across),
        )

    batch = chunks // BATCHES

    def z_hop(group, step, origin):
        zz = (z + step) % lines
        span = pl.ds(group * batch, batch)
        return remote(
            x_box.at[span, zz],
            z_box.at[origin, span],
            r["gz_send"].at[group, step],
            r["gz_recv"].at[group, origin],
            (e, 2 * zz + x),
        )

    def all_hop(group, step, origin):
        span = pl.ds(group * batch, batch)
        return remote(
            all_box.at[e, span],
            all_box.at[origin, span],
            r["ga_send"].at[group, step],
            r["ga_recv"].at[group, origin],
            ((e + step) % experts, s),
        )

    def dense_event(it):
        def stage_of(number):
            ch = it - HOPS[number]
            return ch, (ch >= 0) & (ch < chunks)

        ch0, on0 = stage_of(0)

        @pl.when(on0)
        def _():
            core_hop(ch0).start()

        ch1, on1 = stage_of(1)

        @pl.when(on1)
        def _():
            core_hop(ch1).wait_recv()
            core_box[ch1] = summed(core_box[ch1], dense[ch1 % ring, :, :, core])
            y_hop(ch1).start()
            core_hop(ch1).wait_send()

        ch2, on2 = stage_of(2)

        @pl.when(on2)
        def _():
            y_hop(ch2).wait_recv()
            y_box[ch2] = summed(y_box[ch2], core_box[ch2, :, :, half])
            x_hop(ch2).start()

        ch3, on3 = stage_of(3)

        @pl.when(on3)
        def _():
            x_hop(ch3).wait_recv()
            x_box[ch3] = summed(x_box[ch3], y_box[ch3, :, x])

            @pl.when(ch3 % batch == batch - 1)
            def _():
                for step in range(1, lines):
                    z_hop(ch3 // batch, step, z).start()

    def dense_meet(group):
        span = pl.ds(group * batch, batch)
        total = x_box[span, z].astype(F32)
        for step in range(1, lines):
            origin = (z + lines - step) % lines
            z_hop(group, step, origin).wait_recv()
            total = total + z_box[origin, span].astype(F32)
        all_box[e, span] = total.astype(BF)
        for step in range(1, experts):
            all_hop(group, step, e).start()

    def dense_write(group):
        for step in range(1, experts):
            all_hop(group, step, (e + experts - step) % experts).wait_recv()
        for owner in range(experts):
            place = (owner % 2) * 2 + owner // 2
            at = slice(place * quarter, (place + 1) * quarter)
            for ch in range(group * batch, (group + 1) * batch):
                total = all_box[owner, ch].astype(F32)
                if ch < out_chunks:
                    spot = slice(ch * chunk_cols, (ch + 1) * chunk_cols)
                    r["own_out_w_out"][at, spot] = total
                else:
                    for part in range(3):
                        begin_at = part * D + (ch - out_chunks) * LANES
                        r["own_qkv_out"][at, begin_at : begin_at + LANES] = total[
                            :, part * LANES : (part + 1) * LANES
                        ]

    def dense_events_sent():
        def one(ch, _):
            y_hop(ch).wait_send()
            x_hop(ch).wait_send()
            return 0

        lax.fori_loop(0, chunks, one, 0)
        for group in range(BATCHES):
            for step in range(1, lines):
                z_hop(group, step, z).wait_send()
            for step in range(1, experts):
                all_hop(group, step, e).wait_send()

    grad_normed = ffn.at[tok_rows : 2 * tok_rows, :]
    grad_normed[...] = jnp.zeros_like(grad_normed)
    out_grads = dot_tn(mixed[...], grad_attn[...])
    for ch in range(out_chunks):
        dense[ch] = as_chunk(out_grads[:, ch * chunk_cols : (ch + 1) * chunk_cols])

    def attend_back(p):
        query, key, value = heads[p], heads[pairs + p], heads[2 * pairs + p]
        upper = dot_nt(grad_attn[...], weights[rows(p, LANES), 3 * D : 4 * D]).astype(BF)
        grads = []
        for head in range(2):
            scores = dot_nt(key, one_head(query, head)) * score_scale
            probs = jnp.where(
                allowed_pairs(), jnp.exp(scores - log_sums[p, head : head + 1, :]), 0.0
            )
            grad_probs = dot_nt(value, one_head(upper, head))
            delta = jnp.sum(grad_probs * probs, axis=0, keepdims=True)
            grad_scores = (probs * (grad_probs - delta)).astype(BF)
            grads.append(
                (
                    dot_tn(grad_scores, key),
                    dot(grad_scores, query),
                    dot(probs.astype(BF), upper),
                )
            )
        joined = [jnp.where(first_head, a, b) for a, b in zip(*grads)]
        parts = []
        for part in range(3):
            block = joined[part]
            if part < 2:
                block = block * score_scale
                block = block * cosine[...] - swap_halves(block) * sine[...]
            parts.append(block.astype(BF))
        total = grad_normed[...]
        for part in range(3):
            spot = pl.ds(pl.multiple_of(part * D + p * LANES, LANES), LANES)
            total = total + dot_nt(parts[part], weights[:, spot])
        grad_normed[...] = total
        dense[(out_chunks + p) % ring] = as_chunk(
            dot_tn(normed[...], jnp.concatenate(parts, axis=1))
        )

    def back_step(it, _):
        @pl.when(it >= out_chunks)
        def _():
            attend_back(it - out_chunks)

        dense_event(it)

        @pl.when(it == out_chunks + 2)
        def _():
            sum_passed(4, 1)

        @pl.when(it == out_chunks + 5)
        def _():
            sum_passed(5, 1)

        return 0

    def tail_step(it, _):
        dense_event(it)

        return 0

    lax.fori_loop(0, chunks, back_step, 0)

    gain_sum = jnp.zeros((1, D), F32)
    for block in range(row_blocks):
        at = slice(block * LANES, (block + 1) * LANES)
        inputs = tokens[at, :].astype(F32)
        scale = cols[at, 0:1]
        grad_norm = grad_normed[at, :]
        gain_sum = gain_sum + jnp.sum(grad_norm * inputs * scale, axis=0, keepdims=True)
        scaled = gain_one * grad_norm
        grad_hidden[at, :] = (
            grad_hidden[at, :]
            + scale * scaled
            - inputs * (scale * scale * scale) * jnp.mean(scaled * inputs, axis=1, keepdims=True)
        )
    own_sums[gate_cols + 7 : gate_cols + 8, :] = gain_sum

    store("tokens_out").start()

    layer_sums = r["layer_sums"]

    def final_step(index, _):
        sum_final(turn(index))
        return 0

    def sums_z(step, origin):
        return remote(
            sums.at[z],
            sums.at[origin],
            r["az_send"].at[step],
            r["az_recv"].at[origin],
            (e, ((z + step) % lines) * 2 + x),
        )

    def sums_layer(step, side, origin):
        return remote(
            layer_sums.at[mine],
            layer_sums.at[origin],
            r["al_send"].at[step, side],
            r["al_recv"].at[origin],
            ((e + step) % experts, 2 * z + side),
        )

    sums[z] = own_sums[...].astype(BF)
    for step in range(1, lines):
        sums_z(step, z).start()
    lax.fori_loop(chunks, chunks + HOPS[3], tail_step, 0)
    lax.fori_loop(0, lines - 1, final_step, 0)
    for step in range(1, lines):
        sums_z(step, (z + lines - step) % lines).wait_recv()
    total = sums[0].astype(F32)
    for zz in range(1, lines):
        total = total + sums[zz].astype(F32)
    layer_sums[mine] = total
    others(lambda step, other, side, origin: sums_layer(step, side, mine).start())
    sum_passed(6, len(sum_passes))
    for group in range(BATCHES):
        dense_meet(group)
    final_step(lines - 1, 0)
    for group in range(BATCHES):
        dense_write(group)
    others(lambda step, other, side, origin: sums_layer(step, side, origin).wait_recv())
    total = layer_sums[0]
    for other in range(1, layer):
        total = total + layer_sums[other]
    mine_only = pltpu.roll(total, (2 * lines - s) * share % D, 1)[:, 0:share]
    r["own_gate_out"][...] = mine_only[0:gate_cols, :]
    r["own_const_out"][...] = mine_only[gate_cols : gate_cols + 4, :]
    r["own_vec_out"][...] = mine_only[gate_cols + 4 : gate_cols + 6, :]
    r["own_two_out"][...] = mine_only[gate_cols + 6 : gate_cols + 7, :]
    r["own_one_out"][...] = mine_only[gate_cols + 7 : gate_cols + 8, :]
    r["own_mix_out"][...] = total[mix_rows : mix_rows + gate_cols, 0:gate_cols]

    for jj in range(lines):
        final_hop(jj).wait_recv()
        for part in range(2):
            up_out[:, up_columns(part, jj, 1 - x)] = final_box[
                jj, :, part * hidden_block : (part + 1) * hidden_block
            ].astype(F32)

    for name in OUT_NAMES:
        if name not in ("block_out", "prev_out", "tokens_out"):
            store(name).start()

    for kind in range(2):
        dense_sent(kind)
    chain_sent()
    for step in range(1, 2 * lines):
        small_copy(step, s).wait_send()
    for which in range(2):
        others(lambda step, other, side, origin: come(which, other, side, e, x).wait_send())
    sum_sent()
    for jj in range(lines):
        final_hop(jj).wait_send()
    dense_events_sent()
    for step in range(1, lines):
        sums_z(step, z).wait_send()
    others(lambda step, other, side, origin: sums_layer(step, side, mine).wait_send())
    for name in OUT_NAMES:
        store(name).wait()

SMALL_ROWS = 24
IN_NAMES = (
    "length", "tokens", "out_grad", "routes_in", "order_row", "prev_in", "mix",
    "cosine", "sine", "qkv_in", "out_in", "gate_in", "const_in", "vec_in", "one_in", "two_in",
    "up_in", "down_in",
)
LOADED = (
    "qkv_in", "gate_in", "const_in", "vec_in", "one_in", "two_in", "routes_in", "prev_in",
    "order_row", "tokens", "out_in", "down_in", "mix", "cosine", "sine", "out_grad",
)
OUT_NAMES = (
    "block_out", "tokens_out", "prev_out", "qkv_out", "out_w_out", "gate_out", "const_out",
    "vec_out", "one_out", "two_out", "mix_out", "up_out", "down_out",
)


def scratch_list(dims, held):
    tok_rows, experts, lines, share, hidden_block, capacity, gate_cols = dims
    pairs = D // LANES
    chunk_cols = 3 * LANES
    chunks = D // chunk_cols + pairs
    slots = experts * capacity
    gathered = 2 * experts * capacity
    quarter = share // 4
    last = lines - 1
    wide = 2 * hidden_block
    vmem = {
        "weights": ((D, 4 * D), BF),
        "small": ((D, LANES), BF),
        "up": ((lines, D, wide), BF),
        "down": ((lines, hidden_block, D), BF),
        "stage": ((lines, share, wide), BF),
        "put": ((2, slots, tok_rows), BF),
        "take": ((2, tok_rows, slots), BF),
        "rows": ((8, D), F32),
        "cols": ((tok_rows, 16), F32),
        "normed": ((tok_rows, D), BF),
        "heads": ((3 * pairs, tok_rows, LANES), BF),
        "mixed": ((tok_rows, D), BF),
        "log_sums": ((pairs, 8, tok_rows), F32),
        "hidden": ((tok_rows, D), F32),
        "normed_low": ((tok_rows, D), BF),
        "grad_low": ((2 * tok_rows, D), BF),
        "sent": ((gathered, D), BF),
        "sent_wide": ((slots, D + LANES), BF),
        "gate_parts": ((2, tok_rows, LANES), BF),
        "buffer": ((gathered, D + LANES), BF),
        "slot_grad": ((gathered, D), BF),
        "up_sum": ((lines, D, wide), BF),
        "down_sum": ((lines, hidden_block, D), BF),
        "up_box": ((2, last, lines, 2 * share, wide), BF),
        "down_box": ((lines + 1, hidden_block, D), BF),
        "final_box": ((lines, share, wide), BF),
        "ffn": ((gathered, D), F32),
        "slot_back": ((gathered, D), F32),
        "act": ((gathered, hidden_block), BF),
        "grad_gu": ((gathered, wide), BF),
        "back_box": ((2, 2, slots, D), BF),
        "grad_attn": ((tok_rows, D), BF),
        "thin": ((tok_rows, LANES), BF),
        "wide": ((tok_rows, LANES), BF),
        "grad_logits": ((tok_rows, gate_cols), F32),
        "sums": ((lines, SMALL_ROWS, D), BF),
        "own_sums": ((SMALL_ROWS, D), F32),
        "layer_sums": ((2 * experts, SMALL_ROWS, D), F32),
        "dense": ((RING, lines, 2, 2, 2, quarter, chunk_cols), BF),
        "core_box": ((chunks, lines, 2, 2, quarter, chunk_cols), BF),
        "y_box": ((chunks, lines, 2, quarter, chunk_cols), BF),
        "x_box": ((chunks, lines, quarter, chunk_cols), BF),
        "z_box": ((lines, chunks, quarter, chunk_cols), BF),
        "all_box": ((experts, chunks, quarter, chunk_cols), BF),
        "pack": ((LANES, LANES), F32),
        "token_rows": ((16, tok_rows), F32),
        "token_cols": ((tok_rows, 16), F32),
    }
    vmem.update(held)
    sems = {
        "in_sem": (len(LOADED),),
        "out_sem": (len(OUT_NAMES),),
        "up_sem": (2, lines, 2),
        "dz_send": (2, 2, last),
        "dx_send": (2, lines),
        "dc_send": (2, lines, 2),
        "d_recv": (2, lines, 2, 2),
        "dy_send": (2, lines, 2),
        "dr_send": (2, lines, 2),
        "dy_recv": (2, lines, 2, 2),
        "sm_send": (2 * lines,),
        "sm_recv": (2 * lines,),
        "ux_send": (lines,),
        "ux_recv": (lines,),
        "ch_send": (1 + PARTS, 2, last, lines),
        "ch_recv": (1 + PARTS, 2, last, lines),
        "go_send": (2, experts, 2),
        "go_recv": (2, 2 * experts),
        "come_send": (2, experts, 2),
        "come_recv": (2, experts, 2),
        "ru_send": (2, last, lines),
        "ru_recv": (2, last, lines),
        "rd_send": (2, lines, PARTS),
        "rd_recv": (2, lines, PARTS),
        "fx_send": (lines,),
        "fx_recv": (lines,),
        "gc_send": (chunks,),
        "gc_recv": (chunks,),
        "gy_send": (chunks,),
        "gy_recv": (chunks,),
        "gx_send": (chunks,),
        "gx_recv": (chunks,),
        "gz_send": (BATCHES, lines),
        "gz_recv": (BATCHES, lines),
        "ga_send": (BATCHES, experts),
        "ga_recv": (BATCHES, experts),
        "az_send": (lines,),
        "az_recv": (lines,),
        "al_send": (experts, 2),
        "al_recv": (2 * experts,),
    }
    names = tuple(vmem) + tuple(sems)
    shapes = [pltpu.VMEM(*spec) for spec in vmem.values()]
    shapes += [pltpu.SemaphoreType.DMA(shape) for shape in sems.values()]
    return names, shapes


def kernel_body(
    tokens,
    seq_lengths,
    routes,
    pair_order,
    prev_logits,
    out_grad,
    qkv_weight,
    out_weight,
    gate_weight,
    const_weight,
    const_vector,
    norm1_gain,
    norm2_gain,
    gate_mix,
    expert_up,
    expert_down,
):
    tok_rows = tokens.shape[0]
    experts = lax.axis_size("expert")
    shards = lax.axis_size("shard")
    share = qkv_weight.shape[0]
    gate_cols = gate_weight.shape[1]
    hidden_block = expert_down.shape[1]
    capacity = 2 * tok_rows // (experts + 4)
    dims = (tok_rows, experts, shards // 2, share, hidden_block, capacity, gate_cols)
    cosine, sine_table = turn_tables(tok_rows)
    args = (
        seq_lengths,
        tokens,
        out_grad,
        routes.T,
        pair_order,
        prev_logits.T,
        gate_mix,
        cosine,
        sine_table,
        qkv_weight,
        out_weight,
        gate_weight.T,
        const_weight.T,
        const_vector.T,
        norm1_gain[None],
        norm2_gain[None],
        expert_up[0],
        expert_down[0],
    )
    results = (
        ((tok_rows, D), BF),
        ((tok_rows, D), F32),
        ((gate_cols, tok_rows), F32),
        ((share, 3 * D), F32),
        ((share, D), F32),
        ((gate_cols, share), F32),
        ((4, share), F32),
        ((2, share), F32),
        ((1, share), F32),
        ((1, share), F32),
        ((gate_cols, gate_cols), F32),
        ((share, 2 * FF), F32),
        ((hidden_block, D), F32),
    )
    held = {
        "own_" + name: (arg.shape, arg.dtype)
        for name, arg in zip(IN_NAMES, args)
        if name in LOADED and name not in ("qkv_in", "out_in", "down_in")
    }
    held.update(
        {"own_" + name: spec for name, spec in zip(OUT_NAMES, results) if name != "tokens_out"}
    )
    names, shapes = scratch_list(dims, held)
    anywhere = pl.BlockSpec(memory_space=pl.ANY)
    outs = pl.pallas_call(
        functools.partial(step_kernel, dims, names),
        out_shape=tuple(jax.ShapeDtypeStruct(*spec) for spec in results),
        in_specs=[pl.BlockSpec(memory_space=pltpu.SMEM)] + [anywhere] * (len(args) - 1),
        out_specs=(anywhere,) * len(OUT_NAMES),
        scratch_shapes=shapes,
        compiler_params=pltpu.CompilerParams(
            collective_id=0, has_side_effects=True, vmem_limit_bytes=VMEM_BYTES
        ),
        name="step",
    )(*args)
    (
        block_out,
        tokens_grad,
        prev_grad,
        qkv_grad,
        out_w_grad,
        gate_grad,
        const_grad,
        vec_grad,
        one_grad,
        two_grad,
        mix_grad,
        up_grad,
        down_grad,
    ) = hand_over(outs)
    return (
        block_out,
        tokens_grad,
        prev_grad.T,
        qkv_grad,
        out_w_grad,
        gate_grad.T,
        const_grad.T,
        vec_grad.T,
        one_grad[0],
        two_grad[0],
        mix_grad,
        up_grad[None],
        down_grad[None],
    )


def copy_kernel(count, *refs):
    held = refs[2 * count : 3 * count]
    in_sems, out_sems = refs[3 * count :]
    reads = [pltpu.make_async_copy(refs[i], held[i], in_sems.at[i]) for i in range(count)]
    writes = [
        pltpu.make_async_copy(held[i], refs[count + i], out_sems.at[i]) for i in range(count)
    ]
    for copy in reads:
        copy.start()
    for read, write in zip(reads, writes):
        read.wait()
        write.start()
    for copy in writes:
        copy.wait()


def hand_over(arrays):
    count = len(arrays)
    anywhere = pl.BlockSpec(memory_space=pl.ANY)
    return pl.pallas_call(
        functools.partial(copy_kernel, count),
        out_shape=tuple(jax.ShapeDtypeStruct(a.shape, a.dtype) for a in arrays),
        in_specs=[anywhere] * count,
        out_specs=(anywhere,) * count,
        scratch_shapes=[pltpu.VMEM(a.shape, a.dtype) for a in arrays]
        + [pltpu.SemaphoreType.DMA((count,))] * 2,
        name="hand_over",
    )(*arrays)


def turn_tables(tok_rows):
    half_dim = HEAD_DIM // 2
    steps = np.arange(half_dim, dtype=np.float32) * np.float32(2.0 / HEAD_DIM)
    frequency = np.power(np.float32(rotary_base), -steps).astype(np.float32)
    angles = np.arange(tok_rows, dtype=np.float32)[:, None] * frequency[None, :]
    cosine = np.cos(angles.astype(np.float64)).astype(np.float32)
    sine = np.sin(angles.astype(np.float64)).astype(np.float32)
    cosine = np.tile(cosine, (1, LANES // half_dim))
    sine = np.tile(np.concatenate([-sine, sine], axis=1), (1, LANES // HEAD_DIM))
    return jnp.asarray(cosine), jnp.asarray(sine)


def fits_kernel(mesh):
    experts, shards = mesh.shape["expert"], mesh.shape["shard"]
    share, hidden_block = D // shards, FF // shards
    return (
        experts == 4
        and shards % 2 == 0
        and share % 96 == 0
        and hidden_block % LANES == 0
    )


def solution(mesh):
    placed = (
        P(("expert", "shard"), None),
        P(("expert", "shard")),
        P(("expert", "shard"), None),
        P(("expert", "shard"), None),
        P(("expert", "shard"), None),
        P(("expert", "shard"), None),
        P("shard", None),
        P("shard", None),
        P("shard", None),
        P("shard", None),
        P("shard", None),
        P("shard"),
        P("shard"),
        P(),
        P("expert", "shard", None),
        P("expert", "shard", None),
    )
    return jax.shard_map(
        kernel_body if fits_kernel(mesh) else body,
        mesh=mesh,
        in_specs=placed,
        out_specs=(
            P(("expert", "shard"), None),
            P(("expert", "shard"), None),
            P(("expert", "shard"), None),
            P("shard", None),
            P("shard", None),
            P("shard", None),
            P("shard", None),
            P("shard", None),
            P("shard"),
            P("shard"),
            P(),
            P("expert", "shard", None),
            P("expert", "shard", None),
        ),
        check_vma=False,
    )
```
